32 devices in a mesh: dp: 8 (over z, x), fsdp: 4 (over y, core).
Axes of the slice: x: 2, y: 2, z: 4, core: 2. Of those that a mesh axis runs over, the one named last changes fastest.
Arguments:
- tokens: bfloat16 [32, 512, 1536], P(('dp', 'fsdp')), may hold values from -6 to 6
- seg_ids: int32 [16, 4], replicated, may hold values from 0 to 3
- timesteps: int32 [16], replicated, may hold values from 0 to 999
- labels: int32 [16], replicated, may hold values from 0 to 999
- cotangent: bfloat16 [32, 512, 1536], P(('dp', 'fsdp')), may hold values from -6 to 6
- mod_weight: bfloat16 [1536, 9216], P(('dp', 'fsdp')), may hold values from -0.15625 to 0.15625
- class_table: bfloat16 [1000, 1536], P(None, ('dp', 'fsdp')), may hold values from -6 to 6
- attn_kernel: bfloat16 [9, 1536], P(None, ('dp', 'fsdp')), may hold values from -2 to 2
- qkv_weight: bfloat16 [1536, 4608], P(('dp', 'fsdp')), may hold values from -0.15625 to 0.15625
- proj_weight: bfloat16 [1536, 1536], P(('dp', 'fsdp')), may hold values from -1.25 to 1.25
- up_weight: bfloat16 [1536, 6144], P(('dp', 'fsdp')), may hold values from -0.15625 to 0.15625
- ffn_kernel: bfloat16 [9, 6144], P(None, ('dp', 'fsdp')), may hold values from -2 to 2
- down_weight: bfloat16 [6144, 1536], P(('dp', 'fsdp')), may hold values from -0.078125 to 0.078125
Outputs:
- layer_out: bfloat16 [32, 512, 1536], P(('dp', 'fsdp'))
- input_grad: float32 [32, 512, 1536], P(('dp', 'fsdp'))
- mod_grad: float32 [1536, 9216], P(('dp', 'fsdp'))
- table_grad: float32 [1000, 1536], P(None, ('dp', 'fsdp'))
- attn_kernel_grad: float32 [9, 1536], P(None, ('dp', 'fsdp'))
- qkv_grad: float32 [1536, 4608], P(('dp', 'fsdp'))
- proj_grad: float32 [1536, 1536], P(('dp', 'fsdp'))
- up_grad: float32 [1536, 6144], P(('dp', 'fsdp'))
- ffn_kernel_grad: float32 [9, 6144], P(None, ('dp', 'fsdp'))
- down_grad: float32 [6144, 1536], P(('dp', 'fsdp'))
- shift_grad: float32 [32, 1536], P(('dp', 'fsdp'))
The draws below stay inside these ranges and needn't reach their ends.
All inputs are finite; a program needn't handle non-finite values.
Results may differ from the reference program's by a relative error of at most 0.018.
The reference program's roundings to bfloat16 on the way count: a program that leaves them out, or rounds other values in their place, can miss the bound.
Values may be sent and summed in bfloat16 or wider, within the bound.
A program may use at most 448 MiB of HBM per device.

```python
import math
import jax
import jax.numpy as jnp
from jax import lax

D = 1536
HEADS = 24
HEAD = 64
FF = 6144
NCLASS = 1000
SIDE = 32
CAN_PAIR = 1
PAIRS = 16
CANVASES = 16
HALVES = 32
HALF_TOK = 512


def with_ends(drawn, rng, smallest, high):
    longest = drawn.shape.index(max(drawn.shape))
    spots = []
    for shift in (0, 1):
        where = [jax.random.randint(jax.random.fold_in(rng, axis), (), 0, length) for axis, length in enumerate(drawn.shape)]
        where[longest] = (where[longest] + shift) % drawn.shape[longest]
        spots.append(tuple(where))
    return drawn.at[spots[0]].set(smallest).at[spots[1]].set(high)


def shard_levels(key, shape, cuts, least, top_value):
    gain = 1.0
    for dim, parts in cuts:
        heights = jax.random.uniform(jax.random.fold_in(jax.random.fold_in(key, 6), dim), (parts,), jnp.float32, least / len(cuts), top_value / len(cuts))
        gain = gain * jnp.repeat(jnp.exp(heights), shape[dim] // parts).reshape((-1,) + (1,) * (len(shape) - 1 - dim))
    return gain


def scatter_about(key, extent, scale, most, cuts=(), kind=jnp.bfloat16):
    level = shard_levels(key, extent, cuts, -0.22, 0.18) if cuts else 1.0
    entries = jax.random.normal(key, extent, jnp.float32) * scale * level
    return jnp.minimum(jnp.maximum(entries, -most), most).astype(kind)


def setup_inputs(seed: int = 0) -> dict:
    key_list = jax.random.split(jax.random.key(seed), 14)
    return {
        "tokens": scatter_about(key_list[0], (HALVES, HALF_TOK, D), 1.0, 6.0, ((0, 32),)),
        "seg_ids": with_ends(jax.random.randint(key_list[1], (CANVASES, 4), 0, 4), jax.random.fold_in(key_list[1], 1), 0, 3).astype(jnp.int32),
        "timesteps": with_ends(jax.random.randint(key_list[2], (CANVASES,), 0, 1000), jax.random.fold_in(key_list[2], 1), 0, 999).astype(jnp.int32),
        "labels": with_ends(jax.random.randint(key_list[3], (CANVASES,), 0, NCLASS), jax.random.fold_in(key_list[3], 1), 0, NCLASS - 1).astype(jnp.int32),
        "cotangent": scatter_about(key_list[4], (HALVES, HALF_TOK, D), 1.0, 6.0, ((0, 32),)),
        "mod_weight": scatter_about(key_list[5], (D, 6 * D), D ** -0.5, 0.15625, ((0, 32),)),
        "class_table": scatter_about(key_list[6], (NCLASS, D), 1.0, 6.0, ((1, 32),)),
        "attn_kernel": scatter_about(key_list[7], (9, D), 9 ** -0.5, 2.0, ((1, 32),)),
        "qkv_weight": scatter_about(key_list[8], (D, 3 * D), D ** -0.5, 0.15625, ((0, 32),)),
        "proj_weight": scatter_about(key_list[9], (D, D), (D // 64) ** -0.5, 1.25, ((0, 32),)),
        "up_weight": scatter_about(key_list[10], (D, FF), D ** -0.5, 0.15625, ((0, 32),)),
        "ffn_kernel": scatter_about(key_list[11], (9, FF), 9 ** -0.5, 2.0, ((1, 32),)),
        "down_weight": scatter_about(key_list[12], (FF, D), FF ** -0.5, 0.078125, ((0, 32),)),
    }


highest = lax.Precision.HIGHEST
ln_epsilon = 1e-06
masked_score = -1000000000.0

@jax.custom_vjp
def low(v):
    return lax.optimization_barrier(v.astype(jnp.bfloat16)).astype(jnp.float32)

@jax.custom_vjp
def low_back(v):
    return v

def low_keep(v):
    return (low(v), None)

def low_pass(kept, grad):
    return (grad,)

def back_keep(v):
    return (v, None)

def back_low(kept, grad):
    return (low(grad),)
low.defvjp(low_keep, low_pass)
low_back.defvjp(back_keep, back_low)

def rounded_both(values):
    return low_back(low(values))

def product(left, right):
    return jnp.dot(left, right, precision=highest)

def layer_norm(values):
    average = lax.optimization_barrier(jnp.mean(values, axis=-1, keepdims=True))
    centred = values - average
    variance = lax.optimization_barrier(jnp.mean(centred * centred, axis=-1, keepdims=True))
    return centred * lax.rsqrt(variance + ln_epsilon)

def sinusoid(steps_in):
    halfway = D // 2
    frequency = jnp.exp(-math.log(10000.0) * jnp.arange(halfway, dtype=jnp.float32) / halfway)
    angles = steps_in.astype(jnp.float32)[..., None] * frequency
    return jnp.concatenate([jnp.cos(angles), jnp.sin(angles)], axis=-1)

def depthwise(grid_values, kernel):
    padded = jnp.pad(grid_values, ((1, 1), (1, 1), (0, 0)))
    result = jnp.zeros_like(grid_values)
    for tap_index in range(9):
        row_shift = tap_index // 3
        column_shift = tap_index % 3
        result = result + padded[row_shift:row_shift + SIDE, column_shift:column_shift + SIDE] * kernel[tap_index]
    return result

def segment_mask(quadrant_ids):
    halves_of = jnp.arange(SIDE) // (SIDE // 2)
    quadrants = 2 * halves_of[:, None] + halves_of[None, :]
    matches = quadrants[:, :, None] == jnp.arange(4)[None, None, :]
    segment = lax.optimization_barrier(jnp.sum(jnp.where(matches, quadrant_ids[None, None, :], 0), axis=2))
    grouped = segment.reshape(SIDE // 2, 2, SIDE // 2, 2).transpose(1, 3, 0, 2).reshape(4, -1)
    return grouped[:, :, None] == grouped[:, None, :]

def attend(queries, key_rows, value_rows, allowed):

    def phased(block_in):
        return block_in.reshape(SIDE // 2, 2, SIDE // 2, 2, HEADS, HEAD).transpose(1, 3, 4, 0, 2, 5).reshape(4, HEADS, -1, HEAD)
    query_ph, key_ph, value_ph = (phased(queries), phased(key_rows), phased(value_rows))
    raw_scores = jnp.einsum('phqe,phke->phqk', query_ph, key_ph, precision=highest) * HEAD ** (-0.5)
    scores = low_back(jnp.where(allowed[:, None], raw_scores, masked_score))
    probs = low(jax.nn.softmax(scores, axis=-1))
    mixed_ph = jnp.einsum('phqk,phke->phqe', probs, value_ph, precision=highest)
    return mixed_ph.reshape(2, 2, HEADS, SIDE // 2, SIDE // 2, HEAD).transpose(3, 0, 4, 1, 2, 5).reshape(SIDE * SIDE, D)

def canvas_forward(weights_in, canvas, shift_extra, quadrant_ids, step_id, label_id):
    mod_weight, class_table, attn_kernel, qkv_weight, proj_weight, up_weight, ffn_kernel, down_weight = weights_in
    cond = sinusoid(step_id) + lax.dynamic_index_in_dim(class_table, label_id, 0, keepdims=False)
    lifted = low(jax.nn.silu(cond))
    mods = low_back(product(lifted[None, :], mod_weight)[0])
    shift_a, scale_a, gate_a, shift_f, scale_f, gate_f = jnp.split(mods, 6)
    normed_a = layer_norm(canvas) * (1.0 + scale_a) + shift_a
    convolved = low(depthwise(normed_a.reshape(SIDE, SIDE, D), attn_kernel).reshape(SIDE * SIDE, D))
    qkv = product(convolved, qkv_weight)
    queries = rounded_both(qkv[:, :D])
    key_rows = rounded_both(qkv[:, D:2 * D])
    value_rows = rounded_both(qkv[:, 2 * D:])
    allowed = segment_mask(quadrant_ids)
    attended = rounded_both(jax.checkpoint(attend)(queries, key_rows, value_rows, allowed))
    branch_a = low_back(product(attended, proj_weight))
    middle = canvas + gate_a * branch_a
    extra_rows = jnp.repeat(shift_extra, HALF_TOK, axis=0)
    normed_f = low(layer_norm(middle) * (1.0 + scale_f) + shift_f + extra_rows)
    hidden = low_back(product(normed_f, up_weight))
    widened = depthwise(hidden.reshape(SIDE, SIDE, FF), ffn_kernel).reshape(SIDE * SIDE, FF)
    activated = low(jax.nn.gelu(widened, approximate=True))
    branch_f = low_back(product(activated, down_weight))
    return middle + gate_f * branch_f

def to_canvases(halves_in):
    return halves_in.reshape(PAIRS, 2, CAN_PAIR, HALF_TOK, -1).transpose(0, 2, 1, 3, 4).reshape(CANVASES, 2 * HALF_TOK, -1)

def to_halves(canvases_in):
    return canvases_in.reshape(PAIRS, CAN_PAIR, 2, HALF_TOK, -1).transpose(0, 2, 1, 3, 4).reshape(HALVES, HALF_TOK, -1)

def reference(tokens, seg_ids, timesteps, labels, cotangent, mod_weight, class_table, attn_kernel, qkv_weight, proj_weight, up_weight, ffn_kernel, down_weight):
    weights_in = tuple((matrix.astype(jnp.float32) for matrix in (mod_weight, class_table, attn_kernel, qkv_weight, proj_weight, up_weight, ffn_kernel, down_weight)))
    canvases = to_canvases(tokens.astype(jnp.float32))
    upstream = to_canvases(cotangent.astype(jnp.float32))

    def canvas_step(running, item_in):
        canvas, canvas_grad, quadrant_ids, step_id, label_id = item_in

        def forward(weights_arg, canvas_arg, extra_arg):
            return canvas_forward(weights_arg, canvas_arg, extra_arg, quadrant_ids, step_id, label_id)
        extra_zero = jnp.zeros((2, D), jnp.float32)
        result, pull_back = jax.vjp(forward, weights_in, canvas, extra_zero)
        weight_grads, canvas_input_grad, extra_grad = pull_back(canvas_grad)
        return (jax.tree.map(jnp.add, running, weight_grads), (result, canvas_input_grad, extra_grad))
    zero_grads = jax.tree.map(jnp.zeros_like, weights_in)
    totals, (results, input_grads, extra_grads) = lax.scan(canvas_step, zero_grads, (canvases, upstream, seg_ids, timesteps, labels))
    layer_out = to_halves(results).astype(jnp.bfloat16)
    input_grad = to_halves(input_grads)
    shift_grad = extra_grads.reshape(PAIRS, CAN_PAIR, 2, D).transpose(0, 2, 1, 3).reshape(HALVES, D)
    return (layer_out, input_grad, totals[0], totals[1], totals[2], totals[3], totals[4], totals[5], totals[6], totals[7], shift_grad)
```

```python
import functools
import math

import jax
import jax.numpy as jnp
from jax import lax
from jax.experimental import pallas as pl
from jax.experimental.pallas import tpu as pltpu
from jax.sharding import PartitionSpec as P

HEAD = 64
SIDE = 32
HALF_SIDE = SIDE // 2
STRIP = HALF_SIDE
PLANE = HALF_SIDE * HALF_SIDE
PADDED = PLANE + 2 * STRIP
TILE = 256
CHUNKS = 3

highest = lax.Precision.HIGHEST
ln_epsilon = 1e-06
masked_score = -1000000000.0
low = jnp.bfloat16
full = jnp.float32
AXES = ("dp", "fsdp")


def device_count():
    return lax.axis_size("dp") * lax.axis_size("fsdp")


def swap(x, bit):
    return lax.ppermute(x, AXES, [(i, i ^ 1 << bit) for i in range(device_count())])


def swap_core(x):
    return swap(x, 0)


def gather_order(chip_bits, colour):
    order = list(range(chip_bits - 1, -1, -1))
    if colour and chip_bits > 1:
        order[-1], order[-2] = order[-2], order[-1]
    return order


def gather_pieces(shard, order):
    pieces = [shard[None]]
    for step, bit in enumerate(order):
        pieces = pieces + [swap(piece, bit + 1) for piece in pieces]
        if len(pieces) == 4 and step + 1 < len(order):
            pieces = [jnp.concatenate(pieces, axis=0)]
    return pieces


def assemble_body(steps, chip_ref, *refs):
    *piece_refs, out_ref = refs
    which = pl.program_id(0) // steps
    top = chip_ref[1]
    for index, piece_ref in enumerate(piece_refs):

        @pl.when(which == index)
        def _():
            for k in range(4):
                out_ref[jnp.bitwise_xor(top, (k & 1) << 1 | k >> 1), 0] = piece_ref[k]


def assemble(pieces, order, chip):
    chips = sum(piece.shape[0] for piece in pieces)
    rows, columns = pieces[0].shape[1:]
    if chips < 4 or len(pieces) * pieces[0].shape[0] != chips or pieces[0].shape[0] % 4:
        raise ValueError("unexpected mesh")
    rest = len(order) - 2
    steps = pieces[0].shape[0] // 4
    chip_words = jnp.stack([jnp.bitwise_and(chip, (1 << rest) - 1), chip >> rest]).astype(jnp.int32)

    def out_map(step, words):
        at = words[0]
        for position, bit in enumerate(order[2:]):
            at = jnp.bitwise_xor(at, jnp.bitwise_and(step >> position, 1) << bit)
        return (0, at, 0, 0)

    def piece_map(index):
        return lambda step, words: (jnp.clip(step - index * steps, 0, steps - 1), 0, 0)

    out = pl.pallas_call(
        functools.partial(assemble_body, steps),
        grid_spec=pltpu.PrefetchScalarGridSpec(
            num_scalar_prefetch=1,
            grid=(chips // 4,),
            in_specs=[
                pl.BlockSpec((4, rows, columns), piece_map(index)) for index in range(len(pieces))
            ],
            out_specs=pl.BlockSpec((4, 1, rows, columns), out_map),
        ),
        out_shape=jax.ShapeDtypeStruct((4, chips // 4, rows, columns), pieces[0].dtype),
        cost_estimate=pl.CostEstimate(
            flops=0, bytes_accessed=4 * chips * rows * columns, transcendentals=0
        ),
        name="assemble",
    )(chip_words, *pieces)
    return out.reshape(chips, rows, columns)


def gather_weights(shard, colour, chip, chip_bits):
    order = gather_order(chip_bits, colour)
    return assemble(gather_pieces(shard, order), order, chip)


def at_bit(array, axis, bit):
    return lax.dynamic_index_in_dim(array, bit, axis, keepdims=False)


def scatter_sum(parts, colour, chip, chip_bits, sent=low):
    order = gather_order(chip_bits, colour)[::-1]
    left = list(range(chip_bits - 1, -1, -1))
    held = [parts.reshape((2,) * chip_bits + parts.shape[1:])]
    for bit in order:
        axis = left.index(bit)
        left.remove(bit)
        mine = jnp.bitwise_and(chip >> bit, 1)
        leaving = sum(at_bit(h, axis, 1 - mine).astype(full) for h in held).astype(sent)
        staying = sum(at_bit(h, axis, mine).astype(full) for h in held).astype(sent)
        held = [staying, swap(leaving, bit + 1)]
    return held[0].astype(full) + held[1].astype(full)


def gather_rows(row, chip, chip_bits):
    order = gather_order(chip_bits, 0)
    held = row[None]
    for bit in order:
        held = jnp.concatenate([held, swap(held, bit + 1)], axis=0)
    places = jnp.arange(1 << chip_bits)
    position = jnp.zeros_like(places)
    apart = jnp.bitwise_xor(places, chip)
    for step, bit in enumerate(order):
        position = position + (jnp.bitwise_and(apart >> bit, 1) << step)
    pick = position[:, None] == places[None, :]
    return jnp.dot(pick.astype(held.dtype), held, preferred_element_type=full).astype(held.dtype)


def to_phases(block_in, row_count):
    width = block_in.shape[-1]
    split_grid = block_in.reshape(row_count // 2, 2, HALF_SIDE, 2, width)
    return split_grid.transpose(1, 3, 0, 2, 4).reshape(4, row_count // 2 * HALF_SIDE, width)


def from_phases(block_in, row_count):
    width = block_in.shape[-1]
    split_grid = block_in.reshape(2, 2, row_count // 2, HALF_SIDE, width)
    return split_grid.transpose(2, 0, 3, 1, 4).reshape(row_count * SIDE, width)


def in_core_order(mine, other, core):
    return jnp.where(core == 0, mine, other), jnp.where(core == 0, other, mine)


def join_halves(mine, other, core):
    return jnp.stack(in_core_order(mine, other, core), axis=1).reshape(-1, mine.shape[-1])


def half_of(joined, which):
    width = joined.shape[-1]
    return at_bit(joined.reshape(4, 2, -1, width), 1, which)


def layer_norm(values):
    average = jnp.mean(values, axis=-1, keepdims=True)
    centred = values - average
    variance = jnp.mean(centred * centred, axis=-1, keepdims=True)
    return centred * lax.rsqrt(variance + ln_epsilon)


def modulate(values, shift_by, scale_by):
    return layer_norm(values) * (1.0 + scale_by) + shift_by


def sinusoid(steps_in, width):
    halfway = width // 2
    frequency = jnp.exp(-math.log(10000.0) * jnp.arange(halfway, dtype=jnp.float32) / halfway)
    angles = steps_in.astype(jnp.float32)[..., None] * frequency
    return jnp.concatenate([jnp.cos(angles), jnp.sin(angles)], axis=-1)


def depthwise(framed, kernel):
    row_count = framed.shape[0] - 2
    result = jnp.zeros((row_count, SIDE, framed.shape[2]), jnp.float32)
    for tap in range(9):
        r, s = divmod(tap, 3)
        result = result + framed[r : r + row_count, s : s + SIDE] * kernel[tap].astype(full)
    return result


def kernel_grad(framed, upstream):
    row_count = upstream.shape[0]
    sums = []
    for tap in range(9):
        r, s = divmod(tap, 3)
        sums.append(jnp.sum(framed[r : r + row_count, s : s + SIDE] * upstream, axis=(0, 1)))
    return jnp.stack(sums)


def softmax_of(query, key, allowed):
    raw = lax.dot_general(query, key, (((1,), (1,)), ((), ())), preferred_element_type=full)
    scores = jnp.where(allowed, raw * HEAD ** (-0.5), masked_score)
    shifted = jnp.exp(scores - jnp.max(scores, axis=-1, keepdims=True))
    return shifted / jnp.sum(shifted, axis=-1, keepdims=True)


def head_lanes(shape, head):
    lanes = lax.broadcasted_iota(jnp.int32, shape, 1)
    return jnp.logical_and(lanes >= head * HEAD, lanes < (head + 1) * HEAD)


def attend_body(mask_ref, qkv_ref, out_ref):
    allowed = mask_ref[...] > 0.5

    @pl.loop(0, 4)
    def _(phase):
        rows = pl.ds(pl.multiple_of(phase * PLANE, PLANE), PLANE)
        query = qkv_ref[rows, :128]
        key = qkv_ref[rows, 128:256]
        value = qkv_ref[rows, 256:]
        total = None
        for head in range(2):
            here = head_lanes(key.shape, head)
            probs = softmax_of(query, jnp.where(here, key, jnp.zeros_like(key)), allowed)
            part = jnp.dot(
                probs.astype(low),
                jnp.where(here, value, jnp.zeros_like(value)),
                preferred_element_type=full,
            )
            total = part if total is None else total + part
        out_ref[rows, :] = total.astype(low)


def attend_back_body(mask_ref, qkv_ref, grad_ref, out_ref):
    allowed = mask_ref[...] > 0.5

    @pl.loop(0, 4)
    def _(phase):
        rows = pl.ds(pl.multiple_of(phase * PLANE, PLANE), PLANE)
        query = qkv_ref[rows, :128]
        key = qkv_ref[rows, 128:256]
        value = qkv_ref[rows, 256:]
        grad = grad_ref[rows, :]
        by_rows = (((0,), (0,)), ((), ()))
        totals = [None, None, None]
        for head in range(2):
            here = head_lanes(key.shape, head)
            blank = jnp.zeros_like(key)
            key_here = jnp.where(here, key, blank)
            query_here = jnp.where(here, query, blank)
            value_here = jnp.where(here, value, blank)
            grad_here = jnp.where(here, grad, blank)
            weights = softmax_of(query, key_here, allowed)
            grad_probs = lax.dot_general(
                grad, value_here, (((1,), (1,)), ((), ())), preferred_element_type=full
            )
            delta = jnp.sum(grad_probs * weights, axis=-1, keepdims=True)
            grad_scores = (weights * (grad_probs - delta)).astype(low)
            parts = (
                jnp.dot(grad_scores, key_here, preferred_element_type=full),
                lax.dot_general(grad_scores, query_here, by_rows, preferred_element_type=full),
                lax.dot_general(
                    weights.astype(low), grad_here, by_rows, preferred_element_type=full
                ),
            )
            totals = [p if t is None else t + p for t, p in zip(totals, parts)]
        out_ref[rows, :128] = (totals[0] * HEAD ** (-0.5)).astype(low)
        out_ref[rows, 128:256] = (totals[1] * HEAD ** (-0.5)).astype(low)
        out_ref[rows, 256:] = totals[2].astype(low)


def attend(mask, qkv):
    tokens, width = qkv.shape
    pairs = width // 384
    return pl.pallas_call(
        attend_body,
        grid=(pairs,),
        in_specs=[
            pl.BlockSpec((PLANE, PLANE), lambda j: (0, 0)),
            pl.BlockSpec((tokens, 384), lambda j: (0, j)),
        ],
        out_specs=pl.BlockSpec((tokens, 128), lambda j: (0, j)),
        out_shape=jax.ShapeDtypeStruct((tokens, pairs * 128), low),
        cost_estimate=pl.CostEstimate(
            flops=pairs * 2 * 4 * 4 * PLANE * PLANE * 256,
            bytes_accessed=8 * tokens * pairs * 128,
            transcendentals=pairs * 8 * PLANE * PLANE,
        ),
        name="attend",
    )(mask, qkv)


def attend_back(mask, qkv, grad):
    tokens, width = qkv.shape
    pairs = width // 384
    return pl.pallas_call(
        attend_back_body,
        grid=(pairs,),
        in_specs=[
            pl.BlockSpec((PLANE, PLANE), lambda j: (0, 0)),
            pl.BlockSpec((tokens, 384), lambda j: (0, j)),
            pl.BlockSpec((tokens, 128), lambda j: (0, j)),
        ],
        out_specs=pl.BlockSpec((tokens, 384), lambda j: (0, j)),
        out_shape=jax.ShapeDtypeStruct((tokens, width), low),
        cost_estimate=pl.CostEstimate(
            flops=pairs * 2 * 4 * 10 * PLANE * PLANE * 256,
            bytes_accessed=14 * tokens * pairs * 128,
            transcendentals=pairs * 8 * PLANE * PLANE,
        ),
        name="attend_back",
    )(mask, qkv, grad)


def strip_at(ref, row_phase, column_phase, row):
    start = pl.multiple_of((row + 1) * STRIP, STRIP)
    return ref[2 * row_phase + column_phase, pl.ds(start, STRIP), :]


def near_strips(ref, row):
    tokens = lax.broadcasted_iota(jnp.int32, (STRIP, ref.shape[-1]), 0)
    loaded = {}
    for row_phase, at in ((1, row - 1), (0, row), (1, row), (0, row + 1)):
        even = strip_at(ref, row_phase, 0, at)
        odd = strip_at(ref, row_phase, 1, at)
        before = jnp.where(tokens == 0, 0.0, pltpu.roll(odd, 1, 0))
        after = jnp.where(tokens == STRIP - 1, 0.0, pltpu.roll(even, STRIP - 1, 0))
        loaded[len(loaded)] = ((before, even, odd), (even, odd, after))
    return {0: (loaded[0], loaded[1], loaded[2]), 1: (loaded[1], loaded[2], loaded[3])}


def conv_strip(near, kernel, row_phase, column_phase):
    total = None
    for i in range(3):
        for j in range(3):
            term = near[row_phase][i][column_phase][j] * kernel[3 * i + j : 3 * i + j + 1, :]
            total = term if total is None else total + term
    return total


def feed_body(
    norm_ref,
    norm_t_ref,
    grad_ref,
    up_ref,
    down_ref,
    kernel_ref,
    branch_ref,
    back_ref,
    up_grad_ref,
    down_grad_ref,
    kernel_grad_ref,
    branch_acc,
    back_acc,
    hidden,
    widened_grad,
    act_grad,
    act,
    hidden_grad,
):
    step = pl.program_id(0)
    by_columns = (((1,), (1,)), ((), ()))
    width = up_ref.shape[1]

    @pl.when(step == 0)
    def _():
        blank = jnp.zeros((STRIP, width), full)
        for plane in range(4):
            for ref in (hidden, widened_grad):
                ref[plane, pl.ds(0, STRIP), :] = blank
                ref[plane, pl.ds(PLANE + STRIP, STRIP), :] = blank
        branch_acc[...] = jnp.zeros_like(branch_acc)
        back_acc[...] = jnp.zeros_like(back_acc)

    @pl.loop(0, 4)
    def _(plane):
        rows = pl.ds(pl.multiple_of(plane * PLANE, PLANE), PLANE)
        hidden[plane, pl.ds(STRIP, PLANE), :] = jnp.dot(
            norm_ref[rows, :], up_ref[...], preferred_element_type=full
        )
        act_grad[rows, :] = lax.dot_general(
            grad_ref[rows, :], down_ref[...], by_columns, preferred_element_type=full
        )

    kernel = kernel_ref[...]

    def forward_strip(row, sums):
        near = near_strips(hidden, row)
        sums = list(sums)
        for row_phase in range(2):
            for column_phase in range(2):
                plane = 2 * row_phase + column_phase
                wide = conv_strip(near, kernel, row_phase, column_phase)
                square = wide * wide
                bend = math.sqrt(2.0 / math.pi) * (wide + 0.044715 * wide * square)
                curve = jnp.tanh(bend)
                half = 0.5 * (1.0 + curve)
                slope = half + 0.5 * wide * (1.0 - curve * curve) * (
                    math.sqrt(2.0 / math.pi) * (1.0 + 3 * 0.044715 * square)
                )
                at = pl.ds(pl.multiple_of(plane * PLANE + row * STRIP, STRIP), STRIP)
                act[at, :] = (wide * half).astype(low)
                grad_here = slope * act_grad[at, :]
                widened_grad[plane, pl.ds(pl.multiple_of((row + 1) * STRIP, STRIP), STRIP), :] = (
                    grad_here
                )
                for i in range(3):
                    for j in range(3):
                        product = near[row_phase][i][column_phase][j] * grad_here
                        sums[3 * i + j] = sums[3 * i + j] + (product[:8] + product[8:])
        return tuple(sums)

    sums = lax.fori_loop(
        0, HALF_SIDE, forward_strip, tuple(jnp.zeros((8, width), full) for _ in range(9))
    )
    kernel_grad_ref[...] = jnp.concatenate(
        [jnp.sum(s, axis=0, keepdims=True) for s in sums] + [jnp.zeros((7, width), full)], axis=0
    )

    flipped = [kernel[8 - t : 9 - t, :] for t in range(9)]
    flipped = jnp.concatenate(flipped, axis=0)

    @pl.loop(0, HALF_SIDE)
    def _(row):
        near = near_strips(widened_grad, row)
        for row_phase in range(2):
            for column_phase in range(2):
                plane = 2 * row_phase + column_phase
                at = pl.ds(pl.multiple_of(plane * PLANE + row * STRIP, STRIP), STRIP)
                hidden_grad[at, :] = conv_strip(near, flipped, row_phase, column_phase).astype(low)

    @pl.loop(0, 4)
    def _(plane):
        rows = pl.ds(pl.multiple_of(plane * PLANE, PLANE), PLANE)
        branch_acc[rows, :] += jnp.dot(act[rows, :], down_ref[...], preferred_element_type=full)
        back_acc[rows, :] += lax.dot_general(
            hidden_grad[rows, :], up_ref[...], by_columns, preferred_element_type=full
        )

    model = norm_t_ref.shape[0]

    @pl.loop(0, model // TILE)
    def _(tile):
        rows = pl.ds(pl.multiple_of(tile * TILE, TILE), TILE)
        up_grad_ref[rows, :] = jnp.dot(
            norm_t_ref[rows, :], hidden_grad[...], preferred_element_type=full
        ).astype(low)

    down_grad_ref[...] = lax.dot_general(
        act[...], grad_ref[...], (((0,), (0,)), ((), ())), preferred_element_type=full
    ).astype(low)

    @pl.when(step == pl.num_programs(0) - 1)
    def _():
        branch_ref[...] = branch_acc[...].astype(low)
        back_ref[...] = back_acc[...].astype(low)


def feed_forward(norm, norm_t, grad, up, down, kernel):
    tokens, model = norm.shape
    channels = up.shape[1]
    width = TILE
    whole = lambda j: (0, 0)
    once = pl.Buffered(1)
    return pl.pallas_call(
        feed_body,
        grid=(channels // width,),
        in_specs=[
            pl.BlockSpec((tokens, model), whole, pipeline_mode=once),
            pl.BlockSpec((model, tokens), whole, pipeline_mode=once),
            pl.BlockSpec((tokens, model), whole, pipeline_mode=once),
            pl.BlockSpec((model, width), lambda j: (0, j)),
            pl.BlockSpec((width, model), lambda j: (j, 0)),
            pl.BlockSpec((16, width), lambda j: (0, j)),
        ],
        out_specs=[
            pl.BlockSpec((tokens, model), whole),
            pl.BlockSpec((tokens, model), whole),
            pl.BlockSpec((model, width), lambda j: (0, j)),
            pl.BlockSpec((width, model), lambda j: (j, 0)),
            pl.BlockSpec((16, width), lambda j: (0, j)),
        ],
        out_shape=[
            jax.ShapeDtypeStruct((tokens, model), low),
            jax.ShapeDtypeStruct((tokens, model), low),
            jax.ShapeDtypeStruct((model, channels), low),
            jax.ShapeDtypeStruct((channels, model), low),
            jax.ShapeDtypeStruct((16, channels), full),
        ],
        scratch_shapes=[
            pltpu.VMEM((tokens, model), full),
            pltpu.VMEM((tokens, model), full),
            pltpu.VMEM((4, PADDED, width), full),
            pltpu.VMEM((4, PADDED, width), full),
            pltpu.VMEM((tokens, width), full),
            pltpu.VMEM((tokens, width), low),
            pltpu.VMEM((tokens, width), low),
        ],
        compiler_params=pltpu.CompilerParams(vmem_limit_bytes=62 * 1024 * 1024),
        cost_estimate=pl.CostEstimate(
            flops=12 * tokens * model * channels,
            bytes_accessed=8 * model * channels + 10 * tokens * model,
            transcendentals=tokens * channels,
        ),
        name="feed_forward",
    )(norm, norm_t, grad, up, down, kernel)


def on_device(
    tokens,
    seg_ids,
    timesteps,
    labels,
    cotangent,
    mod_weight,
    class_table,
    attn_kernel,
    qkv_weight,
    proj_weight,
    up_weight,
    ffn_kernel,
    down_weight,
):
    devices = device_count()
    chips = devices // 2
    chip_bits = chips.bit_length() - 1
    rank = lax.axis_index("dp") * lax.axis_size("fsdp") + lax.axis_index("fsdp")
    core = rank % 2
    chip = rank // 2
    _, half_tokens, model = tokens.shape
    half_rows = half_tokens // SIDE
    class_count = class_table.shape[0]
    part = model // devices
    share = down_weight.shape[0]
    piece = share // CHUNKS
    pairs = model // HEAD // 4

    picks = labels[:, None] == jnp.arange(class_count)[None, :]
    angles_here = lax.dynamic_slice_in_dim(sinusoid(timesteps, model), rank * part, part, axis=1)
    cond = angles_here + jnp.dot(picks.astype(low), class_table, preferred_element_type=full)
    lift_value, lift_pull = jax.vjp(jax.nn.silu, cond)
    lifted = lift_value.astype(low)
    mods_part = jnp.dot(lifted, mod_weight, preferred_element_type=full)
    mods_half = scatter_sum(mods_part, 0, chip, chip_bits, sent=full)
    mods = mods_half + swap_core(mods_half)
    shift_a, scale_a, gate_a, shift_f, scale_f, gate_f = jnp.split(mods, 6)

    def halves_of(array, axis):
        return at_bit(array, axis, core), at_bit(array, axis, 1 - core)

    def row_pair(array, axis):
        kept, leaving = halves_of(array, axis)
        arriving = swap_core(leaving)
        return jnp.concatenate(in_core_order(kept, arriving, core), axis=0)

    qkv_split = qkv_weight.reshape(part, 3, 2, pairs, 128).transpose(0, 2, 3, 1, 4)
    qkv_rows = row_pair(qkv_split.reshape(part, 2, pairs * 384), 1)
    qkv_half = pairs * 384 // 2
    up_split = up_weight.reshape(part, chips, 2, CHUNKS, piece).transpose(0, 2, 3, 1, 4)
    up_rows = row_pair(up_split.reshape(part, 2, CHUNKS, chips * piece), 1)
    proj_there = [(r, r % chips * 2 + r // chips) for r in range(devices)]
    proj_back = [(b, a) for a, b in proj_there]
    proj_rows = lax.ppermute(proj_weight, AXES, proj_there)

    qkv_full = jnp.concatenate(
        [
            gather_weights(qkv_rows[:, :qkv_half], 0, chip, chip_bits).reshape(model, qkv_half),
            gather_weights(qkv_rows[:, qkv_half:], 1, chip, chip_bits).reshape(model, qkv_half),
        ],
        axis=1,
    )
    proj_halves = [
        gather_weights(proj_rows[:, : model // 2], 0, chip, chip_bits).reshape(-1, model // 2),
        gather_weights(proj_rows[:, model // 2 :], 1, chip, chip_bits).reshape(-1, model // 2),
    ]
    proj_full = jnp.concatenate(proj_halves, axis=1)
    up_full = [
        gather_weights(up_rows[:, t], 0, chip, chip_bits).reshape(model, -1)
        for t in range(CHUNKS)
    ]
    down_full = [
        gather_weights(down_weight[t * piece : (t + 1) * piece], 1, chip, chip_bits).reshape(
            -1, model
        )
        for t in range(CHUNKS)
    ]

    tap_count = 9 * (share + part)
    tap_words = jnp.concatenate([ffn_kernel.reshape(-1), attn_kernel.reshape(-1)])
    tap_rows = -(-tap_count // 2048) * 16
    tap_words = jnp.pad(tap_words, (0, tap_rows * 128 - tap_count)).reshape(tap_rows, 128)
    taps = lax.all_gather(tap_words, AXES, axis=0, tiled=True).reshape(devices, -1)
    ffn_taps = taps[:, : 9 * share].reshape(chips, 2, 9, share)
    ffn_taps = at_bit(ffn_taps, 1, core).reshape(chips, 9, CHUNKS, piece)
    ffn_taps = ffn_taps.transpose(2, 1, 0, 3).reshape(CHUNKS, 9, chips * piece).astype(full)
    ffn_taps = jnp.pad(ffn_taps, ((0, 0), (0, 7), (0, 0)))
    attn_taps = taps[:, 9 * share : tap_count].reshape(devices, 9, part)
    attn_taps = attn_taps.transpose(1, 0, 2).reshape(9, model)

    mine = tokens[0]
    canvas = jnp.concatenate(in_core_order(mine, swap_core(mine), core), axis=0)
    grad_mine = to_phases(cotangent[0], half_rows)
    grad_ph = join_halves(grad_mine, swap_core(grad_mine), core)

    normed_all = modulate(canvas.astype(full), shift_a, scale_a).reshape(SIDE, SIDE, model)
    normed_pad = jnp.pad(normed_all, ((1, 1), (1, 1), (0, 0)))
    convolved = depthwise(normed_pad, attn_taps).astype(low)
    convolved = to_phases(convolved.reshape(SIDE * SIDE, model), SIDE).reshape(SIDE * SIDE, model)

    qkv = jnp.dot(convolved, qkv_full, preferred_element_type=full).astype(low)

    spot = jnp.arange(PLANE)
    quadrant = 2 * (spot // (PLANE // 2)) + spot % HALF_SIDE // (HALF_SIDE // 2)
    quadrants_here = at_bit(seg_ids, 0, chip)
    segment = jnp.sum(
        jnp.where(quadrant[:, None] == jnp.arange(4)[None, :], quadrants_here[None, :], 0), axis=1
    )
    mask = (segment[:, None] == segment[None, :]).astype(full)

    attended = attend(mask, qkv)
    branch_part = jnp.dot(attended, proj_full, preferred_element_type=full)
    branch_a = half_of(branch_part, core) + swap_core(
        half_of(branch_part, 1 - core).astype(low)
    ).astype(full)
    source_ph = to_phases(mine, half_rows).astype(full)
    middle = source_ph + gate_a * branch_a
    normed_f, norm_pull_f = jax.vjp(modulate, middle, shift_f, scale_f)
    normed_low = normed_f.astype(low)
    norm = join_halves(normed_low, swap_core(normed_low), core)
    norm_t = norm.T
    grad_branch_f = (grad_ph.astype(full) * gate_f).astype(low)

    branch_sum, back_sum = 0.0, 0.0
    up_shares, down_shares, tap_grads = [], [], []
    for t in range(CHUNKS):
        branch, back, up_grad, down_grad, tap_grad = feed_forward(
            norm, norm_t, grad_branch_f, up_full[t], down_full[t], ffn_taps[t]
        )
        both = jnp.stack([branch, back]).reshape(2, 4, 2, -1, model)
        staying = at_bit(both, 2, core)
        arriving = swap_core(at_bit(both, 2, 1 - core))
        total = staying.astype(full) + arriving.astype(full)
        branch_sum = branch_sum + total[0]
        back_sum = back_sum + total[1]
        up_shares.append(
            scatter_sum(up_grad.reshape(chips, 2 * part, -1), 0, chip, chip_bits)
        )
        down_shares.append(scatter_sum(down_grad.reshape(chips, piece, model), 1, chip, chip_bits))
        tap_grads.append(tap_grad[:9].reshape(9, chips, piece))

    upstream = to_phases(cotangent[0], half_rows).astype(full)
    layer_out = (middle + gate_f * branch_sum).astype(low)
    layer_out = from_phases(layer_out, half_rows)[None]
    grad_gate_f = jnp.sum(upstream * branch_sum, axis=(0, 1))
    grad_middle, grad_shift_f, grad_scale_f = norm_pull_f(back_sum)
    grad_middle = grad_middle + upstream

    grad_gate_a = jnp.sum(grad_middle * branch_a, axis=(0, 1))
    grad_branch_mine = (grad_middle * gate_a).astype(low)
    grad_branch_a = join_halves(grad_branch_mine, swap_core(grad_branch_mine), core)
    grad_attended = jnp.dot(grad_branch_a, proj_full.T, preferred_element_type=full).astype(low)
    proj_grad = jnp.dot(attended.T, grad_branch_a, preferred_element_type=full).astype(low)
    proj_grad = proj_grad.reshape(chips, -1, model)
    proj_share = jnp.concatenate(
        [
            scatter_sum(proj_grad[..., : model // 2], 0, chip, chip_bits),
            scatter_sum(proj_grad[..., model // 2 :], 1, chip, chip_bits),
        ],
        axis=1,
    )
    proj_share = lax.ppermute(proj_share, AXES, proj_back)

    grad_qkv = attend_back(mask, qkv, grad_attended)
    qkv_grad = jnp.dot(convolved.T, grad_qkv, preferred_element_type=full).astype(low)
    qkv_grad = qkv_grad.reshape(chips, 2 * part, -1)
    qkv_share = jnp.concatenate(
        [
            scatter_sum(qkv_grad[..., :qkv_half], 0, chip, chip_bits),
            scatter_sum(qkv_grad[..., qkv_half:], 1, chip, chip_bits),
        ],
        axis=1,
    )

    grad_conv_part = jnp.dot(grad_qkv, qkv_full.T, preferred_element_type=full)
    grad_conv_part = from_phases(grad_conv_part.reshape(4, PLANE, model), SIDE)
    grad_conv_part = jnp.pad(
        grad_conv_part.reshape(SIDE, SIDE, model), ((1, 1), (0, 0), (0, 0))
    )

    def rows_near(array, which):
        return lax.dynamic_slice_in_dim(array, which * half_rows, half_rows + 2, axis=0)

    grad_conv = rows_near(grad_conv_part, core) + swap_core(
        rows_near(grad_conv_part, 1 - core).astype(low)
    ).astype(full)
    normed_near = rows_near(normed_pad, core)
    attn_tap_grad = kernel_grad(normed_near, grad_conv[1:-1])
    grad_normed_a = depthwise(
        jnp.pad(grad_conv, ((0, 0), (1, 1), (0, 0))), attn_taps[::-1]
    ).reshape(half_tokens, model)
    _, norm_pull_a = jax.vjp(modulate, mine.astype(full), shift_a, scale_a)
    grad_source, grad_shift_a, grad_scale_a = norm_pull_a(grad_normed_a)
    input_grad = grad_source + from_phases(grad_middle, half_rows)

    grad_mods = jnp.concatenate(
        [grad_shift_a, grad_scale_a, grad_gate_a, grad_shift_f, grad_scale_f, grad_gate_f]
    )
    grad_mods = (grad_mods + swap_core(grad_mods)).astype(low)
    grad_mods_all = gather_rows(grad_mods, chip, chip_bits)
    mod_grad = jnp.dot(lifted.T, grad_mods_all, preferred_element_type=full)
    (cond_grad,) = lift_pull(jnp.dot(grad_mods_all, mod_weight.T, preferred_element_type=full))
    table_grad = jnp.dot(picks.astype(full).T, cond_grad, precision=highest)

    ffn_tap_grad = jnp.concatenate(tap_grads, axis=2).transpose(1, 0, 2)
    attn_split = attn_tap_grad.reshape(9, chips, 2, part)
    attn_kept, attn_leaving = halves_of(attn_split, 2)
    attn_tap_grad = (attn_kept + swap_core(attn_leaving)).transpose(1, 0, 2)
    tap_parts = jnp.concatenate(
        [ffn_tap_grad.reshape(chips, -1), attn_tap_grad.reshape(chips, -1)], axis=1
    )
    tap_share = scatter_sum(tap_parts, 0, chip, chip_bits, sent=full)
    ffn_share = tap_share[: 9 * share].reshape(9, share)
    kernel_share = tap_share[9 * share :].reshape(9, part)

    def row_split(array, axis):
        pair = array.reshape((2, part) + array.shape[1:])
        kept, leaving = halves_of(pair, 0)
        arriving = swap_core(leaving)
        return jnp.stack(in_core_order(kept, arriving, core), axis=axis)

    up_all = jnp.stack(up_shares, axis=1).reshape(2 * part, CHUNKS, chips, piece)
    up_share = row_split(up_all.transpose(0, 2, 1, 3), 2).reshape(part, -1)
    down_share = jnp.concatenate(down_shares, axis=0)
    qkv_all = qkv_share.reshape(2 * part, pairs, 3, 128).transpose(0, 2, 1, 3)
    qkv_out = row_split(qkv_all, 2).reshape(part, -1)

    return (
        layer_out,
        input_grad[None],
        mod_grad,
        table_grad,
        kernel_share,
        qkv_out,
        proj_share,
        up_share,
        ffn_share,
        down_share,
        grad_shift_f[None],
    )


def solution(mesh):
    return jax.shard_map(
        on_device,
        mesh=mesh,
        in_specs=(
            P(AXES, None, None),
            P(),
            P(),
            P(),
            P(AXES, None, None),
            P(AXES, None),
            P(None, AXES),
            P(None, AXES),
            P(AXES, None),
            P(AXES, None),
            P(AXES, None),
            P(None, AXES),
            P(AXES, None),
        ),
        out_specs=(
            P(AXES, None, None),
            P(AXES, None, None),
            P(AXES, None),
            P(None, AXES),
            P(None, AXES),
            P(AXES, None),
            P(AXES, None),
            P(AXES, None),
            P(None, AXES),
            P(AXES, None),
            P(AXES, None),
        ),
        check_vma=False,
    )
```

```python
import functools
import math

import jax
import jax.numpy as jnp
from jax import lax
from jax.experimental import pallas as pl
from jax.experimental.pallas import tpu as pltpu
from jax.sharding import PartitionSpec as P

HEAD = 64
SIDE = 32
HALF_SIDE = SIDE // 2
STRIP = HALF_SIDE
PLANE = HALF_SIDE * HALF_SIDE
PADDED = PLANE + 2 * STRIP
TILE = 256
CHUNKS = 3

highest = lax.Precision.HIGHEST
ln_epsilon = 1e-06
masked_score = -1000000000.0
low = jnp.bfloat16
full = jnp.float32
AXES = ("dp", "fsdp")


def device_count():
    return lax.axis_size("dp") * lax.axis_size("fsdp")


def swap(x, bit):
    return lax.ppermute(x, AXES, [(i, i ^ 1 << bit) for i in range(device_count())])


def swap_core(x):
    return swap(x, 0)


def gather_order(chip_bits, colour):
    order = list(range(chip_bits - 1, -1, -1))
    if colour and chip_bits > 1:
        order[-1], order[-2] = order[-2], order[-1]
    return order


class Flow:
    def __init__(self, steps):
        self.steps = steps
        self.wanted = next(steps)
        self.result = None

    def arrive(self, array):
        try:
            self.wanted = self.steps.send(array)
        except StopIteration as end:
            self.wanted, self.result = None, end.value


class Slots:
    def __init__(self, token):
        self.token = token

    def finish(self, flows):
        while any(flow.wanted is not None for flow in flows):
            self(flows)

    def __call__(self, flows, work=lambda: ()):
        flows = [flow for flow in flows if flow.wanted is not None]
        wanted = [flow.wanted for flow in flows]
        leaving, self.token = lax.optimization_barrier(([w[0] for w in wanted], self.token))
        arriving = [swap(array, bit + 1) for array, (_, bit) in zip(leaving, wanted)]
        arriving, result, self.token = lax.optimization_barrier((arriving, work(), self.token))
        for flow, array in zip(flows, arriving):
            flow.arrive(array)
        return result


def gather_steps(shard, order):
    held = shard[None]
    for bit in order[:-1]:
        arriving = yield held, bit
        held = jnp.concatenate([held, arriving], axis=0)
    arriving = yield held, order[-1]
    return held, arriving


def assemble_body(steps, chip_ref, *refs):
    *piece_refs, out_ref = refs
    which = pl.program_id(0) // steps
    top = chip_ref[1]
    for index, piece_ref in enumerate(piece_refs):

        @pl.when(which == index)
        def _():
            for k in range(4):
                out_ref[jnp.bitwise_xor(top, (k & 1) << 1 | k >> 1), 0] = piece_ref[k]


def assemble(pieces, order, chip):
    chips = sum(piece.shape[0] for piece in pieces)
    rows, columns = pieces[0].shape[1:]
    if chips < 4 or len(pieces) * pieces[0].shape[0] != chips or pieces[0].shape[0] % 4:
        raise ValueError("unexpected mesh")
    rest = len(order) - 2
    steps = pieces[0].shape[0] // 4
    chip_words = jnp.stack([jnp.bitwise_and(chip, (1 << rest) - 1), chip >> rest]).astype(jnp.int32)

    def out_map(step, words):
        at = words[0]
        for position, bit in enumerate(order[2:]):
            at = jnp.bitwise_xor(at, jnp.bitwise_and(step >> position, 1) << bit)
        return (0, at, 0, 0)

    def piece_map(index):
        return lambda step, words: (jnp.clip(step - index * steps, 0, steps - 1), 0, 0)

    out = pl.pallas_call(
        functools.partial(assemble_body, steps),
        grid_spec=pltpu.PrefetchScalarGridSpec(
            num_scalar_prefetch=1,
            grid=(chips // 4,),
            in_specs=[
                pl.BlockSpec((4, rows, columns), piece_map(index)) for index in range(len(pieces))
            ],
            out_specs=pl.BlockSpec((4, 1, rows, columns), out_map),
        ),
        out_shape=jax.ShapeDtypeStruct((4, chips // 4, rows, columns), pieces[0].dtype),
        cost_estimate=pl.CostEstimate(
            flops=0, bytes_accessed=4 * chips * rows * columns, transcendentals=0
        ),
        name="assemble",
    )(chip_words, *pieces)
    return out.reshape(chips, rows, columns)


def gather_flow(shard, colour, chip_bits):
    return Flow(gather_steps(shard, gather_order(chip_bits, colour)))


def gathered(flow, colour, chip, chip_bits):
    return assemble(flow.result, gather_order(chip_bits, colour), chip)


def at_bit(array, axis, bit):
    return lax.dynamic_index_in_dim(array, bit, axis, keepdims=False)


def scatter_steps(parts, order, chip, chip_bits, sent):
    left = list(range(chip_bits - 1, -1, -1))
    held = [parts.reshape((2,) * chip_bits + parts.shape[1:])]
    for bit in order:
        axis = left.index(bit)
        left.remove(bit)
        mine = jnp.bitwise_and(chip >> bit, 1)
        leaving = sum(at_bit(h, axis, 1 - mine).astype(full) for h in held).astype(sent)
        staying = sum(at_bit(h, axis, mine).astype(full) for h in held).astype(sent)
        arriving = yield leaving, bit
        held = [staying, arriving]
    return held[0].astype(full) + held[1].astype(full)


def scatter_flow(parts, colour, chip, chip_bits, sent=low):
    order = gather_order(chip_bits, colour)[::-1]
    return Flow(scatter_steps(parts, order, chip, chip_bits, sent))


def scatter_sum(parts, colour, chip, chip_bits, sent=low):
    flow = scatter_flow(parts, colour, chip, chip_bits, sent)
    while flow.wanted is not None:
        array, bit = flow.wanted
        flow.arrive(swap(array, bit + 1))
    return flow.result


def gather_rows(row, chip, chip_bits, first_bit=1):
    order = gather_order(chip_bits, 0)
    held = row[None]
    for bit in order:
        held = jnp.concatenate([held, swap(held, bit + first_bit)], axis=0)
    places = jnp.arange(1 << chip_bits)
    position = jnp.zeros_like(places)
    apart = jnp.bitwise_xor(places, chip)
    for step, bit in enumerate(order):
        position = position + (jnp.bitwise_and(apart >> bit, 1) << step)
    pick = position[:, None] == places[None, :]
    return jnp.dot(pick.astype(held.dtype), held, preferred_element_type=full).astype(held.dtype)


def to_phases(block_in, row_count):
    width = block_in.shape[-1]
    split_grid = block_in.reshape(row_count // 2, 2, HALF_SIDE, 2, width)
    return split_grid.transpose(1, 3, 0, 2, 4).reshape(4, row_count // 2 * HALF_SIDE, width)


def from_phases(block_in, row_count):
    width = block_in.shape[-1]
    split_grid = block_in.reshape(2, 2, row_count // 2, HALF_SIDE, width)
    return split_grid.transpose(2, 0, 3, 1, 4).reshape(row_count * SIDE, width)


def in_core_order(mine, other, core):
    return jnp.where(core == 0, mine, other), jnp.where(core == 0, other, mine)


def join_halves(mine, other, core):
    return jnp.stack(in_core_order(mine, other, core), axis=1).reshape(-1, mine.shape[-1])


def half_of(joined, which):
    width = joined.shape[-1]
    return at_bit(joined.reshape(4, 2, -1, width), 1, which)


def layer_norm(values):
    average = jnp.mean(values, axis=-1, keepdims=True)
    centred = values - average
    variance = jnp.mean(centred * centred, axis=-1, keepdims=True)
    return centred * lax.rsqrt(variance + ln_epsilon)


def modulate(values, shift_by, scale_by):
    return layer_norm(values) * (1.0 + scale_by) + shift_by


def sinusoid(steps_in, width):
    halfway = width // 2
    frequency = jnp.exp(-math.log(10000.0) * jnp.arange(halfway, dtype=jnp.float32) / halfway)
    angles = steps_in.astype(jnp.float32)[..., None] * frequency
    return jnp.concatenate([jnp.cos(angles), jnp.sin(angles)], axis=-1)


def depthwise(framed, kernel):
    row_count = framed.shape[0] - 2
    result = jnp.zeros((row_count, SIDE, framed.shape[2]), jnp.float32)
    for tap in range(9):
        r, s = divmod(tap, 3)
        result = result + framed[r : r + row_count, s : s + SIDE] * kernel[tap].astype(full)
    return result


def kernel_grad(framed, upstream):
    row_count = upstream.shape[0]
    sums = []
    for tap in range(9):
        r, s = divmod(tap, 3)
        sums.append(jnp.sum(framed[r : r + row_count, s : s + SIDE] * upstream, axis=(0, 1)))
    return jnp.stack(sums)


def softmax_of(query, key, allowed):
    raw = lax.dot_general(query, key, (((1,), (1,)), ((), ())), preferred_element_type=full)
    scores = jnp.where(allowed, raw * HEAD ** (-0.5), masked_score)
    shifted = jnp.exp(scores - jnp.max(scores, axis=-1, keepdims=True))
    return shifted / jnp.sum(shifted, axis=-1, keepdims=True)


def head_lanes(shape, head):
    lanes = lax.broadcasted_iota(jnp.int32, shape, 1)
    return jnp.logical_and(lanes >= head * HEAD, lanes < (head + 1) * HEAD)


def attend_body(mask_ref, qkv_ref, out_ref):
    allowed = mask_ref[...] > 0.5

    @pl.loop(0, 4)
    def _(phase):
        rows = pl.ds(pl.multiple_of(phase * PLANE, PLANE), PLANE)
        query = qkv_ref[rows, :128]
        key = qkv_ref[rows, 128:256]
        value = qkv_ref[rows, 256:]
        total = None
        for head in range(2):
            here = head_lanes(key.shape, head)
            probs = softmax_of(query, jnp.where(here, key, jnp.zeros_like(key)), allowed)
            part = jnp.dot(
                probs.astype(low),
                jnp.where(here, value, jnp.zeros_like(value)),
                preferred_element_type=full,
            )
            total = part if total is None else total + part
        out_ref[rows, :] = total.astype(low)


def attend_back_body(mask_ref, qkv_ref, grad_ref, out_ref):
    allowed = mask_ref[...] > 0.5

    @pl.loop(0, 4)
    def _(phase):
        rows = pl.ds(pl.multiple_of(phase * PLANE, PLANE), PLANE)
        query = qkv_ref[rows, :128]
        key = qkv_ref[rows, 128:256]
        value = qkv_ref[rows, 256:]
        grad = grad_ref[rows, :]
        by_rows = (((0,), (0,)), ((), ()))
        totals = [None, None, None]
        for head in range(2):
            here = head_lanes(key.shape, head)
            blank = jnp.zeros_like(key)
            key_here = jnp.where(here, key, blank)
            query_here = jnp.where(here, query, blank)
            value_here = jnp.where(here, value, blank)
            grad_here = jnp.where(here, grad, blank)
            weights = softmax_of(query, key_here, allowed)
            grad_probs = lax.dot_general(
                grad, value_here, (((1,), (1,)), ((), ())), preferred_element_type=full
            )
            delta = jnp.sum(grad_probs * weights, axis=-1, keepdims=True)
            grad_scores = (weights * (grad_probs - delta)).astype(low)
            parts = (
                jnp.dot(grad_scores, key_here, preferred_element_type=full),
                lax.dot_general(grad_scores, query_here, by_rows, preferred_element_type=full),
                lax.dot_general(
                    weights.astype(low), grad_here, by_rows, preferred_element_type=full
                ),
            )
            totals = [p if t is None else t + p for t, p in zip(totals, parts)]
        out_ref[rows, :128] = (totals[0] * HEAD ** (-0.5)).astype(low)
        out_ref[rows, 128:256] = (totals[1] * HEAD ** (-0.5)).astype(low)
        out_ref[rows, 256:] = totals[2].astype(low)


def attend(mask, qkv):
    tokens, width = qkv.shape
    pairs = width // 384
    return pl.pallas_call(
        attend_body,
        grid=(pairs,),
        in_specs=[
            pl.BlockSpec((PLANE, PLANE), lambda j: (0, 0)),
            pl.BlockSpec((tokens, 384), lambda j: (0, j)),
        ],
        out_specs=pl.BlockSpec((tokens, 128), lambda j: (0, j)),
        out_shape=jax.ShapeDtypeStruct((tokens, pairs * 128), low),
        cost_estimate=pl.CostEstimate(
            flops=pairs * 2 * 4 * 4 * PLANE * PLANE * 256,
            bytes_accessed=8 * tokens * pairs * 128,
            transcendentals=pairs * 8 * PLANE * PLANE,
        ),
        name="attend",
    )(mask, qkv)


def attend_back(mask, qkv, grad):
    tokens, width = qkv.shape
    pairs = width // 384
    return pl.pallas_call(
        attend_back_body,
        grid=(pairs,),
        in_specs=[
            pl.BlockSpec((PLANE, PLANE), lambda j: (0, 0)),
            pl.BlockSpec((tokens, 384), lambda j: (0, j)),
            pl.BlockSpec((tokens, 128), lambda j: (0, j)),
        ],
        out_specs=pl.BlockSpec((tokens, 384), lambda j: (0, j)),
        out_shape=jax.ShapeDtypeStruct((tokens, width), low),
        cost_estimate=pl.CostEstimate(
            flops=pairs * 2 * 4 * 10 * PLANE * PLANE * 256,
            bytes_accessed=14 * tokens * pairs * 128,
            transcendentals=pairs * 8 * PLANE * PLANE,
        ),
        name="attend_back",
    )(mask, qkv, grad)


def strip_at(ref, row_phase, column_phase, row):
    start = pl.multiple_of((row + 1) * STRIP, STRIP)
    return ref[2 * row_phase + column_phase, pl.ds(start, STRIP), :]


def near_strips(ref, row):
    tokens = lax.broadcasted_iota(jnp.int32, (STRIP, ref.shape[-1]), 0)
    loaded = {}
    for row_phase, at in ((1, row - 1), (0, row), (1, row), (0, row + 1)):
        even = strip_at(ref, row_phase, 0, at)
        odd = strip_at(ref, row_phase, 1, at)
        before = jnp.where(tokens == 0, 0.0, pltpu.roll(odd, 1, 0))
        after = jnp.where(tokens == STRIP - 1, 0.0, pltpu.roll(even, STRIP - 1, 0))
        loaded[len(loaded)] = ((before, even, odd), (even, odd, after))
    return {0: (loaded[0], loaded[1], loaded[2]), 1: (loaded[1], loaded[2], loaded[3])}


def conv_strip(near, kernel, row_phase, column_phase):
    total = None
    for i in range(3):
        for j in range(3):
            term = near[row_phase][i][column_phase][j] * kernel[3 * i + j : 3 * i + j + 1, :]
            total = term if total is None else total + term
    return total


def feed_body(
    core_ref,
    norm_ref,
    norm_t_ref,
    grad_ref,
    up_ref,
    down_ref,
    kernel_ref,
    up_held_ref,
    down_held_ref,
    kernel_held_ref,
    staying_ref,
    leaving_ref,
    up_grad_ref,
    down_grad_ref,
    kernel_grad_ref,
    branch_acc,
    back_acc,
    hidden,
    widened_grad,
    act_grad,
    act,
    hidden_grad,
):
    step = pl.program_id(0)
    by_columns = (((1,), (1,)), ((), ()))
    width = up_ref.shape[1]

    @pl.when(step == 0)
    def _():
        blank = jnp.zeros((STRIP, width), full)
        for plane in range(4):
            for ref in (hidden, widened_grad):
                ref[plane, pl.ds(0, STRIP), :] = blank
                ref[plane, pl.ds(PLANE + STRIP, STRIP), :] = blank
        branch_acc[...] = jnp.zeros_like(branch_acc)
        back_acc[...] = jnp.zeros_like(back_acc)

    @pl.loop(0, 4)
    def _(plane):
        rows = pl.ds(pl.multiple_of(plane * PLANE, PLANE), PLANE)
        hidden[plane, pl.ds(STRIP, PLANE), :] = jnp.dot(
            norm_ref[rows, :], up_ref[...], preferred_element_type=full
        )
        act_grad[rows, :] = lax.dot_general(
            grad_ref[rows, :], down_ref[...], by_columns, preferred_element_type=full
        )

    kernel = kernel_ref[...]

    def forward_strip(row, sums):
        near = near_strips(hidden, row)
        sums = list(sums)
        for row_phase in range(2):
            for column_phase in range(2):
                plane = 2 * row_phase + column_phase
                wide = conv_strip(near, kernel, row_phase, column_phase)
                square = wide * wide
                bend = math.sqrt(2.0 / math.pi) * (wide + 0.044715 * wide * square)
                curve = jnp.tanh(bend)
                half = 0.5 * (1.0 + curve)
                slope = half + 0.5 * wide * (1.0 - curve * curve) * (
                    math.sqrt(2.0 / math.pi) * (1.0 + 3 * 0.044715 * square)
                )
                at = pl.ds(pl.multiple_of(plane * PLANE + row * STRIP, STRIP), STRIP)
                act[at, :] = (wide * half).astype(low)
                grad_here = slope * act_grad[at, :]
                widened_grad[plane, pl.ds(pl.multiple_of((row + 1) * STRIP, STRIP), STRIP), :] = (
                    grad_here
                )
                for i in range(3):
                    for j in range(3):
                        product = near[row_phase][i][column_phase][j] * grad_here
                        sums[3 * i + j] = sums[3 * i + j] + (product[:8] + product[8:])
        return tuple(sums)

    sums = lax.fori_loop(
        0, HALF_SIDE, forward_strip, tuple(jnp.zeros((8, width), full) for _ in range(9))
    )
    kernel_grad_ref[...] = jnp.concatenate(
        [jnp.sum(s, axis=0, keepdims=True) for s in sums] + [jnp.zeros((7, width), full)], axis=0
    )

    flipped = [kernel[8 - t : 9 - t, :] for t in range(9)]
    flipped = jnp.concatenate(flipped, axis=0)

    @pl.loop(0, HALF_SIDE)
    def _(row):
        near = near_strips(widened_grad, row)
        for row_phase in range(2):
            for column_phase in range(2):
                plane = 2 * row_phase + column_phase
                at = pl.ds(pl.multiple_of(plane * PLANE + row * STRIP, STRIP), STRIP)
                hidden_grad[at, :] = conv_strip(near, flipped, row_phase, column_phase).astype(low)

    @pl.loop(0, 4)
    def _(plane):
        rows = pl.ds(pl.multiple_of(plane * PLANE, PLANE), PLANE)
        branch_acc[rows, :] += jnp.dot(act[rows, :], down_ref[...], preferred_element_type=full)
        back_acc[rows, :] += lax.dot_general(
            hidden_grad[rows, :], up_ref[...], by_columns, preferred_element_type=full
        )

    model = norm_t_ref.shape[0]

    @pl.loop(0, model // TILE)
    def _(tile):
        rows = pl.ds(pl.multiple_of(tile * TILE, TILE), TILE)
        up_grad_ref[rows, :] = jnp.dot(
            norm_t_ref[rows, :], hidden_grad[...], preferred_element_type=full
        ).astype(low)

    down_grad_ref[...] = lax.dot_general(
        act[...], grad_ref[...], (((0,), (0,)), ((), ())), preferred_element_type=full
    ).astype(low)

    @pl.when(step == pl.num_programs(0) - 1)
    def _():
        for ref, which in ((staying_ref, core_ref[0]), (leaving_ref, 1 - core_ref[0])):
            for index, acc in enumerate((branch_acc, back_acc)):
                for plane in range(4):
                    start = plane * PLANE + pl.multiple_of(which * (PLANE // 2), PLANE // 2)
                    ref[index, plane] = acc[pl.ds(start, PLANE // 2), :].astype(low)


def feed_forward(norm, norm_t, grad, up, down, kernel, core, first, count, held=None):
    tokens, model = norm.shape
    channels = up.shape[1]
    width = TILE
    whole = lambda j, words: (0, 0)
    half = lambda j, words: (0, 0, 0, 0)
    across = lambda j, words: (0, first + j)
    down_rows = lambda j, words: (first + j, 0)
    once = pl.Buffered(1)
    grads = [
        jax.ShapeDtypeStruct((model, channels), low),
        jax.ShapeDtypeStruct((channels, model), low),
        jax.ShapeDtypeStruct((16, channels), full),
    ]
    halves = jax.ShapeDtypeStruct((2, 4, PLANE // 2, model), low)
    body = feed_body
    if held is None:
        held = ()

        def body(*refs):
            feed_body(*refs[:7], None, None, None, *refs[7:])

    return pl.pallas_call(
        body,
        grid_spec=pltpu.PrefetchScalarGridSpec(
            num_scalar_prefetch=1,
            grid=(count,),
            in_specs=[
                pl.BlockSpec((tokens, model), whole, pipeline_mode=once),
                pl.BlockSpec((model, tokens), whole, pipeline_mode=once),
                pl.BlockSpec((tokens, model), whole, pipeline_mode=once),
                pl.BlockSpec((model, width), across),
                pl.BlockSpec((width, model), down_rows),
                pl.BlockSpec((16, width), across),
            ]
            + [pl.BlockSpec(memory_space=pl.ANY)] * len(held),
            out_specs=[
                pl.BlockSpec(halves.shape, half),
                pl.BlockSpec(halves.shape, half),
                pl.BlockSpec((model, width), across),
                pl.BlockSpec((width, model), down_rows),
                pl.BlockSpec((16, width), across),
            ],
            scratch_shapes=[
                pltpu.VMEM((tokens, model), full),
                pltpu.VMEM((tokens, model), full),
                pltpu.VMEM((4, PADDED, width), full),
                pltpu.VMEM((4, PADDED, width), full),
                pltpu.VMEM((tokens, width), full),
                pltpu.VMEM((tokens, width), low),
                pltpu.VMEM((tokens, width), low),
            ],
        ),
        out_shape=[halves, halves] + grads,
        input_output_aliases={7 + i: 2 + i for i in range(len(held))},
        compiler_params=pltpu.CompilerParams(vmem_limit_bytes=62 * 1024 * 1024),
        cost_estimate=pl.CostEstimate(
            flops=12 * tokens * model * count * width,
            bytes_accessed=8 * model * count * width + 10 * tokens * model,
            transcendentals=tokens * count * width,
        ),
        name="feed_forward",
    )(core[None].astype(jnp.int32), norm, norm_t, grad, up, down, kernel, *held)


def on_device(
    tokens,
    seg_ids,
    timesteps,
    labels,
    cotangent,
    mod_weight,
    class_table,
    attn_kernel,
    qkv_weight,
    proj_weight,
    up_weight,
    ffn_kernel,
    down_weight,
):
    devices = device_count()
    chips = devices // 2
    chip_bits = chips.bit_length() - 1
    rank = lax.axis_index("dp") * lax.axis_size("fsdp") + lax.axis_index("fsdp")
    core = rank % 2
    chip = rank // 2
    _, half_tokens, model = tokens.shape
    half_rows = half_tokens // SIDE
    class_count = class_table.shape[0]
    part = model // devices
    share = down_weight.shape[0]
    piece = share // CHUNKS
    pairs = model // HEAD // 4

    def halves_of(array, axis):
        return at_bit(array, axis, core), at_bit(array, axis, 1 - core)

    def row_pair(array, axis):
        kept, leaving = halves_of(array, axis)
        arriving = swap_core(leaving)
        return jnp.concatenate(in_core_order(kept, arriving, core), axis=0)

    qkv_split = qkv_weight.reshape(part, 3, 2, pairs, 128).transpose(0, 2, 3, 1, 4)
    qkv_rows = row_pair(qkv_split.reshape(part, 2, pairs * 384), 1)
    qkv_half = pairs * 384 // 2
    up_split = up_weight.reshape(part, chips, 2, CHUNKS, piece).transpose(0, 2, 3, 1, 4)
    up_rows = row_pair(up_split.reshape(part, 2, CHUNKS, chips * piece), 1)
    proj_there = [(r, r % chips * 2 + r // chips) for r in range(devices)]
    proj_back = [(b, a) for a, b in proj_there]
    proj_rows = lax.ppermute(proj_weight, AXES, proj_there)
    mine = tokens[0]
    canvas = jnp.concatenate(in_core_order(mine, swap_core(mine), core), axis=0)
    grad_mine = to_phases(cotangent[0], half_rows)
    grad_ph = join_halves(grad_mine, swap_core(grad_mine), core)

    picks = labels[:, None] == jnp.arange(class_count)[None, :]
    angles_here = lax.dynamic_slice_in_dim(sinusoid(timesteps, model), rank * part, part, axis=1)
    cond = angles_here + jnp.dot(picks.astype(low), class_table, preferred_element_type=full)
    lift_value, lift_pull = jax.vjp(jax.nn.silu, cond)
    lifted = lift_value.astype(low)
    mods_part = jnp.dot(lifted, mod_weight, preferred_element_type=full)
    mods_half = scatter_sum(mods_part, 0, chip, chip_bits, sent=full)
    mods = mods_half + swap_core(mods_half)
    shift_a, scale_a, gate_a, shift_f, scale_f, gate_f = jnp.split(mods, 6)

    tap_count = 9 * (share + part)
    tap_words = jnp.concatenate([ffn_kernel.reshape(-1), attn_kernel.reshape(-1)])
    tap_words = jnp.pad(tap_words, (0, -tap_count % 128))
    taps = gather_rows(tap_words, rank, chip_bits + 1, 0)
    ffn_taps = taps[:, : 9 * share].reshape(chips, 2, 9, share)
    ffn_taps = at_bit(ffn_taps, 1, core).reshape(chips, 9, CHUNKS, piece)
    ffn_taps = ffn_taps.transpose(2, 1, 0, 3).reshape(CHUNKS, 9, chips * piece).astype(full)
    ffn_taps = jnp.pad(ffn_taps, ((0, 0), (0, 7), (0, 0)))
    attn_taps = taps[:, 9 * share : tap_count].reshape(devices, 9, part)
    attn_taps = attn_taps.transpose(1, 0, 2).reshape(9, model)

    spot = jnp.arange(PLANE)
    quadrant = 2 * (spot // (PLANE // 2)) + spot % HALF_SIDE // (HALF_SIDE // 2)
    quadrants_here = at_bit(seg_ids, 0, chip)
    segment = jnp.sum(
        jnp.where(quadrant[:, None] == jnp.arange(4)[None, :], quadrants_here[None, :], 0), axis=1
    )
    mask = (segment[:, None] == segment[None, :]).astype(full)

    slot = Slots(jnp.zeros((8, 128), full))
    flow = lambda shard, colour: gather_flow(shard, colour, chip_bits)
    sums = lambda parts, colour: scatter_flow(parts, colour, chip, chip_bits)
    joined = lambda flows: [
        gathered(f, colour, chip, chip_bits) for colour, f in enumerate(flows)
    ]
    qkv_flows = [flow(qkv_rows[:, :qkv_half], 0), flow(qkv_rows[:, qkv_half:], 1)]
    proj_flows = [flow(proj_rows[:, : model // 2], 0), flow(proj_rows[:, model // 2 :], 1)]
    feed_flows = [
        [flow(up_rows[:, t], 0), flow(down_weight[t * piece : (t + 1) * piece], 1)]
        for t in range(CHUNKS)
    ]

    slot(qkv_flows)
    slot(qkv_flows)

    def prepare():
        normed = modulate(canvas.astype(full), shift_a, scale_a).reshape(SIDE, SIDE, model)
        normed = jnp.pad(normed, ((1, 1), (1, 1), (0, 0)))
        return normed, depthwise(normed, attn_taps).astype(low)

    normed_pad, convolved = slot(qkv_flows + proj_flows, prepare)
    convolved = slot(
        qkv_flows + proj_flows, lambda: to_phases(convolved.reshape(SIDE * SIDE, model), SIDE)
    ).reshape(SIDE * SIDE, model)

    def project_in():
        weight = jnp.concatenate(
            [array.reshape(model, qkv_half) for array in joined(qkv_flows)], axis=1
        )
        return weight, jnp.dot(convolved, weight, preferred_element_type=full).astype(low)

    slot.finish(qkv_flows)
    qkv_full, qkv = slot(proj_flows + feed_flows[0], project_in)
    attended = slot(proj_flows + feed_flows[0], lambda: attend(mask, qkv))

    def project_out():
        weight = jnp.concatenate(
            [array.reshape(-1, model // 2) for array in joined(proj_flows)], axis=1
        )
        branch_part = jnp.dot(attended, weight, preferred_element_type=full)
        branch = half_of(branch_part, core) + swap_core(
            half_of(branch_part, 1 - core).astype(low)
        ).astype(full)
        return weight, branch

    source_ph = to_phases(mine, half_rows).astype(full)
    slot.finish(proj_flows)
    proj_full, branch_a = slot(feed_flows[0] + feed_flows[1], project_out)

    def enter_feed():
        middle = source_ph + gate_a * branch_a
        normed_low = modulate(middle, shift_f, scale_f).astype(low)
        norm = join_halves(normed_low, swap_core(normed_low), core)
        return middle, norm, norm.T, (grad_ph.astype(full) * gate_f).astype(low)

    middle, norm, norm_t, grad_branch_f = slot(feed_flows[0] + feed_flows[1], enter_feed)

    kept = []
    grads = [None] * CHUNKS

    def feed(t, first, count):
        def work():
            if first == 0:
                feed_weights[t] = [
                    array.reshape(shape)
                    for array, shape in zip(joined(feed_flows[t]), ((model, -1), (-1, model)))
                ]
            staying, leaving, *grads_now = feed_forward(
                norm, norm_t, grad_branch_f, *feed_weights[t], ffn_taps[t], core, first, count,
                grads[t],
            )
            return feed_weights[t], staying, leaving, grads_now

        return work

    feed_weights = [None] * CHUNKS
    back_flows = [None] * CHUNKS

    def run_feed(flows, t, first, count):
        slot.finish(feed_flows[t])
        feed_weights[t], staying, leaving, grads[t] = slot(flows, feed(t, first, count))
        kept.append((staying, leaving))

    blocks = chips * piece // TILE
    run_feed(feed_flows[1] + feed_flows[2], 0, 0, 1)
    run_feed(feed_flows[1] + feed_flows[2], 0, 1, blocks - 1)
    run_feed(feed_flows[2], 1, 0, 1)
    run_feed(feed_flows[2], 1, 1, blocks - 1)

    def begin_back(t):
        back_flows[t] = [
            sums(grads[t][0].reshape(chips, 2 * part, -1), 0),
            sums(grads[t][1].reshape(chips, piece, model), 1),
        ]

    begin_back(0)
    begin_back(1)
    run_feed(back_flows[0], 2, 0, blocks - 1)
    run_feed(back_flows[0], 2, blocks - 1, 1)
    begin_back(2)

    upstream = to_phases(cotangent[0], half_rows).astype(full)

    def leave_feed():
        total = sum(
            staying.astype(full) + swap_core(leaving).astype(full) for staying, leaving in kept
        )
        branch_sum, back_sum = total[0], total[1]
        layer_out = from_phases((middle + gate_f * branch_sum).astype(low), half_rows)
        grad_gate_f = jnp.sum(upstream * branch_sum, axis=(0, 1))
        _, norm_pull_f = jax.vjp(modulate, middle, shift_f, scale_f)
        grad_middle, grad_shift_f, grad_scale_f = norm_pull_f(back_sum)
        grad_middle = grad_middle + upstream
        grad_gate_a = jnp.sum(grad_middle * branch_a, axis=(0, 1))
        grad_branch_mine = (grad_middle * gate_a).astype(low)
        return (
            layer_out, grad_middle, grad_branch_mine,
            grad_gate_f, grad_shift_f, grad_scale_f, grad_gate_a,
        )

    (
        layer_out, grad_middle, grad_branch_mine,
        grad_gate_f, grad_shift_f, grad_scale_f, grad_gate_a,
    ) = slot(back_flows[0] + back_flows[1], leave_feed)
    layer_out = layer_out[None]

    def enter_attend():
        grad_branch_a = join_halves(grad_branch_mine, swap_core(grad_branch_mine), core)
        grad_attended = jnp.dot(grad_branch_a, proj_full.T, preferred_element_type=full)
        proj_grad = jnp.dot(attended.T, grad_branch_a, preferred_element_type=full)
        return grad_attended.astype(low), proj_grad.astype(low)

    grad_attended, proj_grad = slot(back_flows[0] + back_flows[1], enter_attend)
    proj_grad = proj_grad.reshape(chips, -1, model)
    proj_flows = [sums(proj_grad[..., : model // 2], 0), sums(proj_grad[..., model // 2 :], 1)]
    grad_qkv = slot(
        back_flows[1] + back_flows[2], lambda: attend_back(mask, qkv, grad_attended)
    )
    qkv_grad = slot(
        back_flows[1] + back_flows[2],
        lambda: jnp.dot(convolved.T, grad_qkv, preferred_element_type=full).astype(low),
    )
    qkv_grad = qkv_grad.reshape(chips, 2 * part, -1)
    qkv_flows = [sums(qkv_grad[..., :qkv_half], 0), sums(qkv_grad[..., qkv_half:], 1)]

    def rows_near(array, which):
        return lax.dynamic_slice_in_dim(array, which * half_rows, half_rows + 2, axis=0)

    def leave_attend():
        grad_conv_part = jnp.dot(grad_qkv, qkv_full.T, preferred_element_type=full)
        grad_conv_part = from_phases(grad_conv_part.reshape(4, PLANE, model), SIDE)
        grad_conv_part = jnp.pad(
            grad_conv_part.reshape(SIDE, SIDE, model), ((1, 1), (0, 0), (0, 0))
        )
        return rows_near(grad_conv_part, core) + swap_core(
            rows_near(grad_conv_part, 1 - core).astype(low)
        ).astype(full)

    grad_conv = slot(qkv_flows + back_flows[2], leave_attend)

    def leave_block():
        attn_tap_grad = kernel_grad(rows_near(normed_pad, core), grad_conv[1:-1])
        grad_normed_a = depthwise(
            jnp.pad(grad_conv, ((0, 0), (1, 1), (0, 0))), attn_taps[::-1]
        ).reshape(half_tokens, model)
        _, norm_pull_a = jax.vjp(modulate, mine.astype(full), shift_a, scale_a)
        grad_source, grad_shift_a, grad_scale_a = norm_pull_a(grad_normed_a)
        input_grad = grad_source + from_phases(grad_middle, half_rows)
        return attn_tap_grad, input_grad, grad_shift_a, grad_scale_a

    attn_tap_grad, input_grad, grad_shift_a, grad_scale_a = slot(
        qkv_flows + back_flows[2], leave_block
    )
    slot(qkv_flows + proj_flows)
    slot(qkv_flows + proj_flows)
    slot.finish(sum(back_flows, proj_flows + qkv_flows))
    up_shares = [flows[0].result for flows in back_flows]
    down_shares = [flows[1].result for flows in back_flows]
    tap_grads = [g[2][:9].reshape(9, chips, piece) for g in grads]
    qkv_share = jnp.concatenate([f.result for f in qkv_flows], axis=1)
    proj_share = jnp.concatenate([f.result for f in proj_flows], axis=1)
    proj_share = lax.ppermute(proj_share, AXES, proj_back)

    grad_mods = jnp.concatenate(
        [grad_shift_a, grad_scale_a, grad_gate_a, grad_shift_f, grad_scale_f, grad_gate_f]
    )
    grad_mods = (grad_mods + swap_core(grad_mods)).astype(low)
    grad_mods_all = gather_rows(grad_mods, chip, chip_bits)
    mod_grad = jnp.dot(lifted.T, grad_mods_all, preferred_element_type=full)
    (cond_grad,) = lift_pull(jnp.dot(grad_mods_all, mod_weight.T, preferred_element_type=full))
    table_grad = jnp.dot(picks.astype(full).T, cond_grad, precision=highest)

    ffn_tap_grad = jnp.concatenate(tap_grads, axis=2).transpose(1, 0, 2)
    attn_split = attn_tap_grad.reshape(9, chips, 2, part)
    attn_kept, attn_leaving = halves_of(attn_split, 2)
    attn_tap_grad = (attn_kept + swap_core(attn_leaving)).transpose(1, 0, 2)
    tap_parts = jnp.concatenate(
        [ffn_tap_grad.reshape(chips, -1), attn_tap_grad.reshape(chips, -1)], axis=1
    )
    tap_share = scatter_sum(tap_parts, 0, chip, chip_bits, sent=full)
    ffn_share = tap_share[: 9 * share].reshape(9, share)
    kernel_share = tap_share[9 * share :].reshape(9, part)

    def row_split(array, axis):
        pair = array.reshape((2, part) + array.shape[1:])
        kept, leaving = halves_of(pair, 0)
        arriving = swap_core(leaving)
        return jnp.stack(in_core_order(kept, arriving, core), axis=axis)

    up_all = jnp.stack(up_shares, axis=1).reshape(2 * part, CHUNKS, chips, piece)
    up_share = row_split(up_all.transpose(0, 2, 1, 3), 2).reshape(part, -1)
    down_share = jnp.concatenate(down_shares, axis=0)
    qkv_all = qkv_share.reshape(2 * part, pairs, 3, 128).transpose(0, 2, 1, 3)
    qkv_out = row_split(qkv_all, 2).reshape(part, -1)

    return (
        layer_out,
        input_grad[None],
        mod_grad,
        table_grad,
        kernel_share,
        qkv_out,
        proj_share,
        up_share,
        ffn_share,
        down_share,
        grad_shift_f[None],
    )


def solution(mesh):
    return jax.shard_map(
        on_device,
        mesh=mesh,
        in_specs=(
            P(AXES, None, None),
            P(),
            P(),
            P(),
            P(AXES, None, None),
            P(AXES, None),
            P(None, AXES),
            P(None, AXES),
            P(AXES, None),
            P(AXES, None),
            P(AXES, None),
            P(None, AXES),
            P(AXES, None),
        ),
        out_specs=(
            P(AXES, None, None),
            P(AXES, None, None),
            P(AXES, None),
            P(None, AXES),
            P(None, AXES),
            P(AXES, None),
            P(AXES, None),
            P(AXES, None),
            P(None, AXES),
            P(AXES, None),
            P(AXES, None),
        ),
        check_vma=False,
    )
```

```python
import functools
import math

import jax
import jax.numpy as jnp
from jax import lax
from jax.experimental import pallas as pl
from jax.experimental.pallas import tpu as pltpu
from jax.sharding import PartitionSpec as P

HEAD = 64
SIDE = 32
HALF_SIDE = SIDE // 2
STRIP = HALF_SIDE
PLANE = HALF_SIDE * HALF_SIDE
PADDED = PLANE + 2 * STRIP
TILE = 256
CHUNKS = 3

highest = lax.Precision.HIGHEST
ln_epsilon = 1e-06
masked_score = -1000000000.0
low = jnp.bfloat16
full = jnp.float32
AXES = ("dp", "fsdp")


def device_count():
    return lax.axis_size("dp") * lax.axis_size("fsdp")


def swap(x, bit):
    return lax.ppermute(x, AXES, [(i, i ^ 1 << bit) for i in range(device_count())])


def swap_core(x):
    return swap(x, 0)


def gather_order(chip_bits, colour):
    order = list(range(chip_bits - 1, -1, -1))
    if colour and chip_bits > 1:
        order[-1], order[-2] = order[-2], order[-1]
    return order


class Flow:
    def __init__(self, steps):
        self.steps = steps
        self.wanted = next(steps)
        self.result = None

    def arrive(self, array):
        try:
            self.wanted = self.steps.send(array)
        except StopIteration as end:
            self.wanted, self.result = None, end.value


class Slots:
    def __init__(self, token):
        self.token = token

    def finish(self, flows):
        while any(flow.wanted is not None for flow in flows):
            self(flows)

    def __call__(self, flows, work=lambda: ()):
        flows = [flow for flow in flows if flow.wanted is not None]
        wanted = [flow.wanted for flow in flows]
        leaving, self.token = lax.optimization_barrier(([w[0] for w in wanted], self.token))
        arriving = [swap(array, bit + 1) for array, (_, bit) in zip(leaving, wanted)]
        arriving, result, self.token = lax.optimization_barrier((arriving, work(), self.token))
        for flow, array in zip(flows, arriving):
            flow.arrive(array)
        return result


def gather_steps(shard, order):
    held = shard[None]
    for bit in order[:-1]:
        arriving = yield held, bit
        held = jnp.concatenate([held, arriving], axis=0)
    arriving = yield held, order[-1]
    return held, arriving


def assemble_body(steps, chip_ref, *refs):
    *piece_refs, out_ref = refs
    which = pl.program_id(0) // steps
    top = chip_ref[1]
    for index, piece_ref in enumerate(piece_refs):

        @pl.when(which == index)
        def _():
            for k in range(4):
                out_ref[jnp.bitwise_xor(top, (k & 1) << 1 | k >> 1), 0] = piece_ref[k]


def assemble(pieces, order, chip):
    chips = sum(piece.shape[0] for piece in pieces)
    rows, columns = pieces[0].shape[1:]
    if chips < 4 or len(pieces) * pieces[0].shape[0] != chips or pieces[0].shape[0] % 4:
        raise ValueError("unexpected mesh")
    rest = len(order) - 2
    steps = pieces[0].shape[0] // 4
    chip_words = jnp.stack([jnp.bitwise_and(chip, (1 << rest) - 1), chip >> rest]).astype(jnp.int32)

    def out_map(step, words):
        at = words[0]
        for position, bit in enumerate(order[2:]):
            at = jnp.bitwise_xor(at, jnp.bitwise_and(step >> position, 1) << bit)
        return (0, at, 0, 0)

    def piece_map(index):
        return lambda step, words: (jnp.clip(step - index * steps, 0, steps - 1), 0, 0)

    out = pl.pallas_call(
        functools.partial(assemble_body, steps),
        grid_spec=pltpu.PrefetchScalarGridSpec(
            num_scalar_prefetch=1,
            grid=(chips // 4,),
            in_specs=[
                pl.BlockSpec((4, rows, columns), piece_map(index)) for index in range(len(pieces))
            ],
            out_specs=pl.BlockSpec((4, 1, rows, columns), out_map),
        ),
        out_shape=jax.ShapeDtypeStruct((4, chips // 4, rows, columns), pieces[0].dtype),
        cost_estimate=pl.CostEstimate(
            flops=0, bytes_accessed=4 * chips * rows * columns, transcendentals=0
        ),
        name="assemble",
    )(chip_words, *pieces)
    return out.reshape(chips, rows, columns)


def gather_flow(shard, colour, chip_bits):
    return Flow(gather_steps(shard, gather_order(chip_bits, colour)))


def gathered(flow, colour, chip, chip_bits):
    return assemble(flow.result, gather_order(chip_bits, colour), chip)


def at_bit(array, axis, bit):
    return lax.dynamic_index_in_dim(array, bit, axis, keepdims=False)


def scatter_steps(parts, order, chip, chip_bits, sent):
    left = list(range(chip_bits - 1, -1, -1))
    held = [parts.reshape((2,) * chip_bits + parts.shape[1:])]
    for bit in order:
        axis = left.index(bit)
        left.remove(bit)
        mine = jnp.bitwise_and(chip >> bit, 1)
        leaving = sum(at_bit(h, axis, 1 - mine).astype(full) for h in held).astype(sent)
        staying = sum(at_bit(h, axis, mine).astype(full) for h in held).astype(sent)
        arriving = yield leaving, bit
        held = [staying, arriving]
    return held[0].astype(full) + held[1].astype(full)


def scatter_flow(parts, colour, chip, chip_bits, sent=low):
    order = gather_order(chip_bits, colour)[::-1]
    return Flow(scatter_steps(parts, order, chip, chip_bits, sent))


def scatter_sum(parts, colour, chip, chip_bits, sent=low):
    flow = scatter_flow(parts, colour, chip, chip_bits, sent)
    while flow.wanted is not None:
        array, bit = flow.wanted
        flow.arrive(swap(array, bit + 1))
    return flow.result


def gather_rows(row, chip, chip_bits, first_bit=1):
    order = gather_order(chip_bits, 0)
    held = row[None]
    for bit in order:
        held = jnp.concatenate([held, swap(held, bit + first_bit)], axis=0)
    places = jnp.arange(1 << chip_bits)
    position = jnp.zeros_like(places)
    apart = jnp.bitwise_xor(places, chip)
    for step, bit in enumerate(order):
        position = position + (jnp.bitwise_and(apart >> bit, 1) << step)
    pick = position[:, None] == places[None, :]
    return jnp.dot(pick.astype(held.dtype), held, preferred_element_type=full).astype(held.dtype)


def to_phases(block_in, row_count):
    width = block_in.shape[-1]
    split_grid = block_in.reshape(row_count // 2, 2, HALF_SIDE, 2, width)
    return split_grid.transpose(1, 3, 0, 2, 4).reshape(4, row_count // 2 * HALF_SIDE, width)


def from_phases(block_in, row_count):
    width = block_in.shape[-1]
    split_grid = block_in.reshape(2, 2, row_count // 2, HALF_SIDE, width)
    return split_grid.transpose(2, 0, 3, 1, 4).reshape(row_count * SIDE, width)


def in_core_order(mine, other, core):
    return jnp.where(core == 0, mine, other), jnp.where(core == 0, other, mine)


def join_halves(mine, other, core):
    return jnp.stack(in_core_order(mine, other, core), axis=1).reshape(-1, mine.shape[-1])


def half_of(joined, which):
    width = joined.shape[-1]
    return at_bit(joined.reshape(4, 2, -1, width), 1, which)


def layer_norm(values):
    average = jnp.mean(values, axis=-1, keepdims=True)
    centred = values - average
    variance = jnp.mean(centred * centred, axis=-1, keepdims=True)
    return centred * lax.rsqrt(variance + ln_epsilon)


def modulate(values, shift_by, scale_by):
    return layer_norm(values) * (1.0 + scale_by) + shift_by


def sinusoid(steps_in, width):
    halfway = width // 2
    frequency = jnp.exp(-math.log(10000.0) * jnp.arange(halfway, dtype=jnp.float32) / halfway)
    angles = steps_in.astype(jnp.float32)[..., None] * frequency
    return jnp.concatenate([jnp.cos(angles), jnp.sin(angles)], axis=-1)


def softmax_of(query, key, allowed):
    raw = lax.dot_general(query, key, (((1,), (1,)), ((), ())), preferred_element_type=full)
    scores = jnp.where(allowed, raw * HEAD ** (-0.5), masked_score)
    shifted = jnp.exp(scores - jnp.max(scores, axis=-1, keepdims=True))
    return shifted / jnp.sum(shifted, axis=-1, keepdims=True)


def head_lanes(shape, head):
    lanes = lax.broadcasted_iota(jnp.int32, shape, 1)
    return jnp.logical_and(lanes >= head * HEAD, lanes < (head + 1) * HEAD)


def attend_body(mask_ref, qkv_ref, out_ref):
    allowed = mask_ref[...] > 0.5

    @pl.loop(0, 4)
    def _(phase):
        rows = pl.ds(pl.multiple_of(phase * PLANE, PLANE), PLANE)
        query = qkv_ref[rows, :128]
        key = qkv_ref[rows, 128:256]
        value = qkv_ref[rows, 256:]
        total = None
        for head in range(2):
            here = head_lanes(key.shape, head)
            probs = softmax_of(query, jnp.where(here, key, jnp.zeros_like(key)), allowed)
            part = jnp.dot(
                probs.astype(low),
                jnp.where(here, value, jnp.zeros_like(value)),
                preferred_element_type=full,
            )
            total = part if total is None else total + part
        out_ref[rows, :] = total.astype(low)


def attend_back_body(mask_ref, qkv_ref, grad_ref, out_ref):
    allowed = mask_ref[...] > 0.5

    @pl.loop(0, 4)
    def _(phase):
        rows = pl.ds(pl.multiple_of(phase * PLANE, PLANE), PLANE)
        query = qkv_ref[rows, :128]
        key = qkv_ref[rows, 128:256]
        value = qkv_ref[rows, 256:]
        grad = grad_ref[rows, :]
        by_rows = (((0,), (0,)), ((), ()))
        totals = [None, None, None]
        for head in range(2):
            here = head_lanes(key.shape, head)
            blank = jnp.zeros_like(key)
            key_here = jnp.where(here, key, blank)
            query_here = jnp.where(here, query, blank)
            value_here = jnp.where(here, value, blank)
            grad_here = jnp.where(here, grad, blank)
            weights = softmax_of(query, key_here, allowed)
            grad_probs = lax.dot_general(
                grad, value_here, (((1,), (1,)), ((), ())), preferred_element_type=full
            )
            delta = jnp.sum(grad_probs * weights, axis=-1, keepdims=True)
            grad_scores = (weights * (grad_probs - delta)).astype(low)
            parts = (
                jnp.dot(grad_scores, key_here, preferred_element_type=full),
                lax.dot_general(grad_scores, query_here, by_rows, preferred_element_type=full),
                lax.dot_general(
                    weights.astype(low), grad_here, by_rows, preferred_element_type=full
                ),
            )
            totals = [p if t is None else t + p for t, p in zip(totals, parts)]
        out_ref[rows, :128] = (totals[0] * HEAD ** (-0.5)).astype(low)
        out_ref[rows, 128:256] = (totals[1] * HEAD ** (-0.5)).astype(low)
        out_ref[rows, 256:] = totals[2].astype(low)


def attend(mask, qkv):
    tokens, width = qkv.shape
    pairs = width // 384
    return pl.pallas_call(
        attend_body,
        grid=(pairs,),
        in_specs=[
            pl.BlockSpec((PLANE, PLANE), lambda j: (0, 0)),
            pl.BlockSpec((tokens, 384), lambda j: (0, j)),
        ],
        out_specs=pl.BlockSpec((tokens, 128), lambda j: (0, j)),
        out_shape=jax.ShapeDtypeStruct((tokens, pairs * 128), low),
        cost_estimate=pl.CostEstimate(
            flops=pairs * 2 * 4 * 4 * PLANE * PLANE * 256,
            bytes_accessed=8 * tokens * pairs * 128,
            transcendentals=pairs * 8 * PLANE * PLANE,
        ),
        name="attend",
    )(mask, qkv)


def attend_back(mask, qkv, grad):
    tokens, width = qkv.shape
    pairs = width // 384
    return pl.pallas_call(
        attend_back_body,
        grid=(pairs,),
        in_specs=[
            pl.BlockSpec((PLANE, PLANE), lambda j: (0, 0)),
            pl.BlockSpec((tokens, 384), lambda j: (0, j)),
            pl.BlockSpec((tokens, 128), lambda j: (0, j)),
        ],
        out_specs=pl.BlockSpec((tokens, 384), lambda j: (0, j)),
        out_shape=jax.ShapeDtypeStruct((tokens, width), low),
        cost_estimate=pl.CostEstimate(
            flops=pairs * 2 * 4 * 10 * PLANE * PLANE * 256,
            bytes_accessed=14 * tokens * pairs * 128,
            transcendentals=pairs * 8 * PLANE * PLANE,
        ),
        name="attend_back",
    )(mask, qkv, grad)


def strip_at(ref, row_phase, column_phase, row):
    start = pl.multiple_of((row + 1) * STRIP, STRIP)
    return ref[2 * row_phase + column_phase, pl.ds(start, STRIP), :]


def near_strips(ref, row):
    tokens = lax.broadcasted_iota(jnp.int32, (STRIP, ref.shape[-1]), 0)
    loaded = {}
    for row_phase, at in ((1, row - 1), (0, row), (1, row), (0, row + 1)):
        even = strip_at(ref, row_phase, 0, at)
        odd = strip_at(ref, row_phase, 1, at)
        before = jnp.where(tokens == 0, 0.0, pltpu.roll(odd, 1, 0))
        after = jnp.where(tokens == STRIP - 1, 0.0, pltpu.roll(even, STRIP - 1, 0))
        loaded[len(loaded)] = ((before, even, odd), (even, odd, after))
    return {0: (loaded[0], loaded[1], loaded[2]), 1: (loaded[1], loaded[2], loaded[3])}


def conv_strip(near, kernel, row_phase, column_phase):
    total = None
    for i in range(3):
        for j in range(3):
            term = near[row_phase][i][column_phase][j] * kernel[3 * i + j : 3 * i + j + 1, :]
            total = term if total is None else total + term
    return total


def feed_body(
    core_ref,
    norm_ref,
    norm_t_ref,
    grad_ref,
    up_ref,
    down_ref,
    kernel_ref,
    up_held_ref,
    down_held_ref,
    kernel_held_ref,
    staying_ref,
    leaving_ref,
    up_grad_ref,
    down_grad_ref,
    kernel_grad_ref,
    branch_acc,
    back_acc,
    hidden,
    widened_grad,
    act_grad,
    act,
    hidden_grad,
):
    step = pl.program_id(0)
    by_columns = (((1,), (1,)), ((), ()))
    width = up_ref.shape[1]

    @pl.when(step == 0)
    def _():
        blank = jnp.zeros((STRIP, width), full)
        for plane in range(4):
            for ref in (hidden, widened_grad):
                ref[plane, pl.ds(0, STRIP), :] = blank
                ref[plane, pl.ds(PLANE + STRIP, STRIP), :] = blank
        branch_acc[...] = jnp.zeros_like(branch_acc)
        back_acc[...] = jnp.zeros_like(back_acc)

    @pl.loop(0, 4)
    def _(plane):
        rows = pl.ds(pl.multiple_of(plane * PLANE, PLANE), PLANE)
        hidden[plane, pl.ds(STRIP, PLANE), :] = jnp.dot(
            norm_ref[rows, :], up_ref[...], preferred_element_type=full
        )
        act_grad[rows, :] = lax.dot_general(
            grad_ref[rows, :], down_ref[...], by_columns, preferred_element_type=full
        )

    kernel = kernel_ref[...]

    def forward_strip(row, sums):
        near = near_strips(hidden, row)
        sums = list(sums)
        for row_phase in range(2):
            for column_phase in range(2):
                plane = 2 * row_phase + column_phase
                wide = conv_strip(near, kernel, row_phase, column_phase)
                square = wide * wide
                bend = math.sqrt(2.0 / math.pi) * (wide + 0.044715 * wide * square)
                curve = jnp.tanh(bend)
                half = 0.5 * (1.0 + curve)
                slope = half + 0.5 * wide * (1.0 - curve * curve) * (
                    math.sqrt(2.0 / math.pi) * (1.0 + 3 * 0.044715 * square)
                )
                at = pl.ds(pl.multiple_of(plane * PLANE + row * STRIP, STRIP), STRIP)
                act[at, :] = (wide * half).astype(low)
                grad_here = slope * act_grad[at, :]
                widened_grad[plane, pl.ds(pl.multiple_of((row + 1) * STRIP, STRIP), STRIP), :] = (
                    grad_here
                )
                for i in range(3):
                    for j in range(3):
                        product = near[row_phase][i][column_phase][j] * grad_here
                        sums[3 * i + j] = sums[3 * i + j] + (product[:8] + product[8:])
        return tuple(sums)

    sums = lax.fori_loop(
        0, HALF_SIDE, forward_strip, tuple(jnp.zeros((8, width), full) for _ in range(9))
    )
    kernel_grad_ref[...] = jnp.concatenate(
        [jnp.sum(s, axis=0, keepdims=True) for s in sums] + [jnp.zeros((7, width), full)], axis=0
    )

    flipped = [kernel[8 - t : 9 - t, :] for t in range(9)]
    flipped = jnp.concatenate(flipped, axis=0)

    @pl.loop(0, HALF_SIDE)
    def _(row):
        near = near_strips(widened_grad, row)
        for row_phase in range(2):
            for column_phase in range(2):
                plane = 2 * row_phase + column_phase
                at = pl.ds(pl.multiple_of(plane * PLANE + row * STRIP, STRIP), STRIP)
                hidden_grad[at, :] = conv_strip(near, flipped, row_phase, column_phase).astype(low)

    @pl.loop(0, 4)
    def _(plane):
        rows = pl.ds(pl.multiple_of(plane * PLANE, PLANE), PLANE)
        branch_acc[rows, :] += jnp.dot(act[rows, :], down_ref[...], preferred_element_type=full)
        back_acc[rows, :] += lax.dot_general(
            hidden_grad[rows, :], up_ref[...], by_columns, preferred_element_type=full
        )

    model = norm_t_ref.shape[0]

    @pl.loop(0, model // TILE)
    def _(tile):
        rows = pl.ds(pl.multiple_of(tile * TILE, TILE), TILE)
        up_grad_ref[rows, :] = jnp.dot(
            norm_t_ref[rows, :], hidden_grad[...], preferred_element_type=full
        ).astype(low)

    down_grad_ref[...] = lax.dot_general(
        act[...], grad_ref[...], (((0,), (0,)), ((), ())), preferred_element_type=full
    ).astype(low)

    @pl.when(step == pl.num_programs(0) - 1)
    def _():
        for ref, which in ((staying_ref, core_ref[0]), (leaving_ref, 1 - core_ref[0])):
            for index, acc in enumerate((branch_acc, back_acc)):
                for plane in range(4):
                    start = plane * PLANE + pl.multiple_of(which * (PLANE // 2), PLANE // 2)
                    ref[index, plane] = acc[pl.ds(start, PLANE // 2), :].astype(low)


def feed_forward(norm, norm_t, grad, up, down, kernel, core, first, count, held=None):
    tokens, model = norm.shape
    channels = up.shape[1]
    width = TILE
    whole = lambda j, words: (0, 0)
    half = lambda j, words: (0, 0, 0, 0)
    across = lambda j, words: (0, first + j)
    down_rows = lambda j, words: (first + j, 0)
    once = pl.Buffered(1)
    grads = [
        jax.ShapeDtypeStruct((model, channels), low),
        jax.ShapeDtypeStruct((channels, model), low),
        jax.ShapeDtypeStruct((16, channels), full),
    ]
    halves = jax.ShapeDtypeStruct((2, 4, PLANE // 2, model), low)
    body = feed_body
    if held is None:
        held = ()

        def body(*refs):
            feed_body(*refs[:7], None, None, None, *refs[7:])

    return pl.pallas_call(
        body,
        grid_spec=pltpu.PrefetchScalarGridSpec(
            num_scalar_prefetch=1,
            grid=(count,),
            in_specs=[
                pl.BlockSpec((tokens, model), whole, pipeline_mode=once),
                pl.BlockSpec((model, tokens), whole, pipeline_mode=once),
                pl.BlockSpec((tokens, model), whole, pipeline_mode=once),
                pl.BlockSpec((model, width), across),
                pl.BlockSpec((width, model), down_rows),
                pl.BlockSpec((16, width), across),
            ]
            + [pl.BlockSpec(memory_space=pl.ANY)] * len(held),
            out_specs=[
                pl.BlockSpec(halves.shape, half),
                pl.BlockSpec(halves.shape, half),
                pl.BlockSpec((model, width), across),
                pl.BlockSpec((width, model), down_rows),
                pl.BlockSpec((16, width), across),
            ],
            scratch_shapes=[
                pltpu.VMEM((tokens, model), full),
                pltpu.VMEM((tokens, model), full),
                pltpu.VMEM((4, PADDED, width), full),
                pltpu.VMEM((4, PADDED, width), full),
                pltpu.VMEM((tokens, width), full),
                pltpu.VMEM((tokens, width), low),
                pltpu.VMEM((tokens, width), low),
            ],
        ),
        out_shape=[halves, halves] + grads,
        input_output_aliases={7 + i: 2 + i for i in range(len(held))},
        compiler_params=pltpu.CompilerParams(vmem_limit_bytes=62 * 1024 * 1024),
        cost_estimate=pl.CostEstimate(
            flops=12 * tokens * model * count * width,
            bytes_accessed=8 * model * count * width + 10 * tokens * model,
            transcendentals=tokens * count * width,
        ),
        name="feed_forward",
    )(core[None].astype(jnp.int32), norm, norm_t, grad, up, down, kernel, *held)


def token_stats(x_ref, average, scale):
    @pl.loop(0, x_ref.shape[0] // STRIP)
    def _(strip):
        rows = pl.ds(pl.multiple_of(strip * STRIP, STRIP), STRIP)
        values = x_ref[rows, :].astype(full)
        mean = jnp.mean(values, axis=-1, keepdims=True)
        centred = values - mean
        variance = jnp.mean(centred * centred, axis=-1, keepdims=True)
        average[rows, :] = jnp.broadcast_to(mean, (STRIP, 128))
        scale[rows, :] = jnp.broadcast_to(lax.rsqrt(variance + ln_epsilon), (STRIP, 128))


def normed_strip(x_ref, average, scale, rows, columns):
    width = columns.size
    wide = lambda ref: jnp.concatenate([ref[rows, :]] * (width // 128), axis=1)
    return (x_ref[rows, columns].astype(full) - wide(average)) * wide(scale)


def frame_zeros(refs):
    for ref in refs:
        blank = jnp.zeros((STRIP, ref.shape[-1]), full)
        for plane in range(4):
            ref[plane, pl.ds(0, STRIP), :] = blank
            ref[plane, pl.ds(ref.shape[1] - STRIP, STRIP), :] = blank


def conv_in_body(x_ref, kernel_ref, mods_ref, out_ref, average, scale, normed):
    step = pl.program_id(0)
    width = out_ref.shape[1]
    columns = pl.ds(pl.multiple_of(step * width, width), width)

    @pl.when(step == 0)
    def _():
        token_stats(x_ref, average, scale)
        frame_zeros([normed])

    shift_by = mods_ref[0:1, :]
    scale_by = 1.0 + mods_ref[1:2, :]

    @pl.loop(0, HALF_SIDE)
    def _(row):
        for plane in range(4):
            rows = pl.ds(pl.multiple_of(plane * PLANE + row * STRIP, STRIP), STRIP)
            normed[plane, pl.ds(pl.multiple_of((row + 1) * STRIP, STRIP), STRIP), :] = (
                normed_strip(x_ref, average, scale, rows, columns) * scale_by + shift_by
            )

    kernel = kernel_ref[...]

    @pl.loop(0, HALF_SIDE)
    def _(row):
        near = near_strips(normed, row)
        for row_phase in range(2):
            for column_phase in range(2):
                plane = 2 * row_phase + column_phase
                at = pl.ds(pl.multiple_of(plane * PLANE + row * STRIP, STRIP), STRIP)
                out_ref[at, :] = conv_strip(near, kernel, row_phase, column_phase).astype(low)


def conv_in(canvas, kernel, mods):
    tokens, model = canvas.shape
    return pl.pallas_call(
        conv_in_body,
        grid=(model // TILE,),
        in_specs=[
            pl.BlockSpec((tokens, model), lambda j: (0, 0), pipeline_mode=pl.Buffered(1)),
            pl.BlockSpec((16, TILE), lambda j: (0, j)),
            pl.BlockSpec((8, TILE), lambda j: (0, j)),
        ],
        out_specs=pl.BlockSpec((tokens, TILE), lambda j: (0, j)),
        out_shape=jax.ShapeDtypeStruct((tokens, model), low),
        scratch_shapes=[
            pltpu.VMEM((tokens, 128), full),
            pltpu.VMEM((tokens, 128), full),
            pltpu.VMEM((4, PADDED, TILE), full),
        ],
        cost_estimate=pl.CostEstimate(
            flops=30 * tokens * model, bytes_accessed=4 * tokens * model, transcendentals=tokens
        ),
        name="conv_in",
    )(canvas, kernel, mods)


def conv_back_body(
    core_ref,
    x_ref,
    kept_ref,
    arriving_ref,
    kernel_ref,
    mods_ref,
    middle_ref,
    out_ref,
    kernel_grad_ref,
    mods_grad_ref,
    average,
    scale,
    normed,
    upstream,
    held,
    sum_plain,
    sum_normed,
):
    step = pl.program_id(0)
    core = core_ref[0]
    width = kept_ref.shape[1]
    near_rows = x_ref.shape[0] // 4 // STRIP
    own_rows = near_rows - 1
    columns = pl.ds(pl.multiple_of(step * width, width), width)

    def near_at(plane, row):
        return pl.ds(pl.multiple_of((plane * near_rows + row) * STRIP, STRIP), STRIP)

    def own_at(plane, row):
        return pl.ds(pl.multiple_of((plane * own_rows + row) * STRIP, STRIP), STRIP)

    @pl.when(step == 0)
    def _():
        token_stats(x_ref, average, scale)
        frame_zeros([normed, upstream])
        sum_plain[...] = jnp.zeros_like(sum_plain)
        sum_normed[...] = jnp.zeros_like(sum_normed)

    shift_by = mods_ref[0:1, :]
    scale_by = 1.0 + mods_ref[1:2, :]

    @pl.loop(0, near_rows)
    def _(row):
        for plane in range(4):
            rows = near_at(plane, row)
            padded = pl.ds(pl.multiple_of((row + 1) * STRIP, STRIP), STRIP)
            normed[plane, padded, :] = (
                normed_strip(x_ref, average, scale, rows, columns) * scale_by + shift_by
            )
            upstream[plane, padded, :] = kept_ref[rows, :].astype(full) + arriving_ref[
                rows, :
            ].astype(full)

    kernel = kernel_ref[...]
    flipped = jnp.concatenate([kernel[8 - t : 9 - t, :] for t in range(9)], axis=0)

    def kernel_strip(row, sums):
        near = near_strips(normed, row + core)
        sums = list(sums)
        for row_phase in range(2):
            for column_phase in range(2):
                grad_here = strip_at(upstream, row_phase, column_phase, row + core)
                for i in range(3):
                    for j in range(3):
                        product = near[row_phase][i][column_phase][j] * grad_here
                        sums[3 * i + j] = sums[3 * i + j] + (product[:8] + product[8:])
        return tuple(sums)

    def fold(sums, rows):
        return jnp.concatenate(
            [jnp.sum(s, axis=0, keepdims=True) for s in sums]
            + [jnp.zeros((rows - len(sums), width), full)],
            axis=0,
        )

    blank = jnp.zeros((8, width), full)
    kernel_grad_ref[...] = fold(lax.fori_loop(0, own_rows, kernel_strip, (blank,) * 9), 16)

    def input_strip(row, sums):
        near = near_strips(upstream, row + core)
        shift_sum, scale_sum = sums
        for row_phase in range(2):
            for column_phase in range(2):
                plane = 2 * row_phase + column_phase
                grad = conv_strip(near, flipped, row_phase, column_phase)
                plain = normed_strip(x_ref, average, scale, near_at(plane, row + core), columns)
                shift_sum = shift_sum + (grad[:8] + grad[8:])
                product = grad * plain
                scale_sum = scale_sum + (product[:8] + product[8:])
                scaled = grad * scale_by
                rows = own_at(plane, row)
                held[step, rows, :] = scaled
                product = scaled * plain
                sum_plain[rows, :] += sum(scaled[:, k : k + 128] for k in range(0, width, 128))
                sum_normed[rows, :] += sum(product[:, k : k + 128] for k in range(0, width, 128))
        return shift_sum, scale_sum

    mods_grad_ref[...] = fold(lax.fori_loop(0, own_rows, input_strip, (blank,) * 2), 8)

    @pl.when(step == pl.num_programs(0) - 1)
    def _():
        model = x_ref.shape[1]

        @pl.loop(0, own_rows)
        def _(row):
            for plane in range(4):
                rows = own_at(plane, row)
                near = near_at(plane, row + core)
                mean_plain = jnp.sum(sum_plain[rows, :], axis=-1, keepdims=True) / model
                mean_normed = jnp.sum(sum_normed[rows, :], axis=-1, keepdims=True) / model
                for block in range(model // width):
                    at = pl.ds(block * width, width)
                    plain = normed_strip(x_ref, average, scale, near, at)
                    spread = jnp.concatenate([scale[near, :]] * (width // 128), axis=1)
                    out_ref[rows, at] = middle_ref[rows, at] + spread * (
                        held[block, rows, :] - mean_plain - plain * mean_normed
                    )


def conv_back(core, x_near, kept, arriving, kernel, mods, grad_middle):
    near_tokens, model = x_near.shape
    own_tokens = grad_middle.shape[0]
    once = pl.Buffered(1)
    whole = lambda j, words: (0, 0)
    across = lambda j, words: (0, j)
    padded = near_tokens // 4 + 2 * STRIP
    return pl.pallas_call(
        conv_back_body,
        grid_spec=pltpu.PrefetchScalarGridSpec(
            num_scalar_prefetch=1,
            grid=(model // TILE,),
            in_specs=[
                pl.BlockSpec((near_tokens, model), whole, pipeline_mode=once),
                pl.BlockSpec((near_tokens, TILE), across),
                pl.BlockSpec((near_tokens, TILE), across),
                pl.BlockSpec((16, TILE), across),
                pl.BlockSpec((8, TILE), across),
                pl.BlockSpec((own_tokens, model), whole, pipeline_mode=once),
            ],
            out_specs=[
                pl.BlockSpec((own_tokens, model), whole),
                pl.BlockSpec((16, TILE), across),
                pl.BlockSpec((8, TILE), across),
            ],
            scratch_shapes=[
                pltpu.VMEM((near_tokens, 128), full),
                pltpu.VMEM((near_tokens, 128), full),
                pltpu.VMEM((4, padded, TILE), full),
                pltpu.VMEM((4, padded, TILE), full),
                pltpu.VMEM((model // TILE, own_tokens, TILE), full),
                pltpu.VMEM((own_tokens, 128), full),
                pltpu.VMEM((own_tokens, 128), full),
            ],
        ),
        out_shape=[
            jax.ShapeDtypeStruct((own_tokens, model), full),
            jax.ShapeDtypeStruct((16, model), full),
            jax.ShapeDtypeStruct((8, model), full),
        ],
        cost_estimate=pl.CostEstimate(
            flops=70 * own_tokens * model,
            bytes_accessed=14 * own_tokens * model,
            transcendentals=near_tokens,
        ),
        name="conv_back",
    )(core[None].astype(jnp.int32), x_near, kept, arriving, kernel, mods, grad_middle)


def on_device(
    tokens,
    seg_ids,
    timesteps,
    labels,
    cotangent,
    mod_weight,
    class_table,
    attn_kernel,
    qkv_weight,
    proj_weight,
    up_weight,
    ffn_kernel,
    down_weight,
):
    devices = device_count()
    chips = devices // 2
    chip_bits = chips.bit_length() - 1
    rank = lax.axis_index("dp") * lax.axis_size("fsdp") + lax.axis_index("fsdp")
    core = rank % 2
    chip = rank // 2
    _, half_tokens, model = tokens.shape
    half_rows = half_tokens // SIDE
    class_count = class_table.shape[0]
    part = model // devices
    share = down_weight.shape[0]
    piece = share // CHUNKS
    pairs = model // HEAD // 4

    def halves_of(array, axis):
        return at_bit(array, axis, core), at_bit(array, axis, 1 - core)

    def row_pair(array, axis):
        kept, leaving = halves_of(array, axis)
        arriving = swap_core(leaving)
        return jnp.concatenate(in_core_order(kept, arriving, core), axis=0)

    qkv_split = qkv_weight.reshape(part, 3, 2, pairs, 128).transpose(0, 2, 3, 1, 4)
    qkv_rows = row_pair(qkv_split.reshape(part, 2, pairs * 384), 1)
    qkv_half = pairs * 384 // 2
    up_split = up_weight.reshape(part, chips, 2, CHUNKS, piece).transpose(0, 2, 3, 1, 4)
    up_rows = row_pair(up_split.reshape(part, 2, CHUNKS, chips * piece), 1)
    proj_there = [(r, r % chips * 2 + r // chips) for r in range(devices)]
    proj_back = [(b, a) for a, b in proj_there]
    proj_rows = lax.ppermute(proj_weight, AXES, proj_there)
    mine = to_phases(tokens[0], half_rows)
    canvas = join_halves(mine, swap_core(mine), core)
    grad_mine = to_phases(cotangent[0], half_rows)
    grad_ph = join_halves(grad_mine, swap_core(grad_mine), core)

    picks = labels[:, None] == jnp.arange(class_count)[None, :]
    angles_here = lax.dynamic_slice_in_dim(sinusoid(timesteps, model), rank * part, part, axis=1)
    cond = angles_here + jnp.dot(picks.astype(low), class_table, preferred_element_type=full)
    lift_value, lift_pull = jax.vjp(jax.nn.silu, cond)
    lifted = lift_value.astype(low)
    mods_part = jnp.dot(lifted, mod_weight, preferred_element_type=full)
    mods_half = scatter_sum(mods_part, 0, chip, chip_bits, sent=full)
    mods = mods_half + swap_core(mods_half)
    shift_a, scale_a, gate_a, shift_f, scale_f, gate_f = jnp.split(mods, 6)

    tap_count = 9 * (share + part)
    tap_words = jnp.concatenate([ffn_kernel.reshape(-1), attn_kernel.reshape(-1)])
    tap_words = jnp.pad(tap_words, (0, -tap_count % 128))
    taps = gather_rows(tap_words, rank, chip_bits + 1, 0)
    ffn_taps = taps[:, : 9 * share].reshape(chips, 2, 9, share)
    ffn_taps = at_bit(ffn_taps, 1, core).reshape(chips, 9, CHUNKS, piece)
    ffn_taps = ffn_taps.transpose(2, 1, 0, 3).reshape(CHUNKS, 9, chips * piece).astype(full)
    ffn_taps = jnp.pad(ffn_taps, ((0, 0), (0, 7), (0, 0)))
    attn_taps = taps[:, 9 * share : tap_count].reshape(devices, 9, part)
    attn_taps = attn_taps.transpose(1, 0, 2).reshape(9, model).astype(full)
    attn_taps = jnp.pad(attn_taps, ((0, 7), (0, 0)))

    spot = jnp.arange(PLANE)
    quadrant = 2 * (spot // (PLANE // 2)) + spot % HALF_SIDE // (HALF_SIDE // 2)
    quadrants_here = at_bit(seg_ids, 0, chip)
    segment = jnp.sum(
        jnp.where(quadrant[:, None] == jnp.arange(4)[None, :], quadrants_here[None, :], 0), axis=1
    )
    mask = (segment[:, None] == segment[None, :]).astype(full)

    slot = Slots(jnp.zeros((8, 128), full))
    flow = lambda shard, colour: gather_flow(shard, colour, chip_bits)
    sums = lambda parts, colour: scatter_flow(parts, colour, chip, chip_bits)
    joined = lambda flows: [
        gathered(f, colour, chip, chip_bits) for colour, f in enumerate(flows)
    ]
    qkv_flows = [flow(qkv_rows[:, :qkv_half], 0), flow(qkv_rows[:, qkv_half:], 1)]
    proj_flows = [flow(proj_rows[:, : model // 2], 0), flow(proj_rows[:, model // 2 :], 1)]
    feed_flows = [
        [flow(up_rows[:, t], 0), flow(down_weight[t * piece : (t + 1) * piece], 1)]
        for t in range(CHUNKS)
    ]

    slot(qkv_flows)
    slot(qkv_flows)

    mods_a = jnp.concatenate([shift_a[None], scale_a[None], jnp.zeros((6, model), full)], axis=0)
    convolved = slot(qkv_flows + proj_flows, lambda: conv_in(canvas, attn_taps, mods_a))
    slot(qkv_flows + proj_flows)

    def project_in():
        weight = jnp.concatenate(
            [array.reshape(model, qkv_half) for array in joined(qkv_flows)], axis=1
        )
        return weight, jnp.dot(convolved, weight, preferred_element_type=full).astype(low)

    slot.finish(qkv_flows)
    qkv_full, qkv = slot(proj_flows + feed_flows[0], project_in)
    attended = slot(proj_flows + feed_flows[0], lambda: attend(mask, qkv))

    def project_out():
        weight = jnp.concatenate(
            [array.reshape(-1, model // 2) for array in joined(proj_flows)], axis=1
        )
        branch_part = jnp.dot(attended, weight, preferred_element_type=full)
        branch = half_of(branch_part, core) + swap_core(
            half_of(branch_part, 1 - core).astype(low)
        ).astype(full)
        return weight, branch

    source_ph = mine.astype(full)
    slot.finish(proj_flows)
    proj_full, branch_a = slot(feed_flows[0] + feed_flows[1], project_out)

    def enter_feed():
        middle = source_ph + gate_a * branch_a
        normed_low = modulate(middle, shift_f, scale_f).astype(low)
        norm = join_halves(normed_low, swap_core(normed_low), core)
        return middle, norm, norm.T, (grad_ph.astype(full) * gate_f).astype(low)

    middle, norm, norm_t, grad_branch_f = slot(feed_flows[0] + feed_flows[1], enter_feed)

    kept = []
    grads = [None] * CHUNKS

    def feed(t, first, count):
        def work():
            if first == 0:
                feed_weights[t] = [
                    array.reshape(shape)
                    for array, shape in zip(joined(feed_flows[t]), ((model, -1), (-1, model)))
                ]
            staying, leaving, *grads_now = feed_forward(
                norm, norm_t, grad_branch_f, *feed_weights[t], ffn_taps[t], core, first, count,
                grads[t],
            )
            return feed_weights[t], staying, leaving, grads_now

        return work

    feed_weights = [None] * CHUNKS
    back_flows = [None] * CHUNKS

    def run_feed(flows, t, first, count):
        slot.finish(feed_flows[t])
        feed_weights[t], staying, leaving, grads[t] = slot(flows, feed(t, first, count))
        kept.append((staying, leaving))

    blocks = chips * piece // TILE
    run_feed(feed_flows[1] + feed_flows[2], 0, 0, 1)
    run_feed(feed_flows[1] + feed_flows[2], 0, 1, blocks - 1)
    run_feed(feed_flows[2], 1, 0, 1)
    run_feed(feed_flows[2], 1, 1, blocks - 1)

    def begin_back(t):
        back_flows[t] = [
            sums(grads[t][0].reshape(chips, 2 * part, -1), 0),
            sums(grads[t][1].reshape(chips, piece, model), 1),
        ]

    begin_back(0)
    begin_back(1)
    run_feed(back_flows[0], 2, 0, blocks - 1)
    run_feed(back_flows[0], 2, blocks - 1, 1)
    begin_back(2)

    upstream = to_phases(cotangent[0], half_rows).astype(full)

    def leave_feed():
        total = sum(
            staying.astype(full) + swap_core(leaving).astype(full) for staying, leaving in kept
        )
        branch_sum, back_sum = total[0], total[1]
        layer_out = from_phases((middle + gate_f * branch_sum).astype(low), half_rows)
        grad_gate_f = jnp.sum(upstream * branch_sum, axis=(0, 1))
        _, norm_pull_f = jax.vjp(modulate, middle, shift_f, scale_f)
        grad_middle, grad_shift_f, grad_scale_f = norm_pull_f(back_sum)
        grad_middle = grad_middle + upstream
        grad_gate_a = jnp.sum(grad_middle * branch_a, axis=(0, 1))
        grad_branch_mine = (grad_middle * gate_a).astype(low)
        return (
            layer_out, grad_middle, grad_branch_mine,
            grad_gate_f, grad_shift_f, grad_scale_f, grad_gate_a,
        )

    (
        layer_out, grad_middle, grad_branch_mine,
        grad_gate_f, grad_shift_f, grad_scale_f, grad_gate_a,
    ) = slot(back_flows[0] + back_flows[1], leave_feed)
    layer_out = layer_out[None]

    def enter_attend():
        grad_branch_a = join_halves(grad_branch_mine, swap_core(grad_branch_mine), core)
        grad_attended = jnp.dot(grad_branch_a, proj_full.T, preferred_element_type=full)
        proj_grad = jnp.dot(attended.T, grad_branch_a, preferred_element_type=full)
        return grad_attended.astype(low), proj_grad.astype(low)

    grad_attended, proj_grad = slot(back_flows[0] + back_flows[1], enter_attend)
    proj_grad = proj_grad.reshape(chips, -1, model)
    proj_flows = [sums(proj_grad[..., : model // 2], 0), sums(proj_grad[..., model // 2 :], 1)]
    grad_qkv = slot(
        back_flows[1] + back_flows[2], lambda: attend_back(mask, qkv, grad_attended)
    )
    qkv_grad = slot(
        back_flows[1] + back_flows[2],
        lambda: jnp.dot(convolved.T, grad_qkv, preferred_element_type=full).astype(low),
    )
    qkv_grad = qkv_grad.reshape(chips, 2 * part, -1)
    qkv_flows = [sums(qkv_grad[..., :qkv_half], 0), sums(qkv_grad[..., qkv_half:], 1)]

    def rows_near(array, which):
        size = PLANE // 2 + STRIP
        near = lax.dynamic_slice_in_dim(
            array.reshape(4, PLANE, model), which * (PLANE - size), size, axis=1
        )
        return near.reshape(4 * size, model)

    def leave_attend():
        part_here = jnp.dot(grad_qkv, qkv_full.T, preferred_element_type=full).astype(low)
        return rows_near(part_here, core), swap_core(rows_near(part_here, 1 - core))

    grad_conv = slot(qkv_flows + back_flows[2], leave_attend)

    def leave_block():
        input_grad, attn_tap_grad, mods_grad = conv_back(
            core, rows_near(canvas, core), *grad_conv, attn_taps, mods_a,
            grad_middle.reshape(half_tokens, model),
        )
        input_grad = from_phases(input_grad.reshape(4, -1, model), half_rows)
        return attn_tap_grad[:9], input_grad, mods_grad[0], mods_grad[1]

    attn_tap_grad, input_grad, grad_shift_a, grad_scale_a = slot(
        qkv_flows + back_flows[2], leave_block
    )
    slot(qkv_flows + proj_flows)
    slot(qkv_flows + proj_flows)
    slot.finish(sum(back_flows, proj_flows + qkv_flows))
    up_shares = [flows[0].result for flows in back_flows]
    down_shares = [flows[1].result for flows in back_flows]
    tap_grads = [g[2][:9].reshape(9, chips, piece) for g in grads]
    qkv_share = jnp.concatenate([f.result for f in qkv_flows], axis=1)
    proj_share = jnp.concatenate([f.result for f in proj_flows], axis=1)
    proj_share = lax.ppermute(proj_share, AXES, proj_back)

    grad_mods = jnp.concatenate(
        [grad_shift_a, grad_scale_a, grad_gate_a, grad_shift_f, grad_scale_f, grad_gate_f]
    )
    grad_mods = (grad_mods + swap_core(grad_mods)).astype(low)
    grad_mods_all = gather_rows(grad_mods, chip, chip_bits)
    mod_grad = jnp.dot(lifted.T, grad_mods_all, preferred_element_type=full)
    (cond_grad,) = lift_pull(jnp.dot(grad_mods_all, mod_weight.T, preferred_element_type=full))
    table_grad = jnp.dot(picks.astype(full).T, cond_grad, precision=highest)

    ffn_tap_grad = jnp.concatenate(tap_grads, axis=2).transpose(1, 0, 2)
    attn_split = attn_tap_grad.reshape(9, chips, 2, part)
    attn_kept, attn_leaving = halves_of(attn_split, 2)
    attn_tap_grad = (attn_kept + swap_core(attn_leaving)).transpose(1, 0, 2)
    tap_parts = jnp.concatenate(
        [ffn_tap_grad.reshape(chips, -1), attn_tap_grad.reshape(chips, -1)], axis=1
    )
    tap_share = scatter_sum(tap_parts, 0, chip, chip_bits, sent=full)
    ffn_share = tap_share[: 9 * share].reshape(9, share)
    kernel_share = tap_share[9 * share :].reshape(9, part)

    def row_split(array, axis):
        pair = array.reshape((2, part) + array.shape[1:])
        kept, leaving = halves_of(pair, 0)
        arriving = swap_core(leaving)
        return jnp.stack(in_core_order(kept, arriving, core), axis=axis)

    up_all = jnp.stack(up_shares, axis=1).reshape(2 * part, CHUNKS, chips, piece)
    up_share = row_split(up_all.transpose(0, 2, 1, 3), 2).reshape(part, -1)
    down_share = jnp.concatenate(down_shares, axis=0)
    qkv_all = qkv_share.reshape(2 * part, pairs, 3, 128).transpose(0, 2, 1, 3)
    qkv_out = row_split(qkv_all, 2).reshape(part, -1)

    return (
        layer_out,
        input_grad[None],
        mod_grad,
        table_grad,
        kernel_share,
        qkv_out,
        proj_share,
        up_share,
        ffn_share,
        down_share,
        grad_shift_f[None],
    )


def solution(mesh):
    return jax.shard_map(
        on_device,
        mesh=mesh,
        in_specs=(
            P(AXES, None, None),
            P(),
            P(),
            P(),
            P(AXES, None, None),
            P(AXES, None),
            P(None, AXES),
            P(None, AXES),
            P(AXES, None),
            P(AXES, None),
            P(AXES, None),
            P(None, AXES),
            P(AXES, None),
        ),
        out_specs=(
            P(AXES, None, None),
            P(AXES, None, None),
            P(AXES, None),
            P(None, AXES),
            P(None, AXES),
            P(AXES, None),
            P(AXES, None),
            P(AXES, None),
            P(None, AXES),
            P(AXES, None),
            P(AXES, None),
        ),
        check_vma=False,
    )
```

```python
import functools
import math

import jax
import jax.numpy as jnp
from jax import lax
from jax.experimental import pallas as pl
from jax.experimental.pallas import tpu as pltpu
from jax.sharding import PartitionSpec as P

HEAD = 64
SIDE = 32
HALF_SIDE = SIDE // 2
STRIP = HALF_SIDE
PLANE = HALF_SIDE * HALF_SIDE
PADDED = PLANE + 2 * STRIP
TILE = 256
CHUNKS = 3

highest = lax.Precision.HIGHEST
ln_epsilon = 1e-06
masked_score = -1000000000.0
low = jnp.bfloat16
full = jnp.float32
AXES = ("dp", "fsdp")


def device_count():
    return lax.axis_size("dp") * lax.axis_size("fsdp")


def swap(x, bit):
    return lax.ppermute(x, AXES, [(i, i ^ 1 << bit) for i in range(device_count())])


def swap_core(x):
    return swap(x, 0)


def gather_order(chip_bits, colour):
    order = list(range(chip_bits - 1, -1, -1))
    if colour and chip_bits > 1:
        order[-1], order[-2] = order[-2], order[-1]
    return order


class Flow:
    def __init__(self, steps):
        self.steps = steps
        self.wanted = next(steps)
        self.result = None

    def arrive(self, array):
        try:
            self.wanted = self.steps.send(array)
        except StopIteration as end:
            self.wanted, self.result = None, end.value


class Slots:
    def __init__(self, token):
        self.token = token

    def after(self, *arrays):
        arrays, self.token = lax.optimization_barrier((arrays, self.token))
        return arrays

    def finish(self, flows):
        while any(flow.wanted is not None for flow in flows):
            self(flows)

    def __call__(self, flows, work=lambda: ()):
        flows = [flow for flow in flows if flow.wanted is not None]
        wanted = [flow.wanted for flow in flows]
        leaving, self.token = lax.optimization_barrier(([w[0] for w in wanted], self.token))
        arriving = [swap(array, bit + 1) for array, (_, bit) in zip(leaving, wanted)]
        arriving, result, self.token = lax.optimization_barrier((arriving, work(), self.token))
        for flow, array in zip(flows, arriving):
            flow.arrive(array)
        return result


def gather_steps(shard, order):
    held = shard[None]
    for bit in order[:-1]:
        arriving = yield held, bit
        held = jnp.concatenate([held, arriving], axis=0)
    arriving = yield held, order[-1]
    return held, arriving


def assemble_body(steps, chip_ref, *refs):
    *piece_refs, out_ref = refs
    which = pl.program_id(0) // steps
    top = chip_ref[1]
    for index, piece_ref in enumerate(piece_refs):

        @pl.when(which == index)
        def _():
            for k in range(4):
                out_ref[jnp.bitwise_xor(top, (k & 1) << 1 | k >> 1), 0] = piece_ref[k]


def assemble(pieces, order, chip):
    chips = sum(piece.shape[0] for piece in pieces)
    rows, columns = pieces[0].shape[1:]
    if chips < 4 or len(pieces) * pieces[0].shape[0] != chips or pieces[0].shape[0] % 4:
        raise ValueError("unexpected mesh")
    rest = len(order) - 2
    steps = pieces[0].shape[0] // 4
    chip_words = jnp.stack([jnp.bitwise_and(chip, (1 << rest) - 1), chip >> rest]).astype(jnp.int32)

    def out_map(step, words):
        at = words[0]
        for position, bit in enumerate(order[2:]):
            at = jnp.bitwise_xor(at, jnp.bitwise_and(step >> position, 1) << bit)
        return (0, at, 0, 0)

    def piece_map(index):
        return lambda step, words: (jnp.clip(step - index * steps, 0, steps - 1), 0, 0)

    out = pl.pallas_call(
        functools.partial(assemble_body, steps),
        grid_spec=pltpu.PrefetchScalarGridSpec(
            num_scalar_prefetch=1,
            grid=(chips // 4,),
            in_specs=[
                pl.BlockSpec((4, rows, columns), piece_map(index)) for index in range(len(pieces))
            ],
            out_specs=pl.BlockSpec((4, 1, rows, columns), out_map),
        ),
        out_shape=jax.ShapeDtypeStruct((4, chips // 4, rows, columns), pieces[0].dtype),
        cost_estimate=pl.CostEstimate(
            flops=0, bytes_accessed=4 * chips * rows * columns, transcendentals=0
        ),
        name="assemble",
    )(chip_words, *pieces)
    return out.reshape(chips, rows, columns)


def gather_flow(shard, colour, chip_bits):
    return Flow(gather_steps(shard, gather_order(chip_bits, colour)))


def gathered(flow, colour, chip, chip_bits):
    return assemble(flow.result, gather_order(chip_bits, colour), chip)


def at_bit(array, axis, bit):
    return lax.dynamic_index_in_dim(array, bit, axis, keepdims=False)


def scatter_steps(parts, order, chip, chip_bits, sent):
    left = list(range(chip_bits - 1, -1, -1))
    held = [parts.reshape((2,) * chip_bits + parts.shape[1:])]
    for bit in order:
        axis = left.index(bit)
        left.remove(bit)
        mine = jnp.bitwise_and(chip >> bit, 1)
        leaving = sum(at_bit(h, axis, 1 - mine).astype(full) for h in held).astype(sent)
        staying = sum(at_bit(h, axis, mine).astype(full) for h in held).astype(sent)
        arriving = yield leaving, bit
        held = [staying, arriving]
    return held[0].astype(full) + held[1].astype(full)


def scatter_flow(parts, colour, chip, chip_bits, sent=low):
    order = gather_order(chip_bits, colour)[::-1]
    return Flow(scatter_steps(parts, order, chip, chip_bits, sent))


def scatter_sum(parts, colour, chip, chip_bits, sent=low):
    flow = scatter_flow(parts, colour, chip, chip_bits, sent)
    while flow.wanted is not None:
        array, bit = flow.wanted
        flow.arrive(swap(array, bit + 1))
    return flow.result


def gather_rows(row, chip, chip_bits, first_bit=1):
    order = gather_order(chip_bits, 0)
    held = row[None]
    for bit in order:
        held = jnp.concatenate([held, swap(held, bit + first_bit)], axis=0)
    places = jnp.arange(1 << chip_bits)
    position = jnp.zeros_like(places)
    apart = jnp.bitwise_xor(places, chip)
    for step, bit in enumerate(order):
        position = position + (jnp.bitwise_and(apart >> bit, 1) << step)
    pick = position[:, None] == places[None, :]
    return jnp.dot(pick.astype(held.dtype), held, preferred_element_type=full).astype(held.dtype)


def to_phases(block_in, row_count):
    width = block_in.shape[-1]
    split_grid = block_in.reshape(row_count // 2, 2, HALF_SIDE, 2, width)
    return split_grid.transpose(1, 3, 0, 2, 4).reshape(4, row_count // 2 * HALF_SIDE, width)


def from_phases(block_in, row_count):
    width = block_in.shape[-1]
    split_grid = block_in.reshape(2, 2, row_count // 2, HALF_SIDE, width)
    return split_grid.transpose(2, 0, 3, 1, 4).reshape(row_count * SIDE, width)


def in_core_order(mine, other, core):
    return jnp.where(core == 0, mine, other), jnp.where(core == 0, other, mine)


def join_halves(mine, other, core):
    return jnp.stack(in_core_order(mine, other, core), axis=1).reshape(-1, mine.shape[-1])


def half_of(joined, which):
    width = joined.shape[-1]
    return at_bit(joined.reshape(4, 2, -1, width), 1, which)


def layer_norm(values):
    average = jnp.mean(values, axis=-1, keepdims=True)
    centred = values - average
    variance = jnp.mean(centred * centred, axis=-1, keepdims=True)
    return centred * lax.rsqrt(variance + ln_epsilon)


def modulate(values, shift_by, scale_by):
    return layer_norm(values) * (1.0 + scale_by) + shift_by


def sinusoid(steps_in, width):
    halfway = width // 2
    frequency = jnp.exp(-math.log(10000.0) * jnp.arange(halfway, dtype=jnp.float32) / halfway)
    angles = steps_in.astype(jnp.float32)[..., None] * frequency
    return jnp.concatenate([jnp.cos(angles), jnp.sin(angles)], axis=-1)


def softmax_of(query, key, allowed):
    raw = lax.dot_general(query, key, (((1,), (1,)), ((), ())), preferred_element_type=full)
    scores = jnp.where(allowed, raw * HEAD ** (-0.5), masked_score)
    shifted = jnp.exp(scores - jnp.max(scores, axis=-1, keepdims=True))
    return shifted / jnp.sum(shifted, axis=-1, keepdims=True)


def head_lanes(shape, head):
    lanes = lax.broadcasted_iota(jnp.int32, shape, 1)
    return jnp.logical_and(lanes >= head * HEAD, lanes < (head + 1) * HEAD)


def attend_body(mask_ref, qkv_ref, out_ref):
    allowed = mask_ref[...] > 0.5

    @pl.loop(0, 4)
    def _(phase):
        rows = pl.ds(pl.multiple_of(phase * PLANE, PLANE), PLANE)
        query = qkv_ref[rows, :128]
        key = qkv_ref[rows, 128:256]
        value = qkv_ref[rows, 256:]
        total = None
        for head in range(2):
            here = head_lanes(key.shape, head)
            probs = softmax_of(query, jnp.where(here, key, jnp.zeros_like(key)), allowed)
            part = jnp.dot(
                probs.astype(low),
                jnp.where(here, value, jnp.zeros_like(value)),
                preferred_element_type=full,
            )
            total = part if total is None else total + part
        out_ref[rows, :] = total.astype(low)


def attend_back_body(mask_ref, qkv_ref, grad_ref, out_ref):
    allowed = mask_ref[...] > 0.5

    @pl.loop(0, 4)
    def _(phase):
        rows = pl.ds(pl.multiple_of(phase * PLANE, PLANE), PLANE)
        query = qkv_ref[rows, :128]
        key = qkv_ref[rows, 128:256]
        value = qkv_ref[rows, 256:]
        grad = grad_ref[rows, :]
        by_rows = (((0,), (0,)), ((), ()))
        totals = [None, None, None]
        for head in range(2):
            here = head_lanes(key.shape, head)
            blank = jnp.zeros_like(key)
            key_here = jnp.where(here, key, blank)
            query_here = jnp.where(here, query, blank)
            value_here = jnp.where(here, value, blank)
            grad_here = jnp.where(here, grad, blank)
            weights = softmax_of(query, key_here, allowed)
            grad_probs = lax.dot_general(
                grad, value_here, (((1,), (1,)), ((), ())), preferred_element_type=full
            )
            delta = jnp.sum(grad_probs * weights, axis=-1, keepdims=True)
            grad_scores = (weights * (grad_probs - delta)).astype(low)
            parts = (
                jnp.dot(grad_scores, key_here, preferred_element_type=full),
                lax.dot_general(grad_scores, query_here, by_rows, preferred_element_type=full),
                lax.dot_general(
                    weights.astype(low), grad_here, by_rows, preferred_element_type=full
                ),
            )
            totals = [p if t is None else t + p for t, p in zip(totals, parts)]
        out_ref[rows, :128] = (totals[0] * HEAD ** (-0.5)).astype(low)
        out_ref[rows, 128:256] = (totals[1] * HEAD ** (-0.5)).astype(low)
        out_ref[rows, 256:] = totals[2].astype(low)


def attend(mask, qkv):
    tokens, width = qkv.shape
    pairs = width // 384
    return pl.pallas_call(
        attend_body,
        grid=(pairs,),
        in_specs=[
            pl.BlockSpec((PLANE, PLANE), lambda j: (0, 0)),
            pl.BlockSpec((tokens, 384), lambda j: (0, j)),
        ],
        out_specs=pl.BlockSpec((tokens, 128), lambda j: (0, j)),
        out_shape=jax.ShapeDtypeStruct((tokens, pairs * 128), low),
        cost_estimate=pl.CostEstimate(
            flops=pairs * 2 * 4 * 4 * PLANE * PLANE * 256,
            bytes_accessed=8 * tokens * pairs * 128,
            transcendentals=pairs * 8 * PLANE * PLANE,
        ),
        name="attend",
    )(mask, qkv)


def attend_back(mask, qkv, grad):
    tokens, width = qkv.shape
    pairs = width // 384
    return pl.pallas_call(
        attend_back_body,
        grid=(pairs,),
        in_specs=[
            pl.BlockSpec((PLANE, PLANE), lambda j: (0, 0)),
            pl.BlockSpec((tokens, 384), lambda j: (0, j)),
            pl.BlockSpec((tokens, 128), lambda j: (0, j)),
        ],
        out_specs=pl.BlockSpec((tokens, 384), lambda j: (0, j)),
        out_shape=jax.ShapeDtypeStruct((tokens, width), low),
        cost_estimate=pl.CostEstimate(
            flops=pairs * 2 * 4 * 10 * PLANE * PLANE * 256,
            bytes_accessed=14 * tokens * pairs * 128,
            transcendentals=pairs * 8 * PLANE * PLANE,
        ),
        name="attend_back",
    )(mask, qkv, grad)


def strip_at(ref, row_phase, column_phase, row):
    start = pl.multiple_of((row + 1) * STRIP, STRIP)
    return ref[2 * row_phase + column_phase, pl.ds(start, STRIP), :]


def near_strips(ref, row):
    tokens = lax.broadcasted_iota(jnp.int32, (STRIP, ref.shape[-1]), 0)
    loaded = {}
    for row_phase, at in ((1, row - 1), (0, row), (1, row), (0, row + 1)):
        even = strip_at(ref, row_phase, 0, at)
        odd = strip_at(ref, row_phase, 1, at)
        before = jnp.where(tokens == 0, 0.0, pltpu.roll(odd, 1, 0))
        after = jnp.where(tokens == STRIP - 1, 0.0, pltpu.roll(even, STRIP - 1, 0))
        loaded[len(loaded)] = ((before, even, odd), (even, odd, after))
    return {0: (loaded[0], loaded[1], loaded[2]), 1: (loaded[1], loaded[2], loaded[3])}


def conv_strip(near, kernel, row_phase, column_phase):
    total = None
    for i in range(3):
        for j in range(3):
            term = near[row_phase][i][column_phase][j] * kernel[3 * i + j : 3 * i + j + 1, :]
            total = term if total is None else total + term
    return total


def feed_body(
    core_ref,
    norm_ref,
    norm_t_ref,
    grad_ref,
    up_ref,
    down_ref,
    kernel_ref,
    staying_ref,
    leaving_ref,
    up_grad_ref,
    down_grad_ref,
    kernel_grad_ref,
    branch_acc,
    back_acc,
    hidden,
    widened_grad,
    act_grad,
    act,
    hidden_grad,
):
    step = pl.program_id(0)
    by_columns = (((1,), (1,)), ((), ()))
    width = up_ref.shape[1]

    @pl.when(step == 0)
    def _():
        blank = jnp.zeros((STRIP, width), full)
        for plane in range(4):
            for ref in (hidden, widened_grad):
                ref[plane, pl.ds(0, STRIP), :] = blank
                ref[plane, pl.ds(PLANE + STRIP, STRIP), :] = blank
        branch_acc[...] = jnp.zeros_like(branch_acc)
        back_acc[...] = jnp.zeros_like(back_acc)

    @pl.loop(0, 4)
    def _(plane):
        rows = pl.ds(pl.multiple_of(plane * PLANE, PLANE), PLANE)
        hidden[plane, pl.ds(STRIP, PLANE), :] = jnp.dot(
            norm_ref[rows, :], up_ref[...], preferred_element_type=full
        )
        act_grad[rows, :] = lax.dot_general(
            grad_ref[rows, :], down_ref[...], by_columns, preferred_element_type=full
        )

    kernel = kernel_ref[...]

    def forward_strip(row, sums):
        near = near_strips(hidden, row)
        sums = list(sums)
        for row_phase in range(2):
            for column_phase in range(2):
                plane = 2 * row_phase + column_phase
                wide = conv_strip(near, kernel, row_phase, column_phase)
                square = wide * wide
                bend = math.sqrt(2.0 / math.pi) * (wide + 0.044715 * wide * square)
                curve = jnp.tanh(bend)
                half = 0.5 * (1.0 + curve)
                slope = half + 0.5 * wide * (1.0 - curve * curve) * (
                    math.sqrt(2.0 / math.pi) * (1.0 + 3 * 0.044715 * square)
                )
                at = pl.ds(pl.multiple_of(plane * PLANE + row * STRIP, STRIP), STRIP)
                act[at, :] = (wide * half).astype(low)
                grad_here = slope * act_grad[at, :]
                widened_grad[plane, pl.ds(pl.multiple_of((row + 1) * STRIP, STRIP), STRIP), :] = (
                    grad_here
                )
                for i in range(3):
                    for j in range(3):
                        product = near[row_phase][i][column_phase][j] * grad_here
                        sums[3 * i + j] = sums[3 * i + j] + (product[:8] + product[8:])
        return tuple(sums)

    sums = lax.fori_loop(
        0, HALF_SIDE, forward_strip, tuple(jnp.zeros((8, width), full) for _ in range(9))
    )
    kernel_grad_ref[...] = jnp.concatenate(
        [jnp.sum(s, axis=0, keepdims=True) for s in sums] + [jnp.zeros((7, width), full)], axis=0
    )

    flipped = [kernel[8 - t : 9 - t, :] for t in range(9)]
    flipped = jnp.concatenate(flipped, axis=0)

    @pl.loop(0, HALF_SIDE)
    def _(row):
        near = near_strips(widened_grad, row)
        for row_phase in range(2):
            for column_phase in range(2):
                plane = 2 * row_phase + column_phase
                at = pl.ds(pl.multiple_of(plane * PLANE + row * STRIP, STRIP), STRIP)
                hidden_grad[at, :] = conv_strip(near, flipped, row_phase, column_phase).astype(low)

    @pl.loop(0, 4)
    def _(plane):
        rows = pl.ds(pl.multiple_of(plane * PLANE, PLANE), PLANE)
        branch_acc[rows, :] += jnp.dot(act[rows, :], down_ref[...], preferred_element_type=full)
        back_acc[rows, :] += lax.dot_general(
            hidden_grad[rows, :], up_ref[...], by_columns, preferred_element_type=full
        )

    model = norm_t_ref.shape[0]

    @pl.loop(0, model // TILE)
    def _(tile):
        rows = pl.ds(pl.multiple_of(tile * TILE, TILE), TILE)
        up_grad_ref[rows, :] = jnp.dot(
            norm_t_ref[rows, :], hidden_grad[...], preferred_element_type=full
        ).astype(low)

    down_grad_ref[...] = lax.dot_general(
        act[...], grad_ref[...], (((0,), (0,)), ((), ())), preferred_element_type=full
    ).astype(low)

    @pl.when(step == pl.num_programs(0) - 1)
    def _():
        for ref, which in ((staying_ref, core_ref[0]), (leaving_ref, 1 - core_ref[0])):
            for index, acc in enumerate((branch_acc, back_acc)):
                for plane in range(4):
                    start = plane * PLANE + pl.multiple_of(which * (PLANE // 2), PLANE // 2)
                    ref[index, plane] = acc[pl.ds(start, PLANE // 2), :].astype(low)


def feed_forward(norm, norm_t, grad, up, down, kernel, core):
    tokens, model = norm.shape
    channels = up.shape[1]
    width = TILE
    whole = lambda j, words: (0, 0)
    half = lambda j, words: (0, 0, 0, 0)
    across = lambda j, words: (0, j)
    down_rows = lambda j, words: (j, 0)
    once = pl.Buffered(1)
    grads = [
        jax.ShapeDtypeStruct((model, channels), low),
        jax.ShapeDtypeStruct((channels, model), low),
        jax.ShapeDtypeStruct((16, channels), full),
    ]
    halves = jax.ShapeDtypeStruct((2, 4, PLANE // 2, model), low)
    return pl.pallas_call(
        feed_body,
        grid_spec=pltpu.PrefetchScalarGridSpec(
            num_scalar_prefetch=1,
            grid=(channels // width,),
            in_specs=[
                pl.BlockSpec((tokens, model), whole, pipeline_mode=once),
                pl.BlockSpec((model, tokens), whole, pipeline_mode=once),
                pl.BlockSpec((tokens, model), whole, pipeline_mode=once),
                pl.BlockSpec((model, width), across),
                pl.BlockSpec((width, model), down_rows),
                pl.BlockSpec((16, width), across),
            ],
            out_specs=[
                pl.BlockSpec(halves.shape, half),
                pl.BlockSpec(halves.shape, half),
                pl.BlockSpec((model, width), across),
                pl.BlockSpec((width, model), down_rows),
                pl.BlockSpec((16, width), across),
            ],
            scratch_shapes=[
                pltpu.VMEM((tokens, model), full),
                pltpu.VMEM((tokens, model), full),
                pltpu.VMEM((4, PADDED, width), full),
                pltpu.VMEM((4, PADDED, width), full),
                pltpu.VMEM((tokens, width), full),
                pltpu.VMEM((tokens, width), low),
                pltpu.VMEM((tokens, width), low),
            ],
        ),
        out_shape=[halves, halves] + grads,
        compiler_params=pltpu.CompilerParams(vmem_limit_bytes=62 * 1024 * 1024),
        cost_estimate=pl.CostEstimate(
            flops=12 * tokens * model * channels,
            bytes_accessed=8 * model * channels + 10 * tokens * model,
            transcendentals=tokens * channels,
        ),
        name="feed_forward",
    )(core[None].astype(jnp.int32), norm, norm_t, grad, up, down, kernel)


def token_stats(x_ref, average, scale):
    @pl.loop(0, x_ref.shape[0] // STRIP)
    def _(strip):
        rows = pl.ds(pl.multiple_of(strip * STRIP, STRIP), STRIP)
        values = x_ref[rows, :].astype(full)
        mean = jnp.mean(values, axis=-1, keepdims=True)
        centred = values - mean
        variance = jnp.mean(centred * centred, axis=-1, keepdims=True)
        average[rows, :] = jnp.broadcast_to(mean, (STRIP, 128))
        scale[rows, :] = jnp.broadcast_to(lax.rsqrt(variance + ln_epsilon), (STRIP, 128))


def normed_strip(x_ref, average, scale, rows, columns):
    width = columns.size
    wide = lambda ref: jnp.concatenate([ref[rows, :]] * (width // 128), axis=1)
    return (x_ref[rows, columns].astype(full) - wide(average)) * wide(scale)


def frame_zeros(refs):
    for ref in refs:
        blank = jnp.zeros((STRIP, ref.shape[-1]), full)
        for plane in range(4):
            ref[plane, pl.ds(0, STRIP), :] = blank
            ref[plane, pl.ds(ref.shape[1] - STRIP, STRIP), :] = blank


def conv_in_body(x_ref, kernel_ref, mods_ref, out_ref, average, scale, normed):
    step = pl.program_id(0)
    width = out_ref.shape[1]
    columns = pl.ds(pl.multiple_of(step * width, width), width)

    @pl.when(step == 0)
    def _():
        token_stats(x_ref, average, scale)
        frame_zeros([normed])

    shift_by = mods_ref[0:1, :]
    scale_by = 1.0 + mods_ref[1:2, :]

    @pl.loop(0, HALF_SIDE)
    def _(row):
        for plane in range(4):
            rows = pl.ds(pl.multiple_of(plane * PLANE + row * STRIP, STRIP), STRIP)
            normed[plane, pl.ds(pl.multiple_of((row + 1) * STRIP, STRIP), STRIP), :] = (
                normed_strip(x_ref, average, scale, rows, columns) * scale_by + shift_by
            )

    kernel = kernel_ref[...]

    @pl.loop(0, HALF_SIDE)
    def _(row):
        near = near_strips(normed, row)
        for row_phase in range(2):
            for column_phase in range(2):
                plane = 2 * row_phase + column_phase
                at = pl.ds(pl.multiple_of(plane * PLANE + row * STRIP, STRIP), STRIP)
                out_ref[at, :] = conv_strip(near, kernel, row_phase, column_phase).astype(low)


def conv_in(canvas, kernel, mods):
    tokens, model = canvas.shape
    return pl.pallas_call(
        conv_in_body,
        grid=(model // TILE,),
        in_specs=[
            pl.BlockSpec((tokens, model), lambda j: (0, 0), pipeline_mode=pl.Buffered(1)),
            pl.BlockSpec((16, TILE), lambda j: (0, j)),
            pl.BlockSpec((8, TILE), lambda j: (0, j)),
        ],
        out_specs=pl.BlockSpec((tokens, TILE), lambda j: (0, j)),
        out_shape=jax.ShapeDtypeStruct((tokens, model), low),
        scratch_shapes=[
            pltpu.VMEM((tokens, 128), full),
            pltpu.VMEM((tokens, 128), full),
            pltpu.VMEM((4, PADDED, TILE), full),
        ],
        cost_estimate=pl.CostEstimate(
            flops=30 * tokens * model, bytes_accessed=4 * tokens * model, transcendentals=tokens
        ),
        name="conv_in",
    )(canvas, kernel, mods)


def conv_back_body(
    core_ref,
    x_ref,
    kept_ref,
    arriving_ref,
    kernel_ref,
    mods_ref,
    middle_ref,
    out_ref,
    kernel_grad_ref,
    mods_grad_ref,
    average,
    scale,
    normed,
    upstream,
    held,
    sum_plain,
    sum_normed,
):
    step = pl.program_id(0)
    core = core_ref[0]
    width = kept_ref.shape[1]
    near_rows = x_ref.shape[0] // 4 // STRIP
    own_rows = near_rows - 1
    columns = pl.ds(pl.multiple_of(step * width, width), width)

    def near_at(plane, row):
        return pl.ds(pl.multiple_of((plane * near_rows + row) * STRIP, STRIP), STRIP)

    def own_at(plane, row):
        return pl.ds(pl.multiple_of((plane * own_rows + row) * STRIP, STRIP), STRIP)

    @pl.when(step == 0)
    def _():
        token_stats(x_ref, average, scale)
        frame_zeros([normed, upstream])
        sum_plain[...] = jnp.zeros_like(sum_plain)
        sum_normed[...] = jnp.zeros_like(sum_normed)

    shift_by = mods_ref[0:1, :]
    scale_by = 1.0 + mods_ref[1:2, :]

    @pl.loop(0, near_rows)
    def _(row):
        for plane in range(4):
            rows = near_at(plane, row)
            padded = pl.ds(pl.multiple_of((row + 1) * STRIP, STRIP), STRIP)
            normed[plane, padded, :] = (
                normed_strip(x_ref, average, scale, rows, columns) * scale_by + shift_by
            )
            upstream[plane, padded, :] = kept_ref[rows, :].astype(full) + arriving_ref[
                rows, :
            ].astype(full)

    kernel = kernel_ref[...]
    flipped = jnp.concatenate([kernel[8 - t : 9 - t, :] for t in range(9)], axis=0)

    def kernel_strip(row, sums):
        near = near_strips(normed, row + core)
        sums = list(sums)
        for row_phase in range(2):
            for column_phase in range(2):
                grad_here = strip_at(upstream, row_phase, column_phase, row + core)
                for i in range(3):
                    for j in range(3):
                        product = near[row_phase][i][column_phase][j] * grad_here
                        sums[3 * i + j] = sums[3 * i + j] + (product[:8] + product[8:])
        return tuple(sums)

    def fold(sums, rows):
        return jnp.concatenate(
            [jnp.sum(s, axis=0, keepdims=True) for s in sums]
            + [jnp.zeros((rows - len(sums), width), full)],
            axis=0,
        )

    blank = jnp.zeros((8, width), full)
    kernel_grad_ref[...] = fold(lax.fori_loop(0, own_rows, kernel_strip, (blank,) * 9), 16)

    def input_strip(row, sums):
        near = near_strips(upstream, row + core)
        shift_sum, scale_sum = sums
        for row_phase in range(2):
            for column_phase in range(2):
                plane = 2 * row_phase + column_phase
                grad = conv_strip(near, flipped, row_phase, column_phase)
                plain = normed_strip(x_ref, average, scale, near_at(plane, row + core), columns)
                shift_sum = shift_sum + (grad[:8] + grad[8:])
                product = grad * plain
                scale_sum = scale_sum + (product[:8] + product[8:])
                scaled = grad * scale_by
                rows = own_at(plane, row)
                held[step, rows, :] = scaled
                product = scaled * plain
                sum_plain[rows, :] += sum(scaled[:, k : k + 128] for k in range(0, width, 128))
                sum_normed[rows, :] += sum(product[:, k : k + 128] for k in range(0, width, 128))
        return shift_sum, scale_sum

    mods_grad_ref[...] = fold(lax.fori_loop(0, own_rows, input_strip, (blank,) * 2), 8)

    @pl.when(step == pl.num_programs(0) - 1)
    def _():
        model = x_ref.shape[1]

        @pl.loop(0, own_rows)
        def _(row):
            for plane in range(4):
                rows = own_at(plane, row)
                near = near_at(plane, row + core)
                mean_plain = jnp.sum(sum_plain[rows, :], axis=-1, keepdims=True) / model
                mean_normed = jnp.sum(sum_normed[rows, :], axis=-1, keepdims=True) / model
                for block in range(model // width):
                    at = pl.ds(block * width, width)
                    plain = normed_strip(x_ref, average, scale, near, at)
                    spread = jnp.concatenate([scale[near, :]] * (width // 128), axis=1)
                    out_ref[rows, at] = middle_ref[rows, at] + spread * (
                        held[block, rows, :] - mean_plain - plain * mean_normed
                    )


def conv_back(core, x_near, kept, arriving, kernel, mods, grad_middle):
    near_tokens, model = x_near.shape
    own_tokens = grad_middle.shape[0]
    once = pl.Buffered(1)
    whole = lambda j, words: (0, 0)
    across = lambda j, words: (0, j)
    padded = near_tokens // 4 + 2 * STRIP
    return pl.pallas_call(
        conv_back_body,
        grid_spec=pltpu.PrefetchScalarGridSpec(
            num_scalar_prefetch=1,
            grid=(model // TILE,),
            in_specs=[
                pl.BlockSpec((near_tokens, model), whole, pipeline_mode=once),
                pl.BlockSpec((near_tokens, TILE), across),
                pl.BlockSpec((near_tokens, TILE), across),
                pl.BlockSpec((16, TILE), across),
                pl.BlockSpec((8, TILE), across),
                pl.BlockSpec((own_tokens, model), whole, pipeline_mode=once),
            ],
            out_specs=[
                pl.BlockSpec((own_tokens, model), whole),
                pl.BlockSpec((16, TILE), across),
                pl.BlockSpec((8, TILE), across),
            ],
            scratch_shapes=[
                pltpu.VMEM((near_tokens, 128), full),
                pltpu.VMEM((near_tokens, 128), full),
                pltpu.VMEM((4, padded, TILE), full),
                pltpu.VMEM((4, padded, TILE), full),
                pltpu.VMEM((model // TILE, own_tokens, TILE), full),
                pltpu.VMEM((own_tokens, 128), full),
                pltpu.VMEM((own_tokens, 128), full),
            ],
        ),
        out_shape=[
            jax.ShapeDtypeStruct((own_tokens, model), full),
            jax.ShapeDtypeStruct((16, model), full),
            jax.ShapeDtypeStruct((8, model), full),
        ],
        cost_estimate=pl.CostEstimate(
            flops=70 * own_tokens * model,
            bytes_accessed=14 * own_tokens * model,
            transcendentals=near_tokens,
        ),
        name="conv_back",
    )(core[None].astype(jnp.int32), x_near, kept, arriving, kernel, mods, grad_middle)


def on_device(
    tokens,
    seg_ids,
    timesteps,
    labels,
    cotangent,
    mod_weight,
    class_table,
    attn_kernel,
    qkv_weight,
    proj_weight,
    up_weight,
    ffn_kernel,
    down_weight,
):
    devices = device_count()
    chips = devices // 2
    chip_bits = chips.bit_length() - 1
    rank = lax.axis_index("dp") * lax.axis_size("fsdp") + lax.axis_index("fsdp")
    core = rank % 2
    chip = rank // 2
    _, half_tokens, model = tokens.shape
    half_rows = half_tokens // SIDE
    class_count = class_table.shape[0]
    part = model // devices
    share = down_weight.shape[0]
    piece = share // CHUNKS
    pairs = model // HEAD // 4

    def halves_of(array, axis):
        return at_bit(array, axis, core), at_bit(array, axis, 1 - core)

    def row_pair(array, axis):
        kept, leaving = halves_of(array, axis)
        arriving = swap_core(leaving)
        return jnp.concatenate(in_core_order(kept, arriving, core), axis=0)

    qkv_split = qkv_weight.reshape(part, 3, 2, pairs, 128).transpose(0, 2, 3, 1, 4)
    qkv_rows = row_pair(qkv_split.reshape(part, 2, pairs * 384), 1)
    qkv_half = pairs * 384 // 2

    picks = labels[:, None] == jnp.arange(class_count)[None, :]
    angles_here = lax.dynamic_slice_in_dim(sinusoid(timesteps, model), rank * part, part, axis=1)
    cond = angles_here + jnp.dot(picks.astype(low), class_table, preferred_element_type=full)
    lift_value, lift_pull = jax.vjp(jax.nn.silu, cond)
    lifted = lift_value.astype(low)
    mods_part = jnp.dot(lifted, mod_weight, preferred_element_type=full)

    slot = Slots(jnp.zeros((8, 128), full))
    flow = lambda shard, colour: gather_flow(shard, colour, chip_bits)
    sums = lambda parts, colour: scatter_flow(parts, colour, chip, chip_bits)
    joined = lambda flows: [
        gathered(f, colour, chip, chip_bits) for colour, f in enumerate(flows)
    ]
    mods_flow = scatter_flow(mods_part, 0, chip, chip_bits, sent=full)
    qkv_flows = [flow(qkv_rows[:, :qkv_half], 0), flow(qkv_rows[:, qkv_half:], 1)]
    slot(qkv_flows + [mods_flow])

    tokens, cotangent, up_weight, proj_weight, ffn_kernel, attn_kernel = slot.after(
        tokens, cotangent, up_weight, proj_weight, ffn_kernel, attn_kernel
    )
    up_split = up_weight.reshape(part, chips, 2, CHUNKS, piece).transpose(0, 2, 3, 1, 4)
    up_rows = row_pair(up_split.reshape(part, 2, CHUNKS, chips * piece), 1)
    proj_there = [(r, r % chips * 2 + r // chips) for r in range(devices)]
    proj_back = [(b, a) for a, b in proj_there]
    proj_rows = lax.ppermute(proj_weight, AXES, proj_there)
    mine = to_phases(tokens[0], half_rows)
    canvas = join_halves(mine, swap_core(mine), core)

    slot(qkv_flows + [mods_flow])
    while mods_flow.wanted is not None:
        array, bit = mods_flow.wanted
        mods_flow.arrive(swap(array, bit + 1))
    mods = mods_flow.result + swap_core(mods_flow.result)
    shift_a, scale_a, gate_a, shift_f, scale_f, gate_f = jnp.split(mods, 6)

    tap_count = 9 * (share + part)
    tap_words = jnp.concatenate([ffn_kernel.reshape(-1), attn_kernel.reshape(-1)])
    tap_words = jnp.pad(tap_words, (0, -tap_count % 128))
    taps = gather_rows(tap_words, rank, chip_bits + 1, 0)
    ffn_taps = taps[:, : 9 * share].reshape(chips, 2, 9, share)
    ffn_taps = at_bit(ffn_taps, 1, core).reshape(chips, 9, CHUNKS, piece)
    ffn_taps = ffn_taps.transpose(2, 1, 0, 3).reshape(CHUNKS, 9, chips * piece).astype(full)
    ffn_taps = jnp.pad(ffn_taps, ((0, 0), (0, 7), (0, 0)))
    attn_taps = taps[:, 9 * share : tap_count].reshape(devices, 9, part)
    attn_taps = attn_taps.transpose(1, 0, 2).reshape(9, model).astype(full)
    attn_taps = jnp.pad(attn_taps, ((0, 7), (0, 0)))

    spot = jnp.arange(PLANE)
    quadrant = 2 * (spot // (PLANE // 2)) + spot % HALF_SIDE // (HALF_SIDE // 2)
    quadrants_here = at_bit(seg_ids, 0, chip)
    segment = jnp.sum(
        jnp.where(quadrant[:, None] == jnp.arange(4)[None, :], quadrants_here[None, :], 0), axis=1
    )
    mask = (segment[:, None] == segment[None, :]).astype(full)

    proj_flows = [flow(proj_rows[:, : model // 2], 0), flow(proj_rows[:, model // 2 :], 1)]
    feed_flows = [
        [flow(up_rows[:, t], 0), flow(down_weight[t * piece : (t + 1) * piece], 1)]
        for t in range(CHUNKS)
    ]
    mods_a = jnp.concatenate([shift_a[None], scale_a[None], jnp.zeros((6, model), full)], axis=0)

    slot(qkv_flows + proj_flows + feed_flows[0])
    convolved = slot(
        qkv_flows + proj_flows + feed_flows[0], lambda: conv_in(canvas, attn_taps, mods_a)
    )

    (cotangent,) = slot.after(cotangent)
    upstream = to_phases(cotangent[0], half_rows)
    grad_ph = join_halves(upstream, swap_core(upstream), core)

    def project_in():
        weight = jnp.concatenate(
            [array.reshape(model, qkv_half) for array in joined(qkv_flows)], axis=1
        )
        return weight, jnp.dot(convolved, weight, preferred_element_type=full).astype(low)

    slot.finish(qkv_flows)
    qkv_full, qkv = slot(proj_flows + feed_flows[0] + feed_flows[1], project_in)
    attended = slot(
        proj_flows + feed_flows[1] + feed_flows[2], lambda: attend(mask, qkv)
    )

    def project_out():
        weight = jnp.concatenate(
            [array.reshape(-1, model // 2) for array in joined(proj_flows)], axis=1
        )
        branch_part = jnp.dot(attended, weight, preferred_element_type=full)
        branch = half_of(branch_part, core) + swap_core(
            half_of(branch_part, 1 - core).astype(low)
        ).astype(full)
        return weight, branch

    source_ph = mine.astype(full)
    slot.finish(proj_flows)
    def enter_feed():
        proj_full, branch_a = project_out()
        middle = source_ph + gate_a * branch_a
        normed_low = modulate(middle, shift_f, scale_f).astype(low)
        norm = join_halves(normed_low, swap_core(normed_low), core)
        grad_branch_f = (grad_ph.astype(full) * gate_f).astype(low)
        return proj_full, branch_a, middle, norm, norm.T, grad_branch_f

    proj_full, branch_a, middle, norm, norm_t, grad_branch_f = slot(
        sum(feed_flows, []), enter_feed
    )

    kept = []
    grads = [None] * CHUNKS

    def feed(t):
        def work():
            up, down = joined(feed_flows[t])
            staying, leaving, *grads_now = feed_forward(
                norm, norm_t, grad_branch_f, up.reshape(model, -1), down.reshape(-1, model),
                ffn_taps[t], core,
            )
            return staying, leaving, grads_now

        return work

    back_flows = [[] for _ in range(CHUNKS)]

    def run_feed(flows, t):
        slot.finish(feed_flows[t])
        staying, leaving, grads[t] = slot(flows, feed(t))
        kept.append((staying, leaving))
        back_flows[t] = [
            sums(grads[t][0].reshape(chips, 2 * part, -1), 0),
            sums(grads[t][1].reshape(chips, piece, model), 1),
        ]

    run_feed(feed_flows[1] + feed_flows[2], 0)
    run_feed(feed_flows[2] + back_flows[0], 1)
    run_feed(back_flows[0] + back_flows[1], 2)
    upstream = upstream.astype(full)

    def leave_feed():
        total = sum(
            staying.astype(full) + swap_core(leaving).astype(full) for staying, leaving in kept
        )
        branch_sum, back_sum = total[0], total[1]
        layer_out = from_phases((middle + gate_f * branch_sum).astype(low), half_rows)
        grad_gate_f = jnp.sum(upstream * branch_sum, axis=(0, 1))
        _, norm_pull_f = jax.vjp(modulate, middle, shift_f, scale_f)
        grad_middle, grad_shift_f, grad_scale_f = norm_pull_f(back_sum)
        grad_middle = grad_middle + upstream
        grad_gate_a = jnp.sum(grad_middle * branch_a, axis=(0, 1))
        grad_branch_mine = (grad_middle * gate_a).astype(low)
        return (
            layer_out, grad_middle, grad_branch_mine,
            grad_gate_f, grad_shift_f, grad_scale_f, grad_gate_a,
        )

    (
        layer_out, grad_middle, grad_branch_mine,
        grad_gate_f, grad_shift_f, grad_scale_f, grad_gate_a,
    ) = slot(sum(back_flows, []), leave_feed)
    layer_out = layer_out[None]

    def enter_attend():
        grad_branch_a = join_halves(grad_branch_mine, swap_core(grad_branch_mine), core)
        grad_attended = jnp.dot(grad_branch_a, proj_full.T, preferred_element_type=full)
        proj_grad = jnp.dot(attended.T, grad_branch_a, preferred_element_type=full)
        return grad_attended.astype(low), proj_grad.astype(low)

    grad_attended, proj_grad = slot(sum(back_flows, []), enter_attend)
    proj_grad = proj_grad.reshape(chips, -1, model)
    proj_flows = [sums(proj_grad[..., : model // 2], 0), sums(proj_grad[..., model // 2 :], 1)]
    grad_qkv = slot(
        proj_flows + sum(back_flows, []), lambda: attend_back(mask, qkv, grad_attended)
    )
    qkv_grad = slot(
        proj_flows + sum(back_flows, []),
        lambda: jnp.dot(convolved.T, grad_qkv, preferred_element_type=full).astype(low),
    )
    qkv_grad = qkv_grad.reshape(chips, 2 * part, -1)
    qkv_flows = [sums(qkv_grad[..., :qkv_half], 0), sums(qkv_grad[..., qkv_half:], 1)]

    def rows_near(array, which):
        size = PLANE // 2 + STRIP
        near = lax.dynamic_slice_in_dim(
            array.reshape(4, PLANE, model), which * (PLANE - size), size, axis=1
        )
        return near.reshape(4 * size, model)

    def leave_attend():
        part_here = jnp.dot(grad_qkv, qkv_full.T, preferred_element_type=full).astype(low)
        return rows_near(part_here, core), swap_core(rows_near(part_here, 1 - core))

    grad_conv = slot(qkv_flows + proj_flows + back_flows[2], leave_attend)

    def leave_block():
        input_grad, attn_tap_grad, mods_grad = conv_back(
            core, rows_near(canvas, core), *grad_conv, attn_taps, mods_a,
            grad_middle.reshape(half_tokens, model),
        )
        input_grad = from_phases(input_grad.reshape(4, -1, model), half_rows)
        return attn_tap_grad[:9], input_grad, mods_grad[0], mods_grad[1]

    attn_tap_grad, input_grad, grad_shift_a, grad_scale_a = slot(
        qkv_flows + proj_flows + back_flows[2], leave_block
    )
    slot.finish(sum(back_flows, proj_flows + qkv_flows))
    up_shares = [flows[0].result for flows in back_flows]
    down_shares = [flows[1].result for flows in back_flows]
    tap_grads = [g[2][:9].reshape(9, chips, piece) for g in grads]
    qkv_share = jnp.concatenate([f.result for f in qkv_flows], axis=1)
    proj_share = jnp.concatenate([f.result for f in proj_flows], axis=1)
    proj_share = lax.ppermute(proj_share, AXES, proj_back)

    grad_mods = jnp.concatenate(
        [grad_shift_a, grad_scale_a, grad_gate_a, grad_shift_f, grad_scale_f, grad_gate_f]
    )
    grad_mods = (grad_mods + swap_core(grad_mods)).astype(low)
    grad_mods_all = gather_rows(grad_mods, chip, chip_bits)
    mod_grad = jnp.dot(lifted.T, grad_mods_all, preferred_element_type=full)
    (cond_grad,) = lift_pull(jnp.dot(grad_mods_all, mod_weight.T, preferred_element_type=full))
    table_grad = jnp.dot(picks.astype(full).T, cond_grad, precision=highest)

    ffn_tap_grad = jnp.concatenate(tap_grads, axis=2).transpose(1, 0, 2)
    attn_split = attn_tap_grad.reshape(9, chips, 2, part)
    attn_kept, attn_leaving = halves_of(attn_split, 2)
    attn_tap_grad = (attn_kept + swap_core(attn_leaving)).transpose(1, 0, 2)
    tap_parts = jnp.concatenate(
        [ffn_tap_grad.reshape(chips, -1), attn_tap_grad.reshape(chips, -1)], axis=1
    )
    tap_share = scatter_sum(tap_parts, 0, chip, chip_bits, sent=full)
    ffn_share = tap_share[: 9 * share].reshape(9, share)
    kernel_share = tap_share[9 * share :].reshape(9, part)

    def row_split(array, axis):
        pair = array.reshape((2, part) + array.shape[1:])
        kept, leaving = halves_of(pair, 0)
        arriving = swap_core(leaving)
        return jnp.stack(in_core_order(kept, arriving, core), axis=axis)

    up_all = jnp.stack(up_shares, axis=1).reshape(2 * part, CHUNKS, chips, piece)
    up_share = row_split(up_all.transpose(0, 2, 1, 3), 2).reshape(part, -1)
    down_share = jnp.concatenate(down_shares, axis=0)
    qkv_all = qkv_share.reshape(2 * part, pairs, 3, 128).transpose(0, 2, 1, 3)
    qkv_out = row_split(qkv_all, 2).reshape(part, -1)

    return (
        layer_out,
        input_grad[None],
        mod_grad,
        table_grad,
        kernel_share,
        qkv_out,
        proj_share,
        up_share,
        ffn_share,
        down_share,
        grad_shift_f[None],
    )


def solution(mesh):
    return jax.shard_map(
        on_device,
        mesh=mesh,
        in_specs=(
            P(AXES, None, None),
            P(),
            P(),
            P(),
            P(AXES, None, None),
            P(AXES, None),
            P(None, AXES),
            P(None, AXES),
            P(AXES, None),
            P(AXES, None),
            P(AXES, None),
            P(None, AXES),
            P(AXES, None),
        ),
        out_specs=(
            P(AXES, None, None),
            P(AXES, None, None),
            P(AXES, None),
            P(None, AXES),
            P(None, AXES),
            P(AXES, None),
            P(AXES, None),
            P(AXES, None),
            P(None, AXES),
            P(AXES, None),
            P(AXES, None),
        ),
        check_vma=False,
    )
```

```python
import functools
import math

import jax
import jax.numpy as jnp
from jax import lax
from jax.experimental import pallas as pl
from jax.experimental.pallas import tpu as pltpu
from jax.sharding import PartitionSpec as P

HEAD = 64
SIDE = 32
HALF_SIDE = SIDE // 2
STRIP = HALF_SIDE
PLANE = HALF_SIDE * HALF_SIDE
PADDED = PLANE + 2 * STRIP
TILE = 256
CHUNKS = 3

highest = lax.Precision.HIGHEST
ln_epsilon = 1e-06
masked_score = -1000000000.0
low = jnp.bfloat16
full = jnp.float32
AXES = ("dp", "fsdp")


def device_count():
    return lax.axis_size("dp") * lax.axis_size("fsdp")


def swap(x, bit):
    return lax.ppermute(x, AXES, [(i, i ^ 1 << bit) for i in range(device_count())])


def swap_core(x):
    return swap(x, 0)


def gather_order(chip_bits, colour):
    order = list(range(chip_bits - 1, -1, -1))
    if colour and chip_bits > 1:
        order[-1], order[-2] = order[-2], order[-1]
    return order


class Flow:
    def __init__(self, steps):
        self.steps = steps
        self.wanted = next(steps)
        self.result = None

    def arrive(self, array):
        try:
            self.wanted = self.steps.send(array)
        except StopIteration as end:
            self.wanted, self.result = None, end.value


class Slots:
    def __init__(self, token):
        self.token = token

    def after(self, *arrays):
        arrays, self.token = lax.optimization_barrier((arrays, self.token))
        return arrays

    def finish(self, flows):
        while any(flow.wanted is not None for flow in flows):
            self(flows)

    def __call__(self, flows, work=lambda: ()):
        flows = [flow for flow in flows if flow.wanted is not None]
        wanted = [flow.wanted for flow in flows]
        leaving, self.token = lax.optimization_barrier(([w[0] for w in wanted], self.token))
        arriving = [swap(array, bit + 1) for array, (_, bit) in zip(leaving, wanted)]
        arriving, result, self.token = lax.optimization_barrier((arriving, work(), self.token))
        for flow, array in zip(flows, arriving):
            flow.arrive(array)
        return result


def gather_steps(shard, order):
    held = shard[None]
    for bit in order[:-1]:
        arriving = yield held, bit
        held = jnp.concatenate([held, arriving], axis=0)
    arriving = yield held, order[-1]
    return held, arriving


def assemble_body(steps, chip_ref, *refs):
    *piece_refs, out_ref = refs
    which = pl.program_id(0) // steps
    top = chip_ref[1]
    for index, piece_ref in enumerate(piece_refs):

        @pl.when(which == index)
        def _():
            for k in range(4):
                out_ref[jnp.bitwise_xor(top, (k & 1) << 1 | k >> 1), 0] = piece_ref[k]


def assemble(pieces, order, chip):
    chips = sum(piece.shape[0] for piece in pieces)
    rows, columns = pieces[0].shape[1:]
    if chips < 4 or len(pieces) * pieces[0].shape[0] != chips or pieces[0].shape[0] % 4:
        raise ValueError("unexpected mesh")
    rest = len(order) - 2
    steps = pieces[0].shape[0] // 4
    chip_words = jnp.stack([jnp.bitwise_and(chip, (1 << rest) - 1), chip >> rest]).astype(jnp.int32)

    def out_map(step, words):
        at = words[0]
        for position, bit in enumerate(order[2:]):
            at = jnp.bitwise_xor(at, jnp.bitwise_and(step >> position, 1) << bit)
        return (0, at, 0, 0)

    def piece_map(index):
        return lambda step, words: (jnp.clip(step - index * steps, 0, steps - 1), 0, 0)

    out = pl.pallas_call(
        functools.partial(assemble_body, steps),
        grid_spec=pltpu.PrefetchScalarGridSpec(
            num_scalar_prefetch=1,
            grid=(chips // 4,),
            in_specs=[
                pl.BlockSpec((4, rows, columns), piece_map(index)) for index in range(len(pieces))
            ],
            out_specs=pl.BlockSpec((4, 1, rows, columns), out_map),
        ),
        out_shape=jax.ShapeDtypeStruct((4, chips // 4, rows, columns), pieces[0].dtype),
        cost_estimate=pl.CostEstimate(
            flops=0, bytes_accessed=4 * chips * rows * columns, transcendentals=0
        ),
        name="assemble",
    )(chip_words, *pieces)
    return out.reshape(chips, rows, columns)


def gather_flow(shard, colour, chip_bits):
    return Flow(gather_steps(shard, gather_order(chip_bits, colour)))


def gathered(flow, colour, chip, chip_bits):
    return assemble(flow.result, gather_order(chip_bits, colour), chip)


def at_bit(array, axis, bit):
    return lax.dynamic_index_in_dim(array, bit, axis, keepdims=False)


def scatter_steps(parts, order, chip, chip_bits, sent):
    left = list(range(chip_bits - 1, -1, -1))
    held = [parts.reshape((2,) * chip_bits + parts.shape[1:])]
    for bit in order:
        axis = left.index(bit)
        left.remove(bit)
        mine = jnp.bitwise_and(chip >> bit, 1)
        leaving = sum(at_bit(h, axis, 1 - mine).astype(full) for h in held).astype(sent)
        staying = sum(at_bit(h, axis, mine).astype(full) for h in held).astype(sent)
        arriving = yield leaving, bit
        held = [staying, arriving]
    return held[0].astype(full) + held[1].astype(full)


def halving_steps(leaving, staying, order):
    arriving = yield leaving, order[0]
    for bit in order[1:]:
        half = staying.shape[0] // 2
        leaving, staying = [
            (staying[at].astype(full) + arriving[at].astype(full)).astype(low)
            for at in (slice(half, None), slice(half))
        ]
        arriving = yield leaving, bit
    return (staying.astype(full) + arriving.astype(full))[0]


def owners(colour, chip, chip_bits):
    order = gather_order(chip_bits, colour)
    spots = jnp.arange(1 << chip_bits)
    bits = list(enumerate(order))
    owner = sum((jnp.bitwise_and(spots >> at, 1) << bit) for at, bit in bits)
    apart = jnp.bitwise_xor(spots, chip)
    place = sum((jnp.bitwise_and(apart >> bit, 1) << at) for at, bit in bits)
    return jnp.bitwise_xor(owner, chip), place


def scatter_flow(parts, colour, chip, chip_bits, sent=low):
    order = gather_order(chip_bits, colour)[::-1]
    return Flow(scatter_steps(parts, order, chip, chip_bits, sent))


def scatter_sum(parts, colour, chip, chip_bits, sent=low):
    flow = scatter_flow(parts, colour, chip, chip_bits, sent)
    while flow.wanted is not None:
        array, bit = flow.wanted
        flow.arrive(swap(array, bit + 1))
    return flow.result


def gather_rows(row, chip, chip_bits, first_bit=1):
    order = gather_order(chip_bits, 0)
    held = row[None]
    for bit in order:
        held = jnp.concatenate([held, swap(held, bit + first_bit)], axis=0)
    places = jnp.arange(1 << chip_bits)
    position = jnp.zeros_like(places)
    apart = jnp.bitwise_xor(places, chip)
    for step, bit in enumerate(order):
        position = position + (jnp.bitwise_and(apart >> bit, 1) << step)
    pick = position[:, None] == places[None, :]
    return jnp.dot(pick.astype(held.dtype), held, preferred_element_type=full).astype(held.dtype)


def to_phases(block_in, row_count):
    width = block_in.shape[-1]
    split_grid = block_in.reshape(row_count // 2, 2, HALF_SIDE, 2, width)
    return split_grid.transpose(1, 3, 0, 2, 4).reshape(4, row_count // 2 * HALF_SIDE, width)


def from_phases(block_in, row_count):
    width = block_in.shape[-1]
    split_grid = block_in.reshape(2, 2, row_count // 2, HALF_SIDE, width)
    return split_grid.transpose(2, 0, 3, 1, 4).reshape(row_count * SIDE, width)


def in_core_order(mine, other, core):
    return jnp.where(core == 0, mine, other), jnp.where(core == 0, other, mine)


def join_halves(mine, other, core):
    return jnp.stack(in_core_order(mine, other, core), axis=1).reshape(-1, mine.shape[-1])


def half_of(joined, which):
    width = joined.shape[-1]
    return at_bit(joined.reshape(4, 2, -1, width), 1, which)


def layer_norm(values):
    average = jnp.mean(values, axis=-1, keepdims=True)
    centred = values - average
    variance = jnp.mean(centred * centred, axis=-1, keepdims=True)
    return centred * lax.rsqrt(variance + ln_epsilon)


def modulate(values, shift_by, scale_by):
    return layer_norm(values) * (1.0 + scale_by) + shift_by


def sinusoid(steps_in, width):
    halfway = width // 2
    frequency = jnp.exp(-math.log(10000.0) * jnp.arange(halfway, dtype=jnp.float32) / halfway)
    angles = steps_in.astype(jnp.float32)[..., None] * frequency
    return jnp.concatenate([jnp.cos(angles), jnp.sin(angles)], axis=-1)


def softmax_of(query, key, allowed):
    raw = lax.dot_general(query, key, (((1,), (1,)), ((), ())), preferred_element_type=full)
    scores = jnp.where(allowed, raw * HEAD ** (-0.5), masked_score)
    shifted = jnp.exp(scores - jnp.max(scores, axis=-1, keepdims=True))
    return shifted / jnp.sum(shifted, axis=-1, keepdims=True)


def head_lanes(shape, head):
    lanes = lax.broadcasted_iota(jnp.int32, shape, 1)
    return jnp.logical_and(lanes >= head * HEAD, lanes < (head + 1) * HEAD)


def attend_body(mask_ref, qkv_ref, out_ref):
    allowed = mask_ref[...] > 0.5

    @pl.loop(0, 4)
    def _(phase):
        rows = pl.ds(pl.multiple_of(phase * PLANE, PLANE), PLANE)
        query = qkv_ref[rows, :128]
        key = qkv_ref[rows, 128:256]
        value = qkv_ref[rows, 256:]
        total = None
        for head in range(2):
            here = head_lanes(key.shape, head)
            probs = softmax_of(query, jnp.where(here, key, jnp.zeros_like(key)), allowed)
            part = jnp.dot(
                probs.astype(low),
                jnp.where(here, value, jnp.zeros_like(value)),
                preferred_element_type=full,
            )
            total = part if total is None else total + part
        out_ref[rows, :] = total.astype(low)


def attend_back_body(mask_ref, qkv_ref, grad_ref, out_ref):
    allowed = mask_ref[...] > 0.5

    @pl.loop(0, 4)
    def _(phase):
        rows = pl.ds(pl.multiple_of(phase * PLANE, PLANE), PLANE)
        query = qkv_ref[rows, :128]
        key = qkv_ref[rows, 128:256]
        value = qkv_ref[rows, 256:]
        grad = grad_ref[rows, :]
        by_rows = (((0,), (0,)), ((), ()))
        totals = [None, None, None]
        for head in range(2):
            here = head_lanes(key.shape, head)
            blank = jnp.zeros_like(key)
            key_here = jnp.where(here, key, blank)
            query_here = jnp.where(here, query, blank)
            value_here = jnp.where(here, value, blank)
            grad_here = jnp.where(here, grad, blank)
            weights = softmax_of(query, key_here, allowed)
            grad_probs = lax.dot_general(
                grad, value_here, (((1,), (1,)), ((), ())), preferred_element_type=full
            )
            delta = jnp.sum(grad_probs * weights, axis=-1, keepdims=True)
            grad_scores = (weights * (grad_probs - delta)).astype(low)
            parts = (
                jnp.dot(grad_scores, key_here, preferred_element_type=full),
                lax.dot_general(grad_scores, query_here, by_rows, preferred_element_type=full),
                lax.dot_general(
                    weights.astype(low), grad_here, by_rows, preferred_element_type=full
                ),
            )
            totals = [p if t is None else t + p for t, p in zip(totals, parts)]
        out_ref[rows, :128] = (totals[0] * HEAD ** (-0.5)).astype(low)
        out_ref[rows, 128:256] = (totals[1] * HEAD ** (-0.5)).astype(low)
        out_ref[rows, 256:] = totals[2].astype(low)


def attend(mask, qkv):
    tokens, width = qkv.shape
    pairs = width // 384
    return pl.pallas_call(
        attend_body,
        grid=(pairs,),
        in_specs=[
            pl.BlockSpec((PLANE, PLANE), lambda j: (0, 0)),
            pl.BlockSpec((tokens, 384), lambda j: (0, j)),
        ],
        out_specs=pl.BlockSpec((tokens, 128), lambda j: (0, j)),
        out_shape=jax.ShapeDtypeStruct((tokens, pairs * 128), low),
        cost_estimate=pl.CostEstimate(
            flops=pairs * 2 * 4 * 4 * PLANE * PLANE * 256,
            bytes_accessed=8 * tokens * pairs * 128,
            transcendentals=pairs * 8 * PLANE * PLANE,
        ),
        name="attend",
    )(mask, qkv)


def attend_back(mask, qkv, grad):
    tokens, width = qkv.shape
    pairs = width // 384
    return pl.pallas_call(
        attend_back_body,
        grid=(pairs,),
        in_specs=[
            pl.BlockSpec((PLANE, PLANE), lambda j: (0, 0)),
            pl.BlockSpec((tokens, 384), lambda j: (0, j)),
            pl.BlockSpec((tokens, 128), lambda j: (0, j)),
        ],
        out_specs=pl.BlockSpec((tokens, 384), lambda j: (0, j)),
        out_shape=jax.ShapeDtypeStruct((tokens, width), low),
        cost_estimate=pl.CostEstimate(
            flops=pairs * 2 * 4 * 10 * PLANE * PLANE * 256,
            bytes_accessed=14 * tokens * pairs * 128,
            transcendentals=pairs * 8 * PLANE * PLANE,
        ),
        name="attend_back",
    )(mask, qkv, grad)


def strip_at(ref, row_phase, column_phase, row):
    start = pl.multiple_of((row + 1) * STRIP, STRIP)
    return ref[2 * row_phase + column_phase, pl.ds(start, STRIP), :]


def near_strips(ref, row):
    tokens = lax.broadcasted_iota(jnp.int32, (STRIP, ref.shape[-1]), 0)
    loaded = {}
    for row_phase, at in ((1, row - 1), (0, row), (1, row), (0, row + 1)):
        even = strip_at(ref, row_phase, 0, at)
        odd = strip_at(ref, row_phase, 1, at)
        before = jnp.where(tokens == 0, 0.0, pltpu.roll(odd, 1, 0))
        after = jnp.where(tokens == STRIP - 1, 0.0, pltpu.roll(even, STRIP - 1, 0))
        loaded[len(loaded)] = ((before, even, odd), (even, odd, after))
    return {0: (loaded[0], loaded[1], loaded[2]), 1: (loaded[1], loaded[2], loaded[3])}


def conv_strip(near, kernel, row_phase, column_phase):
    total = None
    for i in range(3):
        for j in range(3):
            term = near[row_phase][i][column_phase][j] * kernel[3 * i + j : 3 * i + j + 1, :]
            total = term if total is None else total + term
    return total


def feed_body(
    spread,
    words_ref,
    norm_ref,
    norm_t_ref,
    grad_ref,
    *refs,
):
    pieces = 2 if spread else 1
    up_refs, refs = refs[:pieces], refs[pieces:]
    down_refs, refs = refs[:pieces], refs[pieces:]
    kernel_ref, staying_ref, leaving_ref, *refs = refs
    up_grad_refs, refs = refs[:pieces], refs[pieces:]
    down_grad_refs, refs = refs[:pieces], refs[pieces:]
    kernel_grad_ref, branch_acc, back_acc, hidden, widened_grad, act_grad, act, hidden_grad = refs[
        :8
    ]
    step = pl.program_id(0)
    core = words_ref[0]
    by_columns = (((1,), (1,)), ((), ()))
    width = kernel_ref.shape[1]
    model = norm_t_ref.shape[0]
    up_ref, down_ref = up_refs[0], down_refs[0]
    if spread:
        up_ref, down_all = refs[8:]
        half, share, _ = up_refs[0].shape
        piece = down_refs[0].shape[1]
        chips = 2 * half
        down_ref = down_all.at[pl.ds(pl.multiple_of(step * width, width), width), :]

        for which in range(2):

            @pl.loop(0, half)
            def _(spot):
                start = pl.multiple_of(words_ref[1 + which * half + spot] * share, share)
                up_ref[pl.ds(start, share), :] = up_refs[which][spot]

            @pl.when(step == 0)
            def _():
                @pl.loop(0, half)
                def _(spot):
                    owner = words_ref[1 + chips + which * half + spot]
                    start = pl.multiple_of(owner * piece, piece)
                    down_all[pl.ds(start, piece), :] = down_refs[which][spot]

    @pl.when(step == 0)
    def _():
        blank = jnp.zeros((STRIP, width), full)
        for plane in range(4):
            for ref in (hidden, widened_grad):
                ref[plane, pl.ds(0, STRIP), :] = blank
                ref[plane, pl.ds(PLANE + STRIP, STRIP), :] = blank
        branch_acc[...] = jnp.zeros_like(branch_acc)
        back_acc[...] = jnp.zeros_like(back_acc)

    @pl.loop(0, 4)
    def _(plane):
        rows = pl.ds(pl.multiple_of(plane * PLANE, PLANE), PLANE)
        hidden[plane, pl.ds(STRIP, PLANE), :] = jnp.dot(
            norm_ref[rows, :], up_ref[...], preferred_element_type=full
        )
        act_grad[rows, :] = lax.dot_general(
            grad_ref[rows, :], down_ref[...], by_columns, preferred_element_type=full
        )

    kernel = kernel_ref[...]

    def forward_strip(row, sums):
        near = near_strips(hidden, row)
        sums = list(sums)
        for row_phase in range(2):
            for column_phase in range(2):
                plane = 2 * row_phase + column_phase
                wide = conv_strip(near, kernel, row_phase, column_phase)
                square = wide * wide
                bend = math.sqrt(2.0 / math.pi) * (wide + 0.044715 * wide * square)
                curve = jnp.tanh(bend)
                half = 0.5 * (1.0 + curve)
                slope = half + 0.5 * wide * (1.0 - curve * curve) * (
                    math.sqrt(2.0 / math.pi) * (1.0 + 3 * 0.044715 * square)
                )
                at = pl.ds(pl.multiple_of(plane * PLANE + row * STRIP, STRIP), STRIP)
                act[at, :] = (wide * half).astype(low)
                grad_here = slope * act_grad[at, :]
                widened_grad[plane, pl.ds(pl.multiple_of((row + 1) * STRIP, STRIP), STRIP), :] = (
                    grad_here
                )
                for i in range(3):
                    for j in range(3):
                        product = near[row_phase][i][column_phase][j] * grad_here
                        sums[3 * i + j] = sums[3 * i + j] + (product[:8] + product[8:])
        return tuple(sums)

    sums = lax.fori_loop(
        0, HALF_SIDE, forward_strip, tuple(jnp.zeros((8, width), full) for _ in range(9))
    )
    kernel_grad_ref[...] = jnp.concatenate(
        [jnp.sum(s, axis=0, keepdims=True) for s in sums] + [jnp.zeros((7, width), full)], axis=0
    )

    flipped = [kernel[8 - t : 9 - t, :] for t in range(9)]
    flipped = jnp.concatenate(flipped, axis=0)

    @pl.loop(0, HALF_SIDE)
    def _(row):
        near = near_strips(widened_grad, row)
        for row_phase in range(2):
            for column_phase in range(2):
                plane = 2 * row_phase + column_phase
                at = pl.ds(pl.multiple_of(plane * PLANE + row * STRIP, STRIP), STRIP)
                hidden_grad[at, :] = conv_strip(near, flipped, row_phase, column_phase).astype(low)

    @pl.loop(0, 4)
    def _(plane):
        rows = pl.ds(pl.multiple_of(plane * PLANE, PLANE), PLANE)
        branch_acc[rows, :] += jnp.dot(act[rows, :], down_ref[...], preferred_element_type=full)
        back_acc[rows, :] += lax.dot_general(
            hidden_grad[rows, :], up_ref[...], by_columns, preferred_element_type=full
        )

    if spread:
        for which in range(2):

            @pl.loop(0, half // 4)
            def _(group):
                lhs = []
                for k in range(4):
                    owner = words_ref[1 + which * half + 4 * group + k]
                    start = pl.multiple_of(owner * share, share)
                    lhs.append(norm_t_ref[pl.ds(start, share), :])
                result = jnp.dot(
                    jnp.concatenate(lhs, axis=0), hidden_grad[...], preferred_element_type=full
                ).astype(low)
                for k in range(4):
                    up_grad_refs[which][4 * group + k] = result[k * share : (k + 1) * share]

    else:

        @pl.loop(0, model // TILE)
        def _(tile):
            rows = pl.ds(pl.multiple_of(tile * TILE, TILE), TILE)
            up_grad_refs[0][rows, :] = jnp.dot(
                norm_t_ref[rows, :], hidden_grad[...], preferred_element_type=full
            ).astype(low)

    down_grad = lax.dot_general(
        act[...], grad_ref[...], (((0,), (0,)), ((), ())), preferred_element_type=full
    ).astype(low)
    if spread:
        for k in range(width // piece):
            place = words_ref[1 + 2 * chips + step * (width // piece) + k]
            for which in range(2):

                @pl.when(place // half == which)
                def _():
                    down_grad_refs[which][place - which * half] = down_grad[
                        k * piece : (k + 1) * piece
                    ]

    else:
        down_grad_refs[0][...] = down_grad

    @pl.when(step == pl.num_programs(0) - 1)
    def _():
        for ref, which in ((staying_ref, core), (leaving_ref, 1 - core)):
            for index, acc in enumerate((branch_acc, back_acc)):
                for plane in range(4):
                    start = plane * PLANE + pl.multiple_of(which * (PLANE // 2), PLANE // 2)
                    ref[index, plane] = acc[pl.ds(start, PLANE // 2), :].astype(low)


def feed_forward(norm, norm_t, grad, up, down, kernel, words):
    tokens, model = norm.shape
    channels = kernel.shape[1]
    width = TILE
    spread = len(up) == 2
    whole = lambda j, words: (0, 0)
    half = lambda j, words: (0, 0, 0, 0)
    across = lambda j, words: (0, j)
    once = pl.Buffered(1)
    piece_scratch = []
    if spread:
        deep = lambda j, words: (0, 0, 0)
        up_spec = pl.BlockSpec(up[0].shape[:2] + (width,), lambda j, words: (0, 0, j))
        down_spec = pl.BlockSpec(down[0].shape, deep, pipeline_mode=once)
        down_grad_spec = pl.BlockSpec(down[0].shape, deep)
        piece_scratch = [pltpu.VMEM((model, width), low), pltpu.VMEM((channels, model), low)]
    else:
        up_spec = pl.BlockSpec((model, width), across)
        down_spec = down_grad_spec = pl.BlockSpec((width, model), lambda j, words: (j, 0))
    halves = jax.ShapeDtypeStruct((2, 4, PLANE // 2, model), low)
    like = lambda arrays: [jax.ShapeDtypeStruct(array.shape, low) for array in arrays]
    out = pl.pallas_call(
        functools.partial(feed_body, spread),
        grid_spec=pltpu.PrefetchScalarGridSpec(
            num_scalar_prefetch=1,
            grid=(channels // width,),
            in_specs=[
                pl.BlockSpec((tokens, model), whole, pipeline_mode=once),
                pl.BlockSpec((model, tokens), whole, pipeline_mode=once),
                pl.BlockSpec((tokens, model), whole, pipeline_mode=once),
                *[up_spec] * len(up),
                *[down_spec] * len(down),
                pl.BlockSpec((16, width), across),
            ],
            out_specs=[
                pl.BlockSpec(halves.shape, half),
                pl.BlockSpec(halves.shape, half),
                *[up_spec] * len(up),
                *[down_grad_spec] * len(down),
                pl.BlockSpec((16, width), across),
            ],
            scratch_shapes=[
                pltpu.VMEM((tokens, model), full),
                pltpu.VMEM((tokens, model), full),
                pltpu.VMEM((4, PADDED, width), full),
                pltpu.VMEM((4, PADDED, width), full),
                pltpu.VMEM((tokens, width), full),
                pltpu.VMEM((tokens, width), low),
                pltpu.VMEM((tokens, width), low),
            ]
            + piece_scratch,
        ),
        out_shape=[halves, halves]
        + like(up)
        + like(down)
        + [jax.ShapeDtypeStruct((16, channels), full)],
        compiler_params=pltpu.CompilerParams(vmem_limit_bytes=63 * 1024 * 1024),
        cost_estimate=pl.CostEstimate(
            flops=12 * tokens * model * channels,
            bytes_accessed=8 * model * channels + 10 * tokens * model,
            transcendentals=tokens * channels,
        ),
        name="feed_forward",
    )(words, norm, norm_t, grad, *up, *down, kernel)
    staying, leaving, *grads, kernel_grad = out
    return staying, leaving, grads[: len(up)], grads[len(up) :], kernel_grad


def token_stats(x_ref, average, scale):
    @pl.loop(0, x_ref.shape[0] // STRIP)
    def _(strip):
        rows = pl.ds(pl.multiple_of(strip * STRIP, STRIP), STRIP)
        values = x_ref[rows, :].astype(full)
        mean = jnp.mean(values, axis=-1, keepdims=True)
        centred = values - mean
        variance = jnp.mean(centred * centred, axis=-1, keepdims=True)
        average[rows, :] = jnp.broadcast_to(mean, (STRIP, 128))
        scale[rows, :] = jnp.broadcast_to(lax.rsqrt(variance + ln_epsilon), (STRIP, 128))


def normed_strip(x_ref, average, scale, rows, columns):
    width = columns.size
    wide = lambda ref: jnp.concatenate([ref[rows, :]] * (width // 128), axis=1)
    return (x_ref[rows, columns].astype(full) - wide(average)) * wide(scale)


def frame_zeros(refs):
    for ref in refs:
        blank = jnp.zeros((STRIP, ref.shape[-1]), full)
        for plane in range(4):
            ref[plane, pl.ds(0, STRIP), :] = blank
            ref[plane, pl.ds(ref.shape[1] - STRIP, STRIP), :] = blank


def conv_in_body(x_ref, kernel_ref, mods_ref, out_ref, average, scale, normed):
    step = pl.program_id(0)
    width = out_ref.shape[1]
    columns = pl.ds(pl.multiple_of(step * width, width), width)

    @pl.when(step == 0)
    def _():
        token_stats(x_ref, average, scale)
        frame_zeros([normed])

    shift_by = mods_ref[0:1, :]
    scale_by = 1.0 + mods_ref[1:2, :]

    @pl.loop(0, HALF_SIDE)
    def _(row):
        for plane in range(4):
            rows = pl.ds(pl.multiple_of(plane * PLANE + row * STRIP, STRIP), STRIP)
            normed[plane, pl.ds(pl.multiple_of((row + 1) * STRIP, STRIP), STRIP), :] = (
                normed_strip(x_ref, average, scale, rows, columns) * scale_by + shift_by
            )

    kernel = kernel_ref[...]

    @pl.loop(0, HALF_SIDE)
    def _(row):
        near = near_strips(normed, row)
        for row_phase in range(2):
            for column_phase in range(2):
                plane = 2 * row_phase + column_phase
                at = pl.ds(pl.multiple_of(plane * PLANE + row * STRIP, STRIP), STRIP)
                out_ref[at, :] = conv_strip(near, kernel, row_phase, column_phase).astype(low)


def conv_in(canvas, kernel, mods):
    tokens, model = canvas.shape
    return pl.pallas_call(
        conv_in_body,
        grid=(model // TILE,),
        in_specs=[
            pl.BlockSpec((tokens, model), lambda j: (0, 0), pipeline_mode=pl.Buffered(1)),
            pl.BlockSpec((16, TILE), lambda j: (0, j)),
            pl.BlockSpec((8, TILE), lambda j: (0, j)),
        ],
        out_specs=pl.BlockSpec((tokens, TILE), lambda j: (0, j)),
        out_shape=jax.ShapeDtypeStruct((tokens, model), low),
        scratch_shapes=[
            pltpu.VMEM((tokens, 128), full),
            pltpu.VMEM((tokens, 128), full),
            pltpu.VMEM((4, PADDED, TILE), full),
        ],
        cost_estimate=pl.CostEstimate(
            flops=30 * tokens * model, bytes_accessed=4 * tokens * model, transcendentals=tokens
        ),
        name="conv_in",
    )(canvas, kernel, mods)


def conv_back_body(
    core_ref,
    x_ref,
    kept_ref,
    arriving_ref,
    kernel_ref,
    mods_ref,
    middle_ref,
    out_ref,
    kernel_grad_ref,
    mods_grad_ref,
    average,
    scale,
    normed,
    upstream,
    held,
    sum_plain,
    sum_normed,
):
    step = pl.program_id(0)
    core = core_ref[0]
    width = kept_ref.shape[1]
    near_rows = x_ref.shape[0] // 4 // STRIP
    own_rows = near_rows - 1
    columns = pl.ds(pl.multiple_of(step * width, width), width)

    def near_at(plane, row):
        return pl.ds(pl.multiple_of((plane * near_rows + row) * STRIP, STRIP), STRIP)

    def own_at(plane, row):
        return pl.ds(pl.multiple_of((plane * own_rows + row) * STRIP, STRIP), STRIP)

    @pl.when(step == 0)
    def _():
        token_stats(x_ref, average, scale)
        frame_zeros([normed, upstream])
        sum_plain[...] = jnp.zeros_like(sum_plain)
        sum_normed[...] = jnp.zeros_like(sum_normed)

    shift_by = mods_ref[0:1, :]
    scale_by = 1.0 + mods_ref[1:2, :]

    @pl.loop(0, near_rows)
    def _(row):
        for plane in range(4):
            rows = near_at(plane, row)
            padded = pl.ds(pl.multiple_of((row + 1) * STRIP, STRIP), STRIP)
            normed[plane, padded, :] = (
                normed_strip(x_ref, average, scale, rows, columns) * scale_by + shift_by
            )
            upstream[plane, padded, :] = kept_ref[rows, :].astype(full) + arriving_ref[
                rows, :
            ].astype(full)

    kernel = kernel_ref[...]
    flipped = jnp.concatenate([kernel[8 - t : 9 - t, :] for t in range(9)], axis=0)

    def kernel_strip(row, sums):
        near = near_strips(normed, row + core)
        sums = list(sums)
        for row_phase in range(2):
            for column_phase in range(2):
                grad_here = strip_at(upstream, row_phase, column_phase, row + core)
                for i in range(3):
                    for j in range(3):
                        product = near[row_phase][i][column_phase][j] * grad_here
                        sums[3 * i + j] = sums[3 * i + j] + (product[:8] + product[8:])
        return tuple(sums)

    def fold(sums, rows):
        return jnp.concatenate(
            [jnp.sum(s, axis=0, keepdims=True) for s in sums]
            + [jnp.zeros((rows - len(sums), width), full)],
            axis=0,
        )

    blank = jnp.zeros((8, width), full)
    kernel_grad_ref[...] = fold(lax.fori_loop(0, own_rows, kernel_strip, (blank,) * 9), 16)

    def input_strip(row, sums):
        near = near_strips(upstream, row + core)
        shift_sum, scale_sum = sums
        for row_phase in range(2):
            for column_phase in range(2):
                plane = 2 * row_phase + column_phase
                grad = conv_strip(near, flipped, row_phase, column_phase)
                plain = normed_strip(x_ref, average, scale, near_at(plane, row + core), columns)
                shift_sum = shift_sum + (grad[:8] + grad[8:])
                product = grad * plain
                scale_sum = scale_sum + (product[:8] + product[8:])
                scaled = grad * scale_by
                rows = own_at(plane, row)
                held[step, rows, :] = scaled
                product = scaled * plain
                sum_plain[rows, :] += sum(scaled[:, k : k + 128] for k in range(0, width, 128))
                sum_normed[rows, :] += sum(product[:, k : k + 128] for k in range(0, width, 128))
        return shift_sum, scale_sum

    mods_grad_ref[...] = fold(lax.fori_loop(0, own_rows, input_strip, (blank,) * 2), 8)

    @pl.when(step == pl.num_programs(0) - 1)
    def _():
        model = x_ref.shape[1]

        @pl.loop(0, own_rows)
        def _(row):
            for plane in range(4):
                rows = own_at(plane, row)
                near = near_at(plane, row + core)
                mean_plain = jnp.sum(sum_plain[rows, :], axis=-1, keepdims=True) / model
                mean_normed = jnp.sum(sum_normed[rows, :], axis=-1, keepdims=True) / model
                for block in range(model // width):
                    at = pl.ds(block * width, width)
                    plain = normed_strip(x_ref, average, scale, near, at)
                    spread = jnp.concatenate([scale[near, :]] * (width // 128), axis=1)
                    out_ref[rows, at] = middle_ref[rows, at] + spread * (
                        held[block, rows, :] - mean_plain - plain * mean_normed
                    )


def conv_back(core, x_near, kept, arriving, kernel, mods, grad_middle):
    near_tokens, model = x_near.shape
    own_tokens = grad_middle.shape[0]
    once = pl.Buffered(1)
    whole = lambda j, words: (0, 0)
    across = lambda j, words: (0, j)
    padded = near_tokens // 4 + 2 * STRIP
    return pl.pallas_call(
        conv_back_body,
        grid_spec=pltpu.PrefetchScalarGridSpec(
            num_scalar_prefetch=1,
            grid=(model // TILE,),
            in_specs=[
                pl.BlockSpec((near_tokens, model), whole, pipeline_mode=once),
                pl.BlockSpec((near_tokens, TILE), across),
                pl.BlockSpec((near_tokens, TILE), across),
                pl.BlockSpec((16, TILE), across),
                pl.BlockSpec((8, TILE), across),
                pl.BlockSpec((own_tokens, model), whole, pipeline_mode=once),
            ],
            out_specs=[
                pl.BlockSpec((own_tokens, model), whole),
                pl.BlockSpec((16, TILE), across),
                pl.BlockSpec((8, TILE), across),
            ],
            scratch_shapes=[
                pltpu.VMEM((near_tokens, 128), full),
                pltpu.VMEM((near_tokens, 128), full),
                pltpu.VMEM((4, padded, TILE), full),
                pltpu.VMEM((4, padded, TILE), full),
                pltpu.VMEM((model // TILE, own_tokens, TILE), full),
                pltpu.VMEM((own_tokens, 128), full),
                pltpu.VMEM((own_tokens, 128), full),
            ],
        ),
        out_shape=[
            jax.ShapeDtypeStruct((own_tokens, model), full),
            jax.ShapeDtypeStruct((16, model), full),
            jax.ShapeDtypeStruct((8, model), full),
        ],
        cost_estimate=pl.CostEstimate(
            flops=70 * own_tokens * model,
            bytes_accessed=14 * own_tokens * model,
            transcendentals=near_tokens,
        ),
        name="conv_back",
    )(core[None].astype(jnp.int32), x_near, kept, arriving, kernel, mods, grad_middle)


def on_device(
    tokens,
    seg_ids,
    timesteps,
    labels,
    cotangent,
    mod_weight,
    class_table,
    attn_kernel,
    qkv_weight,
    proj_weight,
    up_weight,
    ffn_kernel,
    down_weight,
):
    devices = device_count()
    chips = devices // 2
    chip_bits = chips.bit_length() - 1
    rank = lax.axis_index("dp") * lax.axis_size("fsdp") + lax.axis_index("fsdp")
    core = rank % 2
    chip = rank // 2
    _, half_tokens, model = tokens.shape
    half_rows = half_tokens // SIDE
    class_count = class_table.shape[0]
    part = model // devices
    share = down_weight.shape[0]
    piece = share // CHUNKS
    pairs = model // HEAD // 4

    def halves_of(array, axis):
        return at_bit(array, axis, core), at_bit(array, axis, 1 - core)

    def row_pair(array, axis):
        kept, leaving = halves_of(array, axis)
        arriving = swap_core(leaving)
        return jnp.concatenate(in_core_order(kept, arriving, core), axis=0)

    qkv_split = qkv_weight.reshape(part, 3, 2, pairs, 128).transpose(0, 2, 3, 1, 4)
    qkv_rows = row_pair(qkv_split.reshape(part, 2, pairs * 384), 1)
    qkv_half = pairs * 384 // 2

    picks = labels[:, None] == jnp.arange(class_count)[None, :]
    angles_here = lax.dynamic_slice_in_dim(sinusoid(timesteps, model), rank * part, part, axis=1)
    cond = angles_here + jnp.dot(picks.astype(low), class_table, preferred_element_type=full)
    lift_value, lift_pull = jax.vjp(jax.nn.silu, cond)
    lifted = lift_value.astype(low)
    mods_part = jnp.dot(lifted, mod_weight, preferred_element_type=full)

    slot = Slots(jnp.zeros((8, 128), full))
    flow = lambda shard, colour: gather_flow(shard, colour, chip_bits)
    sums = lambda parts, colour: scatter_flow(parts, colour, chip, chip_bits)
    joined = lambda flows: [
        gathered(f, colour, chip, chip_bits) for colour, f in enumerate(flows)
    ]
    mods_flow = scatter_flow(mods_part, 0, chip, chip_bits, sent=full)
    qkv_flows = [flow(qkv_rows[:, :qkv_half], 0), flow(qkv_rows[:, qkv_half:], 1)]
    mine, upstream = slot(
        qkv_flows + [mods_flow],
        lambda: (to_phases(tokens[0], half_rows), to_phases(cotangent[0], half_rows)),
    )

    up_weight, proj_weight, ffn_kernel, attn_kernel = slot.after(
        up_weight, proj_weight, ffn_kernel, attn_kernel
    )
    up_split = up_weight.reshape(part, chips, 2, CHUNKS, piece).transpose(0, 2, 3, 1, 4)
    up_rows = row_pair(up_split.reshape(part, 2, CHUNKS, chips * piece), 1)
    proj_there = [(r, r % chips * 2 + r // chips) for r in range(devices)]
    proj_back = [(b, a) for a, b in proj_there]
    proj_rows = lax.ppermute(proj_weight, AXES, proj_there)
    canvas = join_halves(mine, swap_core(mine), core)

    slot(qkv_flows + [mods_flow])
    while mods_flow.wanted is not None:
        array, bit = mods_flow.wanted
        mods_flow.arrive(swap(array, bit + 1))
    mods = mods_flow.result + swap_core(mods_flow.result)
    shift_a, scale_a, gate_a, shift_f, scale_f, gate_f = jnp.split(mods, 6)

    tap_count = 9 * (share + part)
    tap_words = jnp.concatenate([ffn_kernel.reshape(-1), attn_kernel.reshape(-1)])
    tap_words = jnp.pad(tap_words, (0, -tap_count % 128))
    taps = gather_rows(tap_words, rank, chip_bits + 1, 0)
    ffn_taps = taps[:, : 9 * share].reshape(chips, 2, 9, share)
    ffn_taps = at_bit(ffn_taps, 1, core).reshape(chips, 9, CHUNKS, piece)
    ffn_taps = ffn_taps.transpose(2, 1, 0, 3).reshape(CHUNKS, 9, chips * piece).astype(full)
    ffn_taps = jnp.pad(ffn_taps, ((0, 0), (0, 7), (0, 0)))
    attn_taps = taps[:, 9 * share : tap_count].reshape(devices, 9, part)
    attn_taps = attn_taps.transpose(1, 0, 2).reshape(9, model).astype(full)
    attn_taps = jnp.pad(attn_taps, ((0, 7), (0, 0)))

    spot = jnp.arange(PLANE)
    quadrant = 2 * (spot // (PLANE // 2)) + spot % HALF_SIDE // (HALF_SIDE // 2)
    quadrants_here = at_bit(seg_ids, 0, chip)
    segment = jnp.sum(
        jnp.where(quadrant[:, None] == jnp.arange(4)[None, :], quadrants_here[None, :], 0), axis=1
    )
    mask = (segment[:, None] == segment[None, :]).astype(full)

    proj_flows = [flow(proj_rows[:, : model // 2], 0), flow(proj_rows[:, model // 2 :], 1)]
    feed_flows = [
        [flow(up_rows[:, t], 0), flow(down_weight[t * piece : (t + 1) * piece], 1)]
        for t in range(CHUNKS)
    ]
    mods_a = jnp.concatenate([shift_a[None], scale_a[None], jnp.zeros((6, model), full)], axis=0)

    slot(qkv_flows + proj_flows + feed_flows[0])
    convolved = slot(
        qkv_flows + proj_flows + feed_flows[0], lambda: conv_in(canvas, attn_taps, mods_a)
    )

    (upstream,) = slot.after(upstream)
    grad_ph = join_halves(upstream, swap_core(upstream), core)

    def project_in():
        weight = jnp.concatenate(
            [array.reshape(model, qkv_half) for array in joined(qkv_flows)], axis=1
        )
        return weight, jnp.dot(convolved, weight, preferred_element_type=full).astype(low)

    slot.finish(qkv_flows)
    qkv_full, qkv = slot(proj_flows + feed_flows[0] + feed_flows[1], project_in)
    attended = slot(
        proj_flows + feed_flows[1] + feed_flows[2], lambda: attend(mask, qkv)
    )

    def project_out():
        weight = jnp.concatenate(
            [array.reshape(-1, model // 2) for array in joined(proj_flows)], axis=1
        )
        branch_part = jnp.dot(attended, weight, preferred_element_type=full)
        branch = half_of(branch_part, core) + swap_core(
            half_of(branch_part, 1 - core).astype(low)
        ).astype(full)
        return weight, branch

    source_ph = mine.astype(full)
    slot.finish(proj_flows)
    def enter_feed():
        proj_full, branch_a = project_out()
        middle = source_ph + gate_a * branch_a
        normed_low = modulate(middle, shift_f, scale_f).astype(low)
        norm = join_halves(normed_low, swap_core(normed_low), core)
        grad_branch_f = (grad_ph.astype(full) * gate_f).astype(low)
        return proj_full, branch_a, middle, norm, norm.T, grad_branch_f

    proj_full, branch_a, middle, norm, norm_t, grad_branch_f = slot(
        sum(feed_flows, []), enter_feed
    )

    kept = []
    grads = [None] * CHUNKS

    spread = 2 * part % STRIP == 0 and piece % STRIP == 0 and chips >= 8
    up_owner, _ = owners(0, chip, chip_bits)
    down_owner, down_place = owners(1, chip, chip_bits)
    words = jnp.concatenate([core[None], up_owner, down_owner, down_place]).astype(jnp.int32)

    def feed(t):
        def work():
            if spread:
                up, down = [f.result for f in feed_flows[t]]
            else:
                up, down = joined(feed_flows[t])
                up, down = [up.reshape(model, -1)], [down.reshape(-1, model)]
            return feed_forward(norm, norm_t, grad_branch_f, up, down, ffn_taps[t], words)

        return work

    back_flows = [[] for _ in range(CHUNKS)]

    def run_feed(flows, t):
        slot.finish(feed_flows[t])
        staying, leaving, up_grad, down_grad, tap_grad = slot(flows, feed(t))
        kept.append((staying, leaving))
        grads[t] = tap_grad
        if spread:
            back_flows[t] = [
                Flow(halving_steps(*grad[::-1], gather_order(chip_bits, colour)[::-1]))
                for colour, grad in enumerate((up_grad, down_grad))
            ]
        else:
            back_flows[t] = [
                sums(up_grad[0].reshape(chips, 2 * part, -1), 0),
                sums(down_grad[0].reshape(chips, piece, model), 1),
            ]

    run_feed(feed_flows[1] + feed_flows[2], 0)
    run_feed(feed_flows[2] + back_flows[0], 1)
    run_feed(back_flows[0] + back_flows[1], 2)
    upstream = upstream.astype(full)

    def leave_feed():
        total = sum(
            staying.astype(full) + swap_core(leaving).astype(full) for staying, leaving in kept
        )
        branch_sum, back_sum = total[0], total[1]
        layer_out = from_phases((middle + gate_f * branch_sum).astype(low), half_rows)
        grad_gate_f = jnp.sum(upstream * branch_sum, axis=(0, 1))
        _, norm_pull_f = jax.vjp(modulate, middle, shift_f, scale_f)
        grad_middle, grad_shift_f, grad_scale_f = norm_pull_f(back_sum)
        grad_middle = grad_middle + upstream
        grad_gate_a = jnp.sum(grad_middle * branch_a, axis=(0, 1))
        grad_branch_mine = (grad_middle * gate_a).astype(low)
        return (
            layer_out, grad_middle, grad_branch_mine,
            grad_gate_f, grad_shift_f, grad_scale_f, grad_gate_a,
        )

    (
        layer_out, grad_middle, grad_branch_mine,
        grad_gate_f, grad_shift_f, grad_scale_f, grad_gate_a,
    ) = slot(sum(back_flows, []), leave_feed)
    layer_out = layer_out[None]

    def enter_attend():
        grad_branch_a = join_halves(grad_branch_mine, swap_core(grad_branch_mine), core)
        grad_attended = jnp.dot(grad_branch_a, proj_full.T, preferred_element_type=full)
        proj_grad = jnp.dot(attended.T, grad_branch_a, preferred_element_type=full)
        return grad_attended.astype(low), proj_grad.astype(low)

    grad_attended, proj_grad = slot(sum(back_flows, []), enter_attend)
    proj_grad = proj_grad.reshape(chips, -1, model)
    proj_flows = [sums(proj_grad[..., : model // 2], 0), sums(proj_grad[..., model // 2 :], 1)]
    grad_qkv = slot(
        proj_flows + sum(back_flows, []), lambda: attend_back(mask, qkv, grad_attended)
    )
    qkv_grad = slot(
        proj_flows + sum(back_flows, []),
        lambda: jnp.dot(convolved.T, grad_qkv, preferred_element_type=full).astype(low),
    )
    qkv_grad = qkv_grad.reshape(chips, 2 * part, -1)
    qkv_flows = [sums(qkv_grad[..., :qkv_half], 0), sums(qkv_grad[..., qkv_half:], 1)]

    def rows_near(array, which):
        size = PLANE // 2 + STRIP
        near = lax.dynamic_slice_in_dim(
            array.reshape(4, PLANE, model), which * (PLANE - size), size, axis=1
        )
        return near.reshape(4 * size, model)

    def leave_attend():
        part_here = jnp.dot(grad_qkv, qkv_full.T, preferred_element_type=full).astype(low)
        return rows_near(part_here, core), swap_core(rows_near(part_here, 1 - core))

    grad_conv = slot(qkv_flows + proj_flows + back_flows[2], leave_attend)

    def leave_block():
        input_grad, attn_tap_grad, mods_grad = conv_back(
            core, rows_near(canvas, core), *grad_conv, attn_taps, mods_a,
            grad_middle.reshape(half_tokens, model),
        )
        input_grad = from_phases(input_grad.reshape(4, -1, model), half_rows)
        return attn_tap_grad[:9], input_grad, mods_grad[0], mods_grad[1]

    attn_tap_grad, input_grad, grad_shift_a, grad_scale_a = slot(
        qkv_flows + proj_flows + back_flows[2], leave_block
    )
    slot.finish(sum(back_flows, proj_flows + qkv_flows))
    up_shares = [flows[0].result for flows in back_flows]
    down_shares = [flows[1].result for flows in back_flows]
    tap_grads = [g[:9].reshape(9, chips, piece) for g in grads]
    qkv_share = jnp.concatenate([f.result for f in qkv_flows], axis=1)
    proj_share = jnp.concatenate([f.result for f in proj_flows], axis=1)
    proj_share = lax.ppermute(proj_share, AXES, proj_back)

    grad_mods = jnp.concatenate(
        [grad_shift_a, grad_scale_a, grad_gate_a, grad_shift_f, grad_scale_f, grad_gate_f]
    )
    grad_mods = (grad_mods + swap_core(grad_mods)).astype(low)
    grad_mods_all = gather_rows(grad_mods, chip, chip_bits)
    mod_grad = jnp.dot(lifted.T, grad_mods_all, preferred_element_type=full)
    (cond_grad,) = lift_pull(jnp.dot(grad_mods_all, mod_weight.T, preferred_element_type=full))
    table_grad = jnp.dot(picks.astype(full).T, cond_grad, precision=highest)

    ffn_tap_grad = jnp.concatenate(tap_grads, axis=2).transpose(1, 0, 2)
    attn_split = attn_tap_grad.reshape(9, chips, 2, part)
    attn_kept, attn_leaving = halves_of(attn_split, 2)
    attn_tap_grad = (attn_kept + swap_core(attn_leaving)).transpose(1, 0, 2)
    tap_parts = jnp.concatenate(
        [ffn_tap_grad.reshape(chips, -1), attn_tap_grad.reshape(chips, -1)], axis=1
    )
    tap_share = scatter_sum(tap_parts, 0, chip, chip_bits, sent=full)
    ffn_share = tap_share[: 9 * share].reshape(9, share)
    kernel_share = tap_share[9 * share :].reshape(9, part)

    def row_split(array, axis):
        pair = array.reshape((2, part) + array.shape[1:])
        kept, leaving = halves_of(pair, 0)
        arriving = swap_core(leaving)
        return jnp.stack(in_core_order(kept, arriving, core), axis=axis)

    up_all = jnp.stack(up_shares, axis=1).reshape(2 * part, CHUNKS, chips, piece)
    up_share = row_split(up_all.transpose(0, 2, 1, 3), 2).reshape(part, -1)
    down_share = jnp.concatenate(down_shares, axis=0)
    qkv_all = qkv_share.reshape(2 * part, pairs, 3, 128).transpose(0, 2, 1, 3)
    qkv_out = row_split(qkv_all, 2).reshape(part, -1)

    return (
        layer_out,
        input_grad[None],
        mod_grad,
        table_grad,
        kernel_share,
        qkv_out,
        proj_share,
        up_share,
        ffn_share,
        down_share,
        grad_shift_f[None],
    )


def solution(mesh):
    return jax.shard_map(
        on_device,
        mesh=mesh,
        in_specs=(
            P(AXES, None, None),
            P(),
            P(),
            P(),
            P(AXES, None, None),
            P(AXES, None),
            P(None, AXES),
            P(None, AXES),
            P(AXES, None),
            P(AXES, None),
            P(AXES, None),
            P(None, AXES),
            P(AXES, None),
        ),
        out_specs=(
            P(AXES, None, None),
            P(AXES, None, None),
            P(AXES, None),
            P(None, AXES),
            P(None, AXES),
            P(AXES, None),
            P(AXES, None),
            P(AXES, None),
            P(None, AXES),
            P(AXES, None),
            P(AXES, None),
        ),
        check_vma=False,
    )
```

```python
import functools
import math

import jax
import jax.numpy as jnp
from jax import lax
from jax.experimental import pallas as pl
from jax.experimental.pallas import tpu as pltpu
from jax.sharding import PartitionSpec as P

HEAD = 64
SIDE = 32
HALF_SIDE = SIDE // 2
STRIP = HALF_SIDE
PLANE = HALF_SIDE * HALF_SIDE
PADDED = PLANE + 2 * STRIP
TILE = 256
CHUNKS = 3

highest = lax.Precision.HIGHEST
ln_epsilon = 1e-06
masked_score = -1000000000.0
low = jnp.bfloat16
full = jnp.float32
AXES = ("dp", "fsdp")


def device_count():
    return lax.axis_size("dp") * lax.axis_size("fsdp")


def swap(x, bit):
    return lax.ppermute(x, AXES, [(i, i ^ 1 << bit) for i in range(device_count())])


def swap_core(x):
    return swap(x, 0)


def gather_order(chip_bits, colour):
    order = list(range(chip_bits - 1, -1, -1))
    if colour and chip_bits > 1:
        order[-1], order[-2] = order[-2], order[-1]
    return order


class Flow:
    def __init__(self, steps):
        self.steps = steps
        self.wanted = next(steps)
        self.result = None

    def arrive(self, array):
        try:
            self.wanted = self.steps.send(array)
        except StopIteration as end:
            self.wanted, self.result = None, end.value


class Slots:
    def __init__(self, token):
        self.token = token

    def after(self, *arrays):
        arrays, self.token = lax.optimization_barrier((arrays, self.token))
        return arrays

    def finish(self, flows):
        while any(flow.wanted is not None for flow in flows):
            self(flows)

    def __call__(self, flows, work=lambda: ()):
        flows = [flow for flow in flows if flow.wanted is not None]
        wanted = [flow.wanted for flow in flows]
        leaving, self.token = lax.optimization_barrier(([w[0] for w in wanted], self.token))
        arriving = [swap(array, bit + 1) for array, (_, bit) in zip(leaving, wanted)]
        arriving, result, self.token = lax.optimization_barrier((arriving, work(), self.token))
        for flow, array in zip(flows, arriving):
            flow.arrive(array)
        return result


def gather_steps(shard, order):
    held = shard[None]
    for bit in order[:-1]:
        arriving = yield held, bit
        held = jnp.concatenate([held, arriving], axis=0)
    arriving = yield held, order[-1]
    return held, arriving


def assemble_body(steps, chip_ref, *refs):
    *piece_refs, out_ref = refs
    which = pl.program_id(0) // steps
    top = chip_ref[1]
    for index, piece_ref in enumerate(piece_refs):

        @pl.when(which == index)
        def _():
            for k in range(4):
                out_ref[jnp.bitwise_xor(top, (k & 1) << 1 | k >> 1), 0] = piece_ref[k]


def assemble(pieces, order, chip):
    chips = sum(piece.shape[0] for piece in pieces)
    rows, columns = pieces[0].shape[1:]
    if chips < 4 or len(pieces) * pieces[0].shape[0] != chips or pieces[0].shape[0] % 4:
        raise ValueError("unexpected mesh")
    rest = len(order) - 2
    steps = pieces[0].shape[0] // 4
    chip_words = jnp.stack([jnp.bitwise_and(chip, (1 << rest) - 1), chip >> rest]).astype(jnp.int32)

    def out_map(step, words):
        at = words[0]
        for position, bit in enumerate(order[2:]):
            at = jnp.bitwise_xor(at, jnp.bitwise_and(step >> position, 1) << bit)
        return (0, at, 0, 0)

    def piece_map(index):
        return lambda step, words: (jnp.clip(step - index * steps, 0, steps - 1), 0, 0)

    out = pl.pallas_call(
        functools.partial(assemble_body, steps),
        grid_spec=pltpu.PrefetchScalarGridSpec(
            num_scalar_prefetch=1,
            grid=(chips // 4,),
            in_specs=[
                pl.BlockSpec((4, rows, columns), piece_map(index)) for index in range(len(pieces))
            ],
            out_specs=pl.BlockSpec((4, 1, rows, columns), out_map),
        ),
        out_shape=jax.ShapeDtypeStruct((4, chips // 4, rows, columns), pieces[0].dtype),
        cost_estimate=pl.CostEstimate(
            flops=0, bytes_accessed=4 * chips * rows * columns, transcendentals=0
        ),
        name="assemble",
    )(chip_words, *pieces)
    return out.reshape(chips, rows, columns)


def gather_flow(shard, colour, chip_bits):
    return Flow(gather_steps(shard, gather_order(chip_bits, colour)))


def gathered(flow, colour, chip, chip_bits):
    return assemble(flow.result, gather_order(chip_bits, colour), chip)


def at_bit(array, axis, bit):
    return lax.dynamic_index_in_dim(array, bit, axis, keepdims=False)


def scatter_steps(parts, order, chip, chip_bits, sent):
    left = list(range(chip_bits - 1, -1, -1))
    held = [parts.reshape((2,) * chip_bits + parts.shape[1:])]
    for bit in order:
        axis = left.index(bit)
        left.remove(bit)
        mine = jnp.bitwise_and(chip >> bit, 1)
        leaving = sum(at_bit(h, axis, 1 - mine).astype(full) for h in held).astype(sent)
        staying = sum(at_bit(h, axis, mine).astype(full) for h in held).astype(sent)
        arriving = yield leaving, bit
        held = [staying, arriving]
    return held[0].astype(full) + held[1].astype(full)


def halving_steps(leaving, staying, order):
    arriving = yield leaving, order[0]
    for bit in order[1:]:
        half = staying.shape[0] // 2
        leaving, staying = [
            (staying[at].astype(full) + arriving[at].astype(full)).astype(low)
            for at in (slice(half, None), slice(half))
        ]
        arriving = yield leaving, bit
    return (staying.astype(full) + arriving.astype(full))[0]


def owners(colour, chip, chip_bits):
    order = gather_order(chip_bits, colour)
    spots = jnp.arange(1 << chip_bits)
    bits = list(enumerate(order))
    owner = sum((jnp.bitwise_and(spots >> at, 1) << bit) for at, bit in bits)
    apart = jnp.bitwise_xor(spots, chip)
    place = sum((jnp.bitwise_and(apart >> bit, 1) << at) for at, bit in bits)
    return jnp.bitwise_xor(owner, chip), place


def scatter_flow(parts, colour, chip, chip_bits, sent=low):
    order = gather_order(chip_bits, colour)[::-1]
    return Flow(scatter_steps(parts, order, chip, chip_bits, sent))


def scatter_sum(parts, colour, chip, chip_bits, sent=low):
    flow = scatter_flow(parts, colour, chip, chip_bits, sent)
    while flow.wanted is not None:
        array, bit = flow.wanted
        flow.arrive(swap(array, bit + 1))
    return flow.result


def gather_rows(row, chip, chip_bits, first_bit=1):
    order = gather_order(chip_bits, 0)
    held = row[None]
    for bit in order:
        held = jnp.concatenate([held, swap(held, bit + first_bit)], axis=0)
    places = jnp.arange(1 << chip_bits)
    position = jnp.zeros_like(places)
    apart = jnp.bitwise_xor(places, chip)
    for step, bit in enumerate(order):
        position = position + (jnp.bitwise_and(apart >> bit, 1) << step)
    pick = position[:, None] == places[None, :]
    return jnp.dot(pick.astype(held.dtype), held, preferred_element_type=full).astype(held.dtype)


def to_phases(block_in, row_count):
    width = block_in.shape[-1]
    split_grid = block_in.reshape(row_count // 2, 2, HALF_SIDE, 2, width)
    return split_grid.transpose(1, 3, 0, 2, 4).reshape(4, row_count // 2 * HALF_SIDE, width)


def from_phases(block_in, row_count):
    width = block_in.shape[-1]
    split_grid = block_in.reshape(2, 2, row_count // 2, HALF_SIDE, width)
    return split_grid.transpose(2, 0, 3, 1, 4).reshape(row_count * SIDE, width)


def in_core_order(mine, other, core):
    return jnp.where(core == 0, mine, other), jnp.where(core == 0, other, mine)


def join_halves(mine, other, core):
    return jnp.stack(in_core_order(mine, other, core), axis=1).reshape(-1, mine.shape[-1])


def half_of(joined, which):
    width = joined.shape[-1]
    return at_bit(joined.reshape(4, 2, -1, width), 1, which)


def layer_norm(values):
    average = jnp.mean(values, axis=-1, keepdims=True)
    centred = values - average
    variance = jnp.mean(centred * centred, axis=-1, keepdims=True)
    return centred * lax.rsqrt(variance + ln_epsilon)


def modulate(values, shift_by, scale_by):
    return layer_norm(values) * (1.0 + scale_by) + shift_by


def sinusoid(steps_in, width):
    halfway = width // 2
    frequency = jnp.exp(-math.log(10000.0) * jnp.arange(halfway, dtype=jnp.float32) / halfway)
    angles = steps_in.astype(jnp.float32)[..., None] * frequency
    return jnp.concatenate([jnp.cos(angles), jnp.sin(angles)], axis=-1)


def softmax_of(query, key, allowed):
    raw = lax.dot_general(query, key, (((1,), (1,)), ((), ())), preferred_element_type=full)
    scores = jnp.where(allowed, raw * HEAD ** (-0.5), masked_score)
    shifted = jnp.exp(scores - jnp.max(scores, axis=-1, keepdims=True))
    return shifted / jnp.sum(shifted, axis=-1, keepdims=True)


def head_lanes(shape, head):
    lanes = lax.broadcasted_iota(jnp.int32, shape, 1)
    return jnp.logical_and(lanes >= head * HEAD, lanes < (head + 1) * HEAD)


def attend_body(mask_ref, qkv_ref, out_ref):
    allowed = mask_ref[...] > 0.5

    @pl.loop(0, 4)
    def _(phase):
        rows = pl.ds(pl.multiple_of(phase * PLANE, PLANE), PLANE)
        query = qkv_ref[rows, :128]
        key = qkv_ref[rows, 128:256]
        value = qkv_ref[rows, 256:]
        total = None
        for head in range(2):
            here = head_lanes(key.shape, head)
            probs = softmax_of(query, jnp.where(here, key, jnp.zeros_like(key)), allowed)
            part = jnp.dot(
                probs.astype(low),
                jnp.where(here, value, jnp.zeros_like(value)),
                preferred_element_type=full,
            )
            total = part if total is None else total + part
        out_ref[rows, :] = total.astype(low)


def attend_back_body(mask_ref, qkv_ref, grad_ref, out_ref):
    allowed = mask_ref[...] > 0.5

    @pl.loop(0, 4)
    def _(phase):
        rows = pl.ds(pl.multiple_of(phase * PLANE, PLANE), PLANE)
        query = qkv_ref[rows, :128]
        key = qkv_ref[rows, 128:256]
        value = qkv_ref[rows, 256:]
        grad = grad_ref[rows, :]
        by_rows = (((0,), (0,)), ((), ()))
        totals = [None, None, None]
        for head in range(2):
            here = head_lanes(key.shape, head)
            blank = jnp.zeros_like(key)
            key_here = jnp.where(here, key, blank)
            query_here = jnp.where(here, query, blank)
            value_here = jnp.where(here, value, blank)
            grad_here = jnp.where(here, grad, blank)
            weights = softmax_of(query, key_here, allowed)
            grad_probs = lax.dot_general(
                grad, value_here, (((1,), (1,)), ((), ())), preferred_element_type=full
            )
            delta = jnp.sum(grad_probs * weights, axis=-1, keepdims=True)
            grad_scores = (weights * (grad_probs - delta)).astype(low)
            parts = (
                jnp.dot(grad_scores, key_here, preferred_element_type=full),
                lax.dot_general(grad_scores, query_here, by_rows, preferred_element_type=full),
                lax.dot_general(
                    weights.astype(low), grad_here, by_rows, preferred_element_type=full
                ),
            )
            totals = [p if t is None else t + p for t, p in zip(totals, parts)]
        out_ref[rows, :128] = (totals[0] * HEAD ** (-0.5)).astype(low)
        out_ref[rows, 128:256] = (totals[1] * HEAD ** (-0.5)).astype(low)
        out_ref[rows, 256:] = totals[2].astype(low)


def attend(mask, qkv):
    tokens, width = qkv.shape
    pairs = width // 384
    return pl.pallas_call(
        attend_body,
        grid=(pairs,),
        in_specs=[
            pl.BlockSpec((PLANE, PLANE), lambda j: (0, 0)),
            pl.BlockSpec((tokens, 384), lambda j: (0, j)),
        ],
        out_specs=pl.BlockSpec((tokens, 128), lambda j: (0, j)),
        out_shape=jax.ShapeDtypeStruct((tokens, pairs * 128), low),
        cost_estimate=pl.CostEstimate(
            flops=pairs * 2 * 4 * 4 * PLANE * PLANE * 256,
            bytes_accessed=8 * tokens * pairs * 128,
            transcendentals=pairs * 8 * PLANE * PLANE,
        ),
        name="attend",
    )(mask, qkv)


def attend_back(mask, qkv, grad):
    tokens, width = qkv.shape
    pairs = width // 384
    return pl.pallas_call(
        attend_back_body,
        grid=(pairs,),
        in_specs=[
            pl.BlockSpec((PLANE, PLANE), lambda j: (0, 0)),
            pl.BlockSpec((tokens, 384), lambda j: (0, j)),
            pl.BlockSpec((tokens, 128), lambda j: (0, j)),
        ],
        out_specs=pl.BlockSpec((tokens, 384), lambda j: (0, j)),
        out_shape=jax.ShapeDtypeStruct((tokens, width), low),
        cost_estimate=pl.CostEstimate(
            flops=pairs * 2 * 4 * 10 * PLANE * PLANE * 256,
            bytes_accessed=14 * tokens * pairs * 128,
            transcendentals=pairs * 8 * PLANE * PLANE,
        ),
        name="attend_back",
    )(mask, qkv, grad)


def strip_at(ref, row_phase, column_phase, row):
    start = pl.multiple_of((row + 1) * STRIP, STRIP)
    return ref[2 * row_phase + column_phase, pl.ds(start, STRIP), :]


def near_strips(ref, row):
    tokens = lax.broadcasted_iota(jnp.int32, (STRIP, ref.shape[-1]), 0)
    loaded = {}
    for row_phase, at in ((1, row - 1), (0, row), (1, row), (0, row + 1)):
        even = strip_at(ref, row_phase, 0, at)
        odd = strip_at(ref, row_phase, 1, at)
        before = jnp.where(tokens == 0, 0.0, pltpu.roll(odd, 1, 0))
        after = jnp.where(tokens == STRIP - 1, 0.0, pltpu.roll(even, STRIP - 1, 0))
        loaded[len(loaded)] = ((before, even, odd), (even, odd, after))
    return {0: (loaded[0], loaded[1], loaded[2]), 1: (loaded[1], loaded[2], loaded[3])}


def conv_strip(near, kernel, row_phase, column_phase):
    total = None
    for i in range(3):
        for j in range(3):
            term = near[row_phase][i][column_phase][j] * kernel[3 * i + j : 3 * i + j + 1, :]
            total = term if total is None else total + term
    return total


def feed_body(
    spread,
    words_ref,
    norm_ref,
    norm_t_ref,
    grad_ref,
    *refs,
):
    pieces = 2 if spread else 1
    up_refs, refs = refs[:pieces], refs[pieces:]
    down_refs, refs = refs[:pieces], refs[pieces:]
    kernel_ref, staying_ref, leaving_ref, *refs = refs
    up_grad_refs, refs = refs[:pieces], refs[pieces:]
    down_grad_refs, refs = refs[:pieces], refs[pieces:]
    kernel_grad_ref, branch_acc, back_acc, hidden, widened_grad, act_grad, act, hidden_grad = refs[
        :8
    ]
    step = pl.program_id(0)
    core = words_ref[0]
    by_columns = (((1,), (1,)), ((), ()))
    width = kernel_ref.shape[1]
    model = norm_t_ref.shape[0]
    up_ref, down_ref = up_refs[0], down_refs[0]
    if spread:
        up_ref, down_all = refs[8:]
        half, share, _ = up_refs[0].shape
        piece = down_refs[0].shape[1]
        chips = 2 * half
        down_ref = down_all.at[pl.ds(pl.multiple_of(step * width, width), width), :]

        for which in range(2):

            @pl.loop(0, half)
            def _(spot):
                start = pl.multiple_of(words_ref[1 + which * half + spot] * share, share)
                up_ref[pl.ds(start, share), :] = up_refs[which][spot]

            @pl.when(step == 0)
            def _():
                @pl.loop(0, half)
                def _(spot):
                    owner = words_ref[1 + chips + which * half + spot]
                    start = pl.multiple_of(owner * piece, piece)
                    down_all[pl.ds(start, piece), :] = down_refs[which][spot]

    @pl.when(step == 0)
    def _():
        blank = jnp.zeros((STRIP, width), full)
        for plane in range(4):
            for ref in (hidden, widened_grad):
                ref[plane, pl.ds(0, STRIP), :] = blank
                ref[plane, pl.ds(PLANE + STRIP, STRIP), :] = blank
        branch_acc[...] = jnp.zeros_like(branch_acc)
        back_acc[...] = jnp.zeros_like(back_acc)

    @pl.loop(0, 4)
    def _(plane):
        rows = pl.ds(pl.multiple_of(plane * PLANE, PLANE), PLANE)
        hidden[plane, pl.ds(STRIP, PLANE), :] = jnp.dot(
            norm_ref[rows, :], up_ref[...], preferred_element_type=full
        )
        act_grad[rows, :] = lax.dot_general(
            grad_ref[rows, :], down_ref[...], by_columns, preferred_element_type=full
        )

    kernel = kernel_ref[...]

    def forward_strip(row, sums):
        near = near_strips(hidden, row)
        sums = list(sums)
        for row_phase in range(2):
            for column_phase in range(2):
                plane = 2 * row_phase + column_phase
                wide = conv_strip(near, kernel, row_phase, column_phase)
                square = wide * wide
                bend = math.sqrt(2.0 / math.pi) * (wide + 0.044715 * wide * square)
                curve = jnp.tanh(bend)
                half = 0.5 * (1.0 + curve)
                slope = half + 0.5 * wide * (1.0 - curve * curve) * (
                    math.sqrt(2.0 / math.pi) * (1.0 + 3 * 0.044715 * square)
                )
                at = pl.ds(pl.multiple_of(plane * PLANE + row * STRIP, STRIP), STRIP)
                act[at, :] = (wide * half).astype(low)
                grad_here = slope * act_grad[at, :]
                widened_grad[plane, pl.ds(pl.multiple_of((row + 1) * STRIP, STRIP), STRIP), :] = (
                    grad_here
                )
                for i in range(3):
                    for j in range(3):
                        product = near[row_phase][i][column_phase][j] * grad_here
                        sums[3 * i + j] = sums[3 * i + j] + (product[:8] + product[8:])
        return tuple(sums)

    sums = lax.fori_loop(
        0, HALF_SIDE, forward_strip, tuple(jnp.zeros((8, width), full) for _ in range(9))
    )
    kernel_grad_ref[...] = jnp.concatenate(
        [jnp.sum(s, axis=0, keepdims=True) for s in sums] + [jnp.zeros((7, width), full)], axis=0
    )

    flipped = [kernel[8 - t : 9 - t, :] for t in range(9)]
    flipped = jnp.concatenate(flipped, axis=0)

    @pl.loop(0, HALF_SIDE)
    def _(row):
        near = near_strips(widened_grad, row)
        for row_phase in range(2):
            for column_phase in range(2):
                plane = 2 * row_phase + column_phase
                at = pl.ds(pl.multiple_of(plane * PLANE + row * STRIP, STRIP), STRIP)
                hidden_grad[at, :] = conv_strip(near, flipped, row_phase, column_phase).astype(low)

    @pl.loop(0, 4)
    def _(plane):
        rows = pl.ds(pl.multiple_of(plane * PLANE, PLANE), PLANE)
        branch_acc[rows, :] += jnp.dot(act[rows, :], down_ref[...], preferred_element_type=full)
        back_acc[rows, :] += lax.dot_general(
            hidden_grad[rows, :], up_ref[...], by_columns, preferred_element_type=full
        )

    if spread:
        for which in range(2):

            @pl.loop(0, half // 4)
            def _(group):
                lhs = []
                for k in range(4):
                    owner = words_ref[1 + which * half + 4 * group + k]
                    start = pl.multiple_of(owner * share, share)
                    lhs.append(norm_t_ref[pl.ds(start, share), :])
                result = jnp.dot(
                    jnp.concatenate(lhs, axis=0), hidden_grad[...], preferred_element_type=full
                ).astype(low)
                for k in range(4):
                    up_grad_refs[which][4 * group + k] = result[k * share : (k + 1) * share]

    else:

        @pl.loop(0, model // TILE)
        def _(tile):
            rows = pl.ds(pl.multiple_of(tile * TILE, TILE), TILE)
            up_grad_refs[0][rows, :] = jnp.dot(
                norm_t_ref[rows, :], hidden_grad[...], preferred_element_type=full
            ).astype(low)

    down_grad = lax.dot_general(
        act[...], grad_ref[...], (((0,), (0,)), ((), ())), preferred_element_type=full
    ).astype(low)
    if spread:
        for k in range(width // piece):
            place = words_ref[1 + 2 * chips + step * (width // piece) + k]
            for which in range(2):

                @pl.when(place // half == which)
                def _():
                    down_grad_refs[which][place - which * half] = down_grad[
                        k * piece : (k + 1) * piece
                    ]

    else:
        down_grad_refs[0][...] = down_grad

    @pl.when(step == pl.num_programs(0) - 1)
    def _():
        for ref, which in ((staying_ref, core), (leaving_ref, 1 - core)):
            for index, acc in enumerate((branch_acc, back_acc)):
                for plane in range(4):
                    start = plane * PLANE + pl.multiple_of(which * (PLANE // 2), PLANE // 2)
                    ref[index, plane] = acc[pl.ds(start, PLANE // 2), :].astype(low)


def feed_forward(norm, norm_t, grad, up, down, kernel, words):
    tokens, model = norm.shape
    channels = kernel.shape[1]
    width = TILE
    spread = len(up) == 2
    whole = lambda j, words: (0, 0)
    half = lambda j, words: (0, 0, 0, 0)
    across = lambda j, words: (0, j)
    once = pl.Buffered(1)
    piece_scratch = []
    if spread:
        deep = lambda j, words: (0, 0, 0)
        up_spec = pl.BlockSpec(up[0].shape[:2] + (width,), lambda j, words: (0, 0, j))
        down_spec = pl.BlockSpec(down[0].shape, deep, pipeline_mode=once)
        down_grad_spec = pl.BlockSpec(down[0].shape, deep)
        piece_scratch = [pltpu.VMEM((model, width), low), pltpu.VMEM((channels, model), low)]
    else:
        up_spec = pl.BlockSpec((model, width), across)
        down_spec = down_grad_spec = pl.BlockSpec((width, model), lambda j, words: (j, 0))
    halves = jax.ShapeDtypeStruct((2, 4, PLANE // 2, model), low)
    like = lambda arrays: [jax.ShapeDtypeStruct(array.shape, low) for array in arrays]
    out = pl.pallas_call(
        functools.partial(feed_body, spread),
        grid_spec=pltpu.PrefetchScalarGridSpec(
            num_scalar_prefetch=1,
            grid=(channels // width,),
            in_specs=[
                pl.BlockSpec((tokens, model), whole, pipeline_mode=once),
                pl.BlockSpec((model, tokens), whole, pipeline_mode=once),
                pl.BlockSpec((tokens, model), whole, pipeline_mode=once),
                *[up_spec] * len(up),
                *[down_spec] * len(down),
                pl.BlockSpec((16, width), across),
            ],
            out_specs=[
                pl.BlockSpec(halves.shape, half),
                pl.BlockSpec(halves.shape, half),
                *[up_spec] * len(up),
                *[down_grad_spec] * len(down),
                pl.BlockSpec((16, width), across),
            ],
            scratch_shapes=[
                pltpu.VMEM((tokens, model), full),
                pltpu.VMEM((tokens, model), full),
                pltpu.VMEM((4, PADDED, width), full),
                pltpu.VMEM((4, PADDED, width), full),
                pltpu.VMEM((tokens, width), full),
                pltpu.VMEM((tokens, width), low),
                pltpu.VMEM((tokens, width), low),
            ]
            + piece_scratch,
        ),
        out_shape=[halves, halves]
        + like(up)
        + like(down)
        + [jax.ShapeDtypeStruct((16, channels), full)],
        compiler_params=pltpu.CompilerParams(vmem_limit_bytes=63 * 1024 * 1024),
        cost_estimate=pl.CostEstimate(
            flops=12 * tokens * model * channels,
            bytes_accessed=8 * model * channels + 10 * tokens * model,
            transcendentals=tokens * channels,
        ),
        name="feed_forward",
    )(words, norm, norm_t, grad, *up, *down, kernel)
    staying, leaving, *grads, kernel_grad = out
    return staying, leaving, grads[: len(up)], grads[len(up) :], kernel_grad


def token_stats(x_ref, average, scale):
    @pl.loop(0, x_ref.shape[0] // STRIP)
    def _(strip):
        rows = pl.ds(pl.multiple_of(strip * STRIP, STRIP), STRIP)
        values = x_ref[rows, :].astype(full)
        mean = jnp.mean(values, axis=-1, keepdims=True)
        centred = values - mean
        variance = jnp.mean(centred * centred, axis=-1, keepdims=True)
        average[rows, :] = jnp.broadcast_to(mean, (STRIP, 128))
        scale[rows, :] = jnp.broadcast_to(lax.rsqrt(variance + ln_epsilon), (STRIP, 128))


def normed_strip(x_ref, average, scale, rows, columns):
    width = columns.size
    wide = lambda ref: jnp.concatenate([ref[rows, :]] * (width // 128), axis=1)
    return (x_ref[rows, columns].astype(full) - wide(average)) * wide(scale)


def frame_zeros(refs):
    for ref in refs:
        blank = jnp.zeros((STRIP, ref.shape[-1]), full)
        for plane in range(4):
            ref[plane, pl.ds(0, STRIP), :] = blank
            ref[plane, pl.ds(ref.shape[1] - STRIP, STRIP), :] = blank


def conv_in_body(x_ref, kernel_ref, mods_ref, out_ref, average, scale, normed):
    step = pl.program_id(0)
    width = out_ref.shape[1]
    columns = pl.ds(pl.multiple_of(step * width, width), width)

    @pl.when(step == 0)
    def _():
        token_stats(x_ref, average, scale)
        frame_zeros([normed])

    shift_by = mods_ref[0:1, :]
    scale_by = 1.0 + mods_ref[1:2, :]

    @pl.loop(0, HALF_SIDE)
    def _(row):
        for plane in range(4):
            rows = pl.ds(pl.multiple_of(plane * PLANE + row * STRIP, STRIP), STRIP)
            normed[plane, pl.ds(pl.multiple_of((row + 1) * STRIP, STRIP), STRIP), :] = (
                normed_strip(x_ref, average, scale, rows, columns) * scale_by + shift_by
            )

    kernel = kernel_ref[...]

    @pl.loop(0, HALF_SIDE)
    def _(row):
        near = near_strips(normed, row)
        for row_phase in range(2):
            for column_phase in range(2):
                plane = 2 * row_phase + column_phase
                at = pl.ds(pl.multiple_of(plane * PLANE + row * STRIP, STRIP), STRIP)
                out_ref[at, :] = conv_strip(near, kernel, row_phase, column_phase).astype(low)


def conv_in(canvas, kernel, mods):
    tokens, model = canvas.shape
    return pl.pallas_call(
        conv_in_body,
        grid=(model // TILE,),
        in_specs=[
            pl.BlockSpec((tokens, model), lambda j: (0, 0), pipeline_mode=pl.Buffered(1)),
            pl.BlockSpec((16, TILE), lambda j: (0, j)),
            pl.BlockSpec((8, TILE), lambda j: (0, j)),
        ],
        out_specs=pl.BlockSpec((tokens, TILE), lambda j: (0, j)),
        out_shape=jax.ShapeDtypeStruct((tokens, model), low),
        scratch_shapes=[
            pltpu.VMEM((tokens, 128), full),
            pltpu.VMEM((tokens, 128), full),
            pltpu.VMEM((4, PADDED, TILE), full),
        ],
        cost_estimate=pl.CostEstimate(
            flops=30 * tokens * model, bytes_accessed=4 * tokens * model, transcendentals=tokens
        ),
        name="conv_in",
    )(canvas, kernel, mods)


def conv_back_body(
    core_ref,
    x_ref,
    kept_ref,
    arriving_ref,
    kernel_ref,
    mods_ref,
    middle_ref,
    out_ref,
    kernel_grad_ref,
    mods_grad_ref,
    average,
    scale,
    normed,
    upstream,
    held,
    sum_plain,
    sum_normed,
):
    step = pl.program_id(0)
    core = core_ref[0]
    width = kept_ref.shape[1]
    near_rows = x_ref.shape[0] // 4 // STRIP
    own_rows = near_rows - 1
    columns = pl.ds(pl.multiple_of(step * width, width), width)

    def near_at(plane, row):
        return pl.ds(pl.multiple_of((plane * near_rows + row) * STRIP, STRIP), STRIP)

    def own_at(plane, row):
        return pl.ds(pl.multiple_of((plane * own_rows + row) * STRIP, STRIP), STRIP)

    @pl.when(step == 0)
    def _():
        token_stats(x_ref, average, scale)
        frame_zeros([normed, upstream])
        sum_plain[...] = jnp.zeros_like(sum_plain)
        sum_normed[...] = jnp.zeros_like(sum_normed)

    shift_by = mods_ref[0:1, :]
    scale_by = 1.0 + mods_ref[1:2, :]

    @pl.loop(0, near_rows)
    def _(row):
        for plane in range(4):
            rows = near_at(plane, row)
            padded = pl.ds(pl.multiple_of((row + 1) * STRIP, STRIP), STRIP)
            normed[plane, padded, :] = (
                normed_strip(x_ref, average, scale, rows, columns) * scale_by + shift_by
            )
            upstream[plane, padded, :] = kept_ref[rows, :].astype(full) + arriving_ref[
                rows, :
            ].astype(full)

    kernel = kernel_ref[...]
    flipped = jnp.concatenate([kernel[8 - t : 9 - t, :] for t in range(9)], axis=0)

    def kernel_strip(row, sums):
        near = near_strips(normed, row + core)
        sums = list(sums)
        for row_phase in range(2):
            for column_phase in range(2):
                grad_here = strip_at(upstream, row_phase, column_phase, row + core)
                for i in range(3):
                    for j in range(3):
                        product = near[row_phase][i][column_phase][j] * grad_here
                        sums[3 * i + j] = sums[3 * i + j] + (product[:8] + product[8:])
        return tuple(sums)

    def fold(sums, rows):
        return jnp.concatenate(
            [jnp.sum(s, axis=0, keepdims=True) for s in sums]
            + [jnp.zeros((rows - len(sums), width), full)],
            axis=0,
        )

    blank = jnp.zeros((8, width), full)
    kernel_grad_ref[...] = fold(lax.fori_loop(0, own_rows, kernel_strip, (blank,) * 9), 16)

    def input_strip(row, sums):
        near = near_strips(upstream, row + core)
        shift_sum, scale_sum = sums
        for row_phase in range(2):
            for column_phase in range(2):
                plane = 2 * row_phase + column_phase
                grad = conv_strip(near, flipped, row_phase, column_phase)
                plain = normed_strip(x_ref, average, scale, near_at(plane, row + core), columns)
                shift_sum = shift_sum + (grad[:8] + grad[8:])
                product = grad * plain
                scale_sum = scale_sum + (product[:8] + product[8:])
                scaled = grad * scale_by
                rows = own_at(plane, row)
                held[step, rows, :] = scaled
                product = scaled * plain
                sum_plain[rows, :] += sum(scaled[:, k : k + 128] for k in range(0, width, 128))
                sum_normed[rows, :] += sum(product[:, k : k + 128] for k in range(0, width, 128))
        return shift_sum, scale_sum

    mods_grad_ref[...] = fold(lax.fori_loop(0, own_rows, input_strip, (blank,) * 2), 8)

    @pl.when(step == pl.num_programs(0) - 1)
    def _():
        model = x_ref.shape[1]

        @pl.loop(0, own_rows)
        def _(row):
            for plane in range(4):
                rows = own_at(plane, row)
                near = near_at(plane, row + core)
                mean_plain = jnp.sum(sum_plain[rows, :], axis=-1, keepdims=True) / model
                mean_normed = jnp.sum(sum_normed[rows, :], axis=-1, keepdims=True) / model
                for block in range(model // width):
                    at = pl.ds(block * width, width)
                    plain = normed_strip(x_ref, average, scale, near, at)
                    spread = jnp.concatenate([scale[near, :]] * (width // 128), axis=1)
                    out_ref[rows, at] = middle_ref[rows, at] + spread * (
                        held[block, rows, :] - mean_plain - plain * mean_normed
                    )


def conv_back(core, x_near, kept, arriving, kernel, mods, grad_middle):
    near_tokens, model = x_near.shape
    own_tokens = grad_middle.shape[0]
    once = pl.Buffered(1)
    whole = lambda j, words: (0, 0)
    across = lambda j, words: (0, j)
    padded = near_tokens // 4 + 2 * STRIP
    return pl.pallas_call(
        conv_back_body,
        grid_spec=pltpu.PrefetchScalarGridSpec(
            num_scalar_prefetch=1,
            grid=(model // TILE,),
            in_specs=[
                pl.BlockSpec((near_tokens, model), whole, pipeline_mode=once),
                pl.BlockSpec((near_tokens, TILE), across),
                pl.BlockSpec((near_tokens, TILE), across),
                pl.BlockSpec((16, TILE), across),
                pl.BlockSpec((8, TILE), across),
                pl.BlockSpec((own_tokens, model), whole, pipeline_mode=once),
            ],
            out_specs=[
                pl.BlockSpec((own_tokens, model), whole),
                pl.BlockSpec((16, TILE), across),
                pl.BlockSpec((8, TILE), across),
            ],
            scratch_shapes=[
                pltpu.VMEM((near_tokens, 128), full),
                pltpu.VMEM((near_tokens, 128), full),
                pltpu.VMEM((4, padded, TILE), full),
                pltpu.VMEM((4, padded, TILE), full),
                pltpu.VMEM((model // TILE, own_tokens, TILE), full),
                pltpu.VMEM((own_tokens, 128), full),
                pltpu.VMEM((own_tokens, 128), full),
            ],
        ),
        out_shape=[
            jax.ShapeDtypeStruct((own_tokens, model), full),
            jax.ShapeDtypeStruct((16, model), full),
            jax.ShapeDtypeStruct((8, model), full),
        ],
        cost_estimate=pl.CostEstimate(
            flops=70 * own_tokens * model,
            bytes_accessed=14 * own_tokens * model,
            transcendentals=near_tokens,
        ),
        name="conv_back",
    )(core[None].astype(jnp.int32), x_near, kept, arriving, kernel, mods, grad_middle)


def row_stats(values):
    mean = jnp.mean(values, axis=-1, keepdims=True)
    centred = values - mean
    scale = lax.rsqrt(jnp.mean(centred * centred, axis=-1, keepdims=True) + ln_epsilon)
    return centred * scale, scale


def enter_feed_body(x_ref, part_ref, other_ref, grad_ref, mods_ref, norm_ref, norm_t_ref, out_ref):
    @pl.loop(0, x_ref.shape[0] // STRIP)
    def _(strip):
        rows = pl.ds(pl.multiple_of(strip * STRIP, STRIP), STRIP)
        branch = part_ref[rows, :].astype(full) + other_ref[rows, :].astype(full)
        plain, _ = row_stats(x_ref[rows, :].astype(full) + mods_ref[0:1, :] * branch)
        normed = plain * (1.0 + mods_ref[2:3, :]) + mods_ref[1:2, :]
        norm_ref[rows, :] = normed.astype(low)
        out_ref[rows, :] = (grad_ref[rows, :].astype(full) * mods_ref[3:4, :]).astype(low)

    norm_t_ref[...] = norm_ref[...].T


def enter_feed(canvas, part, other, grad, mods):
    tokens, model = canvas.shape
    rows = PLANE // 2
    along = pl.BlockSpec((rows, model), lambda j: (j, 0))
    return pl.pallas_call(
        enter_feed_body,
        grid=(tokens // rows,),
        in_specs=[along] * 4 + [pl.BlockSpec((8, model), lambda j: (0, 0))],
        out_specs=[along, pl.BlockSpec((model, rows), lambda j: (0, j)), along],
        out_shape=[
            jax.ShapeDtypeStruct((tokens, model), low),
            jax.ShapeDtypeStruct((model, tokens), low),
            jax.ShapeDtypeStruct((tokens, model), low),
        ],
        cost_estimate=pl.CostEstimate(flops=1000, bytes_accessed=1000, transcendentals=0),
        name="enter_feed",
    )(canvas, part, other, grad, mods)


def leave_feed_body(words_ref, x_ref, part_ref, other_ref, grad_ref, mods_ref, *refs):
    *kept_refs, out_ref, middle_grad_ref, branch_grad_ref, sums_ref, totals = refs
    plane = pl.program_id(0)

    @pl.when(plane == 0)
    def _():
        totals[...] = jnp.zeros_like(totals)

    @pl.loop(0, x_ref.shape[0] // STRIP)
    def _(strip):
        rows = pl.ds(pl.multiple_of(strip * STRIP, STRIP), STRIP)
        gate_a, gate_f = mods_ref[0:1, :], mods_ref[3:4, :]
        branch_a = part_ref[rows, :].astype(full) + other_ref[rows, :].astype(full)
        middle = x_ref[rows, :].astype(full) + gate_a * branch_a
        plain, scale = row_stats(middle)
        branch_f = sum(ref[0, 0, rows, :].astype(full) for ref in kept_refs)
        back = sum(ref[1, 0, rows, :].astype(full) for ref in kept_refs)
        grad = grad_ref[rows, :].astype(full)
        out_ref[rows, :] = (middle + gate_f * branch_f).astype(low)
        scaled = back * (1.0 + mods_ref[2:3, :])
        mean_plain = jnp.mean(scaled, axis=-1, keepdims=True)
        mean_normed = jnp.mean(scaled * plain, axis=-1, keepdims=True)
        grad_middle = grad + scale * (scaled - mean_plain - plain * mean_normed)
        middle_grad_ref[rows, :] = grad_middle
        branch_grad_ref[rows, :] = (grad_middle * gate_a).astype(low)
        products = (grad * branch_f, back, back * plain, grad_middle * branch_a)
        for index, product in enumerate(products):
            totals[index] += product[:8] + product[8:]

    @pl.when(plane == pl.num_programs(0) - 1)
    def _():
        lines = [jnp.sum(totals[k], axis=0, keepdims=True) for k in range(4)]
        sums_ref[...] = jnp.concatenate(lines + [jnp.zeros_like(sums_ref[:4])], axis=0)


def leave_feed(words, canvas, part, other, grad, mods, kept):
    model = canvas.shape[1]
    rows = PLANE // 2
    own = pl.BlockSpec((rows, model), lambda j, words: (2 * j + words[0], 0))
    half = pl.BlockSpec((rows, model), lambda j, words: (j, 0))
    whole = pl.BlockSpec((8, model), lambda j, words: (0, 0))
    return pl.pallas_call(
        leave_feed_body,
        grid_spec=pltpu.PrefetchScalarGridSpec(
            num_scalar_prefetch=1,
            grid=(4,),
            in_specs=[own] * 4
            + [whole]
            + [pl.BlockSpec((2, 1, rows, model), lambda j, words: (0, j, 0, 0))] * len(kept),
            out_specs=[half, half, half, whole],
            scratch_shapes=[pltpu.VMEM((4, 8, model), full)],
        ),
        out_shape=[
            jax.ShapeDtypeStruct((4 * rows, model), low),
            jax.ShapeDtypeStruct((4 * rows, model), full),
            jax.ShapeDtypeStruct((4 * rows, model), low),
            jax.ShapeDtypeStruct((8, model), full),
        ],
        cost_estimate=pl.CostEstimate(flops=1000, bytes_accessed=1000, transcendentals=0),
        name="leave_feed",
    )(words, canvas, part, other, grad, mods, *kept)


def on_device(
    tokens,
    seg_ids,
    timesteps,
    labels,
    cotangent,
    mod_weight,
    class_table,
    attn_kernel,
    qkv_weight,
    proj_weight,
    up_weight,
    ffn_kernel,
    down_weight,
):
    devices = device_count()
    chips = devices // 2
    chip_bits = chips.bit_length() - 1
    rank = lax.axis_index("dp") * lax.axis_size("fsdp") + lax.axis_index("fsdp")
    core = rank % 2
    chip = rank // 2
    _, half_tokens, model = tokens.shape
    half_rows = half_tokens // SIDE
    class_count = class_table.shape[0]
    part = model // devices
    share = down_weight.shape[0]
    piece = share // CHUNKS
    pairs = model // HEAD // 4

    def halves_of(array, axis):
        return at_bit(array, axis, core), at_bit(array, axis, 1 - core)

    def row_pair(array, axis):
        kept, leaving = halves_of(array, axis)
        arriving = swap_core(leaving)
        return jnp.concatenate(in_core_order(kept, arriving, core), axis=0)

    qkv_split = qkv_weight.reshape(part, 3, 2, pairs, 128).transpose(0, 2, 3, 1, 4)
    qkv_rows = row_pair(qkv_split.reshape(part, 2, pairs * 384), 1)
    qkv_half = pairs * 384 // 2

    picks = labels[:, None] == jnp.arange(class_count)[None, :]
    angles_here = lax.dynamic_slice_in_dim(sinusoid(timesteps, model), rank * part, part, axis=1)
    cond = angles_here + jnp.dot(picks.astype(low), class_table, preferred_element_type=full)
    lift_value, lift_pull = jax.vjp(jax.nn.silu, cond)
    lifted = lift_value.astype(low)
    mods_part = jnp.dot(lifted, mod_weight, preferred_element_type=full)

    slot = Slots(jnp.zeros((8, 128), full))
    flow = lambda shard, colour: gather_flow(shard, colour, chip_bits)
    sums = lambda parts, colour: scatter_flow(parts, colour, chip, chip_bits)
    joined = lambda flows: [
        gathered(f, colour, chip, chip_bits) for colour, f in enumerate(flows)
    ]
    mods_flow = scatter_flow(mods_part, 0, chip, chip_bits, sent=full)
    qkv_flows = [flow(qkv_rows[:, :qkv_half], 0), flow(qkv_rows[:, qkv_half:], 1)]
    mine, upstream = slot(
        qkv_flows + [mods_flow],
        lambda: (to_phases(tokens[0], half_rows), to_phases(cotangent[0], half_rows)),
    )

    up_weight, proj_weight, ffn_kernel, attn_kernel = slot.after(
        up_weight, proj_weight, ffn_kernel, attn_kernel
    )
    up_split = up_weight.reshape(part, chips, 2, CHUNKS, piece).transpose(0, 2, 3, 1, 4)
    up_rows = row_pair(up_split.reshape(part, 2, CHUNKS, chips * piece), 1)
    proj_there = [(r, r % chips * 2 + r // chips) for r in range(devices)]
    proj_back = [(b, a) for a, b in proj_there]
    proj_rows = lax.ppermute(proj_weight, AXES, proj_there)
    canvas = join_halves(mine, swap_core(mine), core)

    slot(qkv_flows + [mods_flow])
    while mods_flow.wanted is not None:
        array, bit = mods_flow.wanted
        mods_flow.arrive(swap(array, bit + 1))
    mods = mods_flow.result + swap_core(mods_flow.result)
    shift_a, scale_a, gate_a, shift_f, scale_f, gate_f = jnp.split(mods, 6)

    tap_count = 9 * (share + part)
    tap_words = jnp.concatenate([ffn_kernel.reshape(-1), attn_kernel.reshape(-1)])
    tap_words = jnp.pad(tap_words, (0, -tap_count % 128))
    taps = gather_rows(tap_words, rank, chip_bits + 1, 0)
    ffn_taps = taps[:, : 9 * share].reshape(chips, 2, 9, share)
    ffn_taps = at_bit(ffn_taps, 1, core).reshape(chips, 9, CHUNKS, piece)
    ffn_taps = ffn_taps.transpose(2, 1, 0, 3).reshape(CHUNKS, 9, chips * piece).astype(full)
    ffn_taps = jnp.pad(ffn_taps, ((0, 0), (0, 7), (0, 0)))
    attn_taps = taps[:, 9 * share : tap_count].reshape(devices, 9, part)
    attn_taps = attn_taps.transpose(1, 0, 2).reshape(9, model).astype(full)
    attn_taps = jnp.pad(attn_taps, ((0, 7), (0, 0)))

    spot = jnp.arange(PLANE)
    quadrant = 2 * (spot // (PLANE // 2)) + spot % HALF_SIDE // (HALF_SIDE // 2)
    quadrants_here = at_bit(seg_ids, 0, chip)
    segment = jnp.sum(
        jnp.where(quadrant[:, None] == jnp.arange(4)[None, :], quadrants_here[None, :], 0), axis=1
    )
    mask = (segment[:, None] == segment[None, :]).astype(full)

    proj_flows = [flow(proj_rows[:, : model // 2], 0), flow(proj_rows[:, model // 2 :], 1)]
    feed_flows = [
        [flow(up_rows[:, t], 0), flow(down_weight[t * piece : (t + 1) * piece], 1)]
        for t in range(CHUNKS)
    ]
    mods_a = jnp.concatenate([shift_a[None], scale_a[None], jnp.zeros((6, model), full)], axis=0)

    slot(qkv_flows + proj_flows + feed_flows[0])
    convolved = slot(
        qkv_flows + proj_flows + feed_flows[0] + feed_flows[1], lambda: conv_in(canvas, attn_taps, mods_a)
    )

    (upstream,) = slot.after(upstream)
    grad_ph = join_halves(upstream, swap_core(upstream), core)

    def project_in():
        weight = jnp.concatenate(
            [array.reshape(model, qkv_half) for array in joined(qkv_flows)], axis=1
        )
        return weight, jnp.dot(convolved, weight, preferred_element_type=full).astype(low)

    slot.finish(qkv_flows)
    qkv_full, qkv = slot(proj_flows + feed_flows[0] + feed_flows[1], project_in)
    attended = slot(
        proj_flows + feed_flows[1] + feed_flows[2], lambda: attend(mask, qkv)
    )

    mods_f = jnp.concatenate(
        [gate_a[None], shift_f[None], scale_f[None], gate_f[None], jnp.zeros((4, model), full)]
    )

    def project_out():
        weight = jnp.concatenate(
            [array.reshape(-1, model // 2) for array in joined(proj_flows)], axis=1
        )
        branch_part = jnp.dot(attended, weight, preferred_element_type=full).astype(low)
        other = swap_core(branch_part)
        return weight, branch_part, other, *enter_feed(canvas, branch_part, other, grad_ph, mods_f)

    slot.finish(proj_flows)
    proj_full, branch_part, branch_other, norm, norm_t, grad_branch_f = slot(
        feed_flows[0] + feed_flows[2], project_out
    )

    kept = []
    grads = [None] * CHUNKS

    spread = 2 * part % STRIP == 0 and piece % STRIP == 0 and chips >= 8
    up_owner, _ = owners(0, chip, chip_bits)
    down_owner, down_place = owners(1, chip, chip_bits)
    words = jnp.concatenate([core[None], up_owner, down_owner, down_place]).astype(jnp.int32)

    def feed(t):
        def work():
            if spread:
                up, down = [f.result for f in feed_flows[t]]
            else:
                up, down = joined(feed_flows[t])
                up, down = [up.reshape(model, -1)], [down.reshape(-1, model)]
            return feed_forward(norm, norm_t, grad_branch_f, up, down, ffn_taps[t], words)

        return work

    back_flows = [[] for _ in range(CHUNKS)]

    def run_feed(flows, t):
        slot.finish(feed_flows[t])
        staying, leaving, up_grad, down_grad, tap_grad = slot(flows, feed(t))
        kept.append((staying, leaving))
        grads[t] = tap_grad
        if spread:
            back_flows[t] = [
                Flow(halving_steps(*grad[::-1], gather_order(chip_bits, colour)[::-1]))
                for colour, grad in enumerate((up_grad, down_grad))
            ]
        else:
            back_flows[t] = [
                sums(up_grad[0].reshape(chips, 2 * part, -1), 0),
                sums(down_grad[0].reshape(chips, piece, model), 1),
            ]

    run_feed(feed_flows[1] + feed_flows[2], 0)
    run_feed(feed_flows[2] + back_flows[0], 1)
    run_feed(back_flows[0] + back_flows[1], 2)

    def after_feed():
        parts = [array for staying, leaving in kept for array in (staying, swap_core(leaving))]
        return leave_feed(words[:1], canvas, branch_part, branch_other, grad_ph, mods_f, parts)

    layer_out, grad_middle, grad_branch_mine, feed_sums = slot(
        back_flows[0] + back_flows[2], after_feed
    )
    grad_gate_f, grad_shift_f, grad_scale_f, grad_gate_a = feed_sums[:4]
    grad_branch_mine = grad_branch_mine.reshape(4, -1, model)
    layer_out = from_phases(layer_out.reshape(4, -1, model), half_rows)[None]

    def enter_attend():
        grad_branch_a = join_halves(grad_branch_mine, swap_core(grad_branch_mine), core)
        grad_attended = jnp.dot(grad_branch_a, proj_full.T, preferred_element_type=full)
        proj_grad = jnp.dot(attended.T, grad_branch_a, preferred_element_type=full)
        return grad_attended.astype(low), proj_grad.astype(low)

    grad_attended, proj_grad = slot(back_flows[0] + back_flows[1], enter_attend)
    proj_grad = proj_grad.reshape(chips, -1, model)
    proj_flows = [sums(proj_grad[..., : model // 2], 0), sums(proj_grad[..., model // 2 :], 1)]
    grad_qkv = slot(
        proj_flows + sum(back_flows, []), lambda: attend_back(mask, qkv, grad_attended)
    )
    qkv_grad = slot(
        proj_flows + sum(back_flows, []),
        lambda: jnp.dot(convolved.T, grad_qkv, preferred_element_type=full).astype(low),
    )
    qkv_grad = qkv_grad.reshape(chips, 2 * part, -1)
    qkv_flows = [sums(qkv_grad[..., :qkv_half], 0), sums(qkv_grad[..., qkv_half:], 1)]

    def rows_near(array, which):
        size = PLANE // 2 + STRIP
        near = lax.dynamic_slice_in_dim(
            array.reshape(4, PLANE, model), which * (PLANE - size), size, axis=1
        )
        return near.reshape(4 * size, model)

    def leave_attend():
        part_here = jnp.dot(grad_qkv, qkv_full.T, preferred_element_type=full).astype(low)
        return rows_near(part_here, core), swap_core(rows_near(part_here, 1 - core))

    grad_conv = slot(qkv_flows + proj_flows + back_flows[2], leave_attend)

    def leave_block():
        input_grad, attn_tap_grad, mods_grad = conv_back(
            core, rows_near(canvas, core), *grad_conv, attn_taps, mods_a,
            grad_middle,
        )
        input_grad = from_phases(input_grad.reshape(4, -1, model), half_rows)
        return attn_tap_grad[:9], input_grad, mods_grad[0], mods_grad[1]

    attn_tap_grad, input_grad, grad_shift_a, grad_scale_a = slot(
        qkv_flows + proj_flows + back_flows[2], leave_block
    )
    slot.finish(sum(back_flows, proj_flows + qkv_flows))
    up_shares = [flows[0].result for flows in back_flows]
    down_shares = [flows[1].result for flows in back_flows]
    tap_grads = [g[:9].reshape(9, chips, piece) for g in grads]
    qkv_share = jnp.concatenate([f.result for f in qkv_flows], axis=1)
    proj_share = jnp.concatenate([f.result for f in proj_flows], axis=1)
    proj_share = lax.ppermute(proj_share, AXES, proj_back)

    grad_mods = jnp.concatenate(
        [grad_shift_a, grad_scale_a, grad_gate_a, grad_shift_f, grad_scale_f, grad_gate_f]
    )
    grad_mods = (grad_mods + swap_core(grad_mods)).astype(low)
    grad_mods_all = gather_rows(grad_mods, chip, chip_bits)
    mod_grad = jnp.dot(lifted.T, grad_mods_all, preferred_element_type=full)
    (cond_grad,) = lift_pull(jnp.dot(grad_mods_all, mod_weight.T, preferred_element_type=full))
    table_grad = jnp.dot(picks.astype(full).T, cond_grad, precision=highest)

    ffn_tap_grad = jnp.concatenate(tap_grads, axis=2).transpose(1, 0, 2)
    attn_split = attn_tap_grad.reshape(9, chips, 2, part)
    attn_kept, attn_leaving = halves_of(attn_split, 2)
    attn_tap_grad = (attn_kept + swap_core(attn_leaving)).transpose(1, 0, 2)
    tap_parts = jnp.concatenate(
        [ffn_tap_grad.reshape(chips, -1), attn_tap_grad.reshape(chips, -1)], axis=1
    )
    tap_share = scatter_sum(tap_parts, 0, chip, chip_bits, sent=full)
    ffn_share = tap_share[: 9 * share].reshape(9, share)
    kernel_share = tap_share[9 * share :].reshape(9, part)

    def row_split(array, axis):
        pair = array.reshape((2, part) + array.shape[1:])
        kept, leaving = halves_of(pair, 0)
        arriving = swap_core(leaving)
        return jnp.stack(in_core_order(kept, arriving, core), axis=axis)

    up_all = jnp.stack(up_shares, axis=1).reshape(2 * part, CHUNKS, chips, piece)
    up_share = row_split(up_all.transpose(0, 2, 1, 3), 2).reshape(part, -1)
    down_share = jnp.concatenate(down_shares, axis=0)
    qkv_all = qkv_share.reshape(2 * part, pairs, 3, 128).transpose(0, 2, 1, 3)
    qkv_out = row_split(qkv_all, 2).reshape(part, -1)

    return (
        layer_out,
        input_grad[None],
        mod_grad,
        table_grad,
        kernel_share,
        qkv_out,
        proj_share,
        up_share,
        ffn_share,
        down_share,
        grad_shift_f[None],
    )


def solution(mesh):
    return jax.shard_map(
        on_device,
        mesh=mesh,
        in_specs=(
            P(AXES, None, None),
            P(),
            P(),
            P(),
            P(AXES, None, None),
            P(AXES, None),
            P(None, AXES),
            P(None, AXES),
            P(AXES, None),
            P(AXES, None),
            P(AXES, None),
            P(None, AXES),
            P(AXES, None),
        ),
        out_specs=(
            P(AXES, None, None),
            P(AXES, None, None),
            P(AXES, None),
            P(None, AXES),
            P(None, AXES),
            P(AXES, None),
            P(AXES, None),
            P(AXES, None),
            P(None, AXES),
            P(AXES, None),
            P(AXES, None),
        ),
        check_vma=False,
    )
```

```python
import functools
import math

import jax
import jax.numpy as jnp
from jax import lax
from jax.experimental import pallas as pl
from jax.experimental.pallas import tpu as pltpu
from jax.sharding import PartitionSpec as P

HEAD = 64
SIDE = 32
HALF_SIDE = SIDE // 2
STRIP = HALF_SIDE
PLANE = HALF_SIDE * HALF_SIDE
PADDED = PLANE + 2 * STRIP
TILE = 256
CHUNKS = 3

highest = lax.Precision.HIGHEST
ln_epsilon = 1e-06
masked_score = -1000000000.0
low = jnp.bfloat16
full = jnp.float32
AXES = ("dp", "fsdp")


def device_count():
    return lax.axis_size("dp") * lax.axis_size("fsdp")


def swap(x, bit):
    return lax.ppermute(x, AXES, [(i, i ^ 1 << bit) for i in range(device_count())])


def swap_core(x):
    return swap(x, 0)


def gather_order(chip_bits, colour):
    order = list(range(chip_bits - 1, -1, -1))
    if colour and chip_bits > 1:
        order[-1], order[-2] = order[-2], order[-1]
    return order


class Flow:
    def __init__(self, steps):
        self.steps = steps
        self.wanted = next(steps)
        self.result = None

    def arrive(self, array):
        try:
            self.wanted = self.steps.send(array)
        except StopIteration as end:
            self.wanted, self.result = None, end.value


class Slots:
    def __init__(self, token):
        self.token = token

    def after(self, *arrays):
        arrays, self.token = lax.optimization_barrier((arrays, self.token))
        return arrays

    def finish(self, flows):
        while any(flow.wanted is not None for flow in flows):
            self(flows)

    def __call__(self, flows, work=lambda: ()):
        flows = [flow for flow in flows if flow.wanted is not None]
        wanted = [flow.wanted for flow in flows]
        leaving, self.token = lax.optimization_barrier(([w[0] for w in wanted], self.token))
        arriving = [swap(array, bit + 1) for array, (_, bit) in zip(leaving, wanted)]
        arriving, result, self.token = lax.optimization_barrier((arriving, work(), self.token))
        for flow, array in zip(flows, arriving):
            flow.arrive(array)
        return result


def gather_steps(shard, order):
    held = shard[None]
    for bit in order[:-1]:
        arriving = yield held, bit
        held = jnp.concatenate([held, arriving], axis=0)
    arriving = yield held, order[-1]
    return held, arriving


def assemble_body(steps, chip_ref, *refs):
    *piece_refs, out_ref = refs
    which = pl.program_id(0) // steps
    top = chip_ref[1]
    for index, piece_ref in enumerate(piece_refs):

        @pl.when(which == index)
        def _():
            for k in range(4):
                out_ref[jnp.bitwise_xor(top, (k & 1) << 1 | k >> 1), 0] = piece_ref[k]


def assemble(pieces, order, chip):
    chips = sum(piece.shape[0] for piece in pieces)
    rows, columns = pieces[0].shape[1:]
    if chips < 4 or len(pieces) * pieces[0].shape[0] != chips or pieces[0].shape[0] % 4:
        raise ValueError("unexpected mesh")
    rest = len(order) - 2
    steps = pieces[0].shape[0] // 4
    chip_words = jnp.stack([jnp.bitwise_and(chip, (1 << rest) - 1), chip >> rest]).astype(jnp.int32)

    def out_map(step, words):
        at = words[0]
        for position, bit in enumerate(order[2:]):
            at = jnp.bitwise_xor(at, jnp.bitwise_and(step >> position, 1) << bit)
        return (0, at, 0, 0)

    def piece_map(index):
        return lambda step, words: (jnp.clip(step - index * steps, 0, steps - 1), 0, 0)

    out = pl.pallas_call(
        functools.partial(assemble_body, steps),
        grid_spec=pltpu.PrefetchScalarGridSpec(
            num_scalar_prefetch=1,
            grid=(chips // 4,),
            in_specs=[
                pl.BlockSpec((4, rows, columns), piece_map(index)) for index in range(len(pieces))
            ],
            out_specs=pl.BlockSpec((4, 1, rows, columns), out_map),
        ),
        out_shape=jax.ShapeDtypeStruct((4, chips // 4, rows, columns), pieces[0].dtype),
        cost_estimate=pl.CostEstimate(
            flops=0, bytes_accessed=4 * chips * rows * columns, transcendentals=0
        ),
        name="assemble",
    )(chip_words, *pieces)
    return out.reshape(chips, rows, columns)


def gather_flow(shard, colour, chip_bits):
    return Flow(gather_steps(shard, gather_order(chip_bits, colour)))


def gathered(flow, colour, chip, chip_bits):
    return assemble(flow.result, gather_order(chip_bits, colour), chip)


def at_bit(array, axis, bit):
    return lax.dynamic_index_in_dim(array, bit, axis, keepdims=False)


def scatter_steps(parts, order, chip, chip_bits, sent):
    left = list(range(chip_bits - 1, -1, -1))
    held = [parts.reshape((2,) * chip_bits + parts.shape[1:])]
    for bit in order:
        axis = left.index(bit)
        left.remove(bit)
        mine = jnp.bitwise_and(chip >> bit, 1)
        leaving = sum(at_bit(h, axis, 1 - mine).astype(full) for h in held).astype(sent)
        staying = sum(at_bit(h, axis, mine).astype(full) for h in held).astype(sent)
        arriving = yield leaving, bit
        held = [staying, arriving]
    return held[0].astype(full) + held[1].astype(full)


def halving_steps(leaving, staying, order):
    arriving = yield leaving, order[0]
    for bit in order[1:]:
        half = staying.shape[0] // 2
        leaving, staying = [
            (staying[at].astype(full) + arriving[at].astype(full)).astype(low)
            for at in (slice(half, None), slice(half))
        ]
        arriving = yield leaving, bit
    return (staying.astype(full) + arriving.astype(full))[0]


def owners(colour, chip, chip_bits):
    order = gather_order(chip_bits, colour)
    spots = jnp.arange(1 << chip_bits)
    bits = list(enumerate(order))
    owner = sum((jnp.bitwise_and(spots >> at, 1) << bit) for at, bit in bits)
    apart = jnp.bitwise_xor(spots, chip)
    place = sum((jnp.bitwise_and(apart >> bit, 1) << at) for at, bit in bits)
    return jnp.bitwise_xor(owner, chip), place


def scatter_flow(parts, colour, chip, chip_bits, sent=low):
    order = gather_order(chip_bits, colour)[::-1]
    return Flow(scatter_steps(parts, order, chip, chip_bits, sent))


def row_steps(row, chip, chip_bits, first_bit):
    held = row[None]
    for bit in range(chip_bits):
        arriving = yield held, bit + first_bit - 1
        held = jnp.concatenate([held, arriving], axis=0)
    places = jnp.arange(1 << chip_bits)
    pick = jnp.bitwise_xor(places, chip)[:, None] == places[None, :]
    return jnp.dot(pick.astype(held.dtype), held, preferred_element_type=full).astype(held.dtype)


def row_flow(row, chip, chip_bits, first_bit=1):
    return Flow(row_steps(row, chip, chip_bits, first_bit))


def run(flow):
    while flow.wanted is not None:
        array, bit = flow.wanted
        flow.arrive(swap(array, bit + 1))
    return flow.result


def to_phases(block_in, row_count):
    width = block_in.shape[-1]
    split_grid = block_in.reshape(row_count // 2, 2, HALF_SIDE, 2, width)
    return split_grid.transpose(1, 3, 0, 2, 4).reshape(4, row_count // 2 * HALF_SIDE, width)


def from_phases(block_in, row_count):
    width = block_in.shape[-1]
    split_grid = block_in.reshape(2, 2, row_count // 2, HALF_SIDE, width)
    return split_grid.transpose(2, 0, 3, 1, 4).reshape(row_count * SIDE, width)


def in_core_order(mine, other, core):
    return jnp.where(core == 0, mine, other), jnp.where(core == 0, other, mine)


def join_halves(mine, other, core):
    return jnp.stack(in_core_order(mine, other, core), axis=1).reshape(-1, mine.shape[-1])


def half_of(joined, which):
    width = joined.shape[-1]
    return at_bit(joined.reshape(4, 2, -1, width), 1, which)


def layer_norm(values):
    average = jnp.mean(values, axis=-1, keepdims=True)
    centred = values - average
    variance = jnp.mean(centred * centred, axis=-1, keepdims=True)
    return centred * lax.rsqrt(variance + ln_epsilon)


def modulate(values, shift_by, scale_by):
    return layer_norm(values) * (1.0 + scale_by) + shift_by


def sinusoid(steps_in, width):
    halfway = width // 2
    frequency = jnp.exp(-math.log(10000.0) * jnp.arange(halfway, dtype=jnp.float32) / halfway)
    angles = steps_in.astype(jnp.float32)[..., None] * frequency
    return jnp.concatenate([jnp.cos(angles), jnp.sin(angles)], axis=-1)


def softmax_of(query, key, allowed):
    raw = lax.dot_general(query, key, (((1,), (1,)), ((), ())), preferred_element_type=full)
    scores = jnp.where(allowed, raw * HEAD ** (-0.5), masked_score)
    shifted = jnp.exp(scores - jnp.max(scores, axis=-1, keepdims=True))
    return shifted / jnp.sum(shifted, axis=-1, keepdims=True)


def head_lanes(shape, head):
    lanes = lax.broadcasted_iota(jnp.int32, shape, 1)
    return jnp.logical_and(lanes >= head * HEAD, lanes < (head + 1) * HEAD)


def attend_body(mask_ref, qkv_ref, out_ref):
    allowed = mask_ref[...] > 0.5

    @pl.loop(0, 4)
    def _(phase):
        rows = pl.ds(pl.multiple_of(phase * PLANE, PLANE), PLANE)
        query = qkv_ref[rows, :128]
        key = qkv_ref[rows, 128:256]
        value = qkv_ref[rows, 256:]
        total = None
        for head in range(2):
            here = head_lanes(key.shape, head)
            probs = softmax_of(query, jnp.where(here, key, jnp.zeros_like(key)), allowed)
            part = jnp.dot(
                probs.astype(low),
                jnp.where(here, value, jnp.zeros_like(value)),
                preferred_element_type=full,
            )
            total = part if total is None else total + part
        out_ref[rows, :] = total.astype(low)


def attend_back_body(mask_ref, qkv_ref, grad_ref, out_ref):
    allowed = mask_ref[...] > 0.5

    @pl.loop(0, 4)
    def _(phase):
        rows = pl.ds(pl.multiple_of(phase * PLANE, PLANE), PLANE)
        query = qkv_ref[rows, :128]
        key = qkv_ref[rows, 128:256]
        value = qkv_ref[rows, 256:]
        grad = grad_ref[rows, :]
        by_rows = (((0,), (0,)), ((), ()))
        totals = [None, None, None]
        for head in range(2):
            here = head_lanes(key.shape, head)
            blank = jnp.zeros_like(key)
            key_here = jnp.where(here, key, blank)
            query_here = jnp.where(here, query, blank)
            value_here = jnp.where(here, value, blank)
            grad_here = jnp.where(here, grad, blank)
            weights = softmax_of(query, key_here, allowed)
            grad_probs = lax.dot_general(
                grad, value_here, (((1,), (1,)), ((), ())), preferred_element_type=full
            )
            delta = jnp.sum(grad_probs * weights, axis=-1, keepdims=True)
            grad_scores = (weights * (grad_probs - delta)).astype(low)
            parts = (
                jnp.dot(grad_scores, key_here, preferred_element_type=full),
                lax.dot_general(grad_scores, query_here, by_rows, preferred_element_type=full),
                lax.dot_general(
                    weights.astype(low), grad_here, by_rows, preferred_element_type=full
                ),
            )
            totals = [p if t is None else t + p for t, p in zip(totals, parts)]
        out_ref[rows, :128] = (totals[0] * HEAD ** (-0.5)).astype(low)
        out_ref[rows, 128:256] = (totals[1] * HEAD ** (-0.5)).astype(low)
        out_ref[rows, 256:] = totals[2].astype(low)


def attend(mask, qkv):
    tokens, width = qkv.shape
    pairs = width // 384
    return pl.pallas_call(
        attend_body,
        grid=(pairs,),
        in_specs=[
            pl.BlockSpec((PLANE, PLANE), lambda j: (0, 0)),
            pl.BlockSpec((tokens, 384), lambda j: (0, j)),
        ],
        out_specs=pl.BlockSpec((tokens, 128), lambda j: (0, j)),
        out_shape=jax.ShapeDtypeStruct((tokens, pairs * 128), low),
        cost_estimate=pl.CostEstimate(
            flops=pairs * 2 * 4 * 4 * PLANE * PLANE * 256,
            bytes_accessed=8 * tokens * pairs * 128,
            transcendentals=pairs * 8 * PLANE * PLANE,
        ),
        name="attend",
    )(mask, qkv)


def attend_back(mask, qkv, grad):
    tokens, width = qkv.shape
    pairs = width // 384
    return pl.pallas_call(
        attend_back_body,
        grid=(pairs,),
        in_specs=[
            pl.BlockSpec((PLANE, PLANE), lambda j: (0, 0)),
            pl.BlockSpec((tokens, 384), lambda j: (0, j)),
            pl.BlockSpec((tokens, 128), lambda j: (0, j)),
        ],
        out_specs=pl.BlockSpec((tokens, 384), lambda j: (0, j)),
        out_shape=jax.ShapeDtypeStruct((tokens, width), low),
        cost_estimate=pl.CostEstimate(
            flops=pairs * 2 * 4 * 10 * PLANE * PLANE * 256,
            bytes_accessed=14 * tokens * pairs * 128,
            transcendentals=pairs * 8 * PLANE * PLANE,
        ),
        name="attend_back",
    )(mask, qkv, grad)


def strip_at(ref, row_phase, column_phase, row):
    start = pl.multiple_of((row + 1) * STRIP, STRIP)
    return ref[2 * row_phase + column_phase, pl.ds(start, STRIP), :]


def near_strips(ref, row):
    tokens = lax.broadcasted_iota(jnp.int32, (STRIP, ref.shape[-1]), 0)
    loaded = {}
    for row_phase, at in ((1, row - 1), (0, row), (1, row), (0, row + 1)):
        even = strip_at(ref, row_phase, 0, at)
        odd = strip_at(ref, row_phase, 1, at)
        before = jnp.where(tokens == 0, 0.0, pltpu.roll(odd, 1, 0))
        after = jnp.where(tokens == STRIP - 1, 0.0, pltpu.roll(even, STRIP - 1, 0))
        loaded[len(loaded)] = ((before, even, odd), (even, odd, after))
    return {0: (loaded[0], loaded[1], loaded[2]), 1: (loaded[1], loaded[2], loaded[3])}


def conv_strip(near, kernel, row_phase, column_phase):
    total = None
    for i in range(3):
        for j in range(3):
            term = near[row_phase][i][column_phase][j] * kernel[3 * i + j : 3 * i + j + 1, :]
            total = term if total is None else total + term
    return total


def feed_body(
    spread,
    words_ref,
    norm_ref,
    norm_t_ref,
    grad_ref,
    *refs,
):
    pieces = 2 if spread else 1
    up_refs, refs = refs[:pieces], refs[pieces:]
    down_refs, refs = refs[:pieces], refs[pieces:]
    kernel_ref, staying_ref, leaving_ref, *refs = refs
    up_grad_refs, refs = refs[:pieces], refs[pieces:]
    down_grad_refs, refs = refs[:pieces], refs[pieces:]
    kernel_grad_ref, branch_acc, back_acc, hidden, widened_grad, act_grad, act, hidden_grad = refs[
        :8
    ]
    step = pl.program_id(0)
    core = words_ref[0]
    by_columns = (((1,), (1,)), ((), ()))
    width = kernel_ref.shape[1]
    model = norm_t_ref.shape[0]
    up_ref, down_ref = up_refs[0], down_refs[0]
    if spread:
        up_ref, down_all = refs[8:]
        half, share, _ = up_refs[0].shape
        piece = down_refs[0].shape[1]
        chips = 2 * half
        down_ref = down_all.at[pl.ds(pl.multiple_of(step * width, width), width), :]

        for which in range(2):

            @pl.loop(0, half)
            def _(spot):
                start = pl.multiple_of(words_ref[1 + which * half + spot] * share, share)
                up_ref[pl.ds(start, share), :] = up_refs[which][spot]

            @pl.when(step == 0)
            def _():
                @pl.loop(0, half)
                def _(spot):
                    owner = words_ref[1 + chips + which * half + spot]
                    start = pl.multiple_of(owner * piece, piece)
                    down_all[pl.ds(start, piece), :] = down_refs[which][spot]

    @pl.when(step == 0)
    def _():
        blank = jnp.zeros((STRIP, width), full)
        for plane in range(4):
            for ref in (hidden, widened_grad):
                ref[plane, pl.ds(0, STRIP), :] = blank
                ref[plane, pl.ds(PLANE + STRIP, STRIP), :] = blank
        branch_acc[...] = jnp.zeros_like(branch_acc)
        back_acc[...] = jnp.zeros_like(back_acc)

    @pl.loop(0, 4)
    def _(plane):
        rows = pl.ds(pl.multiple_of(plane * PLANE, PLANE), PLANE)
        hidden[plane, pl.ds(STRIP, PLANE), :] = jnp.dot(
            norm_ref[rows, :], up_ref[...], preferred_element_type=full
        )
        act_grad[rows, :] = lax.dot_general(
            grad_ref[rows, :], down_ref[...], by_columns, preferred_element_type=full
        )

    kernel = kernel_ref[...]

    def forward_strip(row, sums):
        near = near_strips(hidden, row)
        sums = list(sums)
        for row_phase in range(2):
            for column_phase in range(2):
                plane = 2 * row_phase + column_phase
                wide = conv_strip(near, kernel, row_phase, column_phase)
                square = wide * wide
                bend = math.sqrt(2.0 / math.pi) * (wide + 0.044715 * wide * square)
                curve = jnp.tanh(bend)
                half = 0.5 * (1.0 + curve)
                slope = half + 0.5 * wide * (1.0 - curve * curve) * (
                    math.sqrt(2.0 / math.pi) * (1.0 + 3 * 0.044715 * square)
                )
                at = pl.ds(pl.multiple_of(plane * PLANE + row * STRIP, STRIP), STRIP)
                act[at, :] = (wide * half).astype(low)
                grad_here = slope * act_grad[at, :]
                widened_grad[plane, pl.ds(pl.multiple_of((row + 1) * STRIP, STRIP), STRIP), :] = (
                    grad_here
                )
                for i in range(3):
                    for j in range(3):
                        product = near[row_phase][i][column_phase][j] * grad_here
                        sums[3 * i + j] = sums[3 * i + j] + (product[:8] + product[8:])
        return tuple(sums)

    sums = lax.fori_loop(
        0, HALF_SIDE, forward_strip, tuple(jnp.zeros((8, width), full) for _ in range(9))
    )
    kernel_grad_ref[...] = jnp.concatenate(
        [jnp.sum(s, axis=0, keepdims=True) for s in sums] + [jnp.zeros((7, width), full)], axis=0
    )

    flipped = [kernel[8 - t : 9 - t, :] for t in range(9)]
    flipped = jnp.concatenate(flipped, axis=0)

    @pl.loop(0, HALF_SIDE)
    def _(row):
        near = near_strips(widened_grad, row)
        for row_phase in range(2):
            for column_phase in range(2):
                plane = 2 * row_phase + column_phase
                at = pl.ds(pl.multiple_of(plane * PLANE + row * STRIP, STRIP), STRIP)
                hidden_grad[at, :] = conv_strip(near, flipped, row_phase, column_phase).astype(low)

    @pl.loop(0, 4)
    def _(plane):
        rows = pl.ds(pl.multiple_of(plane * PLANE, PLANE), PLANE)
        branch_acc[rows, :] += jnp.dot(act[rows, :], down_ref[...], preferred_element_type=full)
        back_acc[rows, :] += lax.dot_general(
            hidden_grad[rows, :], up_ref[...], by_columns, preferred_element_type=full
        )

    if spread:
        for which in range(2):

            @pl.loop(0, half // 4)
            def _(group):
                lhs = []
                for k in range(4):
                    owner = words_ref[1 + which * half + 4 * group + k]
                    start = pl.multiple_of(owner * share, share)
                    lhs.append(norm_t_ref[pl.ds(start, share), :])
                result = jnp.dot(
                    jnp.concatenate(lhs, axis=0), hidden_grad[...], preferred_element_type=full
                ).astype(low)
                for k in range(4):
                    up_grad_refs[which][4 * group + k] = result[k * share : (k + 1) * share]

    else:

        @pl.loop(0, model // TILE)
        def _(tile):
            rows = pl.ds(pl.multiple_of(tile * TILE, TILE), TILE)
            up_grad_refs[0][rows, :] = jnp.dot(
                norm_t_ref[rows, :], hidden_grad[...], preferred_element_type=full
            ).astype(low)

    down_grad = lax.dot_general(
        act[...], grad_ref[...], (((0,), (0,)), ((), ())), preferred_element_type=full
    ).astype(low)
    if spread:
        for k in range(width // piece):
            place = words_ref[1 + 2 * chips + step * (width // piece) + k]
            for which in range(2):

                @pl.when(place // half == which)
                def _():
                    down_grad_refs[which][place - which * half] = down_grad[
                        k * piece : (k + 1) * piece
                    ]

    else:
        down_grad_refs[0][...] = down_grad

    @pl.when(step == pl.num_programs(0) - 1)
    def _():
        for ref, which in ((staying_ref, core), (leaving_ref, 1 - core)):
            for index, acc in enumerate((branch_acc, back_acc)):
                for plane in range(4):
                    start = plane * PLANE + pl.multiple_of(which * (PLANE // 2), PLANE // 2)
                    ref[index, plane] = acc[pl.ds(start, PLANE // 2), :].astype(low)


def feed_forward(norm, norm_t, grad, up, down, kernel, words):
    tokens, model = norm.shape
    channels = kernel.shape[1]
    width = TILE
    spread = len(up) == 2
    whole = lambda j, words: (0, 0)
    half = lambda j, words: (0, 0, 0, 0)
    across = lambda j, words: (0, j)
    once = pl.Buffered(1)
    piece_scratch = []
    if spread:
        deep = lambda j, words: (0, 0, 0)
        up_spec = pl.BlockSpec(up[0].shape[:2] + (width,), lambda j, words: (0, 0, j))
        down_spec = pl.BlockSpec(down[0].shape, deep, pipeline_mode=once)
        down_grad_spec = pl.BlockSpec(down[0].shape, deep)
        piece_scratch = [pltpu.VMEM((model, width), low), pltpu.VMEM((channels, model), low)]
    else:
        up_spec = pl.BlockSpec((model, width), across)
        down_spec = down_grad_spec = pl.BlockSpec((width, model), lambda j, words: (j, 0))
    halves = jax.ShapeDtypeStruct((2, 4, PLANE // 2, model), low)
    like = lambda arrays: [jax.ShapeDtypeStruct(array.shape, low) for array in arrays]
    out = pl.pallas_call(
        functools.partial(feed_body, spread),
        grid_spec=pltpu.PrefetchScalarGridSpec(
            num_scalar_prefetch=1,
            grid=(channels // width,),
            in_specs=[
                pl.BlockSpec((tokens, model), whole, pipeline_mode=once),
                pl.BlockSpec((model, tokens), whole, pipeline_mode=once),
                pl.BlockSpec((tokens, model), whole, pipeline_mode=once),
                *[up_spec] * len(up),
                *[down_spec] * len(down),
                pl.BlockSpec((16, width), across),
            ],
            out_specs=[
                pl.BlockSpec(halves.shape, half),
                pl.BlockSpec(halves.shape, half),
                *[up_spec] * len(up),
                *[down_grad_spec] * len(down),
                pl.BlockSpec((16, width), across),
            ],
            scratch_shapes=[
                pltpu.VMEM((tokens, model), full),
                pltpu.VMEM((tokens, model), full),
                pltpu.VMEM((4, PADDED, width), full),
                pltpu.VMEM((4, PADDED, width), full),
                pltpu.VMEM((tokens, width), full),
                pltpu.VMEM((tokens, width), low),
                pltpu.VMEM((tokens, width), low),
            ]
            + piece_scratch,
        ),
        out_shape=[halves, halves]
        + like(up)
        + like(down)
        + [jax.ShapeDtypeStruct((16, channels), full)],
        compiler_params=pltpu.CompilerParams(vmem_limit_bytes=63 * 1024 * 1024),
        cost_estimate=pl.CostEstimate(
            flops=12 * tokens * model * channels,
            bytes_accessed=8 * model * channels + 10 * tokens * model,
            transcendentals=tokens * channels,
        ),
        name="feed_forward",
    )(words, norm, norm_t, grad, *up, *down, kernel)
    staying, leaving, *grads, kernel_grad = out
    return staying, leaving, grads[: len(up)], grads[len(up) :], kernel_grad


def token_stats(x_ref, average, scale):
    @pl.loop(0, x_ref.shape[0] // STRIP)
    def _(strip):
        rows = pl.ds(pl.multiple_of(strip * STRIP, STRIP), STRIP)
        values = x_ref[rows, :].astype(full)
        mean = jnp.mean(values, axis=-1, keepdims=True)
        centred = values - mean
        variance = jnp.mean(centred * centred, axis=-1, keepdims=True)
        average[rows, :] = jnp.broadcast_to(mean, (STRIP, 128))
        scale[rows, :] = jnp.broadcast_to(lax.rsqrt(variance + ln_epsilon), (STRIP, 128))


def normed_strip(x_ref, average, scale, rows, columns):
    width = columns.size
    wide = lambda ref: jnp.concatenate([ref[rows, :]] * (width // 128), axis=1)
    return (x_ref[rows, columns].astype(full) - wide(average)) * wide(scale)


def frame_zeros(refs):
    for ref in refs:
        blank = jnp.zeros((STRIP, ref.shape[-1]), full)
        for plane in range(4):
            ref[plane, pl.ds(0, STRIP), :] = blank
            ref[plane, pl.ds(ref.shape[1] - STRIP, STRIP), :] = blank


def conv_in_body(x_ref, kernel_ref, mods_ref, out_ref, average, scale, normed):
    step = pl.program_id(0)
    width = out_ref.shape[1]
    columns = pl.ds(pl.multiple_of(step * width, width), width)

    @pl.when(step == 0)
    def _():
        token_stats(x_ref, average, scale)
        frame_zeros([normed])

    shift_by = mods_ref[0:1, :]
    scale_by = 1.0 + mods_ref[1:2, :]

    @pl.loop(0, HALF_SIDE)
    def _(row):
        for plane in range(4):
            rows = pl.ds(pl.multiple_of(plane * PLANE + row * STRIP, STRIP), STRIP)
            normed[plane, pl.ds(pl.multiple_of((row + 1) * STRIP, STRIP), STRIP), :] = (
                normed_strip(x_ref, average, scale, rows, columns) * scale_by + shift_by
            )

    kernel = kernel_ref[...]

    @pl.loop(0, HALF_SIDE)
    def _(row):
        near = near_strips(normed, row)
        for row_phase in range(2):
            for column_phase in range(2):
                plane = 2 * row_phase + column_phase
                at = pl.ds(pl.multiple_of(plane * PLANE + row * STRIP, STRIP), STRIP)
                out_ref[at, :] = conv_strip(near, kernel, row_phase, column_phase).astype(low)


def conv_in(canvas, kernel, mods):
    tokens, model = canvas.shape
    return pl.pallas_call(
        conv_in_body,
        grid=(model // TILE,),
        in_specs=[
            pl.BlockSpec((tokens, model), lambda j: (0, 0), pipeline_mode=pl.Buffered(1)),
            pl.BlockSpec((16, TILE), lambda j: (0, j)),
            pl.BlockSpec((8, TILE), lambda j: (0, j)),
        ],
        out_specs=pl.BlockSpec((tokens, TILE), lambda j: (0, j)),
        out_shape=jax.ShapeDtypeStruct((tokens, model), low),
        scratch_shapes=[
            pltpu.VMEM((tokens, 128), full),
            pltpu.VMEM((tokens, 128), full),
            pltpu.VMEM((4, PADDED, TILE), full),
        ],
        cost_estimate=pl.CostEstimate(
            flops=30 * tokens * model, bytes_accessed=4 * tokens * model, transcendentals=tokens
        ),
        name="conv_in",
    )(canvas, kernel, mods)


def conv_back_body(
    core_ref,
    x_ref,
    kept_ref,
    arriving_ref,
    kernel_ref,
    mods_ref,
    middle_ref,
    out_ref,
    kernel_grad_ref,
    mods_grad_ref,
    average,
    scale,
    normed,
    upstream,
    held,
    sum_plain,
    sum_normed,
    woven,
):
    step = pl.program_id(0)
    core = core_ref[0]
    width = kept_ref.shape[1]
    near_rows = x_ref.shape[0] // 4 // STRIP
    own_rows = near_rows - 1
    columns = pl.ds(pl.multiple_of(step * width, width), width)

    def near_at(plane, row):
        return pl.ds(pl.multiple_of((plane * near_rows + row) * STRIP, STRIP), STRIP)

    def own_at(plane, row):
        return pl.ds(pl.multiple_of((plane * own_rows + row) * STRIP, STRIP), STRIP)

    @pl.when(step == 0)
    def _():
        token_stats(x_ref, average, scale)
        frame_zeros([normed, upstream])
        sum_plain[...] = jnp.zeros_like(sum_plain)
        sum_normed[...] = jnp.zeros_like(sum_normed)

    shift_by = mods_ref[0:1, :]
    scale_by = 1.0 + mods_ref[1:2, :]

    @pl.loop(0, near_rows)
    def _(row):
        for plane in range(4):
            rows = near_at(plane, row)
            padded = pl.ds(pl.multiple_of((row + 1) * STRIP, STRIP), STRIP)
            normed[plane, padded, :] = (
                normed_strip(x_ref, average, scale, rows, columns) * scale_by + shift_by
            )
            upstream[plane, padded, :] = kept_ref[rows, :].astype(full) + arriving_ref[
                rows, :
            ].astype(full)

    kernel = kernel_ref[...]
    flipped = jnp.concatenate([kernel[8 - t : 9 - t, :] for t in range(9)], axis=0)

    def kernel_strip(row, sums):
        near = near_strips(normed, row + core)
        sums = list(sums)
        for row_phase in range(2):
            for column_phase in range(2):
                grad_here = strip_at(upstream, row_phase, column_phase, row + core)
                for i in range(3):
                    for j in range(3):
                        product = near[row_phase][i][column_phase][j] * grad_here
                        sums[3 * i + j] = sums[3 * i + j] + (product[:8] + product[8:])
        return tuple(sums)

    def fold(sums, rows):
        return jnp.concatenate(
            [jnp.sum(s, axis=0, keepdims=True) for s in sums]
            + [jnp.zeros((rows - len(sums), width), full)],
            axis=0,
        )

    blank = jnp.zeros((8, width), full)
    kernel_grad_ref[...] = fold(lax.fori_loop(0, own_rows, kernel_strip, (blank,) * 9), 16)

    def input_strip(row, sums):
        near = near_strips(upstream, row + core)
        shift_sum, scale_sum = sums
        for row_phase in range(2):
            for column_phase in range(2):
                plane = 2 * row_phase + column_phase
                grad = conv_strip(near, flipped, row_phase, column_phase)
                plain = normed_strip(x_ref, average, scale, near_at(plane, row + core), columns)
                shift_sum = shift_sum + (grad[:8] + grad[8:])
                product = grad * plain
                scale_sum = scale_sum + (product[:8] + product[8:])
                scaled = grad * scale_by
                rows = own_at(plane, row)
                held[step, rows, :] = scaled
                product = scaled * plain
                sum_plain[rows, :] += sum(scaled[:, k : k + 128] for k in range(0, width, 128))
                sum_normed[rows, :] += sum(product[:, k : k + 128] for k in range(0, width, 128))
        return shift_sum, scale_sum

    mods_grad_ref[...] = fold(lax.fori_loop(0, own_rows, input_strip, (blank,) * 2), 8)

    @pl.when(step == pl.num_programs(0) - 1)
    def _():
        model = x_ref.shape[1]

        @pl.loop(0, own_rows)
        def _(row):
            for plane in range(4):
                rows = own_at(plane, row)
                near = near_at(plane, row + core)
                mean_plain = jnp.sum(sum_plain[rows, :], axis=-1, keepdims=True) / model
                mean_normed = jnp.sum(sum_normed[rows, :], axis=-1, keepdims=True) / model
                for block in range(model // width):
                    at = pl.ds(block * width, width)
                    plain = normed_strip(x_ref, average, scale, near, at)
                    spread = jnp.concatenate([scale[near, :]] * (width // 128), axis=1)
                    result = middle_ref[rows, at] + spread * (
                        held[block, rows, :] - mean_plain - plain * mean_normed
                    )
                    for lane in range(0, width, 128):
                        woven[(block * width + lane) // 128, pl.ds(plane % 2, STRIP, stride=2), :] = (
                            result[:, lane : lane + 128]
                        )
                if plane % 2 == 1:
                    start = pl.multiple_of((2 * row + plane // 2) * SIDE, SIDE)
                    for lane in range(model // 128):
                        out_ref[pl.ds(start, SIDE), lane * 128 : lane * 128 + 128] = woven[lane]


def conv_back(core, x_near, kept, arriving, kernel, mods, grad_middle):
    near_tokens, model = x_near.shape
    own_tokens = grad_middle.shape[0]
    once = pl.Buffered(1)
    whole = lambda j, words: (0, 0)
    across = lambda j, words: (0, j)
    padded = near_tokens // 4 + 2 * STRIP
    return pl.pallas_call(
        conv_back_body,
        grid_spec=pltpu.PrefetchScalarGridSpec(
            num_scalar_prefetch=1,
            grid=(model // TILE,),
            in_specs=[
                pl.BlockSpec((near_tokens, model), whole, pipeline_mode=once),
                pl.BlockSpec((near_tokens, TILE), across),
                pl.BlockSpec((near_tokens, TILE), across),
                pl.BlockSpec((16, TILE), across),
                pl.BlockSpec((8, TILE), across),
                pl.BlockSpec((own_tokens, model), whole, pipeline_mode=once),
            ],
            out_specs=[
                pl.BlockSpec((own_tokens, model), whole),
                pl.BlockSpec((16, TILE), across),
                pl.BlockSpec((8, TILE), across),
            ],
            scratch_shapes=[
                pltpu.VMEM((near_tokens, 128), full),
                pltpu.VMEM((near_tokens, 128), full),
                pltpu.VMEM((4, padded, TILE), full),
                pltpu.VMEM((4, padded, TILE), full),
                pltpu.VMEM((model // TILE, own_tokens, TILE), full),
                pltpu.VMEM((own_tokens, 128), full),
                pltpu.VMEM((own_tokens, 128), full),
                pltpu.VMEM((model // 128, SIDE, 128), full),
            ],
        ),
        out_shape=[
            jax.ShapeDtypeStruct((own_tokens, model), full),
            jax.ShapeDtypeStruct((16, model), full),
            jax.ShapeDtypeStruct((8, model), full),
        ],
        cost_estimate=pl.CostEstimate(
            flops=70 * own_tokens * model,
            bytes_accessed=14 * own_tokens * model,
            transcendentals=near_tokens,
        ),
        name="conv_back",
    )(core[None].astype(jnp.int32), x_near, kept, arriving, kernel, mods, grad_middle)


def row_stats(values):
    mean = jnp.mean(values, axis=-1, keepdims=True)
    centred = values - mean
    scale = lax.rsqrt(jnp.mean(centred * centred, axis=-1, keepdims=True) + ln_epsilon)
    return centred * scale, scale


def enter_feed_body(x_ref, part_ref, other_ref, grad_ref, mods_ref, norm_ref, norm_t_ref, out_ref):
    @pl.loop(0, x_ref.shape[0] // STRIP)
    def _(strip):
        rows = pl.ds(pl.multiple_of(strip * STRIP, STRIP), STRIP)
        branch = part_ref[rows, :].astype(full) + other_ref[rows, :].astype(full)
        plain, _ = row_stats(x_ref[rows, :].astype(full) + mods_ref[0:1, :] * branch)
        normed = plain * (1.0 + mods_ref[2:3, :]) + mods_ref[1:2, :]
        norm_ref[rows, :] = normed.astype(low)
        out_ref[rows, :] = (grad_ref[rows, :].astype(full) * mods_ref[3:4, :]).astype(low)

    norm_t_ref[...] = norm_ref[...].T


def enter_feed(canvas, part, other, grad, mods):
    tokens, model = canvas.shape
    rows = PLANE // 2
    along = pl.BlockSpec((rows, model), lambda j: (j, 0))
    return pl.pallas_call(
        enter_feed_body,
        grid=(tokens // rows,),
        in_specs=[along] * 4 + [pl.BlockSpec((8, model), lambda j: (0, 0))],
        out_specs=[along, pl.BlockSpec((model, rows), lambda j: (0, j)), along],
        out_shape=[
            jax.ShapeDtypeStruct((tokens, model), low),
            jax.ShapeDtypeStruct((model, tokens), low),
            jax.ShapeDtypeStruct((tokens, model), low),
        ],
        cost_estimate=pl.CostEstimate(flops=1000, bytes_accessed=1000, transcendentals=0),
        name="enter_feed",
    )(canvas, part, other, grad, mods)


def leave_feed_body(words_ref, x_ref, part_ref, other_ref, grad_ref, mods_ref, *refs):
    *kept_refs, out_ref, middle_grad_ref, branch_grad_ref, sums_ref, totals = refs
    plane = pl.program_id(0)

    @pl.when(plane == 0)
    def _():
        totals[...] = jnp.zeros_like(totals)

    @pl.loop(0, x_ref.shape[0] // STRIP)
    def _(strip):
        rows = pl.ds(pl.multiple_of(strip * STRIP, STRIP), STRIP)
        gate_a, gate_f = mods_ref[0:1, :], mods_ref[3:4, :]
        branch_a = part_ref[rows, :].astype(full) + other_ref[rows, :].astype(full)
        middle = x_ref[rows, :].astype(full) + gate_a * branch_a
        plain, scale = row_stats(middle)
        branch_f = sum(ref[0, 0, rows, :].astype(full) for ref in kept_refs)
        back = sum(ref[1, 0, rows, :].astype(full) for ref in kept_refs)
        grad = grad_ref[rows, :].astype(full)
        out_ref[rows, :] = (middle + gate_f * branch_f).astype(low)
        scaled = back * (1.0 + mods_ref[2:3, :])
        mean_plain = jnp.mean(scaled, axis=-1, keepdims=True)
        mean_normed = jnp.mean(scaled * plain, axis=-1, keepdims=True)
        grad_middle = grad + scale * (scaled - mean_plain - plain * mean_normed)
        middle_grad_ref[rows, :] = grad_middle
        branch_grad_ref[rows, :] = (grad_middle * gate_a).astype(low)
        products = (grad_middle * branch_a, back, back * plain, grad * branch_f)
        for index, product in enumerate(products):
            totals[index] += product[:8] + product[8:]

    @pl.when(plane == pl.num_programs(0) - 1)
    def _():
        lines = [jnp.sum(totals[k], axis=0, keepdims=True) for k in range(4)]
        sums_ref[...] = jnp.concatenate(lines + [jnp.zeros_like(sums_ref[:4])], axis=0)


def leave_feed(words, canvas, part, other, grad, mods, kept):
    model = canvas.shape[1]
    rows = PLANE // 2
    own = pl.BlockSpec((rows, model), lambda j, words: (2 * j + words[0], 0))
    half = pl.BlockSpec((rows, model), lambda j, words: (j, 0))
    whole = pl.BlockSpec((8, model), lambda j, words: (0, 0))
    return pl.pallas_call(
        leave_feed_body,
        grid_spec=pltpu.PrefetchScalarGridSpec(
            num_scalar_prefetch=1,
            grid=(4,),
            in_specs=[own] * 4
            + [whole]
            + [pl.BlockSpec((2, 1, rows, model), lambda j, words: (0, j, 0, 0))] * len(kept),
            out_specs=[half, half, half, whole],
            scratch_shapes=[pltpu.VMEM((4, 8, model), full)],
        ),
        out_shape=[
            jax.ShapeDtypeStruct((4 * rows, model), low),
            jax.ShapeDtypeStruct((4 * rows, model), full),
            jax.ShapeDtypeStruct((4 * rows, model), low),
            jax.ShapeDtypeStruct((8, model), full),
        ],
        cost_estimate=pl.CostEstimate(flops=1000, bytes_accessed=1000, transcendentals=0),
        name="leave_feed",
    )(words, canvas, part, other, grad, mods, *kept)


def on_device(
    tokens,
    seg_ids,
    timesteps,
    labels,
    cotangent,
    mod_weight,
    class_table,
    attn_kernel,
    qkv_weight,
    proj_weight,
    up_weight,
    ffn_kernel,
    down_weight,
):
    devices = device_count()
    chips = devices // 2
    chip_bits = chips.bit_length() - 1
    rank = lax.axis_index("dp") * lax.axis_size("fsdp") + lax.axis_index("fsdp")
    core = rank % 2
    chip = rank // 2
    _, half_tokens, model = tokens.shape
    half_rows = half_tokens // SIDE
    class_count = class_table.shape[0]
    part = model // devices
    share = down_weight.shape[0]
    piece = share // CHUNKS
    pairs = model // HEAD // 4

    def halves_of(array, axis):
        return at_bit(array, axis, core), at_bit(array, axis, 1 - core)

    def row_pair(array, axis):
        kept, leaving = halves_of(array, axis)
        arriving = swap_core(leaving)
        return jnp.concatenate(in_core_order(kept, arriving, core), axis=0)

    qkv_split = qkv_weight.reshape(part, 3, 2, pairs, 128).transpose(0, 2, 3, 1, 4)
    qkv_rows = row_pair(qkv_split.reshape(part, 2, pairs * 384), 1)
    qkv_half = pairs * 384 // 2

    picks = labels[:, None] == jnp.arange(class_count)[None, :]
    angles_here = lax.dynamic_slice_in_dim(sinusoid(timesteps, model), rank * part, part, axis=1)
    cond = angles_here + jnp.dot(picks.astype(low), class_table, preferred_element_type=full)
    lift_value, lift_pull = jax.vjp(jax.nn.silu, cond)
    lifted = lift_value.astype(low)
    mods_part = jnp.dot(lifted, mod_weight, preferred_element_type=full)

    slot = Slots(jnp.zeros((8, 128), full))
    flow = lambda shard, colour: gather_flow(shard, colour, chip_bits)
    sums = lambda parts, colour: scatter_flow(parts, colour, chip, chip_bits)
    joined = lambda flows: [
        gathered(f, colour, chip, chip_bits) for colour, f in enumerate(flows)
    ]
    mods_flow = scatter_flow(mods_part, 0, chip, chip_bits, sent=full)
    qkv_flows = [flow(qkv_rows[:, :qkv_half], 0), flow(qkv_rows[:, qkv_half:], 1)]
    mine, upstream = slot(
        qkv_flows + [mods_flow],
        lambda: (to_phases(tokens[0], half_rows), to_phases(cotangent[0], half_rows)),
    )

    up_weight, proj_weight, ffn_kernel, attn_kernel = slot.after(
        up_weight, proj_weight, ffn_kernel, attn_kernel
    )
    up_split = up_weight.reshape(part, chips, 2, CHUNKS, piece).transpose(0, 2, 3, 1, 4)
    up_rows = row_pair(up_split.reshape(part, 2, CHUNKS, chips * piece), 1)
    proj_there = [(r, r % chips * 2 + r // chips) for r in range(devices)]
    proj_back = [(b, a) for a, b in proj_there]
    proj_rows = lax.ppermute(proj_weight, AXES, proj_there)
    canvas = join_halves(mine, swap_core(mine), core)

    slot(qkv_flows + [mods_flow])
    mods_half = run(mods_flow)
    mods = mods_half + swap_core(mods_half)
    shift_a, scale_a, gate_a, shift_f, scale_f, gate_f = jnp.split(mods, 6)

    tap_count = 9 * (share + part)
    tap_words = jnp.concatenate([ffn_kernel.reshape(-1), attn_kernel.reshape(-1)])
    tap_words = jnp.pad(tap_words, (0, -tap_count % 128))
    taps = run(row_flow(tap_words, rank, chip_bits + 1, 0))
    ffn_taps = taps[:, : 9 * share].reshape(chips, 2, 9, share)
    ffn_taps = at_bit(ffn_taps, 1, core).reshape(chips, 9, CHUNKS, piece)
    ffn_taps = ffn_taps.transpose(2, 1, 0, 3).reshape(CHUNKS, 9, chips * piece).astype(full)
    ffn_taps = jnp.pad(ffn_taps, ((0, 0), (0, 7), (0, 0)))
    attn_taps = taps[:, 9 * share : tap_count].reshape(devices, 9, part)
    attn_taps = attn_taps.transpose(1, 0, 2).reshape(9, model).astype(full)
    attn_taps = jnp.pad(attn_taps, ((0, 7), (0, 0)))

    spot = jnp.arange(PLANE)
    quadrant = 2 * (spot // (PLANE // 2)) + spot % HALF_SIDE // (HALF_SIDE // 2)
    quadrants_here = at_bit(seg_ids, 0, chip)
    segment = jnp.sum(
        jnp.where(quadrant[:, None] == jnp.arange(4)[None, :], quadrants_here[None, :], 0), axis=1
    )
    mask = (segment[:, None] == segment[None, :]).astype(full)

    proj_flows = [flow(proj_rows[:, : model // 2], 0), flow(proj_rows[:, model // 2 :], 1)]
    feed_flows = [
        [flow(up_rows[:, t], 0), flow(down_weight[t * piece : (t + 1) * piece], 1)]
        for t in range(CHUNKS)
    ]
    mods_a = jnp.concatenate([shift_a[None], scale_a[None], jnp.zeros((6, model), full)], axis=0)

    slot(qkv_flows + proj_flows + feed_flows[0])
    convolved = slot(
        qkv_flows + proj_flows + feed_flows[0] + feed_flows[1], lambda: conv_in(canvas, attn_taps, mods_a)
    )

    (upstream,) = slot.after(upstream)
    grad_ph = join_halves(upstream, swap_core(upstream), core)

    def project_in():
        weight = jnp.concatenate(
            [array.reshape(model, qkv_half) for array in joined(qkv_flows)], axis=1
        )
        return weight, jnp.dot(convolved, weight, preferred_element_type=full).astype(low)

    slot.finish(qkv_flows)
    qkv_full, qkv = slot(proj_flows + feed_flows[0] + feed_flows[1], project_in)
    attended = slot(
        proj_flows + feed_flows[1] + feed_flows[2], lambda: attend(mask, qkv)
    )

    mods_f = jnp.concatenate(
        [gate_a[None], shift_f[None], scale_f[None], gate_f[None], jnp.zeros((4, model), full)]
    )

    def project_out():
        weight = jnp.concatenate(
            [array.reshape(-1, model // 2) for array in joined(proj_flows)], axis=1
        )
        branch_part = jnp.dot(attended, weight, preferred_element_type=full).astype(low)
        other = swap_core(branch_part)
        return weight, branch_part, other, *enter_feed(canvas, branch_part, other, grad_ph, mods_f)

    slot.finish(proj_flows)
    proj_full, branch_part, branch_other, norm, norm_t, grad_branch_f = slot(
        feed_flows[0] + feed_flows[2], project_out
    )

    kept = []
    grads = [None] * CHUNKS

    spread = 2 * part % STRIP == 0 and piece % STRIP == 0 and chips >= 8
    up_owner, _ = owners(0, chip, chip_bits)
    down_owner, down_place = owners(1, chip, chip_bits)
    words = jnp.concatenate([core[None], up_owner, down_owner, down_place]).astype(jnp.int32)

    def feed(t):
        def work():
            if spread:
                up, down = [f.result for f in feed_flows[t]]
            else:
                up, down = joined(feed_flows[t])
                up, down = [up.reshape(model, -1)], [down.reshape(-1, model)]
            return feed_forward(norm, norm_t, grad_branch_f, up, down, ffn_taps[t], words)

        return work

    back_flows = [[] for _ in range(CHUNKS)]

    def run_feed(flows, t):
        slot.finish(feed_flows[t])
        staying, leaving, up_grad, down_grad, tap_grad = slot(flows, feed(t))
        kept.append((staying, leaving))
        grads[t] = tap_grad
        if spread:
            back_flows[t] = [
                Flow(halving_steps(*grad[::-1], gather_order(chip_bits, colour)[::-1]))
                for colour, grad in enumerate((up_grad, down_grad))
            ]
        else:
            back_flows[t] = [
                sums(up_grad[0].reshape(chips, 2 * part, -1), 0),
                sums(down_grad[0].reshape(chips, piece, model), 1),
            ]

    run_feed(feed_flows[1] + feed_flows[2], 0)
    run_feed(feed_flows[2] + back_flows[0], 1)
    run_feed(back_flows[0] + back_flows[1], 2)

    def after_feed():
        parts = [array for staying, leaving in kept for array in (staying, swap_core(leaving))]
        return leave_feed(words[:1], canvas, branch_part, branch_other, grad_ph, mods_f, parts)

    layer_out, grad_middle, grad_branch_mine, feed_sums = slot(
        back_flows[0] + back_flows[2], after_feed
    )
    grad_branch_mine = grad_branch_mine.reshape(4, -1, model)
    layer_out = from_phases(layer_out.reshape(4, -1, model), half_rows)[None]

    def enter_attend():
        grad_branch_a = join_halves(grad_branch_mine, swap_core(grad_branch_mine), core)
        grad_attended = jnp.dot(grad_branch_a, proj_full.T, preferred_element_type=full)
        proj_grad = jnp.dot(attended.T, grad_branch_a, preferred_element_type=full)
        return grad_attended.astype(low), proj_grad.astype(low)

    grad_attended, proj_grad = slot(back_flows[0] + back_flows[1], enter_attend)
    proj_grad = proj_grad.reshape(chips, -1, model)
    proj_flows = [sums(proj_grad[..., : model // 2], 0), sums(proj_grad[..., model // 2 :], 1)]
    grad_qkv = slot(
        proj_flows + sum(back_flows, []), lambda: attend_back(mask, qkv, grad_attended)
    )
    qkv_grad = slot(
        proj_flows + sum(back_flows, []),
        lambda: jnp.dot(convolved.T, grad_qkv, preferred_element_type=full).astype(low),
    )
    qkv_grad = qkv_grad.reshape(chips, 2 * part, -1)
    qkv_flows = [sums(qkv_grad[..., :qkv_half], 0), sums(qkv_grad[..., qkv_half:], 1)]

    def rows_near(array, which):
        size = PLANE // 2 + STRIP
        near = lax.dynamic_slice_in_dim(
            array.reshape(4, PLANE, model), which * (PLANE - size), size, axis=1
        )
        return near.reshape(4 * size, model)

    def leave_attend():
        part_here = jnp.dot(grad_qkv, qkv_full.T, preferred_element_type=full).astype(low)
        return rows_near(part_here, core), swap_core(rows_near(part_here, 1 - core))

    grad_conv = slot(qkv_flows + proj_flows + back_flows[2], leave_attend)

    def leave_block():
        input_grad, attn_tap_grad, mods_grad = conv_back(
            core, rows_near(canvas, core), *grad_conv, attn_taps, mods_a,
            grad_middle,
        )
        return attn_tap_grad[:9], input_grad, mods_grad[:2]

    attn_tap_grad, input_grad, attn_sums = slot(
        qkv_flows + proj_flows + back_flows[2], leave_block
    )
    def row_split(array, axis):
        pair = array.reshape((2, part) + array.shape[1:])
        kept, leaving = halves_of(pair, 0)
        arriving = swap_core(leaving)
        return jnp.stack(in_core_order(kept, arriving, core), axis=axis)

    slot.finish(sum(back_flows, []))
    grad_mods = jnp.concatenate([attn_sums, feed_sums[:4]], axis=0)
    tap_grads = [g[:9].reshape(9, chips, piece) for g in grads]
    ffn_tap_grad = jnp.concatenate(tap_grads, axis=2).transpose(1, 0, 2)
    attn_kept, attn_leaving = halves_of(attn_tap_grad.reshape(9, chips, 2, part), 2)

    def between_cores():
        both = (grad_mods + swap_core(grad_mods)).astype(low)
        return both, attn_kept + swap_core(attn_leaving)

    grad_mods, attn_tap_grad = slot(qkv_flows + proj_flows, between_cores)
    mods_flow = row_flow(grad_mods.reshape(-1), chip, chip_bits)
    tap_parts = jnp.concatenate(
        [ffn_tap_grad.reshape(chips, -1), attn_tap_grad.transpose(1, 0, 2).reshape(chips, -1)],
        axis=1,
    )
    tap_flow = scatter_flow(tap_parts, 0, chip, chip_bits, sent=full)
    up_shares = [flows[0].result for flows in back_flows]
    down_shares = [flows[1].result for flows in back_flows]

    def split_up():
        up_all = jnp.stack(up_shares, axis=1).reshape(2 * part, CHUNKS, chips, piece)
        return row_split(up_all.transpose(0, 2, 1, 3), 2).reshape(part, -1)

    slot.finish(proj_flows)
    proj_share = jnp.concatenate([f.result for f in proj_flows], axis=1)
    up_share = slot(qkv_flows + [mods_flow, tap_flow], split_up)
    slot.finish(qkv_flows)
    qkv_share = jnp.concatenate([f.result for f in qkv_flows], axis=1)

    def split_qkv():
        qkv_all = qkv_share.reshape(2 * part, pairs, 3, 128).transpose(0, 2, 1, 3)
        qkv_out = row_split(qkv_all, 2).reshape(part, -1)
        return qkv_out, lax.ppermute(proj_share, AXES, proj_back)

    qkv_out, proj_share = slot([mods_flow, tap_flow], split_qkv)
    slot.finish([mods_flow, tap_flow])
    down_share = jnp.concatenate(down_shares, axis=0)

    grad_mods_all = mods_flow.result
    mod_grad = jnp.dot(lifted.T, grad_mods_all, preferred_element_type=full)
    (cond_grad,) = lift_pull(jnp.dot(grad_mods_all, mod_weight.T, preferred_element_type=full))
    table_grad = jnp.dot(picks.astype(full).T, cond_grad, precision=highest)
    tap_share = tap_flow.result
    ffn_share = tap_share[: 9 * share].reshape(9, share)
    kernel_share = tap_share[9 * share :].reshape(9, part)

    return (
        layer_out,
        input_grad[None],
        mod_grad,
        table_grad,
        kernel_share,
        qkv_out,
        proj_share,
        up_share,
        ffn_share,
        down_share,
        feed_sums[1:2],
    )


def solution(mesh):
    return jax.shard_map(
        on_device,
        mesh=mesh,
        in_specs=(
            P(AXES, None, None),
            P(),
            P(),
            P(),
            P(AXES, None, None),
            P(AXES, None),
            P(None, AXES),
            P(None, AXES),
            P(AXES, None),
            P(AXES, None),
            P(AXES, None),
            P(None, AXES),
            P(AXES, None),
        ),
        out_specs=(
            P(AXES, None, None),
            P(AXES, None, None),
            P(AXES, None),
            P(None, AXES),
            P(None, AXES),
            P(AXES, None),
            P(AXES, None),
            P(AXES, None),
            P(None, AXES),
            P(AXES, None),
            P(AXES, None),
        ),
        check_vma=False,
    )
```

```python
import functools
import math

import jax
import jax.numpy as jnp
from jax import lax
from jax.experimental import pallas as pl
from jax.experimental.pallas import tpu as pltpu
from jax.sharding import PartitionSpec as P

HEAD = 64
SIDE = 32
HALF_SIDE = SIDE // 2
STRIP = HALF_SIDE
PLANE = HALF_SIDE * HALF_SIDE
PADDED = PLANE + 2 * STRIP
TILE = 256
CHUNKS = 3

highest = lax.Precision.HIGHEST
ln_epsilon = 1e-06
masked_score = -1000000000.0
low = jnp.bfloat16
full = jnp.float32
AXES = ("dp", "fsdp")


def device_count():
    return lax.axis_size("dp") * lax.axis_size("fsdp")


def swap(x, bit):
    return lax.ppermute(x, AXES, [(i, i ^ 1 << bit) for i in range(device_count())])


def swap_core(x):
    return swap(x, 0)


def gather_order(chip_bits, colour):
    order = list(range(chip_bits - 1, -1, -1))
    if colour and chip_bits > 1:
        order[-1], order[-2] = order[-2], order[-1]
    return order


class Flow:
    def __init__(self, steps):
        self.steps = steps
        self.wanted = next(steps)
        self.result = None

    def arrive(self, array):
        try:
            self.wanted = self.steps.send(array)
        except StopIteration as end:
            self.wanted, self.result = None, end.value


class Slots:
    def __init__(self, token):
        self.token = token

    def after(self, *arrays):
        arrays, self.token = lax.optimization_barrier((arrays, self.token))
        return arrays

    def finish(self, flows):
        while any(flow.wanted is not None for flow in flows):
            self(flows)

    def __call__(self, flows, work=lambda: ()):
        flows = [flow for flow in flows if flow.wanted is not None]
        wanted = [flow.wanted for flow in flows]
        leaving, self.token = lax.optimization_barrier(
            ([[array for array, _ in pairs] for pairs in wanted], self.token)
        )
        arriving = [
            [swap(array, bit + 1) for array, (_, bit) in zip(arrays, pairs)]
            for arrays, pairs in zip(leaving, wanted)
        ]
        arriving, result, self.token = lax.optimization_barrier((arriving, work(), self.token))
        for flow, arrays in zip(flows, arriving):
            flow.arrive(arrays)
        return result


def join(held, arriving):
    return [jnp.concatenate(pair, axis=0) for pair in zip(held, arriving)]


def near_steps(shards, chip_bits):
    held = [shard[None] for shard in shards]
    for bit in range(chip_bits - 1, 1, -1):
        arriving = yield [(array, bit) for array in held]
        held = join(held, arriving)
    return held


def far_steps(held):
    arriving = yield [(held[0], 1), (held[1], 0)]
    held = join(held, arriving)
    arriving = yield [(held[0], 0), (held[1], 1)]
    return list(zip(held, arriving))


def assemble_body(steps, chip_ref, *refs):
    *piece_refs, out_ref = refs
    which = pl.program_id(0) // steps
    top = chip_ref[1]
    for index, piece_ref in enumerate(piece_refs):

        @pl.when(which == index)
        def _():
            for k in range(4):
                out_ref[jnp.bitwise_xor(top, (k & 1) << 1 | k >> 1), 0] = piece_ref[k]


def assemble(pieces, order, chip):
    chips = sum(piece.shape[0] for piece in pieces)
    rows, columns = pieces[0].shape[1:]
    if chips < 4 or len(pieces) * pieces[0].shape[0] != chips or pieces[0].shape[0] % 4:
        raise ValueError("unexpected mesh")
    rest = len(order) - 2
    steps = pieces[0].shape[0] // 4
    chip_words = jnp.stack([jnp.bitwise_and(chip, (1 << rest) - 1), chip >> rest]).astype(jnp.int32)

    def out_map(step, words):
        at = words[0]
        for position, bit in enumerate(order[2:]):
            at = jnp.bitwise_xor(at, jnp.bitwise_and(step >> position, 1) << bit)
        return (0, at, 0, 0)

    def piece_map(index):
        return lambda step, words: (jnp.clip(step - index * steps, 0, steps - 1), 0, 0)

    out = pl.pallas_call(
        functools.partial(assemble_body, steps),
        grid_spec=pltpu.PrefetchScalarGridSpec(
            num_scalar_prefetch=1,
            grid=(chips // 4,),
            in_specs=[
                pl.BlockSpec((4, rows, columns), piece_map(index)) for index in range(len(pieces))
            ],
            out_specs=pl.BlockSpec((4, 1, rows, columns), out_map),
        ),
        out_shape=jax.ShapeDtypeStruct((4, chips // 4, rows, columns), pieces[0].dtype),
        cost_estimate=pl.CostEstimate(
            flops=0, bytes_accessed=4 * chips * rows * columns, transcendentals=0
        ),
        name="assemble",
    )(chip_words, *pieces)
    return out.reshape(chips, rows, columns)


def at_bit(array, axis, bit):
    return lax.dynamic_index_in_dim(array, bit, axis, keepdims=False)


def halves_at(held, axis, mine, sent):
    leaving = sum(at_bit(h, axis, 1 - mine).astype(full) for h in held).astype(sent)
    staying = sum(at_bit(h, axis, mine).astype(full) for h in held).astype(sent)
    return leaving, staying


def scatter_steps(parts, chip, chip_bits, sent):
    orders = [gather_order(chip_bits, colour)[::-1] for colour in range(len(parts))]
    lefts = [list(range(chip_bits - 1, -1, -1)) for _ in parts]
    held = [[array.reshape((2,) * chip_bits + array.shape[1:])] for array in parts]
    for step in range(chip_bits):
        if step == 2 and len(held) == 2:
            held = [[jnp.concatenate(pair, axis=-1) for pair in zip(*held)]]
        leaving, staying = [], []
        for order, left, arrays in zip(orders, lefts, held):
            bit = order[step]
            axis = left.index(bit)
            left.remove(bit)
            going, kept = halves_at(arrays, axis, jnp.bitwise_and(chip >> bit, 1), sent)
            leaving.append((going, bit))
            staying.append(kept)
        arriving = yield leaving
        held = [list(pair) for pair in zip(staying, arriving)]
    ((kept, arrived),) = held
    return kept.astype(full) + arrived.astype(full)


def halving_steps(leaving, staying, order):
    (arriving,) = yield [(leaving, order[0])]
    for bit in order[1:]:
        half = staying.shape[0] // 2
        leaving, staying = [
            (staying[at].astype(full) + arriving[at].astype(full)).astype(low)
            for at in (slice(half, None), slice(half))
        ]
        (arriving,) = yield [(leaving, bit)]
    return (staying.astype(full) + arriving.astype(full))[0]


def owners(colour, chip, chip_bits):
    order = gather_order(chip_bits, colour)
    spots = jnp.arange(1 << chip_bits)
    bits = list(enumerate(order))
    owner = sum((jnp.bitwise_and(spots >> at, 1) << bit) for at, bit in bits)
    apart = jnp.bitwise_xor(spots, chip)
    place = sum((jnp.bitwise_and(apart >> bit, 1) << at) for at, bit in bits)
    return jnp.bitwise_xor(owner, chip), place


def scatter_flow(parts, chip, chip_bits, sent=low):
    return Flow(scatter_steps(parts, chip, chip_bits, sent))


def row_steps(row, chip, chip_bits, first_bit):
    held = row[None]
    for bit in range(chip_bits):
        (arriving,) = yield [(held, bit + first_bit - 1)]
        held = jnp.concatenate([held, arriving], axis=0)
    places = jnp.arange(1 << chip_bits)
    pick = jnp.bitwise_xor(places, chip)[:, None] == places[None, :]
    return jnp.dot(pick.astype(held.dtype), held, preferred_element_type=full).astype(held.dtype)


def row_flow(row, chip, chip_bits, first_bit=1):
    return Flow(row_steps(row, chip, chip_bits, first_bit))


def run(flow):
    while flow.wanted is not None:
        flow.arrive([swap(array, bit + 1) for array, bit in flow.wanted])
    return flow.result


def to_phases(block_in, row_count):
    width = block_in.shape[-1]
    split_grid = block_in.reshape(row_count // 2, 2, HALF_SIDE, 2, width)
    return split_grid.transpose(1, 3, 0, 2, 4).reshape(4, row_count // 2 * HALF_SIDE, width)


def from_phases(block_in, row_count):
    width = block_in.shape[-1]
    split_grid = block_in.reshape(2, 2, row_count // 2, HALF_SIDE, width)
    return split_grid.transpose(2, 0, 3, 1, 4).reshape(row_count * SIDE, width)


def in_core_order(mine, other, core):
    return jnp.where(core == 0, mine, other), jnp.where(core == 0, other, mine)


def join_halves(mine, other, core):
    return jnp.stack(in_core_order(mine, other, core), axis=1).reshape(-1, mine.shape[-1])


def half_of(joined, which):
    width = joined.shape[-1]
    return at_bit(joined.reshape(4, 2, -1, width), 1, which)


def layer_norm(values):
    average = jnp.mean(values, axis=-1, keepdims=True)
    centred = values - average
    variance = jnp.mean(centred * centred, axis=-1, keepdims=True)
    return centred * lax.rsqrt(variance + ln_epsilon)


def modulate(values, shift_by, scale_by):
    return layer_norm(values) * (1.0 + scale_by) + shift_by


def sinusoid(steps_in, width):
    halfway = width // 2
    frequency = jnp.exp(-math.log(10000.0) * jnp.arange(halfway, dtype=jnp.float32) / halfway)
    angles = steps_in.astype(jnp.float32)[..., None] * frequency
    return jnp.concatenate([jnp.cos(angles), jnp.sin(angles)], axis=-1)


def softmax_of(query, key, allowed):
    raw = lax.dot_general(query, key, (((1,), (1,)), ((), ())), preferred_element_type=full)
    scores = jnp.where(allowed, raw * HEAD ** (-0.5), masked_score)
    shifted = jnp.exp(scores - jnp.max(scores, axis=-1, keepdims=True))
    return shifted / jnp.sum(shifted, axis=-1, keepdims=True)


def head_lanes(shape, head):
    lanes = lax.broadcasted_iota(jnp.int32, shape, 1)
    return jnp.logical_and(lanes >= head * HEAD, lanes < (head + 1) * HEAD)


def attend_body(mask_ref, qkv_ref, out_ref):
    allowed = mask_ref[...] > 0.5

    @pl.loop(0, 4)
    def _(phase):
        rows = pl.ds(pl.multiple_of(phase * PLANE, PLANE), PLANE)
        query = qkv_ref[rows, :128]
        key = qkv_ref[rows, 128:256]
        value = qkv_ref[rows, 256:]
        total = None
        for head in range(2):
            here = head_lanes(key.shape, head)
            probs = softmax_of(query, jnp.where(here, key, jnp.zeros_like(key)), allowed)
            part = jnp.dot(
                probs.astype(low),
                jnp.where(here, value, jnp.zeros_like(value)),
                preferred_element_type=full,
            )
            total = part if total is None else total + part
        out_ref[rows, :] = total.astype(low)


def attend_back_body(mask_ref, qkv_ref, grad_ref, out_ref):
    allowed = mask_ref[...] > 0.5

    @pl.loop(0, 4)
    def _(phase):
        rows = pl.ds(pl.multiple_of(phase * PLANE, PLANE), PLANE)
        query = qkv_ref[rows, :128]
        key = qkv_ref[rows, 128:256]
        value = qkv_ref[rows, 256:]
        grad = grad_ref[rows, :]
        by_rows = (((0,), (0,)), ((), ()))
        totals = [None, None, None]
        for head in range(2):
            here = head_lanes(key.shape, head)
            blank = jnp.zeros_like(key)
            key_here = jnp.where(here, key, blank)
            query_here = jnp.where(here, query, blank)
            value_here = jnp.where(here, value, blank)
            grad_here = jnp.where(here, grad, blank)
            weights = softmax_of(query, key_here, allowed)
            grad_probs = lax.dot_general(
                grad, value_here, (((1,), (1,)), ((), ())), preferred_element_type=full
            )
            delta = jnp.sum(grad_probs * weights, axis=-1, keepdims=True)
            grad_scores = (weights * (grad_probs - delta)).astype(low)
            parts = (
                jnp.dot(grad_scores, key_here, preferred_element_type=full),
                lax.dot_general(grad_scores, query_here, by_rows, preferred_element_type=full),
                lax.dot_general(
                    weights.astype(low), grad_here, by_rows, preferred_element_type=full
                ),
            )
            totals = [p if t is None else t + p for t, p in zip(totals, parts)]
        out_ref[rows, :128] = (totals[0] * HEAD ** (-0.5)).astype(low)
        out_ref[rows, 128:256] = (totals[1] * HEAD ** (-0.5)).astype(low)
        out_ref[rows, 256:] = totals[2].astype(low)


def attend(mask, qkv):
    tokens, width = qkv.shape
    pairs = width // 384
    return pl.pallas_call(
        attend_body,
        grid=(pairs,),
        in_specs=[
            pl.BlockSpec((PLANE, PLANE), lambda j: (0, 0)),
            pl.BlockSpec((tokens, 384), lambda j: (0, j)),
        ],
        out_specs=pl.BlockSpec((tokens, 128), lambda j: (0, j)),
        out_shape=jax.ShapeDtypeStruct((tokens, pairs * 128), low),
        cost_estimate=pl.CostEstimate(
            flops=pairs * 2 * 4 * 4 * PLANE * PLANE * 256,
            bytes_accessed=8 * tokens * pairs * 128,
            transcendentals=pairs * 8 * PLANE * PLANE,
        ),
        name="attend",
    )(mask, qkv)


def attend_back(mask, qkv, grad):
    tokens, width = qkv.shape
    pairs = width // 384
    return pl.pallas_call(
        attend_back_body,
        grid=(pairs,),
        in_specs=[
            pl.BlockSpec((PLANE, PLANE), lambda j: (0, 0)),
            pl.BlockSpec((tokens, 384), lambda j: (0, j)),
            pl.BlockSpec((tokens, 128), lambda j: (0, j)),
        ],
        out_specs=pl.BlockSpec((tokens, 384), lambda j: (0, j)),
        out_shape=jax.ShapeDtypeStruct((tokens, width), low),
        cost_estimate=pl.CostEstimate(
            flops=pairs * 2 * 4 * 10 * PLANE * PLANE * 256,
            bytes_accessed=14 * tokens * pairs * 128,
            transcendentals=pairs * 8 * PLANE * PLANE,
        ),
        name="attend_back",
    )(mask, qkv, grad)


def strip_at(ref, row_phase, column_phase, row):
    start = pl.multiple_of((row + 1) * STRIP, STRIP)
    return ref[2 * row_phase + column_phase, pl.ds(start, STRIP), :]


def near_strips(ref, row):
    tokens = lax.broadcasted_iota(jnp.int32, (STRIP, ref.shape[-1]), 0)
    loaded = {}
    for row_phase, at in ((1, row - 1), (0, row), (1, row), (0, row + 1)):
        even = strip_at(ref, row_phase, 0, at)
        odd = strip_at(ref, row_phase, 1, at)
        before = jnp.where(tokens == 0, 0.0, pltpu.roll(odd, 1, 0))
        after = jnp.where(tokens == STRIP - 1, 0.0, pltpu.roll(even, STRIP - 1, 0))
        loaded[len(loaded)] = ((before, even, odd), (even, odd, after))
    return {0: (loaded[0], loaded[1], loaded[2]), 1: (loaded[1], loaded[2], loaded[3])}


def conv_strip(near, kernel, row_phase, column_phase):
    total = None
    for i in range(3):
        for j in range(3):
            term = near[row_phase][i][column_phase][j] * kernel[3 * i + j : 3 * i + j + 1, :]
            total = term if total is None else total + term
    return total


def feed_body(
    spread,
    words_ref,
    norm_ref,
    norm_t_ref,
    grad_ref,
    *refs,
):
    pieces = 2 if spread else 1
    up_refs, refs = refs[:pieces], refs[pieces:]
    down_refs, refs = refs[:pieces], refs[pieces:]
    kernel_ref, staying_ref, leaving_ref, *refs = refs
    up_grad_refs, refs = refs[:pieces], refs[pieces:]
    down_grad_refs, refs = refs[:pieces], refs[pieces:]
    kernel_grad_ref, branch_acc, back_acc, hidden, widened_grad, act_grad, act, hidden_grad = refs[
        :8
    ]
    step = pl.program_id(0)
    core = words_ref[0]
    by_columns = (((1,), (1,)), ((), ()))
    width = kernel_ref.shape[1]
    model = norm_t_ref.shape[0]
    up_ref, down_ref = up_refs[0], down_refs[0]
    if spread:
        up_ref, down_all = refs[8:]
        half, share, _ = up_refs[0].shape
        piece = down_refs[0].shape[1]
        chips = 2 * half
        down_ref = down_all.at[pl.ds(pl.multiple_of(step * width, width), width), :]

        for which in range(2):

            @pl.loop(0, half)
            def _(spot):
                start = pl.multiple_of(words_ref[1 + which * half + spot] * share, share)
                up_ref[pl.ds(start, share), :] = up_refs[which][spot]

            @pl.when(step == 0)
            def _():
                @pl.loop(0, half)
                def _(spot):
                    owner = words_ref[1 + chips + which * half + spot]
                    start = pl.multiple_of(owner * piece, piece)
                    down_all[pl.ds(start, piece), :] = down_refs[which][spot]

    @pl.when(step == 0)
    def _():
        blank = jnp.zeros((STRIP, width), full)
        for plane in range(4):
            for ref in (hidden, widened_grad):
                ref[plane, pl.ds(0, STRIP), :] = blank
                ref[plane, pl.ds(PLANE + STRIP, STRIP), :] = blank
        branch_acc[...] = jnp.zeros_like(branch_acc)
        back_acc[...] = jnp.zeros_like(back_acc)

    @pl.loop(0, 4)
    def _(plane):
        rows = pl.ds(pl.multiple_of(plane * PLANE, PLANE), PLANE)
        hidden[plane, pl.ds(STRIP, PLANE), :] = jnp.dot(
            norm_ref[rows, :], up_ref[...], preferred_element_type=full
        )
        act_grad[rows, :] = lax.dot_general(
            grad_ref[rows, :], down_ref[...], by_columns, preferred_element_type=full
        )

    kernel = kernel_ref[...]

    def forward_strip(row, sums):
        near = near_strips(hidden, row)
        sums = list(sums)
        for row_phase in range(2):
            for column_phase in range(2):
                plane = 2 * row_phase + column_phase
                wide = conv_strip(near, kernel, row_phase, column_phase)
                square = wide * wide
                bend = math.sqrt(2.0 / math.pi) * (wide + 0.044715 * wide * square)
                curve = jnp.tanh(bend)
                half = 0.5 * (1.0 + curve)
                slope = half + 0.5 * wide * (1.0 - curve * curve) * (
                    math.sqrt(2.0 / math.pi) * (1.0 + 3 * 0.044715 * square)
                )
                at = pl.ds(pl.multiple_of(plane * PLANE + row * STRIP, STRIP), STRIP)
                act[at, :] = (wide * half).astype(low)
                grad_here = slope * act_grad[at, :]
                widened_grad[plane, pl.ds(pl.multiple_of((row + 1) * STRIP, STRIP), STRIP), :] = (
                    grad_here
                )
                for i in range(3):
                    for j in range(3):
                        product = near[row_phase][i][column_phase][j] * grad_here
                        sums[3 * i + j] = sums[3 * i + j] + (product[:8] + product[8:])
        return tuple(sums)

    sums = lax.fori_loop(
        0, HALF_SIDE, forward_strip, tuple(jnp.zeros((8, width), full) for _ in range(9))
    )
    kernel_grad_ref[...] = jnp.concatenate(
        [jnp.sum(s, axis=0, keepdims=True) for s in sums] + [jnp.zeros((7, width), full)], axis=0
    )

    flipped = [kernel[8 - t : 9 - t, :] for t in range(9)]
    flipped = jnp.concatenate(flipped, axis=0)

    @pl.loop(0, HALF_SIDE)
    def _(row):
        near = near_strips(widened_grad, row)
        for row_phase in range(2):
            for column_phase in range(2):
                plane = 2 * row_phase + column_phase
                at = pl.ds(pl.multiple_of(plane * PLANE + row * STRIP, STRIP), STRIP)
                hidden_grad[at, :] = conv_strip(near, flipped, row_phase, column_phase).astype(low)

    @pl.loop(0, 4)
    def _(plane):
        rows = pl.ds(pl.multiple_of(plane * PLANE, PLANE), PLANE)
        branch_acc[rows, :] += jnp.dot(act[rows, :], down_ref[...], preferred_element_type=full)
        back_acc[rows, :] += lax.dot_general(
            hidden_grad[rows, :], up_ref[...], by_columns, preferred_element_type=full
        )

    if spread:
        for which in range(2):

            @pl.loop(0, half // 4)
            def _(group):
                lhs = []
                for k in range(4):
                    owner = words_ref[1 + which * half + 4 * group + k]
                    start = pl.multiple_of(owner * share, share)
                    lhs.append(norm_t_ref[pl.ds(start, share), :])
                result = jnp.dot(
                    jnp.concatenate(lhs, axis=0), hidden_grad[...], preferred_element_type=full
                ).astype(low)
                for k in range(4):
                    up_grad_refs[which][4 * group + k] = result[k * share : (k + 1) * share]

    else:

        @pl.loop(0, model // TILE)
        def _(tile):
            rows = pl.ds(pl.multiple_of(tile * TILE, TILE), TILE)
            up_grad_refs[0][rows, :] = jnp.dot(
                norm_t_ref[rows, :], hidden_grad[...], preferred_element_type=full
            ).astype(low)

    down_grad = lax.dot_general(
        act[...], grad_ref[...], (((0,), (0,)), ((), ())), preferred_element_type=full
    ).astype(low)
    if spread:
        for k in range(width // piece):
            place = words_ref[1 + 2 * chips + step * (width // piece) + k]
            for which in range(2):

                @pl.when(place // half == which)
                def _():
                    down_grad_refs[which][place - which * half] = down_grad[
                        k * piece : (k + 1) * piece
                    ]

    else:
        down_grad_refs[0][...] = down_grad

    @pl.when(step == pl.num_programs(0) - 1)
    def _():
        for ref, which in ((staying_ref, core), (leaving_ref, 1 - core)):
            for index, acc in enumerate((branch_acc, back_acc)):
                for plane in range(4):
                    start = plane * PLANE + pl.multiple_of(which * (PLANE // 2), PLANE // 2)
                    ref[index, plane] = acc[pl.ds(start, PLANE // 2), :].astype(low)


def feed_forward(norm, norm_t, grad, up, down, kernel, words):
    tokens, model = norm.shape
    channels = kernel.shape[1]
    width = TILE
    spread = len(up) == 2
    whole = lambda j, words: (0, 0)
    half = lambda j, words: (0, 0, 0, 0)
    across = lambda j, words: (0, j)
    once = pl.Buffered(1)
    piece_scratch = []
    if spread:
        deep = lambda j, words: (0, 0, 0)
        up_spec = pl.BlockSpec(up[0].shape[:2] + (width,), lambda j, words: (0, 0, j))
        down_spec = pl.BlockSpec(down[0].shape, deep, pipeline_mode=once)
        down_grad_spec = pl.BlockSpec(down[0].shape, deep)
        piece_scratch = [pltpu.VMEM((model, width), low), pltpu.VMEM((channels, model), low)]
    else:
        up_spec = pl.BlockSpec((model, width), across)
        down_spec = down_grad_spec = pl.BlockSpec((width, model), lambda j, words: (j, 0))
    halves = jax.ShapeDtypeStruct((2, 4, PLANE // 2, model), low)
    like = lambda arrays: [jax.ShapeDtypeStruct(array.shape, low) for array in arrays]
    out = pl.pallas_call(
        functools.partial(feed_body, spread),
        grid_spec=pltpu.PrefetchScalarGridSpec(
            num_scalar_prefetch=1,
            grid=(channels // width,),
            in_specs=[
                pl.BlockSpec((tokens, model), whole, pipeline_mode=once),
                pl.BlockSpec((model, tokens), whole, pipeline_mode=once),
                pl.BlockSpec((tokens, model), whole, pipeline_mode=once),
                *[up_spec] * len(up),
                *[down_spec] * len(down),
                pl.BlockSpec((16, width), across),
            ],
            out_specs=[
                pl.BlockSpec(halves.shape, half),
                pl.BlockSpec(halves.shape, half),
                *[up_spec] * len(up),
                *[down_grad_spec] * len(down),
                pl.BlockSpec((16, width), across),
            ],
            scratch_shapes=[
                pltpu.VMEM((tokens, model), full),
                pltpu.VMEM((tokens, model), full),
                pltpu.VMEM((4, PADDED, width), full),
                pltpu.VMEM((4, PADDED, width), full),
                pltpu.VMEM((tokens, width), full),
                pltpu.VMEM((tokens, width), low),
                pltpu.VMEM((tokens, width), low),
            ]
            + piece_scratch,
        ),
        out_shape=[halves, halves]
        + like(up)
        + like(down)
        + [jax.ShapeDtypeStruct((16, channels), full)],
        compiler_params=pltpu.CompilerParams(vmem_limit_bytes=63 * 1024 * 1024),
        cost_estimate=pl.CostEstimate(
            flops=12 * tokens * model * channels,
            bytes_accessed=8 * model * channels + 10 * tokens * model,
            transcendentals=tokens * channels,
        ),
        name="feed_forward",
    )(words, norm, norm_t, grad, *up, *down, kernel)
    staying, leaving, *grads, kernel_grad = out
    return staying, leaving, grads[: len(up)], grads[len(up) :], kernel_grad


def token_stats(x_ref, average, scale):
    @pl.loop(0, x_ref.shape[0] // STRIP)
    def _(strip):
        rows = pl.ds(pl.multiple_of(strip * STRIP, STRIP), STRIP)
        values = x_ref[rows, :].astype(full)
        mean = jnp.mean(values, axis=-1, keepdims=True)
        centred = values - mean
        variance = jnp.mean(centred * centred, axis=-1, keepdims=True)
        average[rows, :] = jnp.broadcast_to(mean, (STRIP, 128))
        scale[rows, :] = jnp.broadcast_to(lax.rsqrt(variance + ln_epsilon), (STRIP, 128))


def normed_strip(x_ref, average, scale, rows, columns):
    width = columns.size
    wide = lambda ref: jnp.concatenate([ref[rows, :]] * (width // 128), axis=1)
    return (x_ref[rows, columns].astype(full) - wide(average)) * wide(scale)


def frame_zeros(refs):
    for ref in refs:
        blank = jnp.zeros((STRIP, ref.shape[-1]), full)
        for plane in range(4):
            ref[plane, pl.ds(0, STRIP), :] = blank
            ref[plane, pl.ds(ref.shape[1] - STRIP, STRIP), :] = blank


def conv_in_body(x_ref, kernel_ref, mods_ref, out_ref, average, scale, normed):
    step = pl.program_id(0)
    width = out_ref.shape[1]
    columns = pl.ds(pl.multiple_of(step * width, width), width)

    @pl.when(step == 0)
    def _():
        token_stats(x_ref, average, scale)
        frame_zeros([normed])

    shift_by = mods_ref[0:1, :]
    scale_by = 1.0 + mods_ref[1:2, :]

    @pl.loop(0, HALF_SIDE)
    def _(row):
        for plane in range(4):
            rows = pl.ds(pl.multiple_of(plane * PLANE + row * STRIP, STRIP), STRIP)
            normed[plane, pl.ds(pl.multiple_of((row + 1) * STRIP, STRIP), STRIP), :] = (
                normed_strip(x_ref, average, scale, rows, columns) * scale_by + shift_by
            )

    kernel = kernel_ref[...]

    @pl.loop(0, HALF_SIDE)
    def _(row):
        near = near_strips(normed, row)
        for row_phase in range(2):
            for column_phase in range(2):
                plane = 2 * row_phase + column_phase
                at = pl.ds(pl.multiple_of(plane * PLANE + row * STRIP, STRIP), STRIP)
                out_ref[at, :] = conv_strip(near, kernel, row_phase, column_phase).astype(low)


def conv_in(canvas, kernel, mods):
    tokens, model = canvas.shape
    return pl.pallas_call(
        conv_in_body,
        grid=(model // TILE,),
        in_specs=[
            pl.BlockSpec((tokens, model), lambda j: (0, 0), pipeline_mode=pl.Buffered(1)),
            pl.BlockSpec((16, TILE), lambda j: (0, j)),
            pl.BlockSpec((8, TILE), lambda j: (0, j)),
        ],
        out_specs=pl.BlockSpec((tokens, TILE), lambda j: (0, j)),
        out_shape=jax.ShapeDtypeStruct((tokens, model), low),
        scratch_shapes=[
            pltpu.VMEM((tokens, 128), full),
            pltpu.VMEM((tokens, 128), full),
            pltpu.VMEM((4, PADDED, TILE), full),
        ],
        cost_estimate=pl.CostEstimate(
            flops=30 * tokens * model, bytes_accessed=4 * tokens * model, transcendentals=tokens
        ),
        name="conv_in",
    )(canvas, kernel, mods)


def conv_back_body(
    core_ref,
    x_ref,
    kept_ref,
    arriving_ref,
    kernel_ref,
    mods_ref,
    middle_ref,
    out_ref,
    kernel_grad_ref,
    mods_grad_ref,
    average,
    scale,
    normed,
    upstream,
    held,
    sum_plain,
    sum_normed,
    woven,
):
    step = pl.program_id(0)
    core = core_ref[0]
    width = kept_ref.shape[1]
    near_rows = x_ref.shape[0] // 4 // STRIP
    own_rows = near_rows - 1
    columns = pl.ds(pl.multiple_of(step * width, width), width)

    def near_at(plane, row):
        return pl.ds(pl.multiple_of((plane * near_rows + row) * STRIP, STRIP), STRIP)

    def own_at(plane, row):
        return pl.ds(pl.multiple_of((plane * own_rows + row) * STRIP, STRIP), STRIP)

    @pl.when(step == 0)
    def _():
        token_stats(x_ref, average, scale)
        frame_zeros([normed, upstream])
        sum_plain[...] = jnp.zeros_like(sum_plain)
        sum_normed[...] = jnp.zeros_like(sum_normed)

    shift_by = mods_ref[0:1, :]
    scale_by = 1.0 + mods_ref[1:2, :]

    @pl.loop(0, near_rows)
    def _(row):
        for plane in range(4):
            rows = near_at(plane, row)
            padded = pl.ds(pl.multiple_of((row + 1) * STRIP, STRIP), STRIP)
            normed[plane, padded, :] = (
                normed_strip(x_ref, average, scale, rows, columns) * scale_by + shift_by
            )
            upstream[plane, padded, :] = kept_ref[rows, :].astype(full) + arriving_ref[
                rows, :
            ].astype(full)

    kernel = kernel_ref[...]
    flipped = jnp.concatenate([kernel[8 - t : 9 - t, :] for t in range(9)], axis=0)

    def kernel_strip(row, sums):
        near = near_strips(normed, row + core)
        sums = list(sums)
        for row_phase in range(2):
            for column_phase in range(2):
                grad_here = strip_at(upstream, row_phase, column_phase, row + core)
                for i in range(3):
                    for j in range(3):
                        product = near[row_phase][i][column_phase][j] * grad_here
                        sums[3 * i + j] = sums[3 * i + j] + (product[:8] + product[8:])
        return tuple(sums)

    def fold(sums, rows):
        return jnp.concatenate(
            [jnp.sum(s, axis=0, keepdims=True) for s in sums]
            + [jnp.zeros((rows - len(sums), width), full)],
            axis=0,
        )

    blank = jnp.zeros((8, width), full)
    kernel_grad_ref[...] = fold(lax.fori_loop(0, own_rows, kernel_strip, (blank,) * 9), 16)

    def input_strip(row, sums):
        near = near_strips(upstream, row + core)
        shift_sum, scale_sum = sums
        for row_phase in range(2):
            for column_phase in range(2):
                plane = 2 * row_phase + column_phase
                grad = conv_strip(near, flipped, row_phase, column_phase)
                plain = normed_strip(x_ref, average, scale, near_at(plane, row + core), columns)
                shift_sum = shift_sum + (grad[:8] + grad[8:])
                product = grad * plain
                scale_sum = scale_sum + (product[:8] + product[8:])
                scaled = grad * scale_by
                rows = own_at(plane, row)
                held[step, rows, :] = scaled
                product = scaled * plain
                sum_plain[rows, :] += sum(scaled[:, k : k + 128] for k in range(0, width, 128))
                sum_normed[rows, :] += sum(product[:, k : k + 128] for k in range(0, width, 128))
        return shift_sum, scale_sum

    mods_grad_ref[...] = fold(lax.fori_loop(0, own_rows, input_strip, (blank,) * 2), 8)

    @pl.when(step == pl.num_programs(0) - 1)
    def _():
        model = x_ref.shape[1]

        @pl.loop(0, own_rows)
        def _(row):
            for plane in range(4):
                rows = own_at(plane, row)
                near = near_at(plane, row + core)
                mean_plain = jnp.sum(sum_plain[rows, :], axis=-1, keepdims=True) / model
                mean_normed = jnp.sum(sum_normed[rows, :], axis=-1, keepdims=True) / model
                for block in range(model // width):
                    at = pl.ds(block * width, width)
                    plain = normed_strip(x_ref, average, scale, near, at)
                    spread = jnp.concatenate([scale[near, :]] * (width // 128), axis=1)
                    result = middle_ref[rows, at] + spread * (
                        held[block, rows, :] - mean_plain - plain * mean_normed
                    )
                    for lane in range(0, width, 128):
                        woven[(block * width + lane) // 128, pl.ds(plane % 2, STRIP, stride=2), :] = (
                            result[:, lane : lane + 128]
                        )
                if plane % 2 == 1:
                    start = pl.multiple_of((2 * row + plane // 2) * SIDE, SIDE)
                    for lane in range(model // 128):
                        out_ref[pl.ds(start, SIDE), lane * 128 : lane * 128 + 128] = woven[lane]


def conv_back(core, x_near, kept, arriving, kernel, mods, grad_middle):
    near_tokens, model = x_near.shape
    own_tokens = grad_middle.shape[0]
    once = pl.Buffered(1)
    whole = lambda j, words: (0, 0)
    across = lambda j, words: (0, j)
    padded = near_tokens // 4 + 2 * STRIP
    return pl.pallas_call(
        conv_back_body,
        grid_spec=pltpu.PrefetchScalarGridSpec(
            num_scalar_prefetch=1,
            grid=(model // TILE,),
            in_specs=[
                pl.BlockSpec((near_tokens, model), whole, pipeline_mode=once),
                pl.BlockSpec((near_tokens, TILE), across),
                pl.BlockSpec((near_tokens, TILE), across),
                pl.BlockSpec((16, TILE), across),
                pl.BlockSpec((8, TILE), across),
                pl.BlockSpec((own_tokens, model), whole, pipeline_mode=once),
            ],
            out_specs=[
                pl.BlockSpec((own_tokens, model), whole),
                pl.BlockSpec((16, TILE), across),
                pl.BlockSpec((8, TILE), across),
            ],
            scratch_shapes=[
                pltpu.VMEM((near_tokens, 128), full),
                pltpu.VMEM((near_tokens, 128), full),
                pltpu.VMEM((4, padded, TILE), full),
                pltpu.VMEM((4, padded, TILE), full),
                pltpu.VMEM((model // TILE, own_tokens, TILE), full),
                pltpu.VMEM((own_tokens, 128), full),
                pltpu.VMEM((own_tokens, 128), full),
                pltpu.VMEM((model // 128, SIDE, 128), full),
            ],
        ),
        out_shape=[
            jax.ShapeDtypeStruct((own_tokens, model), full),
            jax.ShapeDtypeStruct((16, model), full),
            jax.ShapeDtypeStruct((8, model), full),
        ],
        cost_estimate=pl.CostEstimate(
            flops=70 * own_tokens * model,
            bytes_accessed=14 * own_tokens * model,
            transcendentals=near_tokens,
        ),
        name="conv_back",
    )(core[None].astype(jnp.int32), x_near, kept, arriving, kernel, mods, grad_middle)


def row_stats(values):
    mean = jnp.mean(values, axis=-1, keepdims=True)
    centred = values - mean
    scale = lax.rsqrt(jnp.mean(centred * centred, axis=-1, keepdims=True) + ln_epsilon)
    return centred * scale, scale


def enter_feed_body(x_ref, part_ref, other_ref, grad_ref, mods_ref, norm_ref, norm_t_ref, out_ref):
    @pl.loop(0, x_ref.shape[0] // STRIP)
    def _(strip):
        rows = pl.ds(pl.multiple_of(strip * STRIP, STRIP), STRIP)
        branch = part_ref[rows, :].astype(full) + other_ref[rows, :].astype(full)
        plain, _ = row_stats(x_ref[rows, :].astype(full) + mods_ref[0:1, :] * branch)
        normed = plain * (1.0 + mods_ref[2:3, :]) + mods_ref[1:2, :]
        norm_ref[rows, :] = normed.astype(low)
        out_ref[rows, :] = (grad_ref[rows, :].astype(full) * mods_ref[3:4, :]).astype(low)

    norm_t_ref[...] = norm_ref[...].T


def enter_feed(canvas, part, other, grad, mods):
    tokens, model = canvas.shape
    rows = PLANE // 2
    along = pl.BlockSpec((rows, model), lambda j: (j, 0))
    return pl.pallas_call(
        enter_feed_body,
        grid=(tokens // rows,),
        in_specs=[along] * 4 + [pl.BlockSpec((8, model), lambda j: (0, 0))],
        out_specs=[along, pl.BlockSpec((model, rows), lambda j: (0, j)), along],
        out_shape=[
            jax.ShapeDtypeStruct((tokens, model), low),
            jax.ShapeDtypeStruct((model, tokens), low),
            jax.ShapeDtypeStruct((tokens, model), low),
        ],
        cost_estimate=pl.CostEstimate(flops=1000, bytes_accessed=1000, transcendentals=0),
        name="enter_feed",
    )(canvas, part, other, grad, mods)


def leave_feed_body(words_ref, x_ref, part_ref, other_ref, grad_ref, mods_ref, *refs):
    *kept_refs, out_ref, middle_grad_ref, branch_grad_ref, sums_ref, totals = refs
    plane = pl.program_id(0)

    @pl.when(plane == 0)
    def _():
        totals[...] = jnp.zeros_like(totals)

    @pl.loop(0, x_ref.shape[0] // STRIP)
    def _(strip):
        rows = pl.ds(pl.multiple_of(strip * STRIP, STRIP), STRIP)
        gate_a, gate_f = mods_ref[0:1, :], mods_ref[3:4, :]
        branch_a = part_ref[rows, :].astype(full) + other_ref[rows, :].astype(full)
        middle = x_ref[rows, :].astype(full) + gate_a * branch_a
        plain, scale = row_stats(middle)
        branch_f = sum(ref[0, 0, rows, :].astype(full) for ref in kept_refs)
        back = sum(ref[1, 0, rows, :].astype(full) for ref in kept_refs)
        grad = grad_ref[rows, :].astype(full)
        out_ref[rows, :] = (middle + gate_f * branch_f).astype(low)
        scaled = back * (1.0 + mods_ref[2:3, :])
        mean_plain = jnp.mean(scaled, axis=-1, keepdims=True)
        mean_normed = jnp.mean(scaled * plain, axis=-1, keepdims=True)
        grad_middle = grad + scale * (scaled - mean_plain - plain * mean_normed)
        middle_grad_ref[rows, :] = grad_middle
        branch_grad_ref[rows, :] = (grad_middle * gate_a).astype(low)
        products = (grad_middle * branch_a, back, back * plain, grad * branch_f)
        for index, product in enumerate(products):
            totals[index] += product[:8] + product[8:]

    @pl.when(plane == pl.num_programs(0) - 1)
    def _():
        lines = [jnp.sum(totals[k], axis=0, keepdims=True) for k in range(4)]
        sums_ref[...] = jnp.concatenate(lines + [jnp.zeros_like(sums_ref[:4])], axis=0)


def leave_feed(words, canvas, part, other, grad, mods, kept):
    model = canvas.shape[1]
    rows = PLANE // 2
    own = pl.BlockSpec((rows, model), lambda j, words: (2 * j + words[0], 0))
    half = pl.BlockSpec((rows, model), lambda j, words: (j, 0))
    whole = pl.BlockSpec((8, model), lambda j, words: (0, 0))
    return pl.pallas_call(
        leave_feed_body,
        grid_spec=pltpu.PrefetchScalarGridSpec(
            num_scalar_prefetch=1,
            grid=(4,),
            in_specs=[own] * 4
            + [whole]
            + [pl.BlockSpec((2, 1, rows, model), lambda j, words: (0, j, 0, 0))] * len(kept),
            out_specs=[half, half, half, whole],
            scratch_shapes=[pltpu.VMEM((4, 8, model), full)],
        ),
        out_shape=[
            jax.ShapeDtypeStruct((4 * rows, model), low),
            jax.ShapeDtypeStruct((4 * rows, model), full),
            jax.ShapeDtypeStruct((4 * rows, model), low),
            jax.ShapeDtypeStruct((8, model), full),
        ],
        cost_estimate=pl.CostEstimate(flops=1000, bytes_accessed=1000, transcendentals=0),
        name="leave_feed",
    )(words, canvas, part, other, grad, mods, *kept)


def on_device(
    tokens,
    seg_ids,
    timesteps,
    labels,
    cotangent,
    mod_weight,
    class_table,
    attn_kernel,
    qkv_weight,
    proj_weight,
    up_weight,
    ffn_kernel,
    down_weight,
):
    devices = device_count()
    chips = devices // 2
    chip_bits = chips.bit_length() - 1
    rank = lax.axis_index("dp") * lax.axis_size("fsdp") + lax.axis_index("fsdp")
    core = rank % 2
    chip = rank // 2
    _, half_tokens, model = tokens.shape
    half_rows = half_tokens // SIDE
    class_count = class_table.shape[0]
    part = model // devices
    share = down_weight.shape[0]
    piece = share // CHUNKS
    pairs = model // HEAD // 4

    def halves_of(array, axis):
        return at_bit(array, axis, core), at_bit(array, axis, 1 - core)

    def row_pair(array, axis):
        kept, leaving = halves_of(array, axis)
        arriving = swap_core(leaving)
        return jnp.concatenate(in_core_order(kept, arriving, core), axis=0)

    qkv_split = qkv_weight.reshape(part, 3, 2, pairs, 128).transpose(0, 2, 3, 1, 4)
    qkv_rows = row_pair(qkv_split.reshape(part, 2, pairs * 384), 1)
    qkv_half = pairs * 384 // 2

    picks = labels[:, None] == jnp.arange(class_count)[None, :]
    angles_here = lax.dynamic_slice_in_dim(sinusoid(timesteps, model), rank * part, part, axis=1)
    cond = angles_here + jnp.dot(picks.astype(low), class_table, preferred_element_type=full)
    lift_value, lift_pull = jax.vjp(jax.nn.silu, cond)
    lifted = lift_value.astype(low)
    mods_part = jnp.dot(lifted, mod_weight, preferred_element_type=full)

    slot = Slots(jnp.zeros((8, 128), full))
    near = lambda *shards: Flow(near_steps(shards, chip_bits))
    sums = lambda *parts: scatter_flow(parts, chip, chip_bits)
    joined = lambda flow: [
        assemble(pieces, gather_order(chip_bits, colour), chip)
        for colour, pieces in enumerate(flow.result)
    ]
    mods_flow = scatter_flow([mods_part], chip, chip_bits, sent=full)
    qkv_near = near(qkv_rows)
    mine, upstream = slot(
        [qkv_near, mods_flow],
        lambda: (to_phases(tokens[0], half_rows), to_phases(cotangent[0], half_rows)),
    )

    up_weight, proj_weight, ffn_kernel, attn_kernel = slot.after(
        up_weight, proj_weight, ffn_kernel, attn_kernel
    )
    up_split = up_weight.reshape(part, chips, 2, CHUNKS, piece).transpose(0, 2, 3, 1, 4)
    up_rows = row_pair(up_split.reshape(part, 2, CHUNKS, chips * piece), 1)
    proj_there = [(r, r % chips * 2 + r // chips) for r in range(devices)]
    proj_back = [(b, a) for a, b in proj_there]
    proj_rows = lax.ppermute(proj_weight, AXES, proj_there)
    canvas = slot([qkv_near, mods_flow], lambda: join_halves(mine, swap_core(mine), core))
    slot.finish([qkv_near])
    tap_count = 9 * (share + part)
    tap_words = jnp.concatenate([ffn_kernel.reshape(-1), attn_kernel.reshape(-1)])
    tap_words = jnp.pad(tap_words, (0, -tap_count % 128))
    taps = run(row_flow(tap_words, rank, chip_bits + 1, 0))
    ffn_taps = taps[:, : 9 * share].reshape(chips, 2, 9, share)
    ffn_taps = at_bit(ffn_taps, 1, core).reshape(chips, 9, CHUNKS, piece)
    ffn_taps = ffn_taps.transpose(2, 1, 0, 3).reshape(CHUNKS, 9, chips * piece).astype(full)
    ffn_taps = jnp.pad(ffn_taps, ((0, 0), (0, 7), (0, 0)))
    attn_taps = taps[:, 9 * share : tap_count].reshape(devices, 9, part)
    attn_taps = attn_taps.transpose(1, 0, 2).reshape(9, model).astype(full)
    attn_taps = jnp.pad(attn_taps, ((0, 7), (0, 0)))

    spot = jnp.arange(PLANE)
    quadrant = 2 * (spot // (PLANE // 2)) + spot % HALF_SIDE // (HALF_SIDE // 2)
    quadrants_here = at_bit(seg_ids, 0, chip)
    segment = jnp.sum(
        jnp.where(quadrant[:, None] == jnp.arange(4)[None, :], quadrants_here[None, :], 0), axis=1
    )
    mask = (segment[:, None] == segment[None, :]).astype(full)

    def far(arrays, where):
        return Flow(far_steps([array[at] for array, at in zip(arrays, where)]))

    wide = chips * piece
    later = range(CHUNKS - 1)
    proj_near = near(proj_rows)
    feed_near = [
        near(up_rows[:, 0], down_weight[:piece]),
        near(up_rows[:, 1:].reshape(2 * part, -1), down_weight[piece:]),
    ]
    left, right = (Ellipsis, slice(qkv_half)), (Ellipsis, slice(qkv_half, None))
    qkv_flow = far(qkv_near.result * 2, (left, right))
    slot([qkv_flow, mods_flow, proj_near, feed_near[0]])
    mods_half = run(mods_flow)
    mods = mods_half + swap_core(mods_half)
    shift_a, scale_a, gate_a, shift_f, scale_f, gate_f = jnp.split(mods, 6)

    mods_a = jnp.concatenate([shift_a[None], scale_a[None], jnp.zeros((6, model), full)], axis=0)

    convolved = slot(
        [qkv_flow, proj_near, feed_near[0]], lambda: conv_in(canvas, attn_taps, mods_a)
    )
    slot.finish([qkv_flow, proj_near, feed_near[0]])
    left, right = (Ellipsis, slice(model // 2)), (Ellipsis, slice(model // 2, None))
    proj_flow = far(proj_near.result * 2, (left, right))
    feed_flows = [far(feed_near[0].result, (Ellipsis, Ellipsis))]

    def project_in():
        weight = jnp.concatenate(
            [array.reshape(model, qkv_half) for array in joined(qkv_flow)], axis=1
        )
        return weight, jnp.dot(convolved, weight, preferred_element_type=full).astype(low)

    qkv_full, qkv = slot([proj_flow, feed_flows[0], feed_near[1]], project_in)
    (upstream,) = slot.after(upstream)
    grad_ph = join_halves(upstream, swap_core(upstream), core)
    attended = slot([proj_flow, feed_near[1]], lambda: attend(mask, qkv))
    slot.finish([proj_flow, feed_near[1]])
    for t in later:
        columns, rows = slice(t * wide, t * wide + wide), slice(t * piece, t * piece + piece)
        feed_flows.append(far(feed_near[1].result, ((Ellipsis, columns), (slice(None), rows))))

    mods_f = jnp.concatenate(
        [gate_a[None], shift_f[None], scale_f[None], gate_f[None], jnp.zeros((4, model), full)]
    )

    def project_out():
        weight = jnp.concatenate(
            [array.reshape(-1, model // 2) for array in joined(proj_flow)], axis=1
        )
        branch_part = jnp.dot(attended, weight, preferred_element_type=full).astype(low)
        other = swap_core(branch_part)
        return weight, branch_part, other, *enter_feed(canvas, branch_part, other, grad_ph, mods_f)

    proj_full, branch_part, branch_other, norm, norm_t, grad_branch_f = slot(
        feed_flows[:2], project_out
    )

    kept = []
    grads = [None] * CHUNKS

    spread = 2 * part % STRIP == 0 and piece % STRIP == 0 and chips >= 8
    up_owner, _ = owners(0, chip, chip_bits)
    down_owner, down_place = owners(1, chip, chip_bits)
    words = jnp.concatenate([core[None], up_owner, down_owner, down_place]).astype(jnp.int32)

    def feed(t):
        def work():
            if spread:
                up, down = feed_flows[t].result
            else:
                up, down = joined(feed_flows[t])
                up, down = [up.reshape(model, -1)], [down.reshape(-1, model)]
            return feed_forward(norm, norm_t, grad_branch_f, up, down, ffn_taps[t], words)

        return work

    back_flows = [[] for _ in range(CHUNKS)]

    def run_feed(flows, t):
        slot.finish(feed_flows[t : t + 1])
        staying, leaving, up_grad, down_grad, tap_grad = slot(flows, feed(t))
        kept.append((staying, leaving))
        grads[t] = tap_grad
        if spread:
            back_flows[t] = [
                Flow(halving_steps(*grad[::-1], gather_order(chip_bits, colour)[::-1]))
                for colour, grad in enumerate((up_grad, down_grad))
            ]
        else:
            back_flows[t] = [
                sums(up_grad[0].reshape(chips, 2 * part, -1)),
                sums(down_grad[0].reshape(chips, piece, model)),
            ]

    run_feed(feed_flows[1:], 0)
    run_feed(feed_flows[2:] + back_flows[0], 1)
    run_feed(back_flows[0] + back_flows[1], 2)

    def after_feed():
        parts = [array for staying, leaving in kept for array in (staying, swap_core(leaving))]
        return leave_feed(words[:1], canvas, branch_part, branch_other, grad_ph, mods_f, parts)

    layer_out, grad_middle, grad_branch_mine, feed_sums = slot(
        back_flows[0] + back_flows[2], after_feed
    )
    grad_branch_mine = grad_branch_mine.reshape(4, -1, model)
    layer_out = from_phases(layer_out.reshape(4, -1, model), half_rows)[None]

    def enter_attend():
        grad_branch_a = join_halves(grad_branch_mine, swap_core(grad_branch_mine), core)
        grad_attended = jnp.dot(grad_branch_a, proj_full.T, preferred_element_type=full)
        proj_grad = jnp.dot(attended.T, grad_branch_a, preferred_element_type=full)
        return grad_attended.astype(low), proj_grad.astype(low)

    grad_attended, proj_grad = slot(back_flows[0] + back_flows[1], enter_attend)
    proj_grad = proj_grad.reshape(chips, -1, model)
    proj_flow = sums(proj_grad[..., : model // 2], proj_grad[..., model // 2 :])
    grad_qkv = slot(
        [proj_flow] + sum(back_flows, []), lambda: attend_back(mask, qkv, grad_attended)
    )
    qkv_grad = slot(
        [proj_flow] + sum(back_flows, []),
        lambda: jnp.dot(convolved.T, grad_qkv, preferred_element_type=full).astype(low),
    )
    qkv_grad = qkv_grad.reshape(chips, 2 * part, -1)
    qkv_flow = sums(qkv_grad[..., :qkv_half], qkv_grad[..., qkv_half:])

    def rows_near(array, which):
        size = PLANE // 2 + STRIP
        near = lax.dynamic_slice_in_dim(
            array.reshape(4, PLANE, model), which * (PLANE - size), size, axis=1
        )
        return near.reshape(4 * size, model)

    def leave_attend():
        part_here = jnp.dot(grad_qkv, qkv_full.T, preferred_element_type=full).astype(low)
        return rows_near(part_here, core), swap_core(rows_near(part_here, 1 - core))

    grad_conv = slot([qkv_flow, proj_flow] + back_flows[2], leave_attend)

    def leave_block():
        input_grad, attn_tap_grad, mods_grad = conv_back(
            core, rows_near(canvas, core), *grad_conv, attn_taps, mods_a,
            grad_middle,
        )
        return attn_tap_grad[:9], input_grad, mods_grad[:2]

    attn_tap_grad, input_grad, attn_sums = slot(
        [qkv_flow, proj_flow] + back_flows[2], leave_block
    )
    def row_split(array, axis):
        pair = array.reshape((2, part) + array.shape[1:])
        kept, leaving = halves_of(pair, 0)
        arriving = swap_core(leaving)
        return jnp.stack(in_core_order(kept, arriving, core), axis=axis)

    slot.finish(sum(back_flows, []))
    grad_mods = jnp.concatenate([attn_sums, feed_sums[:4]], axis=0)
    tap_grads = [g[:9].reshape(9, chips, piece) for g in grads]
    ffn_tap_grad = jnp.concatenate(tap_grads, axis=2).transpose(1, 0, 2)
    attn_kept, attn_leaving = halves_of(attn_tap_grad.reshape(9, chips, 2, part), 2)

    def between_cores():
        both = (grad_mods + swap_core(grad_mods)).astype(low)
        return both, attn_kept + swap_core(attn_leaving)

    grad_mods, attn_tap_grad = slot([qkv_flow, proj_flow], between_cores)
    mods_flow = row_flow(grad_mods.reshape(-1), chip, chip_bits)
    tap_parts = jnp.concatenate(
        [ffn_tap_grad.reshape(chips, -1), attn_tap_grad.transpose(1, 0, 2).reshape(chips, -1)],
        axis=1,
    )
    tap_flow = scatter_flow([tap_parts], chip, chip_bits, sent=full)
    up_shares = [flows[0].result for flows in back_flows]
    down_shares = [flows[1].result for flows in back_flows]

    def split_up():
        up_all = jnp.stack(up_shares, axis=1).reshape(2 * part, CHUNKS, chips, piece)
        return row_split(up_all.transpose(0, 2, 1, 3), 2).reshape(part, -1)

    slot.finish([proj_flow])
    proj_share = proj_flow.result
    up_share = slot([qkv_flow, mods_flow, tap_flow], split_up)
    slot.finish([qkv_flow])
    qkv_share = qkv_flow.result

    def split_qkv():
        qkv_all = qkv_share.reshape(2 * part, pairs, 3, 128).transpose(0, 2, 1, 3)
        qkv_out = row_split(qkv_all, 2).reshape(part, -1)
        return qkv_out, lax.ppermute(proj_share, AXES, proj_back)

    qkv_out, proj_share = slot([mods_flow, tap_flow], split_qkv)
    slot.finish([mods_flow, tap_flow])
    down_share = jnp.concatenate(down_shares, axis=0)

    grad_mods_all = mods_flow.result
    mod_grad = jnp.dot(lifted.T, grad_mods_all, preferred_element_type=full)
    (cond_grad,) = lift_pull(jnp.dot(grad_mods_all, mod_weight.T, preferred_element_type=full))
    table_grad = jnp.dot(picks.astype(full).T, cond_grad, precision=highest)
    tap_share = tap_flow.result
    ffn_share = tap_share[: 9 * share].reshape(9, share)
    kernel_share = tap_share[9 * share :].reshape(9, part)

    return (
        layer_out,
        input_grad[None],
        mod_grad,
        table_grad,
        kernel_share,
        qkv_out,
        proj_share,
        up_share,
        ffn_share,
        down_share,
        feed_sums[1:2],
    )


def solution(mesh):
    return jax.shard_map(
        on_device,
        mesh=mesh,
        in_specs=(
            P(AXES, None, None),
            P(),
            P(),
            P(),
            P(AXES, None, None),
            P(AXES, None),
            P(None, AXES),
            P(None, AXES),
            P(AXES, None),
            P(AXES, None),
            P(AXES, None),
            P(None, AXES),
            P(AXES, None),
        ),
        out_specs=(
            P(AXES, None, None),
            P(AXES, None, None),
            P(AXES, None),
            P(None, AXES),
            P(None, AXES),
            P(AXES, None),
            P(AXES, None),
            P(AXES, None),
            P(None, AXES),
            P(AXES, None),
            P(AXES, None),
        ),
        check_vma=False,
    )
```

```python
import functools
import math

import jax
import jax.numpy as jnp
from jax import lax
from jax.experimental import pallas as pl
from jax.experimental.pallas import tpu as pltpu
from jax.sharding import PartitionSpec as P

HEAD = 64
SIDE = 32
HALF_SIDE = SIDE // 2
STRIP = HALF_SIDE
PLANE = HALF_SIDE * HALF_SIDE
PADDED = PLANE + 2 * STRIP
TILE = 256
CHUNKS = 3

highest = lax.Precision.HIGHEST
ln_epsilon = 1e-06
masked_score = -1000000000.0
low = jnp.bfloat16
full = jnp.float32
AXES = ("dp", "fsdp")


def device_count():
    return lax.axis_size("dp") * lax.axis_size("fsdp")


def swap(x, bit):
    return lax.ppermute(x, AXES, [(i, i ^ 1 << bit) for i in range(device_count())])


def swap_core(x):
    return swap(x, 0)


def gather_order(chip_bits, colour):
    order = list(range(chip_bits - 1, -1, -1))
    if colour and chip_bits > 1:
        order[-1], order[-2] = order[-2], order[-1]
    return order


class Flow:
    def __init__(self, steps):
        self.steps = steps
        self.wanted = next(steps)
        self.result = None

    def arrive(self, array):
        try:
            self.wanted = self.steps.send(array)
        except StopIteration as end:
            self.wanted, self.result = None, end.value


class Slots:
    def __init__(self, token):
        self.token = token

    def after(self, *arrays):
        arrays, self.token = lax.optimization_barrier((arrays, self.token))
        return arrays

    def finish(self, flows):
        while any(flow.wanted is not None for flow in flows):
            self(flows)

    def __call__(self, flows, work=lambda: ()):
        flows = [flow for flow in flows if flow.wanted is not None]
        wanted = [flow.wanted for flow in flows]
        leaving, self.token = lax.optimization_barrier(
            ([[array for array, _ in pairs] for pairs in wanted], self.token)
        )
        arriving = [
            [swap(array, bit + 1) for array, (_, bit) in zip(arrays, pairs)]
            for arrays, pairs in zip(leaving, wanted)
        ]
        arriving, result, self.token = lax.optimization_barrier((arriving, work(), self.token))
        for flow, arrays in zip(flows, arriving):
            flow.arrive(arrays)
        return result


def join(held, arriving):
    return [jnp.concatenate(pair, axis=0) for pair in zip(held, arriving)]


def near_steps(shards, chip_bits):
    held = [shard[None] for shard in shards]
    for bit in range(chip_bits - 1, 1, -1):
        arriving = yield [(array, bit) for array in held]
        held = join(held, arriving)
    return held


def core_steps(array):
    (arriving,) = yield [(array, -1)]
    return arriving


def far_steps(held):
    arriving = yield [(held[0], 1), (held[1], 0)]
    held = join(held, arriving)
    arriving = yield [(held[0], 0), (held[1], 1)]
    return list(zip(held, arriving))


def assemble_body(steps, chip_ref, *refs):
    *piece_refs, out_ref = refs
    which = pl.program_id(0) // steps
    top = chip_ref[1]
    for index, piece_ref in enumerate(piece_refs):

        @pl.when(which == index)
        def _():
            for k in range(4):
                out_ref[jnp.bitwise_xor(top, (k & 1) << 1 | k >> 1), 0] = piece_ref[k]


def assemble(pieces, order, chip):
    chips = sum(piece.shape[0] for piece in pieces)
    rows, columns = pieces[0].shape[1:]
    if chips < 4 or len(pieces) * pieces[0].shape[0] != chips or pieces[0].shape[0] % 4:
        raise ValueError("unexpected mesh")
    rest = len(order) - 2
    steps = pieces[0].shape[0] // 4
    chip_words = jnp.stack([jnp.bitwise_and(chip, (1 << rest) - 1), chip >> rest]).astype(jnp.int32)

    def out_map(step, words):
        at = words[0]
        for position, bit in enumerate(order[2:]):
            at = jnp.bitwise_xor(at, jnp.bitwise_and(step >> position, 1) << bit)
        return (0, at, 0, 0)

    def piece_map(index):
        return lambda step, words: (jnp.clip(step - index * steps, 0, steps - 1), 0, 0)

    out = pl.pallas_call(
        functools.partial(assemble_body, steps),
        grid_spec=pltpu.PrefetchScalarGridSpec(
            num_scalar_prefetch=1,
            grid=(chips // 4,),
            in_specs=[
                pl.BlockSpec((4, rows, columns), piece_map(index)) for index in range(len(pieces))
            ],
            out_specs=pl.BlockSpec((4, 1, rows, columns), out_map),
        ),
        out_shape=jax.ShapeDtypeStruct((4, chips // 4, rows, columns), pieces[0].dtype),
        cost_estimate=pl.CostEstimate(
            flops=0, bytes_accessed=4 * chips * rows * columns, transcendentals=0
        ),
        name="assemble",
    )(chip_words, *pieces)
    return out.reshape(chips, rows, columns)


def at_bit(array, axis, bit):
    return lax.dynamic_index_in_dim(array, bit, axis, keepdims=False)


def halves_at(held, axis, mine, sent):
    leaving = sum(at_bit(h, axis, 1 - mine).astype(full) for h in held).astype(sent)
    staying = sum(at_bit(h, axis, mine).astype(full) for h in held).astype(sent)
    return leaving, staying


def scatter_steps(parts, chip, chip_bits, sent):
    orders = [gather_order(chip_bits, colour)[::-1] for colour in range(len(parts))]
    lefts = [list(range(chip_bits - 1, -1, -1)) for _ in parts]
    held = [[array.reshape((2,) * chip_bits + array.shape[1:])] for array in parts]
    for step in range(chip_bits):
        if step == 2 and len(held) == 2:
            held = [[jnp.concatenate(pair, axis=-1) for pair in zip(*held)]]
        leaving, staying = [], []
        for order, left, arrays in zip(orders, lefts, held):
            bit = order[step]
            axis = left.index(bit)
            left.remove(bit)
            going, kept = halves_at(arrays, axis, jnp.bitwise_and(chip >> bit, 1), sent)
            leaving.append((going, bit))
            staying.append(kept)
        arriving = yield leaving
        held = [list(pair) for pair in zip(staying, arriving)]
    ((kept, arrived),) = held
    return kept.astype(full) + arrived.astype(full)


def halving_steps(leaving, staying, order):
    (arriving,) = yield [(leaving, order[0])]
    for bit in order[1:]:
        half = staying.shape[0] // 2
        leaving, staying = [
            (staying[at].astype(full) + arriving[at].astype(full)).astype(low)
            for at in (slice(half, None), slice(half))
        ]
        (arriving,) = yield [(leaving, bit)]
    return (staying.astype(full) + arriving.astype(full))[0]


def owners(colour, chip, chip_bits):
    order = gather_order(chip_bits, colour)
    spots = jnp.arange(1 << chip_bits)
    bits = list(enumerate(order))
    owner = sum((jnp.bitwise_and(spots >> at, 1) << bit) for at, bit in bits)
    apart = jnp.bitwise_xor(spots, chip)
    place = sum((jnp.bitwise_and(apart >> bit, 1) << at) for at, bit in bits)
    return jnp.bitwise_xor(owner, chip), place


def scatter_flow(parts, chip, chip_bits, sent=low):
    return Flow(scatter_steps(parts, chip, chip_bits, sent))


def row_steps(row, chip, chip_bits, first_bit):
    held = row[None]
    for bit in range(chip_bits):
        (arriving,) = yield [(held, bit + first_bit - 1)]
        held = jnp.concatenate([held, arriving], axis=0)
    places = jnp.arange(1 << chip_bits)
    pick = jnp.bitwise_xor(places, chip)[:, None] == places[None, :]
    return jnp.dot(pick.astype(held.dtype), held, preferred_element_type=full).astype(held.dtype)


def row_flow(row, chip, chip_bits, first_bit=1):
    return Flow(row_steps(row, chip, chip_bits, first_bit))


def run(flow):
    while flow.wanted is not None:
        flow.arrive([swap(array, bit + 1) for array, bit in flow.wanted])
    return flow.result


def to_phases(block_in, row_count):
    width = block_in.shape[-1]
    split_grid = block_in.reshape(row_count // 2, 2, HALF_SIDE, 2, width)
    return split_grid.transpose(1, 3, 0, 2, 4).reshape(4, row_count // 2 * HALF_SIDE, width)


def from_phases(block_in, row_count):
    width = block_in.shape[-1]
    split_grid = block_in.reshape(2, 2, row_count // 2, HALF_SIDE, width)
    return split_grid.transpose(2, 0, 3, 1, 4).reshape(row_count * SIDE, width)


def in_core_order(mine, other, core):
    return jnp.where(core == 0, mine, other), jnp.where(core == 0, other, mine)


def join_halves(mine, other, core):
    return jnp.stack(in_core_order(mine, other, core), axis=1).reshape(-1, mine.shape[-1])


def half_of(joined, which):
    width = joined.shape[-1]
    return at_bit(joined.reshape(4, 2, -1, width), 1, which)


def layer_norm(values):
    average = jnp.mean(values, axis=-1, keepdims=True)
    centred = values - average
    variance = jnp.mean(centred * centred, axis=-1, keepdims=True)
    return centred * lax.rsqrt(variance + ln_epsilon)


def modulate(values, shift_by, scale_by):
    return layer_norm(values) * (1.0 + scale_by) + shift_by


def sinusoid(steps_in, width):
    halfway = width // 2
    frequency = jnp.exp(-math.log(10000.0) * jnp.arange(halfway, dtype=jnp.float32) / halfway)
    angles = steps_in.astype(jnp.float32)[..., None] * frequency
    return jnp.concatenate([jnp.cos(angles), jnp.sin(angles)], axis=-1)


def softmax_of(query, key, allowed):
    raw = lax.dot_general(query, key, (((1,), (1,)), ((), ())), preferred_element_type=full)
    scores = jnp.where(allowed, raw * HEAD ** (-0.5), masked_score)
    shifted = jnp.exp(scores - jnp.max(scores, axis=-1, keepdims=True))
    return shifted / jnp.sum(shifted, axis=-1, keepdims=True)


def head_lanes(shape, head):
    lanes = lax.broadcasted_iota(jnp.int32, shape, 1)
    return jnp.logical_and(lanes >= head * HEAD, lanes < (head + 1) * HEAD)


def attend_body(mask_ref, qkv_ref, out_ref):
    allowed = mask_ref[...] > 0.5

    @pl.loop(0, 4)
    def _(phase):
        rows = pl.ds(pl.multiple_of(phase * PLANE, PLANE), PLANE)
        query = qkv_ref[rows, :128]
        key = qkv_ref[rows, 128:256]
        value = qkv_ref[rows, 256:]
        total = None
        for head in range(2):
            here = head_lanes(key.shape, head)
            probs = softmax_of(query, jnp.where(here, key, jnp.zeros_like(key)), allowed)
            part = jnp.dot(
                probs.astype(low),
                jnp.where(here, value, jnp.zeros_like(value)),
                preferred_element_type=full,
            )
            total = part if total is None else total + part
        out_ref[rows, :] = total.astype(low)


def attend_back_body(mask_ref, qkv_ref, grad_ref, out_ref):
    allowed = mask_ref[...] > 0.5

    @pl.loop(0, 4)
    def _(phase):
        rows = pl.ds(pl.multiple_of(phase * PLANE, PLANE), PLANE)
        query = qkv_ref[rows, :128]
        key = qkv_ref[rows, 128:256]
        value = qkv_ref[rows, 256:]
        grad = grad_ref[rows, :]
        by_rows = (((0,), (0,)), ((), ()))
        totals = [None, None, None]
        for head in range(2):
            here = head_lanes(key.shape, head)
            blank = jnp.zeros_like(key)
            key_here = jnp.where(here, key, blank)
            query_here = jnp.where(here, query, blank)
            value_here = jnp.where(here, value, blank)
            grad_here = jnp.where(here, grad, blank)
            weights = softmax_of(query, key_here, allowed)
            grad_probs = lax.dot_general(
                grad, value_here, (((1,), (1,)), ((), ())), preferred_element_type=full
            )
            delta = jnp.sum(grad_probs * weights, axis=-1, keepdims=True)
            grad_scores = (weights * (grad_probs - delta)).astype(low)
            parts = (
                jnp.dot(grad_scores, key_here, preferred_element_type=full),
                lax.dot_general(grad_scores, query_here, by_rows, preferred_element_type=full),
                lax.dot_general(
                    weights.astype(low), grad_here, by_rows, preferred_element_type=full
                ),
            )
            totals = [p if t is None else t + p for t, p in zip(totals, parts)]
        out_ref[rows, :128] = (totals[0] * HEAD ** (-0.5)).astype(low)
        out_ref[rows, 128:256] = (totals[1] * HEAD ** (-0.5)).astype(low)
        out_ref[rows, 256:] = totals[2].astype(low)


def attend(mask, qkv):
    tokens, width = qkv.shape
    pairs = width // 384
    return pl.pallas_call(
        attend_body,
        grid=(pairs,),
        in_specs=[
            pl.BlockSpec((PLANE, PLANE), lambda j: (0, 0)),
            pl.BlockSpec((tokens, 384), lambda j: (0, j)),
        ],
        out_specs=pl.BlockSpec((tokens, 128), lambda j: (0, j)),
        out_shape=jax.ShapeDtypeStruct((tokens, pairs * 128), low),
        cost_estimate=pl.CostEstimate(
            flops=pairs * 2 * 4 * 4 * PLANE * PLANE * 256,
            bytes_accessed=8 * tokens * pairs * 128,
            transcendentals=pairs * 8 * PLANE * PLANE,
        ),
        name="attend",
    )(mask, qkv)


def attend_back(mask, qkv, grad):
    tokens, width = qkv.shape
    pairs = width // 384
    return pl.pallas_call(
        attend_back_body,
        grid=(pairs,),
        in_specs=[
            pl.BlockSpec((PLANE, PLANE), lambda j: (0, 0)),
            pl.BlockSpec((tokens, 384), lambda j: (0, j)),
            pl.BlockSpec((tokens, 128), lambda j: (0, j)),
        ],
        out_specs=pl.BlockSpec((tokens, 384), lambda j: (0, j)),
        out_shape=jax.ShapeDtypeStruct((tokens, width), low),
        cost_estimate=pl.CostEstimate(
            flops=pairs * 2 * 4 * 10 * PLANE * PLANE * 256,
            bytes_accessed=14 * tokens * pairs * 128,
            transcendentals=pairs * 8 * PLANE * PLANE,
        ),
        name="attend_back",
    )(mask, qkv, grad)


def strip_at(ref, row_phase, column_phase, row):
    start = pl.multiple_of((row + 1) * STRIP, STRIP)
    return ref[2 * row_phase + column_phase, pl.ds(start, STRIP), :]


def near_strips(ref, row):
    tokens = lax.broadcasted_iota(jnp.int32, (STRIP, ref.shape[-1]), 0)
    loaded = {}
    for row_phase, at in ((1, row - 1), (0, row), (1, row), (0, row + 1)):
        even = strip_at(ref, row_phase, 0, at)
        odd = strip_at(ref, row_phase, 1, at)
        before = jnp.where(tokens == 0, 0.0, pltpu.roll(odd, 1, 0))
        after = jnp.where(tokens == STRIP - 1, 0.0, pltpu.roll(even, STRIP - 1, 0))
        loaded[len(loaded)] = ((before, even, odd), (even, odd, after))
    return {0: (loaded[0], loaded[1], loaded[2]), 1: (loaded[1], loaded[2], loaded[3])}


def conv_strip(near, kernel, row_phase, column_phase):
    total = None
    for i in range(3):
        for j in range(3):
            term = near[row_phase][i][column_phase][j] * kernel[3 * i + j : 3 * i + j + 1, :]
            total = term if total is None else total + term
    return total


def feed_body(
    spread,
    words_ref,
    norm_ref,
    norm_t_ref,
    grad_ref,
    *refs,
):
    pieces = 2 if spread else 1
    up_refs, refs = refs[:pieces], refs[pieces:]
    down_refs, refs = refs[:pieces], refs[pieces:]
    kernel_ref, staying_ref, leaving_ref, *refs = refs
    up_grad_refs, refs = refs[:pieces], refs[pieces:]
    down_grad_refs, refs = refs[:pieces], refs[pieces:]
    kernel_grad_ref, branch_acc, back_acc, hidden, widened_grad, act_grad, act, hidden_grad = refs[
        :8
    ]
    step = pl.program_id(0)
    core = words_ref[0]
    by_columns = (((1,), (1,)), ((), ()))
    width = kernel_ref.shape[1]
    model = norm_t_ref.shape[0]
    up_ref, down_ref = up_refs[0], down_refs[0]
    if spread:
        up_ref, down_all = refs[8:]
        half, share, _ = up_refs[0].shape
        piece = down_refs[0].shape[1]
        chips = 2 * half
        down_ref = down_all.at[pl.ds(pl.multiple_of(step * width, width), width), :]

        for which in range(2):

            @pl.loop(0, half)
            def _(spot):
                start = pl.multiple_of(words_ref[1 + which * half + spot] * share, share)
                up_ref[pl.ds(start, share), :] = up_refs[which][spot]

            @pl.when(step == 0)
            def _():
                @pl.loop(0, half)
                def _(spot):
                    owner = words_ref[1 + chips + which * half + spot]
                    start = pl.multiple_of(owner * piece, piece)
                    down_all[pl.ds(start, piece), :] = down_refs[which][spot]

    @pl.when(step == 0)
    def _():
        blank = jnp.zeros((STRIP, width), full)
        for plane in range(4):
            for ref in (hidden, widened_grad):
                ref[plane, pl.ds(0, STRIP), :] = blank
                ref[plane, pl.ds(PLANE + STRIP, STRIP), :] = blank
        branch_acc[...] = jnp.zeros_like(branch_acc)
        back_acc[...] = jnp.zeros_like(back_acc)

    @pl.loop(0, 4)
    def _(plane):
        rows = pl.ds(pl.multiple_of(plane * PLANE, PLANE), PLANE)
        hidden[plane, pl.ds(STRIP, PLANE), :] = jnp.dot(
            norm_ref[rows, :], up_ref[...], preferred_element_type=full
        )
        act_grad[rows, :] = lax.dot_general(
            grad_ref[rows, :], down_ref[...], by_columns, preferred_element_type=full
        )

    kernel = kernel_ref[...]

    def forward_strip(row, sums):
        near = near_strips(hidden, row)
        sums = list(sums)
        for row_phase in range(2):
            for column_phase in range(2):
                plane = 2 * row_phase + column_phase
                wide = conv_strip(near, kernel, row_phase, column_phase)
                square = wide * wide
                bend = math.sqrt(2.0 / math.pi) * (wide + 0.044715 * wide * square)
                curve = jnp.tanh(bend)
                half = 0.5 * (1.0 + curve)
                slope = half + 0.5 * wide * (1.0 - curve * curve) * (
                    math.sqrt(2.0 / math.pi) * (1.0 + 3 * 0.044715 * square)
                )
                at = pl.ds(pl.multiple_of(plane * PLANE + row * STRIP, STRIP), STRIP)
                act[at, :] = (wide * half).astype(low)
                grad_here = slope * act_grad[at, :]
                widened_grad[plane, pl.ds(pl.multiple_of((row + 1) * STRIP, STRIP), STRIP), :] = (
                    grad_here
                )
                for i in range(3):
                    for j in range(3):
                        product = near[row_phase][i][column_phase][j] * grad_here
                        sums[3 * i + j] = sums[3 * i + j] + (product[:8] + product[8:])
        return tuple(sums)

    sums = lax.fori_loop(
        0, HALF_SIDE, forward_strip, tuple(jnp.zeros((8, width), full) for _ in range(9))
    )
    kernel_grad_ref[...] = jnp.concatenate(
        [jnp.sum(s, axis=0, keepdims=True) for s in sums] + [jnp.zeros((7, width), full)], axis=0
    )

    flipped = [kernel[8 - t : 9 - t, :] for t in range(9)]
    flipped = jnp.concatenate(flipped, axis=0)

    @pl.loop(0, HALF_SIDE)
    def _(row):
        near = near_strips(widened_grad, row)
        for row_phase in range(2):
            for column_phase in range(2):
                plane = 2 * row_phase + column_phase
                at = pl.ds(pl.multiple_of(plane * PLANE + row * STRIP, STRIP), STRIP)
                hidden_grad[at, :] = conv_strip(near, flipped, row_phase, column_phase).astype(low)

    @pl.loop(0, 4)
    def _(plane):
        rows = pl.ds(pl.multiple_of(plane * PLANE, PLANE), PLANE)
        branch_acc[rows, :] += jnp.dot(act[rows, :], down_ref[...], preferred_element_type=full)
        back_acc[rows, :] += lax.dot_general(
            hidden_grad[rows, :], up_ref[...], by_columns, preferred_element_type=full
        )

    if spread:
        for which in range(2):

            @pl.loop(0, half // 4)
            def _(group):
                lhs = []
                for k in range(4):
                    owner = words_ref[1 + which * half + 4 * group + k]
                    start = pl.multiple_of(owner * share, share)
                    lhs.append(norm_t_ref[pl.ds(start, share), :])
                result = jnp.dot(
                    jnp.concatenate(lhs, axis=0), hidden_grad[...], preferred_element_type=full
                ).astype(low)
                for k in range(4):
                    up_grad_refs[which][4 * group + k] = result[k * share : (k + 1) * share]

    else:

        @pl.loop(0, model // TILE)
        def _(tile):
            rows = pl.ds(pl.multiple_of(tile * TILE, TILE), TILE)
            up_grad_refs[0][rows, :] = jnp.dot(
                norm_t_ref[rows, :], hidden_grad[...], preferred_element_type=full
            ).astype(low)

    down_grad = lax.dot_general(
        act[...], grad_ref[...], (((0,), (0,)), ((), ())), preferred_element_type=full
    ).astype(low)
    if spread:
        for k in range(width // piece):
            place = words_ref[1 + 2 * chips + step * (width // piece) + k]
            for which in range(2):

                @pl.when(place // half == which)
                def _():
                    down_grad_refs[which][place - which * half] = down_grad[
                        k * piece : (k + 1) * piece
                    ]

    else:
        down_grad_refs[0][...] = down_grad

    @pl.when(step == pl.num_programs(0) - 1)
    def _():
        for ref, which in ((staying_ref, core), (leaving_ref, 1 - core)):
            for index, acc in enumerate((branch_acc, back_acc)):
                for plane in range(4):
                    start = plane * PLANE + pl.multiple_of(which * (PLANE // 2), PLANE // 2)
                    ref[index, plane] = acc[pl.ds(start, PLANE // 2), :].astype(low)


def feed_forward(norm, norm_t, grad, up, down, kernel, words):
    tokens, model = norm.shape
    channels = kernel.shape[1]
    width = TILE
    spread = len(up) == 2
    whole = lambda j, words: (0, 0)
    half = lambda j, words: (0, 0, 0, 0)
    across = lambda j, words: (0, j)
    once = pl.Buffered(1)
    piece_scratch = []
    if spread:
        deep = lambda j, words: (0, 0, 0)
        up_spec = pl.BlockSpec(up[0].shape[:2] + (width,), lambda j, words: (0, 0, j))
        down_spec = pl.BlockSpec(down[0].shape, deep, pipeline_mode=once)
        down_grad_spec = pl.BlockSpec(down[0].shape, deep)
        piece_scratch = [pltpu.VMEM((model, width), low), pltpu.VMEM((channels, model), low)]
    else:
        up_spec = pl.BlockSpec((model, width), across)
        down_spec = down_grad_spec = pl.BlockSpec((width, model), lambda j, words: (j, 0))
    halves = jax.ShapeDtypeStruct((2, 4, PLANE // 2, model), low)
    like = lambda arrays: [jax.ShapeDtypeStruct(array.shape, low) for array in arrays]
    out = pl.pallas_call(
        functools.partial(feed_body, spread),
        grid_spec=pltpu.PrefetchScalarGridSpec(
            num_scalar_prefetch=1,
            grid=(channels // width,),
            in_specs=[
                pl.BlockSpec((tokens, model), whole, pipeline_mode=once),
                pl.BlockSpec((model, tokens), whole, pipeline_mode=once),
                pl.BlockSpec((tokens, model), whole, pipeline_mode=once),
                *[up_spec] * len(up),
                *[down_spec] * len(down),
                pl.BlockSpec((16, width), across),
            ],
            out_specs=[
                pl.BlockSpec(halves.shape, half),
                pl.BlockSpec(halves.shape, half),
                *[up_spec] * len(up),
                *[down_grad_spec] * len(down),
                pl.BlockSpec((16, width), across),
            ],
            scratch_shapes=[
                pltpu.VMEM((tokens, model), full),
                pltpu.VMEM((tokens, model), full),
                pltpu.VMEM((4, PADDED, width), full),
                pltpu.VMEM((4, PADDED, width), full),
                pltpu.VMEM((tokens, width), full),
                pltpu.VMEM((tokens, width), low),
                pltpu.VMEM((tokens, width), low),
            ]
            + piece_scratch,
        ),
        out_shape=[halves, halves]
        + like(up)
        + like(down)
        + [jax.ShapeDtypeStruct((16, channels), full)],
        compiler_params=pltpu.CompilerParams(vmem_limit_bytes=63 * 1024 * 1024),
        cost_estimate=pl.CostEstimate(
            flops=12 * tokens * model * channels,
            bytes_accessed=8 * model * channels + 10 * tokens * model,
            transcendentals=tokens * channels,
        ),
        name="feed_forward",
    )(words, norm, norm_t, grad, *up, *down, kernel)
    staying, leaving, *grads, kernel_grad = out
    return staying, leaving, grads[: len(up)], grads[len(up) :], kernel_grad


def token_stats(x_ref, average, scale):
    @pl.loop(0, x_ref.shape[0] // STRIP)
    def _(strip):
        rows = pl.ds(pl.multiple_of(strip * STRIP, STRIP), STRIP)
        values = x_ref[rows, :].astype(full)
        mean = jnp.mean(values, axis=-1, keepdims=True)
        centred = values - mean
        variance = jnp.mean(centred * centred, axis=-1, keepdims=True)
        average[rows, :] = jnp.broadcast_to(mean, (STRIP, 128))
        scale[rows, :] = jnp.broadcast_to(lax.rsqrt(variance + ln_epsilon), (STRIP, 128))


def normed_strip(x_ref, average, scale, rows, columns):
    width = columns.size
    wide = lambda ref: jnp.concatenate([ref[rows, :]] * (width // 128), axis=1)
    return (x_ref[rows, columns].astype(full) - wide(average)) * wide(scale)


def frame_zeros(refs):
    for ref in refs:
        blank = jnp.zeros((STRIP, ref.shape[-1]), full)
        for plane in range(4):
            ref[plane, pl.ds(0, STRIP), :] = blank
            ref[plane, pl.ds(ref.shape[1] - STRIP, STRIP), :] = blank


def conv_in_body(x_ref, kernel_ref, mods_ref, out_ref, average, scale, normed):
    step = pl.program_id(0)
    width = out_ref.shape[1]
    columns = pl.ds(pl.multiple_of(step * width, width), width)

    @pl.when(step == 0)
    def _():
        token_stats(x_ref, average, scale)
        frame_zeros([normed])

    shift_by = mods_ref[0:1, :]
    scale_by = 1.0 + mods_ref[1:2, :]

    @pl.loop(0, HALF_SIDE)
    def _(row):
        for plane in range(4):
            rows = pl.ds(pl.multiple_of(plane * PLANE + row * STRIP, STRIP), STRIP)
            normed[plane, pl.ds(pl.multiple_of((row + 1) * STRIP, STRIP), STRIP), :] = (
                normed_strip(x_ref, average, scale, rows, columns) * scale_by + shift_by
            )

    kernel = kernel_ref[...]

    @pl.loop(0, HALF_SIDE)
    def _(row):
        near = near_strips(normed, row)
        for row_phase in range(2):
            for column_phase in range(2):
                plane = 2 * row_phase + column_phase
                at = pl.ds(pl.multiple_of(plane * PLANE + row * STRIP, STRIP), STRIP)
                out_ref[at, :] = conv_strip(near, kernel, row_phase, column_phase).astype(low)


def conv_in(canvas, kernel, mods):
    tokens, model = canvas.shape
    return pl.pallas_call(
        conv_in_body,
        grid=(model // TILE,),
        in_specs=[
            pl.BlockSpec((tokens, model), lambda j: (0, 0), pipeline_mode=pl.Buffered(1)),
            pl.BlockSpec((16, TILE), lambda j: (0, j)),
            pl.BlockSpec((8, TILE), lambda j: (0, j)),
        ],
        out_specs=pl.BlockSpec((tokens, TILE), lambda j: (0, j)),
        out_shape=jax.ShapeDtypeStruct((tokens, model), low),
        scratch_shapes=[
            pltpu.VMEM((tokens, 128), full),
            pltpu.VMEM((tokens, 128), full),
            pltpu.VMEM((4, PADDED, TILE), full),
        ],
        cost_estimate=pl.CostEstimate(
            flops=30 * tokens * model, bytes_accessed=4 * tokens * model, transcendentals=tokens
        ),
        name="conv_in",
    )(canvas, kernel, mods)


def conv_back_body(
    core_ref,
    x_ref,
    kept_ref,
    arriving_ref,
    kernel_ref,
    mods_ref,
    middle_ref,
    out_ref,
    kernel_grad_ref,
    mods_grad_ref,
    average,
    scale,
    normed,
    upstream,
    held,
    sum_plain,
    sum_normed,
    woven,
):
    step = pl.program_id(0)
    core = core_ref[0]
    width = kept_ref.shape[1]
    near_rows = x_ref.shape[0] // 4 // STRIP
    own_rows = near_rows - 1
    columns = pl.ds(pl.multiple_of(step * width, width), width)

    def near_at(plane, row):
        return pl.ds(pl.multiple_of((plane * near_rows + row) * STRIP, STRIP), STRIP)

    def own_at(plane, row):
        return pl.ds(pl.multiple_of((plane * own_rows + row) * STRIP, STRIP), STRIP)

    @pl.when(step == 0)
    def _():
        token_stats(x_ref, average, scale)
        frame_zeros([normed, upstream])
        sum_plain[...] = jnp.zeros_like(sum_plain)
        sum_normed[...] = jnp.zeros_like(sum_normed)

    shift_by = mods_ref[0:1, :]
    scale_by = 1.0 + mods_ref[1:2, :]

    @pl.loop(0, near_rows)
    def _(row):
        for plane in range(4):
            rows = near_at(plane, row)
            padded = pl.ds(pl.multiple_of((row + 1) * STRIP, STRIP), STRIP)
            normed[plane, padded, :] = (
                normed_strip(x_ref, average, scale, rows, columns) * scale_by + shift_by
            )
            upstream[plane, padded, :] = kept_ref[rows, :].astype(full) + arriving_ref[
                rows, :
            ].astype(full)

    kernel = kernel_ref[...]
    flipped = jnp.concatenate([kernel[8 - t : 9 - t, :] for t in range(9)], axis=0)

    def kernel_strip(row, sums):
        near = near_strips(normed, row + core)
        sums = list(sums)
        for row_phase in range(2):
            for column_phase in range(2):
                grad_here = strip_at(upstream, row_phase, column_phase, row + core)
                for i in range(3):
                    for j in range(3):
                        product = near[row_phase][i][column_phase][j] * grad_here
                        sums[3 * i + j] = sums[3 * i + j] + (product[:8] + product[8:])
        return tuple(sums)

    def fold(sums, rows):
        return jnp.concatenate(
            [jnp.sum(s, axis=0, keepdims=True) for s in sums]
            + [jnp.zeros((rows - len(sums), width), full)],
            axis=0,
        )

    blank = jnp.zeros((8, width), full)
    kernel_grad_ref[...] = fold(lax.fori_loop(0, own_rows, kernel_strip, (blank,) * 9), 16)

    def input_strip(row, sums):
        near = near_strips(upstream, row + core)
        shift_sum, scale_sum = sums
        for row_phase in range(2):
            for column_phase in range(2):
                plane = 2 * row_phase + column_phase
                grad = conv_strip(near, flipped, row_phase, column_phase)
                plain = normed_strip(x_ref, average, scale, near_at(plane, row + core), columns)
                shift_sum = shift_sum + (grad[:8] + grad[8:])
                product = grad * plain
                scale_sum = scale_sum + (product[:8] + product[8:])
                scaled = grad * scale_by
                rows = own_at(plane, row)
                held[step, rows, :] = scaled
                product = scaled * plain
                sum_plain[rows, :] += sum(scaled[:, k : k + 128] for k in range(0, width, 128))
                sum_normed[rows, :] += sum(product[:, k : k + 128] for k in range(0, width, 128))
        return shift_sum, scale_sum

    mods_grad_ref[...] = fold(lax.fori_loop(0, own_rows, input_strip, (blank,) * 2), 8)

    @pl.when(step == pl.num_programs(0) - 1)
    def _():
        model = x_ref.shape[1]

        @pl.loop(0, own_rows)
        def _(row):
            for plane in range(4):
                rows = own_at(plane, row)
                near = near_at(plane, row + core)
                mean_plain = jnp.sum(sum_plain[rows, :], axis=-1, keepdims=True) / model
                mean_normed = jnp.sum(sum_normed[rows, :], axis=-1, keepdims=True) / model
                for block in range(model // width):
                    at = pl.ds(block * width, width)
                    plain = normed_strip(x_ref, average, scale, near, at)
                    spread = jnp.concatenate([scale[near, :]] * (width // 128), axis=1)
                    result = middle_ref[rows, at] + spread * (
                        held[block, rows, :] - mean_plain - plain * mean_normed
                    )
                    for lane in range(0, width, 128):
                        woven[(block * width + lane) // 128, pl.ds(plane % 2, STRIP, stride=2), :] = (
                            result[:, lane : lane + 128]
                        )
                if plane % 2 == 1:
                    start = pl.multiple_of((2 * row + plane // 2) * SIDE, SIDE)
                    for lane in range(model // 128):
                        out_ref[pl.ds(start, SIDE), lane * 128 : lane * 128 + 128] = woven[lane]


def conv_back(core, x_near, kept, arriving, kernel, mods, grad_middle):
    near_tokens, model = x_near.shape
    own_tokens = grad_middle.shape[0]
    once = pl.Buffered(1)
    whole = lambda j, words: (0, 0)
    across = lambda j, words: (0, j)
    padded = near_tokens // 4 + 2 * STRIP
    return pl.pallas_call(
        conv_back_body,
        grid_spec=pltpu.PrefetchScalarGridSpec(
            num_scalar_prefetch=1,
            grid=(model // TILE,),
            in_specs=[
                pl.BlockSpec((near_tokens, model), whole, pipeline_mode=once),
                pl.BlockSpec((near_tokens, TILE), across),
                pl.BlockSpec((near_tokens, TILE), across),
                pl.BlockSpec((16, TILE), across),
                pl.BlockSpec((8, TILE), across),
                pl.BlockSpec((own_tokens, model), whole, pipeline_mode=once),
            ],
            out_specs=[
                pl.BlockSpec((own_tokens, model), whole),
                pl.BlockSpec((16, TILE), across),
                pl.BlockSpec((8, TILE), across),
            ],
            scratch_shapes=[
                pltpu.VMEM((near_tokens, 128), full),
                pltpu.VMEM((near_tokens, 128), full),
                pltpu.VMEM((4, padded, TILE), full),
                pltpu.VMEM((4, padded, TILE), full),
                pltpu.VMEM((model // TILE, own_tokens, TILE), full),
                pltpu.VMEM((own_tokens, 128), full),
                pltpu.VMEM((own_tokens, 128), full),
                pltpu.VMEM((model // 128, SIDE, 128), full),
            ],
        ),
        out_shape=[
            jax.ShapeDtypeStruct((own_tokens, model), full),
            jax.ShapeDtypeStruct((16, model), full),
            jax.ShapeDtypeStruct((8, model), full),
        ],
        cost_estimate=pl.CostEstimate(
            flops=70 * own_tokens * model,
            bytes_accessed=14 * own_tokens * model,
            transcendentals=near_tokens,
        ),
        name="conv_back",
    )(core[None].astype(jnp.int32), x_near, kept, arriving, kernel, mods, grad_middle)


def row_stats(values):
    mean = jnp.mean(values, axis=-1, keepdims=True)
    centred = values - mean
    scale = lax.rsqrt(jnp.mean(centred * centred, axis=-1, keepdims=True) + ln_epsilon)
    return centred * scale, scale


def enter_feed_body(x_ref, part_ref, other_ref, grad_ref, mods_ref, norm_ref, norm_t_ref, out_ref):
    @pl.loop(0, x_ref.shape[0] // STRIP)
    def _(strip):
        rows = pl.ds(pl.multiple_of(strip * STRIP, STRIP), STRIP)
        branch = part_ref[rows, :].astype(full) + other_ref[rows, :].astype(full)
        plain, _ = row_stats(x_ref[rows, :].astype(full) + mods_ref[0:1, :] * branch)
        normed = plain * (1.0 + mods_ref[2:3, :]) + mods_ref[1:2, :]
        norm_ref[rows, :] = normed.astype(low)
        out_ref[rows, :] = (grad_ref[rows, :].astype(full) * mods_ref[3:4, :]).astype(low)

    norm_t_ref[...] = norm_ref[...].T


def enter_feed(canvas, part, other, grad, mods):
    tokens, model = canvas.shape
    rows = PLANE // 2
    along = pl.BlockSpec((rows, model), lambda j: (j, 0))
    return pl.pallas_call(
        enter_feed_body,
        grid=(tokens // rows,),
        in_specs=[along] * 4 + [pl.BlockSpec((8, model), lambda j: (0, 0))],
        out_specs=[along, pl.BlockSpec((model, rows), lambda j: (0, j)), along],
        out_shape=[
            jax.ShapeDtypeStruct((tokens, model), low),
            jax.ShapeDtypeStruct((model, tokens), low),
            jax.ShapeDtypeStruct((tokens, model), low),
        ],
        cost_estimate=pl.CostEstimate(flops=1000, bytes_accessed=1000, transcendentals=0),
        name="enter_feed",
    )(canvas, part, other, grad, mods)


def leave_feed_body(words_ref, x_ref, part_ref, other_ref, grad_ref, mods_ref, *refs):
    *kept_refs, out_ref, middle_grad_ref, branch_grad_ref, sums_ref, totals = refs
    plane = pl.program_id(0)

    @pl.when(plane == 0)
    def _():
        totals[...] = jnp.zeros_like(totals)

    @pl.loop(0, x_ref.shape[0] // STRIP)
    def _(strip):
        rows = pl.ds(pl.multiple_of(strip * STRIP, STRIP), STRIP)
        gate_a, gate_f = mods_ref[0:1, :], mods_ref[3:4, :]
        branch_a = part_ref[rows, :].astype(full) + other_ref[rows, :].astype(full)
        middle = x_ref[rows, :].astype(full) + gate_a * branch_a
        plain, scale = row_stats(middle)
        branch_f = sum(ref[0, 0, rows, :].astype(full) for ref in kept_refs)
        back = sum(ref[1, 0, rows, :].astype(full) for ref in kept_refs)
        grad = grad_ref[rows, :].astype(full)
        out_ref[rows, :] = (middle + gate_f * branch_f).astype(low)
        scaled = back * (1.0 + mods_ref[2:3, :])
        mean_plain = jnp.mean(scaled, axis=-1, keepdims=True)
        mean_normed = jnp.mean(scaled * plain, axis=-1, keepdims=True)
        grad_middle = grad + scale * (scaled - mean_plain - plain * mean_normed)
        middle_grad_ref[rows, :] = grad_middle
        branch_grad_ref[rows, :] = (grad_middle * gate_a).astype(low)
        products = (grad_middle * branch_a, back, back * plain, grad * branch_f)
        for index, product in enumerate(products):
            totals[index] += product[:8] + product[8:]

    @pl.when(plane == pl.num_programs(0) - 1)
    def _():
        lines = [jnp.sum(totals[k], axis=0, keepdims=True) for k in range(4)]
        sums_ref[...] = jnp.concatenate(lines + [jnp.zeros_like(sums_ref[:4])], axis=0)


def leave_feed(words, canvas, part, other, grad, mods, kept):
    model = canvas.shape[1]
    rows = PLANE // 2
    own = pl.BlockSpec((rows, model), lambda j, words: (2 * j + words[0], 0))
    half = pl.BlockSpec((rows, model), lambda j, words: (j, 0))
    whole = pl.BlockSpec((8, model), lambda j, words: (0, 0))
    return pl.pallas_call(
        leave_feed_body,
        grid_spec=pltpu.PrefetchScalarGridSpec(
            num_scalar_prefetch=1,
            grid=(4,),
            in_specs=[own] * 4
            + [whole]
            + [pl.BlockSpec((2, 1, rows, model), lambda j, words: (0, j, 0, 0))] * len(kept),
            out_specs=[half, half, half, whole],
            scratch_shapes=[pltpu.VMEM((4, 8, model), full)],
        ),
        out_shape=[
            jax.ShapeDtypeStruct((4 * rows, model), low),
            jax.ShapeDtypeStruct((4 * rows, model), full),
            jax.ShapeDtypeStruct((4 * rows, model), low),
            jax.ShapeDtypeStruct((8, model), full),
        ],
        cost_estimate=pl.CostEstimate(flops=1000, bytes_accessed=1000, transcendentals=0),
        name="leave_feed",
    )(words, canvas, part, other, grad, mods, *kept)


def on_device(
    tokens,
    seg_ids,
    timesteps,
    labels,
    cotangent,
    mod_weight,
    class_table,
    attn_kernel,
    qkv_weight,
    proj_weight,
    up_weight,
    ffn_kernel,
    down_weight,
):
    devices = device_count()
    chips = devices // 2
    chip_bits = chips.bit_length() - 1
    rank = lax.axis_index("dp") * lax.axis_size("fsdp") + lax.axis_index("fsdp")
    core = rank % 2
    chip = rank // 2
    _, half_tokens, model = tokens.shape
    half_rows = half_tokens // SIDE
    class_count = class_table.shape[0]
    part = model // devices
    share = down_weight.shape[0]
    piece = share // CHUNKS
    pairs = model // HEAD // 4

    def halves_of(array, axis):
        return at_bit(array, axis, core), at_bit(array, axis, 1 - core)

    def row_pair(array, axis):
        kept, leaving = halves_of(array, axis)
        arriving = swap_core(leaving)
        return jnp.concatenate(in_core_order(kept, arriving, core), axis=0)

    qkv_split = qkv_weight.reshape(part, 3, 2, pairs, 128).transpose(0, 2, 3, 1, 4)
    qkv_rows = row_pair(qkv_split.reshape(part, 2, pairs * 384), 1)
    qkv_half = pairs * 384 // 2

    picks = labels[:, None] == jnp.arange(class_count)[None, :]
    angles_here = lax.dynamic_slice_in_dim(sinusoid(timesteps, model), rank * part, part, axis=1)
    cond = angles_here + jnp.dot(picks.astype(low), class_table, preferred_element_type=full)
    lift_value, lift_pull = jax.vjp(jax.nn.silu, cond)
    lifted = lift_value.astype(low)
    mods_part = jnp.dot(lifted, mod_weight, preferred_element_type=full)

    slot = Slots(jnp.zeros((8, 128), full))
    near = lambda *shards: Flow(near_steps(shards, chip_bits))
    sums = lambda *parts: scatter_flow(parts, chip, chip_bits)
    joined = lambda flow: [
        assemble(pieces, gather_order(chip_bits, colour), chip)
        for colour, pieces in enumerate(flow.result)
    ]
    mods_flow = scatter_flow([mods_part], chip, chip_bits, sent=full)
    qkv_near = near(qkv_rows)
    mine, upstream = slot(
        [qkv_near, mods_flow],
        lambda: (to_phases(tokens[0], half_rows), to_phases(cotangent[0], half_rows)),
    )

    up_weight, proj_weight, ffn_kernel, attn_kernel = slot.after(
        up_weight, proj_weight, ffn_kernel, attn_kernel
    )
    up_split = up_weight.reshape(part, chips, 2, CHUNKS, piece).transpose(0, 2, 3, 1, 4)
    up_rows = row_pair(up_split.reshape(part, 2, CHUNKS, chips * piece), 1)
    proj_there = [(r, r % chips * 2 + r // chips) for r in range(devices)]
    proj_back = [(b, a) for a, b in proj_there]
    proj_rows = lax.ppermute(proj_weight, AXES, proj_there)
    proj_near = near(proj_rows)
    canvas = slot(
        [qkv_near, mods_flow, proj_near], lambda: join_halves(mine, swap_core(mine), core)
    )
    slot.finish([qkv_near])
    tap_count = 9 * (share + part)
    tap_words = jnp.concatenate([ffn_kernel.reshape(-1), attn_kernel.reshape(-1)])
    tap_words = jnp.pad(tap_words, (0, -tap_count % 128))
    taps = run(row_flow(tap_words, rank, chip_bits + 1, 0))
    ffn_taps = taps[:, : 9 * share].reshape(chips, 2, 9, share)
    ffn_taps = at_bit(ffn_taps, 1, core).reshape(chips, 9, CHUNKS, piece)
    ffn_taps = ffn_taps.transpose(2, 1, 0, 3).reshape(CHUNKS, 9, chips * piece).astype(full)
    ffn_taps = jnp.pad(ffn_taps, ((0, 0), (0, 7), (0, 0)))
    attn_taps = taps[:, 9 * share : tap_count].reshape(devices, 9, part)
    attn_taps = attn_taps.transpose(1, 0, 2).reshape(9, model).astype(full)
    attn_taps = jnp.pad(attn_taps, ((0, 7), (0, 0)))

    spot = jnp.arange(PLANE)
    quadrant = 2 * (spot // (PLANE // 2)) + spot % HALF_SIDE // (HALF_SIDE // 2)
    quadrants_here = at_bit(seg_ids, 0, chip)
    segment = jnp.sum(
        jnp.where(quadrant[:, None] == jnp.arange(4)[None, :], quadrants_here[None, :], 0), axis=1
    )
    mask = (segment[:, None] == segment[None, :]).astype(full)

    def far(arrays, where):
        return Flow(far_steps([array[at] for array, at in zip(arrays, where)]))

    wide = chips * piece
    later = range(CHUNKS - 1)
    feed_near = [
        near(up_rows[:, 0], down_weight[:piece]),
        near(up_rows[:, 1:].reshape(2 * part, -1), down_weight[piece:]),
    ]
    left, right = (Ellipsis, slice(qkv_half)), (Ellipsis, slice(qkv_half, None))
    qkv_flow = far(qkv_near.result * 2, (left, right))
    slot([qkv_flow, mods_flow, proj_near, feed_near[0]])
    mods_half = run(mods_flow)
    mods = mods_half + swap_core(mods_half)
    shift_a, scale_a, gate_a, shift_f, scale_f, gate_f = jnp.split(mods, 6)

    mods_a = jnp.concatenate([shift_a[None], scale_a[None], jnp.zeros((6, model), full)], axis=0)

    slot.finish([proj_near])
    left, right = (Ellipsis, slice(model // 2)), (Ellipsis, slice(model // 2, None))
    proj_flow = far(proj_near.result * 2, (left, right))
    convolved = slot(
        [qkv_flow, proj_flow, feed_near[0]], lambda: conv_in(canvas, attn_taps, mods_a)
    )
    slot.finish([qkv_flow, feed_near[0]])
    feed_flows = [far(feed_near[0].result, (Ellipsis, Ellipsis))]

    def project_in():
        weight = jnp.concatenate(
            [array.reshape(model, qkv_half) for array in joined(qkv_flow)], axis=1
        )
        return weight, jnp.dot(convolved, weight, preferred_element_type=full).astype(low)

    qkv_full, qkv = slot([proj_flow, feed_flows[0], feed_near[1]], project_in)
    (upstream,) = slot.after(upstream)
    grad_ph = join_halves(upstream, swap_core(upstream), core)
    slot.finish([proj_flow])

    def attend_and_assemble():
        weight = jnp.concatenate(
            [array.reshape(-1, model // 2) for array in joined(proj_flow)], axis=1
        )
        return attend(mask, qkv), weight

    attended, proj_full = slot([feed_flows[0], feed_near[1]], attend_and_assemble)
    slot.finish([feed_near[1]])
    for t in later:
        columns, rows = slice(t * wide, t * wide + wide), slice(t * piece, t * piece + piece)
        feed_flows.append(far(feed_near[1].result, ((Ellipsis, columns), (slice(None), rows))))

    mods_f = jnp.concatenate(
        [gate_a[None], shift_f[None], scale_f[None], gate_f[None], jnp.zeros((4, model), full)]
    )

    def project_out():
        branch_part = jnp.dot(attended, proj_full, preferred_element_type=full).astype(low)
        other = swap_core(branch_part)
        return branch_part, other, *enter_feed(canvas, branch_part, other, grad_ph, mods_f)

    branch_part, branch_other, norm, norm_t, grad_branch_f = slot(feed_flows[:2], project_out)

    kept = []
    grads = [None] * CHUNKS

    spread = 2 * part % STRIP == 0 and piece % STRIP == 0 and chips >= 8
    up_owner, _ = owners(0, chip, chip_bits)
    down_owner, down_place = owners(1, chip, chip_bits)
    words = jnp.concatenate([core[None], up_owner, down_owner, down_place]).astype(jnp.int32)

    def feed(t):
        def work():
            if spread:
                up, down = feed_flows[t].result
            else:
                up, down = joined(feed_flows[t])
                up, down = [up.reshape(model, -1)], [down.reshape(-1, model)]
            return feed_forward(norm, norm_t, grad_branch_f, up, down, ffn_taps[t], words)

        return work

    back_flows = [[] for _ in range(CHUNKS)]

    def run_feed(flows, t):
        slot.finish(feed_flows[t : t + 1])
        staying, leaving, up_grad, down_grad, tap_grad = slot(flows, feed(t))
        kept.append((staying, Flow(core_steps(leaving))))
        grads[t] = tap_grad
        if spread:
            back_flows[t] = [
                Flow(halving_steps(*grad[::-1], gather_order(chip_bits, colour)[::-1]))
                for colour, grad in enumerate((up_grad, down_grad))
            ]
        else:
            back_flows[t] = [
                sums(up_grad[0].reshape(chips, 2 * part, -1)),
                sums(down_grad[0].reshape(chips, piece, model)),
            ]

    run_feed(feed_flows[1:], 0)
    run_feed(feed_flows[2:] + back_flows[0] + [kept[0][1]], 1)
    run_feed(back_flows[0] + back_flows[1] + [kept[1][1]], 2)

    def after_feed():
        parts = [array for staying, exchange in kept for array in (staying, run(exchange))]
        return leave_feed(words[:1], canvas, branch_part, branch_other, grad_ph, mods_f, parts)

    layer_out, grad_middle, grad_branch_mine, feed_sums = slot(
        back_flows[0] + back_flows[2], after_feed
    )
    grad_branch_mine = grad_branch_mine.reshape(4, -1, model)
    layer_out = from_phases(layer_out.reshape(4, -1, model), half_rows)[None]

    def enter_attend():
        grad_branch_a = join_halves(grad_branch_mine, swap_core(grad_branch_mine), core)
        grad_attended = jnp.dot(grad_branch_a, proj_full.T, preferred_element_type=full)
        proj_grad = jnp.dot(attended.T, grad_branch_a, preferred_element_type=full)
        return grad_attended.astype(low), proj_grad.astype(low)

    grad_attended, proj_grad = slot(back_flows[0] + back_flows[1], enter_attend)
    proj_grad = proj_grad.reshape(chips, -1, model)
    proj_flow = sums(proj_grad[..., : model // 2], proj_grad[..., model // 2 :])
    grad_qkv = slot(
        [proj_flow] + back_flows[1] + back_flows[2], lambda: attend_back(mask, qkv, grad_attended)
    )
    qkv_grad = slot(
        [proj_flow] + back_flows[1],
        lambda: jnp.dot(convolved.T, grad_qkv, preferred_element_type=full).astype(low),
    )
    qkv_grad = qkv_grad.reshape(chips, 2 * part, -1)
    qkv_flow = sums(qkv_grad[..., :qkv_half], qkv_grad[..., qkv_half:])

    def rows_near(array, which):
        size = PLANE // 2 + STRIP
        near = lax.dynamic_slice_in_dim(
            array.reshape(4, PLANE, model), which * (PLANE - size), size, axis=1
        )
        return near.reshape(4 * size, model)

    def leave_attend():
        part_here = jnp.dot(grad_qkv, qkv_full.T, preferred_element_type=full).astype(low)
        return rows_near(part_here, core), swap_core(rows_near(part_here, 1 - core))

    grad_conv = slot([qkv_flow] + back_flows[2], leave_attend)

    def leave_block():
        input_grad, attn_tap_grad, mods_grad = conv_back(
            core, rows_near(canvas, core), *grad_conv, attn_taps, mods_a,
            grad_middle,
        )
        return attn_tap_grad[:9], input_grad, mods_grad[:2]

    attn_tap_grad, input_grad, attn_sums = slot(
        [qkv_flow, proj_flow] + back_flows[2], leave_block
    )
    def row_split(array, axis):
        pair = array.reshape((2, part) + array.shape[1:])
        kept, leaving = halves_of(pair, 0)
        arriving = swap_core(leaving)
        return jnp.stack(in_core_order(kept, arriving, core), axis=axis)

    slot.finish(sum(back_flows, []))
    grad_mods = jnp.concatenate([attn_sums, feed_sums[:4]], axis=0)
    tap_grads = [g[:9].reshape(9, chips, piece) for g in grads]
    ffn_tap_grad = jnp.concatenate(tap_grads, axis=2).transpose(1, 0, 2)
    attn_kept, attn_leaving = halves_of(attn_tap_grad.reshape(9, chips, 2, part), 2)

    def between_cores():
        both = (grad_mods + swap_core(grad_mods)).astype(low)
        return both, attn_kept + swap_core(attn_leaving)

    grad_mods, attn_tap_grad = slot([qkv_flow, proj_flow], between_cores)
    mods_flow = row_flow(grad_mods.reshape(-1), chip, chip_bits)
    tap_parts = jnp.concatenate(
        [ffn_tap_grad.reshape(chips, -1), attn_tap_grad.transpose(1, 0, 2).reshape(chips, -1)],
        axis=1,
    )
    tap_flow = scatter_flow([tap_parts], chip, chip_bits, sent=full)
    up_shares = [flows[0].result for flows in back_flows]
    down_shares = [flows[1].result for flows in back_flows]

    def split_up():
        up_all = jnp.stack(up_shares, axis=1).reshape(2 * part, CHUNKS, chips, piece)
        return row_split(up_all.transpose(0, 2, 1, 3), 2).reshape(part, -1)

    slot.finish([proj_flow])
    proj_share = proj_flow.result
    up_share = slot([qkv_flow, mods_flow, tap_flow], split_up)
    slot.finish([qkv_flow])
    qkv_share = qkv_flow.result

    def split_qkv():
        qkv_all = qkv_share.reshape(2 * part, pairs, 3, 128).transpose(0, 2, 1, 3)
        qkv_out = row_split(qkv_all, 2).reshape(part, -1)
        return qkv_out, lax.ppermute(proj_share, AXES, proj_back)

    qkv_out, proj_share = slot([mods_flow, tap_flow], split_qkv)
    slot.finish([mods_flow, tap_flow])
    down_share = jnp.concatenate(down_shares, axis=0)

    grad_mods_all = mods_flow.result
    mod_grad = jnp.dot(lifted.T, grad_mods_all, preferred_element_type=full)
    (cond_grad,) = lift_pull(jnp.dot(grad_mods_all, mod_weight.T, preferred_element_type=full))
    table_grad = jnp.dot(picks.astype(full).T, cond_grad, precision=highest)
    tap_share = tap_flow.result
    ffn_share = tap_share[: 9 * share].reshape(9, share)
    kernel_share = tap_share[9 * share :].reshape(9, part)

    return (
        layer_out,
        input_grad[None],
        mod_grad,
        table_grad,
        kernel_share,
        qkv_out,
        proj_share,
        up_share,
        ffn_share,
        down_share,
        feed_sums[1:2],
    )


def solution(mesh):
    return jax.shard_map(
        on_device,
        mesh=mesh,
        in_specs=(
            P(AXES, None, None),
            P(),
            P(),
            P(),
            P(AXES, None, None),
            P(AXES, None),
            P(None, AXES),
            P(None, AXES),
            P(AXES, None),
            P(AXES, None),
            P(AXES, None),
            P(None, AXES),
            P(AXES, None),
        ),
        out_specs=(
            P(AXES, None, None),
            P(AXES, None, None),
            P(AXES, None),
            P(None, AXES),
            P(None, AXES),
            P(AXES, None),
            P(AXES, None),
            P(AXES, None),
            P(None, AXES),
            P(AXES, None),
            P(AXES, None),
        ),
        check_vma=False,
    )
```

```python
import functools
import math

import jax
import jax.numpy as jnp
from jax import lax
from jax.experimental import pallas as pl
from jax.experimental.pallas import tpu as pltpu
from jax.sharding import PartitionSpec as P

HEAD = 64
SIDE = 32
HALF_SIDE = SIDE // 2
STRIP = HALF_SIDE
PLANE = HALF_SIDE * HALF_SIDE
PADDED = PLANE + 2 * STRIP
TILE = 256
CHUNKS = 3

highest = lax.Precision.HIGHEST
ln_epsilon = 1e-06
masked_score = -1000000000.0
low = jnp.bfloat16
full = jnp.float32
AXES = ("dp", "fsdp")


def device_count():
    return lax.axis_size("dp") * lax.axis_size("fsdp")


def swap(x, bit):
    return lax.ppermute(x, AXES, [(i, i ^ 1 << bit) for i in range(device_count())])


def swap_core(x):
    return swap(x, 0)


def gather_order(chip_bits, colour):
    order = list(range(chip_bits - 1, -1, -1))
    if colour and chip_bits > 1:
        order[-1], order[-2] = order[-2], order[-1]
    return order


class Flow:
    def __init__(self, steps):
        self.steps = steps
        self.wanted = next(steps)
        self.result = None

    def arrive(self, array):
        try:
            self.wanted = self.steps.send(array)
        except StopIteration as end:
            self.wanted, self.result = None, end.value


class Slots:
    def __init__(self, token):
        self.token = token

    def after(self, *arrays):
        arrays, self.token = lax.optimization_barrier((arrays, self.token))
        return arrays

    def finish(self, flows):
        while any(flow.wanted is not None for flow in flows):
            self(flows)

    def __call__(self, flows, work=lambda: ()):
        flows = [flow for flow in flows if flow.wanted is not None]
        wanted = [flow.wanted for flow in flows]
        leaving, self.token = lax.optimization_barrier(
            ([[array for array, _ in pairs] for pairs in wanted], self.token)
        )
        arriving = [
            [swap(array, bit + 1) for array, (_, bit) in zip(arrays, pairs)]
            for arrays, pairs in zip(leaving, wanted)
        ]
        arriving, result, self.token = lax.optimization_barrier((arriving, work(), self.token))
        for flow, arrays in zip(flows, arriving):
            flow.arrive(arrays)
        return result


def join(held, arriving):
    return [jnp.concatenate(pair, axis=0) for pair in zip(held, arriving)]


def near_steps(shards, chip_bits):
    held = [shard[None] for shard in shards]
    for bit in range(chip_bits - 1, 1, -1):
        arriving = yield [(array, bit) for array in held]
        held = join(held, arriving)
    return held


def one_colour_steps(shard, chip_bits):
    held = shard[None]
    for bit in range(chip_bits - 1, 0, -1):
        (arriving,) = yield [(held, bit)]
        held = jnp.concatenate([held, arriving], axis=0)
    (arriving,) = yield [(held, 0)]
    return held, arriving


def core_steps(array):
    (arriving,) = yield [(array, -1)]
    return arriving


def far_steps(held):
    arriving = yield [(held[0], 1), (held[1], 0)]
    held = join(held, arriving)
    arriving = yield [(held[0], 0), (held[1], 1)]
    return list(zip(held, arriving))


def assemble_body(steps, chip_ref, *refs):
    *piece_refs, out_ref = refs
    which = pl.program_id(0) // steps
    top = chip_ref[1]
    for index, piece_ref in enumerate(piece_refs):

        @pl.when(which == index)
        def _():
            for k in range(4):
                out_ref[jnp.bitwise_xor(top, (k & 1) << 1 | k >> 1), 0] = piece_ref[k]


def assemble(pieces, order, chip):
    chips = sum(piece.shape[0] for piece in pieces)
    rows, columns = pieces[0].shape[1:]
    if chips < 4 or len(pieces) * pieces[0].shape[0] != chips or pieces[0].shape[0] % 4:
        raise ValueError("unexpected mesh")
    rest = len(order) - 2
    steps = pieces[0].shape[0] // 4
    chip_words = jnp.stack([jnp.bitwise_and(chip, (1 << rest) - 1), chip >> rest]).astype(jnp.int32)

    def out_map(step, words):
        at = words[0]
        for position, bit in enumerate(order[2:]):
            at = jnp.bitwise_xor(at, jnp.bitwise_and(step >> position, 1) << bit)
        return (0, at, 0, 0)

    def piece_map(index):
        return lambda step, words: (jnp.clip(step - index * steps, 0, steps - 1), 0, 0)

    out = pl.pallas_call(
        functools.partial(assemble_body, steps),
        grid_spec=pltpu.PrefetchScalarGridSpec(
            num_scalar_prefetch=1,
            grid=(chips // 4,),
            in_specs=[
                pl.BlockSpec((4, rows, columns), piece_map(index)) for index in range(len(pieces))
            ],
            out_specs=pl.BlockSpec((4, 1, rows, columns), out_map),
        ),
        out_shape=jax.ShapeDtypeStruct((4, chips // 4, rows, columns), pieces[0].dtype),
        cost_estimate=pl.CostEstimate(
            flops=0, bytes_accessed=4 * chips * rows * columns, transcendentals=0
        ),
        name="assemble",
    )(chip_words, *pieces)
    return out.reshape(chips, rows, columns)


def at_bit(array, axis, bit):
    return lax.dynamic_index_in_dim(array, bit, axis, keepdims=False)


def halves_at(held, axis, mine, sent):
    leaving = sum(at_bit(h, axis, 1 - mine).astype(full) for h in held).astype(sent)
    staying = sum(at_bit(h, axis, mine).astype(full) for h in held).astype(sent)
    return leaving, staying


def scatter_steps(parts, chip, chip_bits, sent):
    orders = [gather_order(chip_bits, colour)[::-1] for colour in range(len(parts))]
    lefts = [list(range(chip_bits - 1, -1, -1)) for _ in parts]
    held = [[array.reshape((2,) * chip_bits + array.shape[1:])] for array in parts]
    for step in range(chip_bits):
        if step == 2 and len(held) == 2:
            held = [[jnp.concatenate(pair, axis=-1) for pair in zip(*held)]]
        leaving, staying = [], []
        for order, left, arrays in zip(orders, lefts, held):
            bit = order[step]
            axis = left.index(bit)
            left.remove(bit)
            going, kept = halves_at(arrays, axis, jnp.bitwise_and(chip >> bit, 1), sent)
            leaving.append((going, bit))
            staying.append(kept)
        arriving = yield leaving
        held = [list(pair) for pair in zip(staying, arriving)]
    ((kept, arrived),) = held
    return kept.astype(full) + arrived.astype(full)


def halving_steps(leaving, staying, order):
    (arriving,) = yield [(leaving, order[0])]
    for bit in order[1:]:
        half = staying.shape[0] // 2
        leaving, staying = [
            (staying[at].astype(full) + arriving[at].astype(full)).astype(low)
            for at in (slice(half, None), slice(half))
        ]
        (arriving,) = yield [(leaving, bit)]
    return (staying.astype(full) + arriving.astype(full))[0]


def owners(colour, chip, chip_bits):
    order = gather_order(chip_bits, colour)
    spots = jnp.arange(1 << chip_bits)
    bits = list(enumerate(order))
    owner = sum((jnp.bitwise_and(spots >> at, 1) << bit) for at, bit in bits)
    apart = jnp.bitwise_xor(spots, chip)
    place = sum((jnp.bitwise_and(apart >> bit, 1) << at) for at, bit in bits)
    return jnp.bitwise_xor(owner, chip), place


def scatter_flow(parts, chip, chip_bits, sent=low):
    return Flow(scatter_steps(parts, chip, chip_bits, sent))


def row_steps(row, chip, chip_bits, first_bit):
    held = row[None]
    for bit in range(chip_bits):
        (arriving,) = yield [(held, bit + first_bit - 1)]
        held = jnp.concatenate([held, arriving], axis=0)
    places = jnp.arange(1 << chip_bits)
    pick = jnp.bitwise_xor(places, chip)[:, None] == places[None, :]
    return jnp.dot(pick.astype(held.dtype), held, preferred_element_type=full).astype(held.dtype)


def row_flow(row, chip, chip_bits, first_bit=1):
    return Flow(row_steps(row, chip, chip_bits, first_bit))


def run(flow):
    while flow.wanted is not None:
        flow.arrive([swap(array, bit + 1) for array, bit in flow.wanted])
    return flow.result


def to_phases(block_in, row_count):
    width = block_in.shape[-1]
    split_grid = block_in.reshape(row_count // 2, 2, HALF_SIDE, 2, width)
    return split_grid.transpose(1, 3, 0, 2, 4).reshape(4, row_count // 2 * HALF_SIDE, width)


def from_phases(block_in, row_count):
    width = block_in.shape[-1]
    split_grid = block_in.reshape(2, 2, row_count // 2, HALF_SIDE, width)
    return split_grid.transpose(2, 0, 3, 1, 4).reshape(row_count * SIDE, width)


def in_core_order(mine, other, core):
    return jnp.where(core == 0, mine, other), jnp.where(core == 0, other, mine)


def join_halves(mine, other, core):
    return jnp.stack(in_core_order(mine, other, core), axis=1).reshape(-1, mine.shape[-1])


def half_of(joined, which):
    width = joined.shape[-1]
    return at_bit(joined.reshape(4, 2, -1, width), 1, which)


def layer_norm(values):
    average = jnp.mean(values, axis=-1, keepdims=True)
    centred = values - average
    variance = jnp.mean(centred * centred, axis=-1, keepdims=True)
    return centred * lax.rsqrt(variance + ln_epsilon)


def modulate(values, shift_by, scale_by):
    return layer_norm(values) * (1.0 + scale_by) + shift_by


def sinusoid(steps_in, width):
    halfway = width // 2
    frequency = jnp.exp(-math.log(10000.0) * jnp.arange(halfway, dtype=jnp.float32) / halfway)
    angles = steps_in.astype(jnp.float32)[..., None] * frequency
    return jnp.concatenate([jnp.cos(angles), jnp.sin(angles)], axis=-1)


def softmax_of(query, key, allowed):
    raw = lax.dot_general(query, key, (((1,), (1,)), ((), ())), preferred_element_type=full)
    scores = jnp.where(allowed, raw * HEAD ** (-0.5), masked_score)
    shifted = jnp.exp(scores - jnp.max(scores, axis=-1, keepdims=True))
    return shifted / jnp.sum(shifted, axis=-1, keepdims=True)


def head_lanes(shape, head):
    lanes = lax.broadcasted_iota(jnp.int32, shape, 1)
    return jnp.logical_and(lanes >= head * HEAD, lanes < (head + 1) * HEAD)


def attend_body(mask_ref, qkv_ref, out_ref):
    allowed = mask_ref[...] > 0.5

    @pl.loop(0, 4)
    def _(phase):
        rows = pl.ds(pl.multiple_of(phase * PLANE, PLANE), PLANE)
        query = qkv_ref[rows, :128]
        key = qkv_ref[rows, 128:256]
        value = qkv_ref[rows, 256:]
        total = None
        for head in range(2):
            here = head_lanes(key.shape, head)
            probs = softmax_of(query, jnp.where(here, key, jnp.zeros_like(key)), allowed)
            part = jnp.dot(
                probs.astype(low),
                jnp.where(here, value, jnp.zeros_like(value)),
                preferred_element_type=full,
            )
            total = part if total is None else total + part
        out_ref[rows, :] = total.astype(low)


def attend_back_body(mask_ref, qkv_ref, grad_ref, out_ref):
    allowed = mask_ref[...] > 0.5

    @pl.loop(0, 4)
    def _(phase):
        rows = pl.ds(pl.multiple_of(phase * PLANE, PLANE), PLANE)
        query = qkv_ref[rows, :128]
        key = qkv_ref[rows, 128:256]
        value = qkv_ref[rows, 256:]
        grad = grad_ref[rows, :]
        by_rows = (((0,), (0,)), ((), ()))
        totals = [None, None, None]
        for head in range(2):
            here = head_lanes(key.shape, head)
            blank = jnp.zeros_like(key)
            key_here = jnp.where(here, key, blank)
            query_here = jnp.where(here, query, blank)
            value_here = jnp.where(here, value, blank)
            grad_here = jnp.where(here, grad, blank)
            weights = softmax_of(query, key_here, allowed)
            grad_probs = lax.dot_general(
                grad, value_here, (((1,), (1,)), ((), ())), preferred_element_type=full
            )
            delta = jnp.sum(grad_probs * weights, axis=-1, keepdims=True)
            grad_scores = (weights * (grad_probs - delta)).astype(low)
            parts = (
                jnp.dot(grad_scores, key_here, preferred_element_type=full),
                lax.dot_general(grad_scores, query_here, by_rows, preferred_element_type=full),
                lax.dot_general(
                    weights.astype(low), grad_here, by_rows, preferred_element_type=full
                ),
            )
            totals = [p if t is None else t + p for t, p in zip(totals, parts)]
        out_ref[rows, :128] = (totals[0] * HEAD ** (-0.5)).astype(low)
        out_ref[rows, 128:256] = (totals[1] * HEAD ** (-0.5)).astype(low)
        out_ref[rows, 256:] = totals[2].astype(low)


def attend(mask, qkv):
    tokens, width = qkv.shape
    pairs = width // 384
    return pl.pallas_call(
        attend_body,
        grid=(pairs,),
        in_specs=[
            pl.BlockSpec((PLANE, PLANE), lambda j: (0, 0)),
            pl.BlockSpec((tokens, 384), lambda j: (0, j)),
        ],
        out_specs=pl.BlockSpec((tokens, 128), lambda j: (0, j)),
        out_shape=jax.ShapeDtypeStruct((tokens, pairs * 128), low),
        cost_estimate=pl.CostEstimate(
            flops=pairs * 2 * 4 * 4 * PLANE * PLANE * 256,
            bytes_accessed=8 * tokens * pairs * 128,
            transcendentals=pairs * 8 * PLANE * PLANE,
        ),
        name="attend",
    )(mask, qkv)


def attend_back(mask, qkv, grad):
    tokens, width = qkv.shape
    pairs = width // 384
    return pl.pallas_call(
        attend_back_body,
        grid=(pairs,),
        in_specs=[
            pl.BlockSpec((PLANE, PLANE), lambda j: (0, 0)),
            pl.BlockSpec((tokens, 384), lambda j: (0, j)),
            pl.BlockSpec((tokens, 128), lambda j: (0, j)),
        ],
        out_specs=pl.BlockSpec((tokens, 384), lambda j: (0, j)),
        out_shape=jax.ShapeDtypeStruct((tokens, width), low),
        cost_estimate=pl.CostEstimate(
            flops=pairs * 2 * 4 * 10 * PLANE * PLANE * 256,
            bytes_accessed=14 * tokens * pairs * 128,
            transcendentals=pairs * 8 * PLANE * PLANE,
        ),
        name="attend_back",
    )(mask, qkv, grad)


def strip_at(ref, row_phase, column_phase, row):
    start = pl.multiple_of((row + 1) * STRIP, STRIP)
    return ref[2 * row_phase + column_phase, pl.ds(start, STRIP), :]


def near_strips(ref, row):
    tokens = lax.broadcasted_iota(jnp.int32, (STRIP, ref.shape[-1]), 0)
    loaded = {}
    for row_phase, at in ((1, row - 1), (0, row), (1, row), (0, row + 1)):
        even = strip_at(ref, row_phase, 0, at)
        odd = strip_at(ref, row_phase, 1, at)
        before = jnp.where(tokens == 0, 0.0, pltpu.roll(odd, 1, 0))
        after = jnp.where(tokens == STRIP - 1, 0.0, pltpu.roll(even, STRIP - 1, 0))
        loaded[len(loaded)] = ((before, even, odd), (even, odd, after))
    return {0: (loaded[0], loaded[1], loaded[2]), 1: (loaded[1], loaded[2], loaded[3])}


def conv_strip(near, kernel, row_phase, column_phase):
    total = None
    for i in range(3):
        for j in range(3):
            term = near[row_phase][i][column_phase][j] * kernel[3 * i + j : 3 * i + j + 1, :]
            total = term if total is None else total + term
    return total


def feed_body(
    spread,
    words_ref,
    norm_ref,
    norm_t_ref,
    grad_ref,
    *refs,
):
    pieces = 2 if spread else 1
    up_refs, refs = refs[:pieces], refs[pieces:]
    down_refs, refs = refs[:pieces], refs[pieces:]
    kernel_ref, staying_ref, leaving_ref, *refs = refs
    up_grad_refs, refs = refs[:pieces], refs[pieces:]
    down_grad_refs, refs = refs[:pieces], refs[pieces:]
    kernel_grad_ref, branch_acc, back_acc, hidden, widened_grad, act_grad, act, hidden_grad = refs[
        :8
    ]
    step = pl.program_id(0)
    core = words_ref[0]
    by_columns = (((1,), (1,)), ((), ()))
    width = kernel_ref.shape[1]
    model = norm_t_ref.shape[0]
    up_ref, down_ref = up_refs[0], down_refs[0]
    if spread:
        up_ref, down_all = refs[8:]
        half, share, _ = up_refs[0].shape
        piece = down_refs[0].shape[1]
        chips = 2 * half
        down_ref = down_all.at[pl.ds(pl.multiple_of(step * width, width), width), :]

        for which in range(2):

            @pl.loop(0, half)
            def _(spot):
                start = pl.multiple_of(words_ref[1 + which * half + spot] * share, share)
                up_ref[pl.ds(start, share), :] = up_refs[which][spot]

            @pl.when(step == 0)
            def _():
                @pl.loop(0, half)
                def _(spot):
                    owner = words_ref[1 + chips + which * half + spot]
                    start = pl.multiple_of(owner * piece, piece)
                    down_all[pl.ds(start, piece), :] = down_refs[which][spot]

    @pl.when(step == 0)
    def _():
        blank = jnp.zeros((STRIP, width), full)
        for plane in range(4):
            for ref in (hidden, widened_grad):
                ref[plane, pl.ds(0, STRIP), :] = blank
                ref[plane, pl.ds(PLANE + STRIP, STRIP), :] = blank
        branch_acc[...] = jnp.zeros_like(branch_acc)
        back_acc[...] = jnp.zeros_like(back_acc)

    @pl.loop(0, 4)
    def _(plane):
        rows = pl.ds(pl.multiple_of(plane * PLANE, PLANE), PLANE)
        hidden[plane, pl.ds(STRIP, PLANE), :] = jnp.dot(
            norm_ref[rows, :], up_ref[...], preferred_element_type=full
        )
        act_grad[rows, :] = lax.dot_general(
            grad_ref[rows, :], down_ref[...], by_columns, preferred_element_type=full
        )

    kernel = kernel_ref[...]

    def forward_strip(row, sums):
        near = near_strips(hidden, row)
        sums = list(sums)
        for row_phase in range(2):
            for column_phase in range(2):
                plane = 2 * row_phase + column_phase
                wide = conv_strip(near, kernel, row_phase, column_phase)
                square = wide * wide
                bend = math.sqrt(2.0 / math.pi) * (wide + 0.044715 * wide * square)
                curve = jnp.tanh(bend)
                half = 0.5 * (1.0 + curve)
                slope = half + 0.5 * wide * (1.0 - curve * curve) * (
                    math.sqrt(2.0 / math.pi) * (1.0 + 3 * 0.044715 * square)
                )
                at = pl.ds(pl.multiple_of(plane * PLANE + row * STRIP, STRIP), STRIP)
                act[at, :] = (wide * half).astype(low)
                grad_here = slope * act_grad[at, :]
                widened_grad[plane, pl.ds(pl.multiple_of((row + 1) * STRIP, STRIP), STRIP), :] = (
                    grad_here
                )
                for i in range(3):
                    for j in range(3):
                        product = near[row_phase][i][column_phase][j] * grad_here
                        sums[3 * i + j] = sums[3 * i + j] + (product[:8] + product[8:])
        return tuple(sums)

    sums = lax.fori_loop(
        0, HALF_SIDE, forward_strip, tuple(jnp.zeros((8, width), full) for _ in range(9))
    )
    kernel_grad_ref[...] = jnp.concatenate(
        [jnp.sum(s, axis=0, keepdims=True) for s in sums] + [jnp.zeros((7, width), full)], axis=0
    )

    flipped = [kernel[8 - t : 9 - t, :] for t in range(9)]
    flipped = jnp.concatenate(flipped, axis=0)

    @pl.loop(0, HALF_SIDE)
    def _(row):
        near = near_strips(widened_grad, row)
        for row_phase in range(2):
            for column_phase in range(2):
                plane = 2 * row_phase + column_phase
                at = pl.ds(pl.multiple_of(plane * PLANE + row * STRIP, STRIP), STRIP)
                hidden_grad[at, :] = conv_strip(near, flipped, row_phase, column_phase).astype(low)

    @pl.loop(0, 4)
    def _(plane):
        rows = pl.ds(pl.multiple_of(plane * PLANE, PLANE), PLANE)
        branch_acc[rows, :] += jnp.dot(act[rows, :], down_ref[...], preferred_element_type=full)
        back_acc[rows, :] += lax.dot_general(
            hidden_grad[rows, :], up_ref[...], by_columns, preferred_element_type=full
        )

    if spread:
        for which in range(2):

            @pl.loop(0, half // 4)
            def _(group):
                lhs = []
                for k in range(4):
                    owner = words_ref[1 + which * half + 4 * group + k]
                    start = pl.multiple_of(owner * share, share)
                    lhs.append(norm_t_ref[pl.ds(start, share), :])
                result = jnp.dot(
                    jnp.concatenate(lhs, axis=0), hidden_grad[...], preferred_element_type=full
                ).astype(low)
                for k in range(4):
                    up_grad_refs[which][4 * group + k] = result[k * share : (k + 1) * share]

    else:

        @pl.loop(0, model // TILE)
        def _(tile):
            rows = pl.ds(pl.multiple_of(tile * TILE, TILE), TILE)
            up_grad_refs[0][rows, :] = jnp.dot(
                norm_t_ref[rows, :], hidden_grad[...], preferred_element_type=full
            ).astype(low)

    down_grad = lax.dot_general(
        act[...], grad_ref[...], (((0,), (0,)), ((), ())), preferred_element_type=full
    ).astype(low)
    if spread:
        for k in range(width // piece):
            place = words_ref[1 + 2 * chips + step * (width // piece) + k]
            for which in range(2):

                @pl.when(place // half == which)
                def _():
                    down_grad_refs[which][place - which * half] = down_grad[
                        k * piece : (k + 1) * piece
                    ]

    else:
        down_grad_refs[0][...] = down_grad

    @pl.when(step == pl.num_programs(0) - 1)
    def _():
        for ref, which in ((staying_ref, core), (leaving_ref, 1 - core)):
            for index, acc in enumerate((branch_acc, back_acc)):
                for plane in range(4):
                    start = plane * PLANE + pl.multiple_of(which * (PLANE // 2), PLANE // 2)
                    ref[index, plane] = acc[pl.ds(start, PLANE // 2), :].astype(low)


def feed_forward(norm, norm_t, grad, up, down, kernel, words):
    tokens, model = norm.shape
    channels = kernel.shape[1]
    width = TILE
    spread = len(up) == 2
    whole = lambda j, words: (0, 0)
    half = lambda j, words: (0, 0, 0, 0)
    across = lambda j, words: (0, j)
    once = pl.Buffered(1)
    piece_scratch = []
    if spread:
        deep = lambda j, words: (0, 0, 0)
        up_spec = pl.BlockSpec(up[0].shape[:2] + (width,), lambda j, words: (0, 0, j))
        down_spec = pl.BlockSpec(down[0].shape, deep, pipeline_mode=once)
        down_grad_spec = pl.BlockSpec(down[0].shape, deep)
        piece_scratch = [pltpu.VMEM((model, width), low), pltpu.VMEM((channels, model), low)]
    else:
        up_spec = pl.BlockSpec((model, width), across)
        down_spec = down_grad_spec = pl.BlockSpec((width, model), lambda j, words: (j, 0))
    halves = jax.ShapeDtypeStruct((2, 4, PLANE // 2, model), low)
    like = lambda arrays: [jax.ShapeDtypeStruct(array.shape, low) for array in arrays]
    out = pl.pallas_call(
        functools.partial(feed_body, spread),
        grid_spec=pltpu.PrefetchScalarGridSpec(
            num_scalar_prefetch=1,
            grid=(channels // width,),
            in_specs=[
                pl.BlockSpec((tokens, model), whole, pipeline_mode=once),
                pl.BlockSpec((model, tokens), whole, pipeline_mode=once),
                pl.BlockSpec((tokens, model), whole, pipeline_mode=once),
                *[up_spec] * len(up),
                *[down_spec] * len(down),
                pl.BlockSpec((16, width), across),
            ],
            out_specs=[
                pl.BlockSpec(halves.shape, half),
                pl.BlockSpec(halves.shape, half),
                *[up_spec] * len(up),
                *[down_grad_spec] * len(down),
                pl.BlockSpec((16, width), across),
            ],
            scratch_shapes=[
                pltpu.VMEM((tokens, model), full),
                pltpu.VMEM((tokens, model), full),
                pltpu.VMEM((4, PADDED, width), full),
                pltpu.VMEM((4, PADDED, width), full),
                pltpu.VMEM((tokens, width), full),
                pltpu.VMEM((tokens, width), low),
                pltpu.VMEM((tokens, width), low),
            ]
            + piece_scratch,
        ),
        out_shape=[halves, halves]
        + like(up)
        + like(down)
        + [jax.ShapeDtypeStruct((16, channels), full)],
        compiler_params=pltpu.CompilerParams(vmem_limit_bytes=63 * 1024 * 1024),
        cost_estimate=pl.CostEstimate(
            flops=12 * tokens * model * channels,
            bytes_accessed=8 * model * channels + 10 * tokens * model,
            transcendentals=tokens * channels,
        ),
        name="feed_forward",
    )(words, norm, norm_t, grad, *up, *down, kernel)
    staying, leaving, *grads, kernel_grad = out
    return staying, leaving, grads[: len(up)], grads[len(up) :], kernel_grad


def token_stats(x_ref, average, scale):
    @pl.loop(0, x_ref.shape[0] // STRIP)
    def _(strip):
        rows = pl.ds(pl.multiple_of(strip * STRIP, STRIP), STRIP)
        values = x_ref[rows, :].astype(full)
        mean = jnp.mean(values, axis=-1, keepdims=True)
        centred = values - mean
        variance = jnp.mean(centred * centred, axis=-1, keepdims=True)
        average[rows, :] = jnp.broadcast_to(mean, (STRIP, 128))
        scale[rows, :] = jnp.broadcast_to(lax.rsqrt(variance + ln_epsilon), (STRIP, 128))


def normed_strip(x_ref, average, scale, rows, columns):
    width = columns.size
    wide = lambda ref: jnp.concatenate([ref[rows, :]] * (width // 128), axis=1)
    return (x_ref[rows, columns].astype(full) - wide(average)) * wide(scale)


def frame_zeros(refs):
    for ref in refs:
        blank = jnp.zeros((STRIP, ref.shape[-1]), full)
        for plane in range(4):
            ref[plane, pl.ds(0, STRIP), :] = blank
            ref[plane, pl.ds(ref.shape[1] - STRIP, STRIP), :] = blank


def conv_in_body(x_ref, kernel_ref, mods_ref, out_ref, average, scale, normed):
    step = pl.program_id(0)
    width = out_ref.shape[1]
    columns = pl.ds(pl.multiple_of(step * width, width), width)

    @pl.when(step == 0)
    def _():
        token_stats(x_ref, average, scale)
        frame_zeros([normed])

    shift_by = mods_ref[0:1, :]
    scale_by = 1.0 + mods_ref[1:2, :]

    @pl.loop(0, HALF_SIDE)
    def _(row):
        for plane in range(4):
            rows = pl.ds(pl.multiple_of(plane * PLANE + row * STRIP, STRIP), STRIP)
            normed[plane, pl.ds(pl.multiple_of((row + 1) * STRIP, STRIP), STRIP), :] = (
                normed_strip(x_ref, average, scale, rows, columns) * scale_by + shift_by
            )

    kernel = kernel_ref[...]

    @pl.loop(0, HALF_SIDE)
    def _(row):
        near = near_strips(normed, row)
        for row_phase in range(2):
            for column_phase in range(2):
                plane = 2 * row_phase + column_phase
                at = pl.ds(pl.multiple_of(plane * PLANE + row * STRIP, STRIP), STRIP)
                out_ref[at, :] = conv_strip(near, kernel, row_phase, column_phase).astype(low)


def conv_in(canvas, kernel, mods):
    tokens, model = canvas.shape
    return pl.pallas_call(
        conv_in_body,
        grid=(model // TILE,),
        in_specs=[
            pl.BlockSpec((tokens, model), lambda j: (0, 0), pipeline_mode=pl.Buffered(1)),
            pl.BlockSpec((16, TILE), lambda j: (0, j)),
            pl.BlockSpec((8, TILE), lambda j: (0, j)),
        ],
        out_specs=pl.BlockSpec((tokens, TILE), lambda j: (0, j)),
        out_shape=jax.ShapeDtypeStruct((tokens, model), low),
        scratch_shapes=[
            pltpu.VMEM((tokens, 128), full),
            pltpu.VMEM((tokens, 128), full),
            pltpu.VMEM((4, PADDED, TILE), full),
        ],
        cost_estimate=pl.CostEstimate(
            flops=30 * tokens * model, bytes_accessed=4 * tokens * model, transcendentals=tokens
        ),
        name="conv_in",
    )(canvas, kernel, mods)


def conv_back_body(
    core_ref,
    x_ref,
    kept_ref,
    arriving_ref,
    kernel_ref,
    mods_ref,
    middle_ref,
    out_ref,
    kernel_grad_ref,
    mods_grad_ref,
    average,
    scale,
    normed,
    upstream,
    held,
    sum_plain,
    sum_normed,
    woven,
):
    step = pl.program_id(0)
    core = core_ref[0]
    width = kept_ref.shape[1]
    near_rows = x_ref.shape[0] // 4 // STRIP
    own_rows = near_rows - 1
    columns = pl.ds(pl.multiple_of(step * width, width), width)

    def near_at(plane, row):
        return pl.ds(pl.multiple_of((plane * near_rows + row) * STRIP, STRIP), STRIP)

    def own_at(plane, row):
        return pl.ds(pl.multiple_of((plane * own_rows + row) * STRIP, STRIP), STRIP)

    @pl.when(step == 0)
    def _():
        token_stats(x_ref, average, scale)
        frame_zeros([normed, upstream])
        sum_plain[...] = jnp.zeros_like(sum_plain)
        sum_normed[...] = jnp.zeros_like(sum_normed)

    shift_by = mods_ref[0:1, :]
    scale_by = 1.0 + mods_ref[1:2, :]

    @pl.loop(0, near_rows)
    def _(row):
        for plane in range(4):
            rows = near_at(plane, row)
            padded = pl.ds(pl.multiple_of((row + 1) * STRIP, STRIP), STRIP)
            normed[plane, padded, :] = (
                normed_strip(x_ref, average, scale, rows, columns) * scale_by + shift_by
            )
            upstream[plane, padded, :] = kept_ref[rows, :].astype(full) + arriving_ref[
                rows, :
            ].astype(full)

    kernel = kernel_ref[...]
    flipped = jnp.concatenate([kernel[8 - t : 9 - t, :] for t in range(9)], axis=0)

    def kernel_strip(row, sums):
        near = near_strips(normed, row + core)
        sums = list(sums)
        for row_phase in range(2):
            for column_phase in range(2):
                grad_here = strip_at(upstream, row_phase, column_phase, row + core)
                for i in range(3):
                    for j in range(3):
                        product = near[row_phase][i][column_phase][j] * grad_here
                        sums[3 * i + j] = sums[3 * i + j] + (product[:8] + product[8:])
        return tuple(sums)

    def fold(sums, rows):
        return jnp.concatenate(
            [jnp.sum(s, axis=0, keepdims=True) for s in sums]
            + [jnp.zeros((rows - len(sums), width), full)],
            axis=0,
        )

    blank = jnp.zeros((8, width), full)
    kernel_grad_ref[...] = fold(lax.fori_loop(0, own_rows, kernel_strip, (blank,) * 9), 16)

    def input_strip(row, sums):
        near = near_strips(upstream, row + core)
        shift_sum, scale_sum = sums
        for row_phase in range(2):
            for column_phase in range(2):
                plane = 2 * row_phase + column_phase
                grad = conv_strip(near, flipped, row_phase, column_phase)
                plain = normed_strip(x_ref, average, scale, near_at(plane, row + core), columns)
                shift_sum = shift_sum + (grad[:8] + grad[8:])
                product = grad * plain
                scale_sum = scale_sum + (product[:8] + product[8:])
                scaled = grad * scale_by
                rows = own_at(plane, row)
                held[step, rows, :] = scaled
                product = scaled * plain
                sum_plain[rows, :] += sum(scaled[:, k : k + 128] for k in range(0, width, 128))
                sum_normed[rows, :] += sum(product[:, k : k + 128] for k in range(0, width, 128))
        return shift_sum, scale_sum

    mods_grad_ref[...] = fold(lax.fori_loop(0, own_rows, input_strip, (blank,) * 2), 8)

    @pl.when(step == pl.num_programs(0) - 1)
    def _():
        model = x_ref.shape[1]

        @pl.loop(0, own_rows)
        def _(row):
            for plane in range(4):
                rows = own_at(plane, row)
                near = near_at(plane, row + core)
                mean_plain = jnp.sum(sum_plain[rows, :], axis=-1, keepdims=True) / model
                mean_normed = jnp.sum(sum_normed[rows, :], axis=-1, keepdims=True) / model
                for block in range(model // width):
                    at = pl.ds(block * width, width)
                    plain = normed_strip(x_ref, average, scale, near, at)
                    spread = jnp.concatenate([scale[near, :]] * (width // 128), axis=1)
                    result = middle_ref[rows, at] + spread * (
                        held[block, rows, :] - mean_plain - plain * mean_normed
                    )
                    for lane in range(0, width, 128):
                        woven[(block * width + lane) // 128, pl.ds(plane % 2, STRIP, stride=2), :] = (
                            result[:, lane : lane + 128]
                        )
                if plane % 2 == 1:
                    start = pl.multiple_of((2 * row + plane // 2) * SIDE, SIDE)
                    for lane in range(model // 128):
                        out_ref[pl.ds(start, SIDE), lane * 128 : lane * 128 + 128] = woven[lane]


def conv_back(core, x_near, kept, arriving, kernel, mods, grad_middle):
    near_tokens, model = x_near.shape
    own_tokens = grad_middle.shape[0]
    once = pl.Buffered(1)
    whole = lambda j, words: (0, 0)
    across = lambda j, words: (0, j)
    padded = near_tokens // 4 + 2 * STRIP
    return pl.pallas_call(
        conv_back_body,
        grid_spec=pltpu.PrefetchScalarGridSpec(
            num_scalar_prefetch=1,
            grid=(model // TILE,),
            in_specs=[
                pl.BlockSpec((near_tokens, model), whole, pipeline_mode=once),
                pl.BlockSpec((near_tokens, TILE), across),
                pl.BlockSpec((near_tokens, TILE), across),
                pl.BlockSpec((16, TILE), across),
                pl.BlockSpec((8, TILE), across),
                pl.BlockSpec((own_tokens, model), whole, pipeline_mode=once),
            ],
            out_specs=[
                pl.BlockSpec((own_tokens, model), whole),
                pl.BlockSpec((16, TILE), across),
                pl.BlockSpec((8, TILE), across),
            ],
            scratch_shapes=[
                pltpu.VMEM((near_tokens, 128), full),
                pltpu.VMEM((near_tokens, 128), full),
                pltpu.VMEM((4, padded, TILE), full),
                pltpu.VMEM((4, padded, TILE), full),
                pltpu.VMEM((model // TILE, own_tokens, TILE), full),
                pltpu.VMEM((own_tokens, 128), full),
                pltpu.VMEM((own_tokens, 128), full),
                pltpu.VMEM((model // 128, SIDE, 128), full),
            ],
        ),
        out_shape=[
            jax.ShapeDtypeStruct((own_tokens, model), full),
            jax.ShapeDtypeStruct((16, model), full),
            jax.ShapeDtypeStruct((8, model), full),
        ],
        cost_estimate=pl.CostEstimate(
            flops=70 * own_tokens * model,
            bytes_accessed=14 * own_tokens * model,
            transcendentals=near_tokens,
        ),
        name="conv_back",
    )(core[None].astype(jnp.int32), x_near, kept, arriving, kernel, mods, grad_middle)


def row_stats(values):
    mean = jnp.mean(values, axis=-1, keepdims=True)
    centred = values - mean
    scale = lax.rsqrt(jnp.mean(centred * centred, axis=-1, keepdims=True) + ln_epsilon)
    return centred * scale, scale


def enter_feed_body(x_ref, part_ref, other_ref, grad_ref, mods_ref, norm_ref, norm_t_ref, out_ref):
    @pl.loop(0, x_ref.shape[0] // STRIP)
    def _(strip):
        rows = pl.ds(pl.multiple_of(strip * STRIP, STRIP), STRIP)
        branch = part_ref[rows, :].astype(full) + other_ref[rows, :].astype(full)
        plain, _ = row_stats(x_ref[rows, :].astype(full) + mods_ref[0:1, :] * branch)
        normed = plain * (1.0 + mods_ref[2:3, :]) + mods_ref[1:2, :]
        norm_ref[rows, :] = normed.astype(low)
        out_ref[rows, :] = (grad_ref[rows, :].astype(full) * mods_ref[3:4, :]).astype(low)

    norm_t_ref[...] = norm_ref[...].T


def enter_feed(canvas, part, other, grad, mods):
    tokens, model = canvas.shape
    rows = PLANE // 2
    along = pl.BlockSpec((rows, model), lambda j: (j, 0))
    return pl.pallas_call(
        enter_feed_body,
        grid=(tokens // rows,),
        in_specs=[along] * 4 + [pl.BlockSpec((8, model), lambda j: (0, 0))],
        out_specs=[along, pl.BlockSpec((model, rows), lambda j: (0, j)), along],
        out_shape=[
            jax.ShapeDtypeStruct((tokens, model), low),
            jax.ShapeDtypeStruct((model, tokens), low),
            jax.ShapeDtypeStruct((tokens, model), low),
        ],
        cost_estimate=pl.CostEstimate(flops=1000, bytes_accessed=1000, transcendentals=0),
        name="enter_feed",
    )(canvas, part, other, grad, mods)


def leave_feed_body(words_ref, x_ref, part_ref, other_ref, grad_ref, mods_ref, *refs):
    *kept_refs, out_ref, middle_grad_ref, branch_grad_ref, sums_ref, totals = refs
    plane = pl.program_id(0)

    @pl.when(plane == 0)
    def _():
        totals[...] = jnp.zeros_like(totals)

    @pl.loop(0, x_ref.shape[0] // STRIP)
    def _(strip):
        rows = pl.ds(pl.multiple_of(strip * STRIP, STRIP), STRIP)
        gate_a, gate_f = mods_ref[0:1, :], mods_ref[3:4, :]
        branch_a = part_ref[rows, :].astype(full) + other_ref[rows, :].astype(full)
        middle = x_ref[rows, :].astype(full) + gate_a * branch_a
        plain, scale = row_stats(middle)
        branch_f = sum(ref[0, 0, rows, :].astype(full) for ref in kept_refs)
        back = sum(ref[1, 0, rows, :].astype(full) for ref in kept_refs)
        grad = grad_ref[rows, :].astype(full)
        out_ref[rows, :] = (middle + gate_f * branch_f).astype(low)
        scaled = back * (1.0 + mods_ref[2:3, :])
        mean_plain = jnp.mean(scaled, axis=-1, keepdims=True)
        mean_normed = jnp.mean(scaled * plain, axis=-1, keepdims=True)
        grad_middle = grad + scale * (scaled - mean_plain - plain * mean_normed)
        middle_grad_ref[rows, :] = grad_middle
        branch_grad_ref[rows, :] = (grad_middle * gate_a).astype(low)
        products = (grad_middle * branch_a, back, back * plain, grad * branch_f)
        for index, product in enumerate(products):
            totals[index] += product[:8] + product[8:]

    @pl.when(plane == pl.num_programs(0) - 1)
    def _():
        lines = [jnp.sum(totals[k], axis=0, keepdims=True) for k in range(4)]
        sums_ref[...] = jnp.concatenate(lines + [jnp.zeros_like(sums_ref[:4])], axis=0)


def leave_feed(words, canvas, part, other, grad, mods, kept):
    model = canvas.shape[1]
    rows = PLANE // 2
    own = pl.BlockSpec((rows, model), lambda j, words: (2 * j + words[0], 0))
    half = pl.BlockSpec((rows, model), lambda j, words: (j, 0))
    whole = pl.BlockSpec((8, model), lambda j, words: (0, 0))
    return pl.pallas_call(
        leave_feed_body,
        grid_spec=pltpu.PrefetchScalarGridSpec(
            num_scalar_prefetch=1,
            grid=(4,),
            in_specs=[own] * 4
            + [whole]
            + [pl.BlockSpec((2, 1, rows, model), lambda j, words: (0, j, 0, 0))] * len(kept),
            out_specs=[half, half, half, whole],
            scratch_shapes=[pltpu.VMEM((4, 8, model), full)],
        ),
        out_shape=[
            jax.ShapeDtypeStruct((4 * rows, model), low),
            jax.ShapeDtypeStruct((4 * rows, model), full),
            jax.ShapeDtypeStruct((4 * rows, model), low),
            jax.ShapeDtypeStruct((8, model), full),
        ],
        cost_estimate=pl.CostEstimate(flops=1000, bytes_accessed=1000, transcendentals=0),
        name="leave_feed",
    )(words, canvas, part, other, grad, mods, *kept)


def on_device(
    tokens,
    seg_ids,
    timesteps,
    labels,
    cotangent,
    mod_weight,
    class_table,
    attn_kernel,
    qkv_weight,
    proj_weight,
    up_weight,
    ffn_kernel,
    down_weight,
):
    devices = device_count()
    chips = devices // 2
    chip_bits = chips.bit_length() - 1
    rank = lax.axis_index("dp") * lax.axis_size("fsdp") + lax.axis_index("fsdp")
    core = rank % 2
    chip = rank // 2
    _, half_tokens, model = tokens.shape
    half_rows = half_tokens // SIDE
    class_count = class_table.shape[0]
    part = model // devices
    share = down_weight.shape[0]
    piece = share // CHUNKS
    pairs = model // HEAD // 4

    def halves_of(array, axis):
        return at_bit(array, axis, core), at_bit(array, axis, 1 - core)

    def row_pair(array, axis):
        kept, leaving = halves_of(array, axis)
        arriving = swap_core(leaving)
        return jnp.concatenate(in_core_order(kept, arriving, core), axis=0)

    qkv_split = qkv_weight.reshape(part, 3, 2, pairs, 128).transpose(0, 2, 3, 1, 4)
    qkv_rows = row_pair(qkv_split.reshape(part, 2, pairs * 384), 1)
    qkv_half = pairs * 384 // 2

    picks = labels[:, None] == jnp.arange(class_count)[None, :]
    angles_here = lax.dynamic_slice_in_dim(sinusoid(timesteps, model), rank * part, part, axis=1)
    cond = angles_here + jnp.dot(picks.astype(low), class_table, preferred_element_type=full)
    lift_value, lift_pull = jax.vjp(jax.nn.silu, cond)
    lifted = lift_value.astype(low)
    mods_part = jnp.dot(lifted, mod_weight, preferred_element_type=full)

    slot = Slots(jnp.zeros((8, 128), full))
    near = lambda *shards: Flow(near_steps(shards, chip_bits))
    sums = lambda *parts: scatter_flow(parts, chip, chip_bits)
    joined = lambda flow: [
        assemble(pieces, gather_order(chip_bits, colour), chip)
        for colour, pieces in enumerate(flow.result)
    ]
    mods_flow = scatter_flow([mods_part], chip, chip_bits, sent=full)
    qkv_near = near(qkv_rows)
    mine, upstream = slot(
        [qkv_near, mods_flow],
        lambda: (to_phases(tokens[0], half_rows), to_phases(cotangent[0], half_rows)),
    )

    up_weight, proj_weight, ffn_kernel, attn_kernel = slot.after(
        up_weight, proj_weight, ffn_kernel, attn_kernel
    )
    up_split = up_weight.reshape(part, chips, 2, CHUNKS, piece).transpose(0, 2, 3, 1, 4)
    up_rows = row_pair(up_split.reshape(part, 2, CHUNKS, chips * piece), 1)
    proj_there = [(r, r % chips * 2 + r // chips) for r in range(devices)]
    proj_back = [(b, a) for a, b in proj_there]
    proj_rows = lax.ppermute(proj_weight, AXES, proj_there)
    proj_flow = Flow(one_colour_steps(proj_rows, chip_bits))
    canvas = slot(
        [qkv_near, mods_flow, proj_flow], lambda: join_halves(mine, swap_core(mine), core)
    )
    slot.finish([qkv_near])
    tap_count = 9 * (share + part)
    tap_words = jnp.concatenate([ffn_kernel.reshape(-1), attn_kernel.reshape(-1)])
    tap_words = jnp.pad(tap_words, (0, -tap_count % 128))
    taps = run(row_flow(tap_words, rank, chip_bits + 1, 0))
    ffn_taps = taps[:, : 9 * share].reshape(chips, 2, 9, share)
    ffn_taps = at_bit(ffn_taps, 1, core).reshape(chips, 9, CHUNKS, piece)
    ffn_taps = ffn_taps.transpose(2, 1, 0, 3).reshape(CHUNKS, 9, chips * piece).astype(full)
    ffn_taps = jnp.pad(ffn_taps, ((0, 0), (0, 7), (0, 0)))
    attn_taps = taps[:, 9 * share : tap_count].reshape(devices, 9, part)
    attn_taps = attn_taps.transpose(1, 0, 2).reshape(9, model).astype(full)
    attn_taps = jnp.pad(attn_taps, ((0, 7), (0, 0)))

    spot = jnp.arange(PLANE)
    quadrant = 2 * (spot // (PLANE // 2)) + spot % HALF_SIDE // (HALF_SIDE // 2)
    quadrants_here = at_bit(seg_ids, 0, chip)
    segment = jnp.sum(
        jnp.where(quadrant[:, None] == jnp.arange(4)[None, :], quadrants_here[None, :], 0), axis=1
    )
    mask = (segment[:, None] == segment[None, :]).astype(full)

    def far(arrays, where):
        return Flow(far_steps([array[at] for array, at in zip(arrays, where)]))

    wide = chips * piece
    later = range(CHUNKS - 1)
    feed_near = [
        near(up_rows[:, 0], down_weight[:piece]),
        near(up_rows[:, 1:].reshape(2 * part, -1), down_weight[piece:]),
    ]
    left, right = (Ellipsis, slice(qkv_half)), (Ellipsis, slice(qkv_half, None))
    qkv_flow = far(qkv_near.result * 2, (left, right))
    slot([qkv_flow, mods_flow, proj_flow, feed_near[0]])
    mods_half = run(mods_flow)
    mods = mods_half + swap_core(mods_half)
    shift_a, scale_a, gate_a, shift_f, scale_f, gate_f = jnp.split(mods, 6)

    mods_a = jnp.concatenate([shift_a[None], scale_a[None], jnp.zeros((6, model), full)], axis=0)

    convolved = slot(
        [qkv_flow, proj_flow, feed_near[0]], lambda: conv_in(canvas, attn_taps, mods_a)
    )
    slot.finish([qkv_flow, feed_near[0]])
    feed_flows = [far(feed_near[0].result, (Ellipsis, Ellipsis))]

    def project_in():
        weight = jnp.concatenate(
            [array.reshape(model, qkv_half) for array in joined(qkv_flow)], axis=1
        )
        return weight, jnp.dot(convolved, weight, preferred_element_type=full).astype(low)

    qkv_full, qkv = slot([proj_flow, feed_flows[0], feed_near[1]], project_in)
    (upstream,) = slot.after(upstream)
    grad_ph = join_halves(upstream, swap_core(upstream), core)
    slot.finish([proj_flow])

    def attend_and_assemble():
        weight = assemble(proj_flow.result, gather_order(chip_bits, 0), chip)
        return attend(mask, qkv), weight.reshape(-1, model)

    attended, proj_full = slot([feed_flows[0], feed_near[1]], attend_and_assemble)
    slot.finish([feed_near[1]])
    for t in later:
        columns, rows = slice(t * wide, t * wide + wide), slice(t * piece, t * piece + piece)
        feed_flows.append(far(feed_near[1].result, ((Ellipsis, columns), (slice(None), rows))))

    mods_f = jnp.concatenate(
        [gate_a[None], shift_f[None], scale_f[None], gate_f[None], jnp.zeros((4, model), full)]
    )

    def project_out():
        branch_part = jnp.dot(attended, proj_full, preferred_element_type=full).astype(low)
        other = swap_core(branch_part)
        return branch_part, other, *enter_feed(canvas, branch_part, other, grad_ph, mods_f)

    branch_part, branch_other, norm, norm_t, grad_branch_f = slot(feed_flows[:2], project_out)

    kept = []
    grads = [None] * CHUNKS

    spread = 2 * part % STRIP == 0 and piece % STRIP == 0 and chips >= 8
    up_owner, _ = owners(0, chip, chip_bits)
    down_owner, down_place = owners(1, chip, chip_bits)
    words = jnp.concatenate([core[None], up_owner, down_owner, down_place]).astype(jnp.int32)

    def feed(t):
        def work():
            if spread:
                up, down = feed_flows[t].result
            else:
                up, down = joined(feed_flows[t])
                up, down = [up.reshape(model, -1)], [down.reshape(-1, model)]
            return feed_forward(norm, norm_t, grad_branch_f, up, down, ffn_taps[t], words)

        return work

    back_flows = [[] for _ in range(CHUNKS)]

    def run_feed(flows, t):
        slot.finish(feed_flows[t : t + 1])
        staying, leaving, up_grad, down_grad, tap_grad = slot(flows, feed(t))
        kept.append((staying, Flow(core_steps(leaving))))
        grads[t] = tap_grad
        if spread:
            back_flows[t] = [
                Flow(halving_steps(*grad[::-1], gather_order(chip_bits, colour)[::-1]))
                for colour, grad in enumerate((up_grad, down_grad))
            ]
        else:
            back_flows[t] = [
                sums(up_grad[0].reshape(chips, 2 * part, -1)),
                sums(down_grad[0].reshape(chips, piece, model)),
            ]

    run_feed(feed_flows[1:], 0)
    run_feed(feed_flows[2:] + back_flows[0] + [kept[0][1]], 1)
    run_feed(back_flows[0] + back_flows[1] + [kept[1][1]], 2)

    def after_feed():
        parts = [array for staying, exchange in kept for array in (staying, run(exchange))]
        return leave_feed(words[:1], canvas, branch_part, branch_other, grad_ph, mods_f, parts)

    layer_out, grad_middle, grad_branch_mine, feed_sums = slot(
        back_flows[0] + back_flows[2], after_feed
    )
    grad_branch_mine = grad_branch_mine.reshape(4, -1, model)
    layer_out = from_phases(layer_out.reshape(4, -1, model), half_rows)[None]

    def enter_attend():
        grad_branch_a = join_halves(grad_branch_mine, swap_core(grad_branch_mine), core)
        grad_attended = jnp.dot(grad_branch_a, proj_full.T, preferred_element_type=full)
        proj_grad = jnp.dot(attended.T, grad_branch_a, preferred_element_type=full)
        return grad_attended.astype(low), proj_grad.astype(low)

    grad_attended, proj_grad = slot(back_flows[0] + back_flows[1], enter_attend)
    proj_grad = proj_grad.reshape(chips, -1, model)
    proj_flow = sums(proj_grad)
    grad_qkv = slot(
        [proj_flow] + back_flows[1] + back_flows[2], lambda: attend_back(mask, qkv, grad_attended)
    )
    qkv_grad = slot(
        [proj_flow] + back_flows[1],
        lambda: jnp.dot(convolved.T, grad_qkv, preferred_element_type=full).astype(low),
    )
    qkv_grad = qkv_grad.reshape(chips, 2 * part, -1)
    qkv_flow = sums(qkv_grad[..., :qkv_half], qkv_grad[..., qkv_half:])

    def rows_near(array, which):
        size = PLANE // 2 + STRIP
        near = lax.dynamic_slice_in_dim(
            array.reshape(4, PLANE, model), which * (PLANE - size), size, axis=1
        )
        return near.reshape(4 * size, model)

    def leave_attend():
        part_here = jnp.dot(grad_qkv, qkv_full.T, preferred_element_type=full).astype(low)
        return rows_near(part_here, core), swap_core(rows_near(part_here, 1 - core))

    grad_conv = slot([qkv_flow] + back_flows[2], leave_attend)

    def leave_block():
        input_grad, attn_tap_grad, mods_grad = conv_back(
            core, rows_near(canvas, core), *grad_conv, attn_taps, mods_a,
            grad_middle,
        )
        return attn_tap_grad[:9], input_grad, mods_grad[:2]

    attn_tap_grad, input_grad, attn_sums = slot(
        [qkv_flow, proj_flow] + back_flows[2], leave_block
    )
    def row_split(array, axis):
        pair = array.reshape((2, part) + array.shape[1:])
        kept, leaving = halves_of(pair, 0)
        arriving = swap_core(leaving)
        return jnp.stack(in_core_order(kept, arriving, core), axis=axis)

    slot.finish(sum(back_flows, []))
    grad_mods = jnp.concatenate([attn_sums, feed_sums[:4]], axis=0)
    tap_grads = [g[:9].reshape(9, chips, piece) for g in grads]
    ffn_tap_grad = jnp.concatenate(tap_grads, axis=2).transpose(1, 0, 2)
    attn_kept, attn_leaving = halves_of(attn_tap_grad.reshape(9, chips, 2, part), 2)

    def between_cores():
        both = (grad_mods + swap_core(grad_mods)).astype(low)
        return both, attn_kept + swap_core(attn_leaving)

    grad_mods, attn_tap_grad = slot([qkv_flow, proj_flow], between_cores)
    mods_flow = row_flow(grad_mods.reshape(-1), chip, chip_bits)
    tap_parts = jnp.concatenate(
        [ffn_tap_grad.reshape(chips, -1), attn_tap_grad.transpose(1, 0, 2).reshape(chips, -1)],
        axis=1,
    )
    tap_flow = scatter_flow([tap_parts], chip, chip_bits, sent=full)
    up_shares = [flows[0].result for flows in back_flows]
    down_shares = [flows[1].result for flows in back_flows]

    def split_up():
        up_all = jnp.stack(up_shares, axis=1).reshape(2 * part, CHUNKS, chips, piece)
        return row_split(up_all.transpose(0, 2, 1, 3), 2).reshape(part, -1)

    slot.finish([proj_flow])
    proj_share = proj_flow.result
    up_share = slot([qkv_flow, mods_flow, tap_flow], split_up)
    slot.finish([qkv_flow])
    qkv_share = qkv_flow.result

    def split_qkv():
        qkv_all = qkv_share.reshape(2 * part, pairs, 3, 128).transpose(0, 2, 1, 3)
        qkv_out = row_split(qkv_all, 2).reshape(part, -1)
        return qkv_out, lax.ppermute(proj_share, AXES, proj_back)

    qkv_out, proj_share = slot([mods_flow, tap_flow], split_qkv)
    slot.finish([mods_flow, tap_flow])
    down_share = jnp.concatenate(down_shares, axis=0)

    grad_mods_all = mods_flow.result
    mod_grad = jnp.dot(lifted.T, grad_mods_all, preferred_element_type=full)
    (cond_grad,) = lift_pull(jnp.dot(grad_mods_all, mod_weight.T, preferred_element_type=full))
    table_grad = jnp.dot(picks.astype(full).T, cond_grad, precision=highest)
    tap_share = tap_flow.result
    ffn_share = tap_share[: 9 * share].reshape(9, share)
    kernel_share = tap_share[9 * share :].reshape(9, part)

    return (
        layer_out,
        input_grad[None],
        mod_grad,
        table_grad,
        kernel_share,
        qkv_out,
        proj_share,
        up_share,
        ffn_share,
        down_share,
        feed_sums[1:2],
    )


def solution(mesh):
    return jax.shard_map(
        on_device,
        mesh=mesh,
        in_specs=(
            P(AXES, None, None),
            P(),
            P(),
            P(),
            P(AXES, None, None),
            P(AXES, None),
            P(None, AXES),
            P(None, AXES),
            P(AXES, None),
            P(AXES, None),
            P(AXES, None),
            P(None, AXES),
            P(AXES, None),
        ),
        out_specs=(
            P(AXES, None, None),
            P(AXES, None, None),
            P(AXES, None),
            P(None, AXES),
            P(None, AXES),
            P(AXES, None),
            P(AXES, None),
            P(AXES, None),
            P(None, AXES),
            P(AXES, None),
            P(AXES, None),
        ),
        check_vma=False,
    )
```

```python
import functools
import math

import jax
import jax.numpy as jnp
from jax import lax
from jax.experimental import pallas as pl
from jax.experimental.pallas import tpu as pltpu
from jax.sharding import PartitionSpec as P

HEAD = 64
SIDE = 32
HALF_SIDE = SIDE // 2
STRIP = HALF_SIDE
PLANE = HALF_SIDE * HALF_SIDE
PADDED = PLANE + 2 * STRIP
TILE = 256
CHUNKS = 3

highest = lax.Precision.HIGHEST
ln_epsilon = 1e-06
masked_score = -1000000000.0
low = jnp.bfloat16
full = jnp.float32
AXES = ("dp", "fsdp")


def device_count():
    return lax.axis_size("dp") * lax.axis_size("fsdp")


def swap(x, bit):
    return lax.ppermute(x, AXES, [(i, i ^ 1 << bit) for i in range(device_count())])


def swap_core(x):
    return swap(x, 0)


def gather_order(chip_bits, colour):
    order = list(range(chip_bits - 1, -1, -1))
    if colour and chip_bits > 1:
        order[-1], order[-2] = order[-2], order[-1]
    return order


class Flow:
    def __init__(self, steps):
        self.steps = steps
        self.wanted = next(steps)
        self.result = None

    def arrive(self, array):
        try:
            self.wanted = self.steps.send(array)
        except StopIteration as end:
            self.wanted, self.result = None, end.value


class Slots:
    def __init__(self, token):
        self.token = token

    def after(self, *arrays):
        arrays, self.token = lax.optimization_barrier((arrays, self.token))
        return arrays

    def finish(self, flows):
        while any(flow.wanted is not None for flow in flows):
            self(flows)

    def __call__(self, flows, work=lambda: ()):
        flows = [flow for flow in flows if flow.wanted is not None]
        wanted = [flow.wanted for flow in flows]
        leaving, self.token = lax.optimization_barrier(
            ([[array for array, _ in pairs] for pairs in wanted], self.token)
        )
        arriving = [
            [swap(array, bit + 1) for array, (_, bit) in zip(arrays, pairs)]
            for arrays, pairs in zip(leaving, wanted)
        ]
        arriving, result, self.token = lax.optimization_barrier((arriving, work(), self.token))
        for flow, arrays in zip(flows, arriving):
            flow.arrive(arrays)
        return result


def join(held, arriving):
    return [jnp.concatenate(pair, axis=0) for pair in zip(held, arriving)]


def near_steps(shards, chip_bits):
    held = [shard[None] for shard in shards]
    for bit in range(chip_bits - 1, 1, -1):
        arriving = yield [(array, bit) for array in held]
        held = join(held, arriving)
    return held


def one_colour_steps(shard, chip_bits):
    held = shard[None]
    for bit in range(chip_bits - 1, 0, -1):
        (arriving,) = yield [(held, bit)]
        held = jnp.concatenate([held, arriving], axis=0)
    (arriving,) = yield [(held, 0)]
    return held, arriving


def core_steps(array):
    (arriving,) = yield [(array, -1)]
    return arriving


def far_steps(held):
    arriving = yield [(held[0], 1), (held[1], 0)]
    held = join(held, arriving)
    arriving = yield [(held[0], 0), (held[1], 1)]
    return list(zip(held, arriving))


def assemble_body(steps, chip_ref, *refs):
    *piece_refs, out_ref = refs
    which = pl.program_id(0) // steps
    top = chip_ref[1]
    for index, piece_ref in enumerate(piece_refs):

        @pl.when(which == index)
        def _():
            for k in range(4):
                out_ref[jnp.bitwise_xor(top, (k & 1) << 1 | k >> 1), 0] = piece_ref[k]


def assemble(pieces, order, chip):
    chips = sum(piece.shape[0] for piece in pieces)
    rows, columns = pieces[0].shape[1:]
    if chips < 4 or len(pieces) * pieces[0].shape[0] != chips or pieces[0].shape[0] % 4:
        raise ValueError("unexpected mesh")
    rest = len(order) - 2
    steps = pieces[0].shape[0] // 4
    chip_words = jnp.stack([jnp.bitwise_and(chip, (1 << rest) - 1), chip >> rest]).astype(jnp.int32)

    def out_map(step, words):
        at = words[0]
        for position, bit in enumerate(order[2:]):
            at = jnp.bitwise_xor(at, jnp.bitwise_and(step >> position, 1) << bit)
        return (0, at, 0, 0)

    def piece_map(index):
        return lambda step, words: (jnp.clip(step - index * steps, 0, steps - 1), 0, 0)

    out = pl.pallas_call(
        functools.partial(assemble_body, steps),
        grid_spec=pltpu.PrefetchScalarGridSpec(
            num_scalar_prefetch=1,
            grid=(chips // 4,),
            in_specs=[
                pl.BlockSpec((4, rows, columns), piece_map(index)) for index in range(len(pieces))
            ],
            out_specs=pl.BlockSpec((4, 1, rows, columns), out_map),
        ),
        out_shape=jax.ShapeDtypeStruct((4, chips // 4, rows, columns), pieces[0].dtype),
        cost_estimate=pl.CostEstimate(
            flops=0, bytes_accessed=4 * chips * rows * columns, transcendentals=0
        ),
        name="assemble",
    )(chip_words, *pieces)
    return out.reshape(chips, rows, columns)


def at_bit(array, axis, bit):
    return lax.dynamic_index_in_dim(array, bit, axis, keepdims=False)


def halves_at(held, axis, mine, sent):
    leaving = sum(at_bit(h, axis, 1 - mine).astype(full) for h in held).astype(sent)
    staying = sum(at_bit(h, axis, mine).astype(full) for h in held).astype(sent)
    return leaving, staying


def scatter_steps(parts, chip, chip_bits, sent):
    orders = [gather_order(chip_bits, colour)[::-1] for colour in range(len(parts))]
    lefts = [list(range(chip_bits - 1, -1, -1)) for _ in parts]
    held = [[array.reshape((2,) * chip_bits + array.shape[1:])] for array in parts]
    for step in range(chip_bits):
        if step == 2 and len(held) == 2:
            held = [[jnp.concatenate(pair, axis=-1) for pair in zip(*held)]]
        leaving, staying = [], []
        for order, left, arrays in zip(orders, lefts, held):
            bit = order[step]
            axis = left.index(bit)
            left.remove(bit)
            going, kept = halves_at(arrays, axis, jnp.bitwise_and(chip >> bit, 1), sent)
            leaving.append((going, bit))
            staying.append(kept)
        arriving = yield leaving
        held = [list(pair) for pair in zip(staying, arriving)]
    ((kept, arrived),) = held
    return kept.astype(full) + arrived.astype(full)


def halving_steps(leaving, staying, order):
    (arriving,) = yield [(leaving, order[0])]
    for bit in order[1:]:
        half = staying.shape[0] // 2
        leaving, staying = [
            (staying[at].astype(full) + arriving[at].astype(full)).astype(low)
            for at in (slice(half, None), slice(half))
        ]
        (arriving,) = yield [(leaving, bit)]
    return (staying.astype(full) + arriving.astype(full))[0]


def owners(colour, chip, chip_bits):
    order = gather_order(chip_bits, colour)
    spots = jnp.arange(1 << chip_bits)
    bits = list(enumerate(order))
    owner = sum((jnp.bitwise_and(spots >> at, 1) << bit) for at, bit in bits)
    apart = jnp.bitwise_xor(spots, chip)
    place = sum((jnp.bitwise_and(apart >> bit, 1) << at) for at, bit in bits)
    return jnp.bitwise_xor(owner, chip), place


def scatter_flow(parts, chip, chip_bits, sent=low):
    return Flow(scatter_steps(parts, chip, chip_bits, sent))


def row_steps(row, chip, chip_bits, first_bit):
    held = row[None]
    for bit in range(chip_bits):
        (arriving,) = yield [(held, bit + first_bit - 1)]
        held = jnp.concatenate([held, arriving], axis=0)
    places = jnp.arange(1 << chip_bits)
    pick = jnp.bitwise_xor(places, chip)[:, None] == places[None, :]
    return jnp.dot(pick.astype(held.dtype), held, preferred_element_type=full).astype(held.dtype)


def row_flow(row, chip, chip_bits, first_bit=1):
    return Flow(row_steps(row, chip, chip_bits, first_bit))


def run(flow):
    while flow.wanted is not None:
        flow.arrive([swap(array, bit + 1) for array, bit in flow.wanted])
    return flow.result


def to_phases(block_in, row_count):
    width = block_in.shape[-1]
    split_grid = block_in.reshape(row_count // 2, 2, HALF_SIDE, 2, width)
    return split_grid.transpose(1, 3, 0, 2, 4).reshape(4, row_count // 2 * HALF_SIDE, width)


def from_phases(block_in, row_count):
    width = block_in.shape[-1]
    split_grid = block_in.reshape(2, 2, row_count // 2, HALF_SIDE, width)
    return split_grid.transpose(2, 0, 3, 1, 4).reshape(row_count * SIDE, width)


def in_core_order(mine, other, core):
    return jnp.where(core == 0, mine, other), jnp.where(core == 0, other, mine)


def join_halves(mine, other, core):
    return jnp.stack(in_core_order(mine, other, core), axis=1).reshape(-1, mine.shape[-1])


def half_of(joined, which):
    width = joined.shape[-1]
    return at_bit(joined.reshape(4, 2, -1, width), 1, which)


def layer_norm(values):
    average = jnp.mean(values, axis=-1, keepdims=True)
    centred = values - average
    variance = jnp.mean(centred * centred, axis=-1, keepdims=True)
    return centred * lax.rsqrt(variance + ln_epsilon)


def modulate(values, shift_by, scale_by):
    return layer_norm(values) * (1.0 + scale_by) + shift_by


def sinusoid(steps_in, width):
    halfway = width // 2
    frequency = jnp.exp(-math.log(10000.0) * jnp.arange(halfway, dtype=jnp.float32) / halfway)
    angles = steps_in.astype(jnp.float32)[..., None] * frequency
    return jnp.concatenate([jnp.cos(angles), jnp.sin(angles)], axis=-1)


def softmax_of(query, key, allowed):
    raw = lax.dot_general(query, key, (((1,), (1,)), ((), ())), preferred_element_type=full)
    scores = jnp.where(allowed, raw * HEAD ** (-0.5), masked_score)
    shifted = jnp.exp(scores - jnp.max(scores, axis=-1, keepdims=True))
    return shifted / jnp.sum(shifted, axis=-1, keepdims=True)


def head_lanes(shape, head):
    lanes = lax.broadcasted_iota(jnp.int32, shape, 1)
    return jnp.logical_and(lanes >= head * HEAD, lanes < (head + 1) * HEAD)


def attend_body(mask_ref, qkv_ref, out_ref):
    allowed = mask_ref[...] > 0.5

    @pl.loop(0, 4)
    def _(phase):
        rows = pl.ds(pl.multiple_of(phase * PLANE, PLANE), PLANE)
        query = qkv_ref[rows, :128]
        key = qkv_ref[rows, 128:256]
        value = qkv_ref[rows, 256:]
        total = None
        for head in range(2):
            here = head_lanes(key.shape, head)
            probs = softmax_of(query, jnp.where(here, key, jnp.zeros_like(key)), allowed)
            part = jnp.dot(
                probs.astype(low),
                jnp.where(here, value, jnp.zeros_like(value)),
                preferred_element_type=full,
            )
            total = part if total is None else total + part
        out_ref[rows, :] = total.astype(low)


def attend_back_body(mask_ref, qkv_ref, grad_ref, out_ref):
    allowed = mask_ref[...] > 0.5

    @pl.loop(0, 4)
    def _(phase):
        rows = pl.ds(pl.multiple_of(phase * PLANE, PLANE), PLANE)
        query = qkv_ref[rows, :128]
        key = qkv_ref[rows, 128:256]
        value = qkv_ref[rows, 256:]
        grad = grad_ref[rows, :]
        by_rows = (((0,), (0,)), ((), ()))
        totals = [None, None, None]
        for head in range(2):
            here = head_lanes(key.shape, head)
            blank = jnp.zeros_like(key)
            key_here = jnp.where(here, key, blank)
            query_here = jnp.where(here, query, blank)
            value_here = jnp.where(here, value, blank)
            grad_here = jnp.where(here, grad, blank)
            weights = softmax_of(query, key_here, allowed)
            grad_probs = lax.dot_general(
                grad, value_here, (((1,), (1,)), ((), ())), preferred_element_type=full
            )
            delta = jnp.sum(grad_probs * weights, axis=-1, keepdims=True)
            grad_scores = (weights * (grad_probs - delta)).astype(low)
            parts = (
                jnp.dot(grad_scores, key_here, preferred_element_type=full),
                lax.dot_general(grad_scores, query_here, by_rows, preferred_element_type=full),
                lax.dot_general(
                    weights.astype(low), grad_here, by_rows, preferred_element_type=full
                ),
            )
            totals = [p if t is None else t + p for t, p in zip(totals, parts)]
        out_ref[rows, :128] = (totals[0] * HEAD ** (-0.5)).astype(low)
        out_ref[rows, 128:256] = (totals[1] * HEAD ** (-0.5)).astype(low)
        out_ref[rows, 256:] = totals[2].astype(low)


def attend(mask, qkv):
    tokens, width = qkv.shape
    pairs = width // 384
    return pl.pallas_call(
        attend_body,
        grid=(pairs,),
        in_specs=[
            pl.BlockSpec((PLANE, PLANE), lambda j: (0, 0)),
            pl.BlockSpec((tokens, 384), lambda j: (0, j)),
        ],
        out_specs=pl.BlockSpec((tokens, 128), lambda j: (0, j)),
        out_shape=jax.ShapeDtypeStruct((tokens, pairs * 128), low),
        cost_estimate=pl.CostEstimate(
            flops=pairs * 2 * 4 * 4 * PLANE * PLANE * 256,
            bytes_accessed=8 * tokens * pairs * 128,
            transcendentals=pairs * 8 * PLANE * PLANE,
        ),
        name="attend",
    )(mask, qkv)


def attend_back(mask, qkv, grad):
    tokens, width = qkv.shape
    pairs = width // 384
    return pl.pallas_call(
        attend_back_body,
        grid=(pairs,),
        in_specs=[
            pl.BlockSpec((PLANE, PLANE), lambda j: (0, 0)),
            pl.BlockSpec((tokens, 384), lambda j: (0, j)),
            pl.BlockSpec((tokens, 128), lambda j: (0, j)),
        ],
        out_specs=pl.BlockSpec((tokens, 384), lambda j: (0, j)),
        out_shape=jax.ShapeDtypeStruct((tokens, width), low),
        cost_estimate=pl.CostEstimate(
            flops=pairs * 2 * 4 * 10 * PLANE * PLANE * 256,
            bytes_accessed=14 * tokens * pairs * 128,
            transcendentals=pairs * 8 * PLANE * PLANE,
        ),
        name="attend_back",
    )(mask, qkv, grad)


def strip_at(ref, row_phase, column_phase, row):
    start = pl.multiple_of((row + 1) * STRIP, STRIP)
    return ref[2 * row_phase + column_phase, pl.ds(start, STRIP), :]


def near_strips(ref, row):
    tokens = lax.broadcasted_iota(jnp.int32, (STRIP, ref.shape[-1]), 0)
    loaded = {}
    for row_phase, at in ((1, row - 1), (0, row), (1, row), (0, row + 1)):
        even = strip_at(ref, row_phase, 0, at)
        odd = strip_at(ref, row_phase, 1, at)
        before = jnp.where(tokens == 0, 0.0, pltpu.roll(odd, 1, 0))
        after = jnp.where(tokens == STRIP - 1, 0.0, pltpu.roll(even, STRIP - 1, 0))
        loaded[len(loaded)] = ((before, even, odd), (even, odd, after))
    return {0: (loaded[0], loaded[1], loaded[2]), 1: (loaded[1], loaded[2], loaded[3])}


def conv_strip(near, kernel, row_phase, column_phase):
    total = None
    for i in range(3):
        for j in range(3):
            term = near[row_phase][i][column_phase][j] * kernel[3 * i + j : 3 * i + j + 1, :]
            total = term if total is None else total + term
    return total


def feed_body(
    spread,
    words_ref,
    norm_ref,
    norm_t_ref,
    grad_ref,
    *refs,
):
    pieces = 2 if spread else 1
    up_refs, refs = refs[:pieces], refs[pieces:]
    down_refs, refs = refs[:pieces], refs[pieces:]
    kernel_ref, staying_ref, leaving_ref, *refs = refs
    up_grad_refs, refs = refs[:pieces], refs[pieces:]
    down_grad_refs, refs = refs[:pieces], refs[pieces:]
    kernel_grad_ref, branch_acc, back_acc, hidden, widened_grad, act_grad, act, hidden_grad = refs[
        :8
    ]
    step = pl.program_id(0)
    core = words_ref[0]
    by_columns = (((1,), (1,)), ((), ()))
    width = kernel_ref.shape[1]
    model = norm_t_ref.shape[0]
    up_ref, down_ref = up_refs[0], down_refs[0]
    if spread:
        up_ref, down_all = refs[8:]
        half, share, _ = up_refs[0].shape
        piece = down_refs[0].shape[1]
        chips = 2 * half
        down_ref = down_all.at[pl.ds(pl.multiple_of(step * width, width), width), :]

        for which in range(2):

            @pl.loop(0, half)
            def _(spot):
                start = pl.multiple_of(words_ref[1 + which * half + spot] * share, share)
                up_ref[pl.ds(start, share), :] = up_refs[which][spot]

            @pl.when(step == 0)
            def _():
                @pl.loop(0, half)
                def _(spot):
                    owner = words_ref[1 + chips + which * half + spot]
                    start = pl.multiple_of(owner * piece, piece)
                    down_all[pl.ds(start, piece), :] = down_refs[which][spot]

    @pl.when(step == 0)
    def _():
        blank = jnp.zeros((STRIP, width), full)
        for plane in range(4):
            for ref in (hidden, widened_grad):
                ref[plane, pl.ds(0, STRIP), :] = blank
                ref[plane, pl.ds(PLANE + STRIP, STRIP), :] = blank
        branch_acc[...] = jnp.zeros_like(branch_acc)
        back_acc[...] = jnp.zeros_like(back_acc)

    @pl.loop(0, 4)
    def _(plane):
        rows = pl.ds(pl.multiple_of(plane * PLANE, PLANE), PLANE)
        hidden[plane, pl.ds(STRIP, PLANE), :] = jnp.dot(
            norm_ref[rows, :], up_ref[...], preferred_element_type=full
        )
        act_grad[rows, :] = lax.dot_general(
            grad_ref[rows, :], down_ref[...], by_columns, preferred_element_type=full
        )

    kernel = kernel_ref[...]

    def forward_strip(row, sums):
        near = near_strips(hidden, row)
        sums = list(sums)
        for row_phase in range(2):
            for column_phase in range(2):
                plane = 2 * row_phase + column_phase
                wide = conv_strip(near, kernel, row_phase, column_phase)
                square = wide * wide
                bend = math.sqrt(2.0 / math.pi) * (wide + 0.044715 * wide * square)
                curve = jnp.tanh(bend)
                half = 0.5 * (1.0 + curve)
                slope = half + 0.5 * wide * (1.0 - curve * curve) * (
                    math.sqrt(2.0 / math.pi) * (1.0 + 3 * 0.044715 * square)
                )
                at = pl.ds(pl.multiple_of(plane * PLANE + row * STRIP, STRIP), STRIP)
                act[at, :] = (wide * half).astype(low)
                grad_here = slope * act_grad[at, :]
                widened_grad[plane, pl.ds(pl.multiple_of((row + 1) * STRIP, STRIP), STRIP), :] = (
                    grad_here
                )
                for i in range(3):
                    for j in range(3):
                        product = near[row_phase][i][column_phase][j] * grad_here
                        sums[3 * i + j] = sums[3 * i + j] + (product[:8] + product[8:])
        return tuple(sums)

    sums = lax.fori_loop(
        0, HALF_SIDE, forward_strip, tuple(jnp.zeros((8, width), full) for _ in range(9))
    )
    kernel_grad_ref[...] = jnp.concatenate(
        [jnp.sum(s, axis=0, keepdims=True) for s in sums] + [jnp.zeros((7, width), full)], axis=0
    )

    flipped = [kernel[8 - t : 9 - t, :] for t in range(9)]
    flipped = jnp.concatenate(flipped, axis=0)

    @pl.loop(0, HALF_SIDE)
    def _(row):
        near = near_strips(widened_grad, row)
        for row_phase in range(2):
            for column_phase in range(2):
                plane = 2 * row_phase + column_phase
                at = pl.ds(pl.multiple_of(plane * PLANE + row * STRIP, STRIP), STRIP)
                hidden_grad[at, :] = conv_strip(near, flipped, row_phase, column_phase).astype(low)

    @pl.loop(0, 4)
    def _(plane):
        rows = pl.ds(pl.multiple_of(plane * PLANE, PLANE), PLANE)
        branch_acc[rows, :] += jnp.dot(act[rows, :], down_ref[...], preferred_element_type=full)
        back_acc[rows, :] += lax.dot_general(
            hidden_grad[rows, :], up_ref[...], by_columns, preferred_element_type=full
        )

    if spread:
        for which in range(2):

            @pl.loop(0, half // 4)
            def _(group):
                lhs = []
                for k in range(4):
                    owner = words_ref[1 + which * half + 4 * group + k]
                    start = pl.multiple_of(owner * share, share)
                    lhs.append(norm_t_ref[pl.ds(start, share), :])
                result = jnp.dot(
                    jnp.concatenate(lhs, axis=0), hidden_grad[...], preferred_element_type=full
                ).astype(low)
                for k in range(4):
                    up_grad_refs[which][4 * group + k] = result[k * share : (k + 1) * share]

    else:

        @pl.loop(0, model // TILE)
        def _(tile):
            rows = pl.ds(pl.multiple_of(tile * TILE, TILE), TILE)
            up_grad_refs[0][rows, :] = jnp.dot(
                norm_t_ref[rows, :], hidden_grad[...], preferred_element_type=full
            ).astype(low)

    down_grad = lax.dot_general(
        act[...], grad_ref[...], (((0,), (0,)), ((), ())), preferred_element_type=full
    ).astype(low)
    if spread:
        for k in range(width // piece):
            place = words_ref[1 + 2 * chips + step * (width // piece) + k]
            for which in range(2):

                @pl.when(place // half == which)
                def _():
                    down_grad_refs[which][place - which * half] = down_grad[
                        k * piece : (k + 1) * piece
                    ]

    else:
        down_grad_refs[0][...] = down_grad

    @pl.when(step == pl.num_programs(0) - 1)
    def _():
        for ref, which in ((staying_ref, core), (leaving_ref, 1 - core)):
            for index, acc in enumerate((branch_acc, back_acc)):
                for plane in range(4):
                    start = plane * PLANE + pl.multiple_of(which * (PLANE // 2), PLANE // 2)
                    ref[index, plane] = acc[pl.ds(start, PLANE // 2), :].astype(low)


def feed_forward(norm, norm_t, grad, up, down, kernel, words):
    tokens, model = norm.shape
    channels = kernel.shape[1]
    width = TILE
    spread = len(up) == 2
    whole = lambda j, words: (0, 0)
    half = lambda j, words: (0, 0, 0, 0)
    across = lambda j, words: (0, j)
    once = pl.Buffered(1)
    piece_scratch = []
    if spread:
        deep = lambda j, words: (0, 0, 0)
        up_spec = pl.BlockSpec(up[0].shape[:2] + (width,), lambda j, words: (0, 0, j))
        down_spec = pl.BlockSpec(down[0].shape, deep, pipeline_mode=once)
        down_grad_spec = pl.BlockSpec(down[0].shape, deep)
        piece_scratch = [pltpu.VMEM((model, width), low), pltpu.VMEM((channels, model), low)]
    else:
        up_spec = pl.BlockSpec((model, width), across)
        down_spec = down_grad_spec = pl.BlockSpec((width, model), lambda j, words: (j, 0))
    halves = jax.ShapeDtypeStruct((2, 4, PLANE // 2, model), low)
    like = lambda arrays: [jax.ShapeDtypeStruct(array.shape, low) for array in arrays]
    out = pl.pallas_call(
        functools.partial(feed_body, spread),
        grid_spec=pltpu.PrefetchScalarGridSpec(
            num_scalar_prefetch=1,
            grid=(channels // width,),
            in_specs=[
                pl.BlockSpec((tokens, model), whole, pipeline_mode=once),
                pl.BlockSpec((model, tokens), whole, pipeline_mode=once),
                pl.BlockSpec((tokens, model), whole, pipeline_mode=once),
                *[up_spec] * len(up),
                *[down_spec] * len(down),
                pl.BlockSpec((16, width), across),
            ],
            out_specs=[
                pl.BlockSpec(halves.shape, half),
                pl.BlockSpec(halves.shape, half),
                *[up_spec] * len(up),
                *[down_grad_spec] * len(down),
                pl.BlockSpec((16, width), across),
            ],
            scratch_shapes=[
                pltpu.VMEM((tokens, model), full),
                pltpu.VMEM((tokens, model), full),
                pltpu.VMEM((4, PADDED, width), full),
                pltpu.VMEM((4, PADDED, width), full),
                pltpu.VMEM((tokens, width), full),
                pltpu.VMEM((tokens, width), low),
                pltpu.VMEM((tokens, width), low),
            ]
            + piece_scratch,
        ),
        out_shape=[halves, halves]
        + like(up)
        + like(down)
        + [jax.ShapeDtypeStruct((16, channels), full)],
        compiler_params=pltpu.CompilerParams(vmem_limit_bytes=63 * 1024 * 1024),
        cost_estimate=pl.CostEstimate(
            flops=12 * tokens * model * channels,
            bytes_accessed=8 * model * channels + 10 * tokens * model,
            transcendentals=tokens * channels,
        ),
        name="feed_forward",
    )(words, norm, norm_t, grad, *up, *down, kernel)
    staying, leaving, *grads, kernel_grad = out
    return staying, leaving, grads[: len(up)], grads[len(up) :], kernel_grad


def token_stats(x_ref, average, scale):
    @pl.loop(0, x_ref.shape[0] // STRIP)
    def _(strip):
        rows = pl.ds(pl.multiple_of(strip * STRIP, STRIP), STRIP)
        values = x_ref[rows, :].astype(full)
        mean = jnp.mean(values, axis=-1, keepdims=True)
        centred = values - mean
        variance = jnp.mean(centred * centred, axis=-1, keepdims=True)
        average[rows, :] = jnp.broadcast_to(mean, (STRIP, 128))
        scale[rows, :] = jnp.broadcast_to(lax.rsqrt(variance + ln_epsilon), (STRIP, 128))


def normed_strip(x_ref, average, scale, rows, columns):
    width = columns.size
    wide = lambda ref: jnp.concatenate([ref[rows, :]] * (width // 128), axis=1)
    return (x_ref[rows, columns].astype(full) - wide(average)) * wide(scale)


def frame_zeros(refs):
    for ref in refs:
        blank = jnp.zeros((STRIP, ref.shape[-1]), full)
        for plane in range(4):
            ref[plane, pl.ds(0, STRIP), :] = blank
            ref[plane, pl.ds(ref.shape[1] - STRIP, STRIP), :] = blank


def conv_in_body(x_ref, kernel_ref, mods_ref, out_ref, average, scale, normed):
    step = pl.program_id(0)
    width = out_ref.shape[1]
    columns = pl.ds(pl.multiple_of(step * width, width), width)

    @pl.when(step == 0)
    def _():
        token_stats(x_ref, average, scale)
        frame_zeros([normed])

    shift_by = mods_ref[0:1, :]
    scale_by = 1.0 + mods_ref[1:2, :]

    @pl.loop(0, HALF_SIDE)
    def _(row):
        for plane in range(4):
            rows = pl.ds(pl.multiple_of(plane * PLANE + row * STRIP, STRIP), STRIP)
            normed[plane, pl.ds(pl.multiple_of((row + 1) * STRIP, STRIP), STRIP), :] = (
                normed_strip(x_ref, average, scale, rows, columns) * scale_by + shift_by
            )

    kernel = kernel_ref[...]

    @pl.loop(0, HALF_SIDE)
    def _(row):
        near = near_strips(normed, row)
        for row_phase in range(2):
            for column_phase in range(2):
                plane = 2 * row_phase + column_phase
                at = pl.ds(pl.multiple_of(plane * PLANE + row * STRIP, STRIP), STRIP)
                out_ref[at, :] = conv_strip(near, kernel, row_phase, column_phase).astype(low)


def conv_in(canvas, kernel, mods):
    tokens, model = canvas.shape
    return pl.pallas_call(
        conv_in_body,
        grid=(model // TILE,),
        in_specs=[
            pl.BlockSpec((tokens, model), lambda j: (0, 0), pipeline_mode=pl.Buffered(1)),
            pl.BlockSpec((16, TILE), lambda j: (0, j)),
            pl.BlockSpec((8, TILE), lambda j: (0, j)),
        ],
        out_specs=pl.BlockSpec((tokens, TILE), lambda j: (0, j)),
        out_shape=jax.ShapeDtypeStruct((tokens, model), low),
        scratch_shapes=[
            pltpu.VMEM((tokens, 128), full),
            pltpu.VMEM((tokens, 128), full),
            pltpu.VMEM((4, PADDED, TILE), full),
        ],
        cost_estimate=pl.CostEstimate(
            flops=30 * tokens * model, bytes_accessed=4 * tokens * model, transcendentals=tokens
        ),
        name="conv_in",
    )(canvas, kernel, mods)


def conv_back_body(
    core_ref,
    x_ref,
    kept_ref,
    arriving_ref,
    kernel_ref,
    mods_ref,
    middle_ref,
    out_ref,
    kernel_grad_ref,
    mods_grad_ref,
    average,
    scale,
    normed,
    upstream,
    held,
    sum_plain,
    sum_normed,
    woven,
):
    step = pl.program_id(0)
    core = core_ref[0]
    width = kept_ref.shape[1]
    near_rows = x_ref.shape[0] // 4 // STRIP
    own_rows = near_rows - 1
    columns = pl.ds(pl.multiple_of(step * width, width), width)

    def near_at(plane, row):
        return pl.ds(pl.multiple_of((plane * near_rows + row) * STRIP, STRIP), STRIP)

    def own_at(plane, row):
        return pl.ds(pl.multiple_of((plane * own_rows + row) * STRIP, STRIP), STRIP)

    @pl.when(step == 0)
    def _():
        token_stats(x_ref, average, scale)
        frame_zeros([normed, upstream])
        sum_plain[...] = jnp.zeros_like(sum_plain)
        sum_normed[...] = jnp.zeros_like(sum_normed)

    shift_by = mods_ref[0:1, :]
    scale_by = 1.0 + mods_ref[1:2, :]

    @pl.loop(0, near_rows)
    def _(row):
        for plane in range(4):
            rows = near_at(plane, row)
            padded = pl.ds(pl.multiple_of((row + 1) * STRIP, STRIP), STRIP)
            normed[plane, padded, :] = (
                normed_strip(x_ref, average, scale, rows, columns) * scale_by + shift_by
            )
            upstream[plane, padded, :] = kept_ref[rows, :].astype(full) + arriving_ref[
                rows, :
            ].astype(full)

    kernel = kernel_ref[...]
    flipped = jnp.concatenate([kernel[8 - t : 9 - t, :] for t in range(9)], axis=0)

    def kernel_strip(row, sums):
        near = near_strips(normed, row + core)
        sums = list(sums)
        for row_phase in range(2):
            for column_phase in range(2):
                grad_here = strip_at(upstream, row_phase, column_phase, row + core)
                for i in range(3):
                    for j in range(3):
                        product = near[row_phase][i][column_phase][j] * grad_here
                        sums[3 * i + j] = sums[3 * i + j] + (product[:8] + product[8:])
        return tuple(sums)

    def fold(sums, rows):
        return jnp.concatenate(
            [jnp.sum(s, axis=0, keepdims=True) for s in sums]
            + [jnp.zeros((rows - len(sums), width), full)],
            axis=0,
        )

    blank = jnp.zeros((8, width), full)
    kernel_grad_ref[...] = fold(lax.fori_loop(0, own_rows, kernel_strip, (blank,) * 9), 16)

    def input_strip(row, sums):
        near = near_strips(upstream, row + core)
        shift_sum, scale_sum = sums
        for row_phase in range(2):
            for column_phase in range(2):
                plane = 2 * row_phase + column_phase
                grad = conv_strip(near, flipped, row_phase, column_phase)
                plain = normed_strip(x_ref, average, scale, near_at(plane, row + core), columns)
                shift_sum = shift_sum + (grad[:8] + grad[8:])
                product = grad * plain
                scale_sum = scale_sum + (product[:8] + product[8:])
                scaled = grad * scale_by
                rows = own_at(plane, row)
                held[step, rows, :] = scaled
                product = scaled * plain
                sum_plain[rows, :] += sum(scaled[:, k : k + 128] for k in range(0, width, 128))
                sum_normed[rows, :] += sum(product[:, k : k + 128] for k in range(0, width, 128))
        return shift_sum, scale_sum

    mods_grad_ref[...] = fold(lax.fori_loop(0, own_rows, input_strip, (blank,) * 2), 8)

    @pl.when(step == pl.num_programs(0) - 1)
    def _():
        model = x_ref.shape[1]

        @pl.loop(0, own_rows)
        def _(row):
            for plane in range(4):
                rows = own_at(plane, row)
                near = near_at(plane, row + core)
                mean_plain = jnp.sum(sum_plain[rows, :], axis=-1, keepdims=True) / model
                mean_normed = jnp.sum(sum_normed[rows, :], axis=-1, keepdims=True) / model
                for block in range(model // width):
                    at = pl.ds(block * width, width)
                    plain = normed_strip(x_ref, average, scale, near, at)
                    spread = jnp.concatenate([scale[near, :]] * (width // 128), axis=1)
                    result = middle_ref[rows, at] + spread * (
                        held[block, rows, :] - mean_plain - plain * mean_normed
                    )
                    for lane in range(0, width, 128):
                        woven[(block * width + lane) // 128, pl.ds(plane % 2, STRIP, stride=2), :] = (
                            result[:, lane : lane + 128]
                        )
                if plane % 2 == 1:
                    start = pl.multiple_of((2 * row + plane // 2) * SIDE, SIDE)
                    for lane in range(model // 128):
                        out_ref[pl.ds(start, SIDE), lane * 128 : lane * 128 + 128] = woven[lane]


def conv_back(core, x_near, kept, arriving, kernel, mods, grad_middle):
    near_tokens, model = x_near.shape
    own_tokens = grad_middle.shape[0]
    once = pl.Buffered(1)
    whole = lambda j, words: (0, 0)
    across = lambda j, words: (0, j)
    padded = near_tokens // 4 + 2 * STRIP
    return pl.pallas_call(
        conv_back_body,
        grid_spec=pltpu.PrefetchScalarGridSpec(
            num_scalar_prefetch=1,
            grid=(model // TILE,),
            in_specs=[
                pl.BlockSpec((near_tokens, model), whole, pipeline_mode=once),
                pl.BlockSpec((near_tokens, TILE), across),
                pl.BlockSpec((near_tokens, TILE), across),
                pl.BlockSpec((16, TILE), across),
                pl.BlockSpec((8, TILE), across),
                pl.BlockSpec((own_tokens, model), whole, pipeline_mode=once),
            ],
            out_specs=[
                pl.BlockSpec((own_tokens, model), whole),
                pl.BlockSpec((16, TILE), across),
                pl.BlockSpec((8, TILE), across),
            ],
            scratch_shapes=[
                pltpu.VMEM((near_tokens, 128), full),
                pltpu.VMEM((near_tokens, 128), full),
                pltpu.VMEM((4, padded, TILE), full),
                pltpu.VMEM((4, padded, TILE), full),
                pltpu.VMEM((model // TILE, own_tokens, TILE), full),
                pltpu.VMEM((own_tokens, 128), full),
                pltpu.VMEM((own_tokens, 128), full),
                pltpu.VMEM((model // 128, SIDE, 128), full),
            ],
        ),
        out_shape=[
            jax.ShapeDtypeStruct((own_tokens, model), full),
            jax.ShapeDtypeStruct((16, model), full),
            jax.ShapeDtypeStruct((8, model), full),
        ],
        cost_estimate=pl.CostEstimate(
            flops=70 * own_tokens * model,
            bytes_accessed=14 * own_tokens * model,
            transcendentals=near_tokens,
        ),
        name="conv_back",
    )(core[None].astype(jnp.int32), x_near, kept, arriving, kernel, mods, grad_middle)


def row_stats(values):
    mean = jnp.mean(values, axis=-1, keepdims=True)
    centred = values - mean
    scale = lax.rsqrt(jnp.mean(centred * centred, axis=-1, keepdims=True) + ln_epsilon)
    return centred * scale, scale


def enter_feed_body(x_ref, part_ref, other_ref, grad_ref, mods_ref, norm_ref, norm_t_ref, out_ref):
    @pl.loop(0, x_ref.shape[0] // STRIP)
    def _(strip):
        rows = pl.ds(pl.multiple_of(strip * STRIP, STRIP), STRIP)
        branch = part_ref[rows, :].astype(full) + other_ref[rows, :].astype(full)
        plain, _ = row_stats(x_ref[rows, :].astype(full) + mods_ref[0:1, :] * branch)
        normed = plain * (1.0 + mods_ref[2:3, :]) + mods_ref[1:2, :]
        norm_ref[rows, :] = normed.astype(low)
        out_ref[rows, :] = (grad_ref[rows, :].astype(full) * mods_ref[3:4, :]).astype(low)

    norm_t_ref[...] = norm_ref[...].T


def enter_feed(canvas, part, other, grad, mods):
    tokens, model = canvas.shape
    rows = PLANE // 2
    along = pl.BlockSpec((rows, model), lambda j: (j, 0))
    return pl.pallas_call(
        enter_feed_body,
        grid=(tokens // rows,),
        in_specs=[along] * 4 + [pl.BlockSpec((8, model), lambda j: (0, 0))],
        out_specs=[along, pl.BlockSpec((model, rows), lambda j: (0, j)), along],
        out_shape=[
            jax.ShapeDtypeStruct((tokens, model), low),
            jax.ShapeDtypeStruct((model, tokens), low),
            jax.ShapeDtypeStruct((tokens, model), low),
        ],
        cost_estimate=pl.CostEstimate(flops=1000, bytes_accessed=1000, transcendentals=0),
        name="enter_feed",
    )(canvas, part, other, grad, mods)


def leave_feed_body(words_ref, x_ref, part_ref, other_ref, grad_ref, mods_ref, *refs):
    *kept_refs, out_ref, middle_grad_ref, branch_grad_ref, sums_ref, totals = refs
    plane = pl.program_id(0)

    @pl.when(plane == 0)
    def _():
        totals[...] = jnp.zeros_like(totals)

    @pl.loop(0, x_ref.shape[0] // STRIP)
    def _(strip):
        rows = pl.ds(pl.multiple_of(strip * STRIP, STRIP), STRIP)
        gate_a, gate_f = mods_ref[0:1, :], mods_ref[3:4, :]
        branch_a = part_ref[rows, :].astype(full) + other_ref[rows, :].astype(full)
        middle = x_ref[rows, :].astype(full) + gate_a * branch_a
        plain, scale = row_stats(middle)
        branch_f = sum(ref[0, 0, rows, :].astype(full) for ref in kept_refs)
        back = sum(ref[1, 0, rows, :].astype(full) for ref in kept_refs)
        grad = grad_ref[rows, :].astype(full)
        out_ref[rows, :] = (middle + gate_f * branch_f).astype(low)
        scaled = back * (1.0 + mods_ref[2:3, :])
        mean_plain = jnp.mean(scaled, axis=-1, keepdims=True)
        mean_normed = jnp.mean(scaled * plain, axis=-1, keepdims=True)
        grad_middle = grad + scale * (scaled - mean_plain - plain * mean_normed)
        middle_grad_ref[rows, :] = grad_middle
        branch_grad_ref[rows, :] = (grad_middle * gate_a).astype(low)
        products = (grad_middle * branch_a, back, back * plain, grad * branch_f)
        for index, product in enumerate(products):
            totals[index] += product[:8] + product[8:]

    @pl.when(plane == pl.num_programs(0) - 1)
    def _():
        lines = [jnp.sum(totals[k], axis=0, keepdims=True) for k in range(4)]
        sums_ref[...] = jnp.concatenate(lines + [jnp.zeros_like(sums_ref[:4])], axis=0)


def leave_feed(words, canvas, part, other, grad, mods, kept):
    model = canvas.shape[1]
    rows = PLANE // 2
    own = pl.BlockSpec((rows, model), lambda j, words: (2 * j + words[0], 0))
    half = pl.BlockSpec((rows, model), lambda j, words: (j, 0))
    whole = pl.BlockSpec((8, model), lambda j, words: (0, 0))
    return pl.pallas_call(
        leave_feed_body,
        grid_spec=pltpu.PrefetchScalarGridSpec(
            num_scalar_prefetch=1,
            grid=(4,),
            in_specs=[own] * 4
            + [whole]
            + [pl.BlockSpec((2, 1, rows, model), lambda j, words: (0, j, 0, 0))] * len(kept),
            out_specs=[half, half, half, whole],
            scratch_shapes=[pltpu.VMEM((4, 8, model), full)],
        ),
        out_shape=[
            jax.ShapeDtypeStruct((4 * rows, model), low),
            jax.ShapeDtypeStruct((4 * rows, model), full),
            jax.ShapeDtypeStruct((4 * rows, model), low),
            jax.ShapeDtypeStruct((8, model), full),
        ],
        cost_estimate=pl.CostEstimate(flops=1000, bytes_accessed=1000, transcendentals=0),
        name="leave_feed",
    )(words, canvas, part, other, grad, mods, *kept)


def on_device(
    tokens,
    seg_ids,
    timesteps,
    labels,
    cotangent,
    mod_weight,
    class_table,
    attn_kernel,
    qkv_weight,
    proj_weight,
    up_weight,
    ffn_kernel,
    down_weight,
):
    devices = device_count()
    chips = devices // 2
    chip_bits = chips.bit_length() - 1
    rank = lax.axis_index("dp") * lax.axis_size("fsdp") + lax.axis_index("fsdp")
    core = rank % 2
    chip = rank // 2
    _, half_tokens, model = tokens.shape
    half_rows = half_tokens // SIDE
    class_count = class_table.shape[0]
    part = model // devices
    share = down_weight.shape[0]
    piece = share // CHUNKS
    pairs = model // HEAD // 4

    def halves_of(array, axis):
        return at_bit(array, axis, core), at_bit(array, axis, 1 - core)

    def row_pair(array, axis):
        kept, leaving = halves_of(array, axis)
        arriving = swap_core(leaving)
        return jnp.concatenate(in_core_order(kept, arriving, core), axis=0)

    qkv_split = qkv_weight.reshape(part, 3, 2, pairs, 128).transpose(0, 2, 3, 1, 4)
    qkv_rows = row_pair(qkv_split.reshape(part, 2, pairs * 384), 1)
    qkv_half = pairs * 384 // 2

    picks = labels[:, None] == jnp.arange(class_count)[None, :]
    angles_here = lax.dynamic_slice_in_dim(sinusoid(timesteps, model), rank * part, part, axis=1)
    cond = angles_here + jnp.dot(picks.astype(low), class_table, preferred_element_type=full)
    lift_value, lift_pull = jax.vjp(jax.nn.silu, cond)
    lifted = lift_value.astype(low)
    mods_part = jnp.dot(lifted, mod_weight, preferred_element_type=full)

    slot = Slots(jnp.zeros((8, 128), full))
    near = lambda *shards: Flow(near_steps(shards, chip_bits))
    sums = lambda *parts: scatter_flow(parts, chip, chip_bits)
    joined = lambda flow: [
        assemble(pieces, gather_order(chip_bits, colour), chip)
        for colour, pieces in enumerate(flow.result)
    ]
    mods_flow = scatter_flow([mods_part], chip, chip_bits, sent=full)
    qkv_near = near(qkv_rows)
    proj_there = [(r, r % chips * 2 + r // chips) for r in range(devices)]
    proj_back = [(b, a) for a, b in proj_there]

    def first_work():
        phases = [to_phases(array[0], half_rows) for array in (tokens, cotangent)]
        return *phases, lax.ppermute(proj_weight, AXES, proj_there)

    mine, upstream, proj_rows = slot([qkv_near, mods_flow], first_work)

    up_weight, ffn_kernel, attn_kernel = slot.after(up_weight, ffn_kernel, attn_kernel)
    up_split = up_weight.reshape(part, chips, 2, CHUNKS, piece).transpose(0, 2, 3, 1, 4)
    up_rows = row_pair(up_split.reshape(part, 2, CHUNKS, chips * piece), 1)
    proj_flow = Flow(one_colour_steps(proj_rows, chip_bits))
    canvas = slot(
        [qkv_near, mods_flow, proj_flow], lambda: join_halves(mine, swap_core(mine), core)
    )
    slot.finish([qkv_near])
    tap_count = 9 * (share + part)
    tap_words = jnp.concatenate([ffn_kernel.reshape(-1), attn_kernel.reshape(-1)])
    tap_words = jnp.pad(tap_words, (0, -tap_count % 128))
    taps = run(row_flow(tap_words, rank, chip_bits + 1, 0))
    ffn_taps = taps[:, : 9 * share].reshape(chips, 2, 9, share)
    ffn_taps = at_bit(ffn_taps, 1, core).reshape(chips, 9, CHUNKS, piece)
    ffn_taps = ffn_taps.transpose(2, 1, 0, 3).reshape(CHUNKS, 9, chips * piece).astype(full)
    ffn_taps = jnp.pad(ffn_taps, ((0, 0), (0, 7), (0, 0)))
    attn_taps = taps[:, 9 * share : tap_count].reshape(devices, 9, part)
    attn_taps = attn_taps.transpose(1, 0, 2).reshape(9, model).astype(full)
    attn_taps = jnp.pad(attn_taps, ((0, 7), (0, 0)))

    spot = jnp.arange(PLANE)
    quadrant = 2 * (spot // (PLANE // 2)) + spot % HALF_SIDE // (HALF_SIDE // 2)
    quadrants_here = at_bit(seg_ids, 0, chip)
    segment = jnp.sum(
        jnp.where(quadrant[:, None] == jnp.arange(4)[None, :], quadrants_here[None, :], 0), axis=1
    )
    mask = (segment[:, None] == segment[None, :]).astype(full)

    def far(arrays, where):
        return Flow(far_steps([array[at] for array, at in zip(arrays, where)]))

    wide = chips * piece
    later = range(CHUNKS - 1)
    feed_near = [
        near(up_rows[:, 0], down_weight[:piece]),
        near(up_rows[:, 1:].reshape(2 * part, -1), down_weight[piece:]),
    ]
    left, right = (Ellipsis, slice(qkv_half)), (Ellipsis, slice(qkv_half, None))
    qkv_flow = far(qkv_near.result * 2, (left, right))
    slot([qkv_flow, mods_flow, proj_flow, feed_near[0]])
    mods_half = run(mods_flow)
    mods = mods_half + swap_core(mods_half)
    shift_a, scale_a, gate_a, shift_f, scale_f, gate_f = jnp.split(mods, 6)

    mods_a = jnp.concatenate([shift_a[None], scale_a[None], jnp.zeros((6, model), full)], axis=0)

    convolved = slot(
        [qkv_flow, proj_flow, feed_near[0]], lambda: conv_in(canvas, attn_taps, mods_a)
    )
    slot.finish([qkv_flow, feed_near[0]])
    feed_flows = [far(feed_near[0].result, (Ellipsis, Ellipsis))]

    def project_in():
        weight = jnp.concatenate(
            [array.reshape(model, qkv_half) for array in joined(qkv_flow)], axis=1
        )
        return weight, jnp.dot(convolved, weight, preferred_element_type=full).astype(low)

    qkv_full, qkv = slot([proj_flow, feed_flows[0], feed_near[1]], project_in)
    (upstream,) = slot.after(upstream)
    grad_ph = join_halves(upstream, swap_core(upstream), core)
    slot.finish([proj_flow])

    def attend_and_assemble():
        weight = assemble(proj_flow.result, gather_order(chip_bits, 0), chip)
        return attend(mask, qkv), weight.reshape(-1, model)

    attended, proj_full = slot([feed_flows[0], feed_near[1]], attend_and_assemble)
    slot.finish([feed_near[1]])
    for t in later:
        columns, rows = slice(t * wide, t * wide + wide), slice(t * piece, t * piece + piece)
        feed_flows.append(far(feed_near[1].result, ((Ellipsis, columns), (slice(None), rows))))

    mods_f = jnp.concatenate(
        [gate_a[None], shift_f[None], scale_f[None], gate_f[None], jnp.zeros((4, model), full)]
    )

    def project_out():
        branch_part = jnp.dot(attended, proj_full, preferred_element_type=full).astype(low)
        other = swap_core(branch_part)
        return branch_part, other, *enter_feed(canvas, branch_part, other, grad_ph, mods_f)

    branch_part, branch_other, norm, norm_t, grad_branch_f = slot(feed_flows[:2], project_out)

    kept = []
    grads = [None] * CHUNKS

    spread = 2 * part % STRIP == 0 and piece % STRIP == 0 and chips >= 8
    up_owner, _ = owners(0, chip, chip_bits)
    down_owner, down_place = owners(1, chip, chip_bits)
    words = jnp.concatenate([core[None], up_owner, down_owner, down_place]).astype(jnp.int32)

    def feed(t):
        def work():
            if spread:
                up, down = feed_flows[t].result
            else:
                up, down = joined(feed_flows[t])
                up, down = [up.reshape(model, -1)], [down.reshape(-1, model)]
            return feed_forward(norm, norm_t, grad_branch_f, up, down, ffn_taps[t], words)

        return work

    back_flows = [[] for _ in range(CHUNKS)]

    def run_feed(flows, t):
        slot.finish(feed_flows[t : t + 1])
        staying, leaving, up_grad, down_grad, tap_grad = slot(flows, feed(t))
        kept.append((staying, Flow(core_steps(leaving))))
        grads[t] = tap_grad
        if spread:
            back_flows[t] = [
                Flow(halving_steps(*grad[::-1], gather_order(chip_bits, colour)[::-1]))
                for colour, grad in enumerate((up_grad, down_grad))
            ]
        else:
            back_flows[t] = [
                sums(up_grad[0].reshape(chips, 2 * part, -1)),
                sums(down_grad[0].reshape(chips, piece, model)),
            ]

    run_feed(feed_flows[1:], 0)
    run_feed(feed_flows[2:] + back_flows[0] + [kept[0][1]], 1)
    run_feed(back_flows[0] + back_flows[1] + [kept[1][1]], 2)

    def after_feed():
        parts = [array for staying, exchange in kept for array in (staying, run(exchange))]
        return leave_feed(words[:1], canvas, branch_part, branch_other, grad_ph, mods_f, parts)

    layer_out, grad_middle, grad_branch_mine, feed_sums = slot(
        back_flows[0] + back_flows[2], after_feed
    )
    grad_branch_mine = grad_branch_mine.reshape(4, -1, model)
    layer_out = from_phases(layer_out.reshape(4, -1, model), half_rows)[None]

    def enter_attend():
        grad_branch_a = join_halves(grad_branch_mine, swap_core(grad_branch_mine), core)
        grad_attended = jnp.dot(grad_branch_a, proj_full.T, preferred_element_type=full)
        proj_grad = jnp.dot(attended.T, grad_branch_a, preferred_element_type=full)
        return grad_attended.astype(low), proj_grad.astype(low)

    grad_attended, proj_grad = slot(back_flows[0] + back_flows[1], enter_attend)
    proj_grad = proj_grad.reshape(chips, -1, model)
    proj_flow = sums(proj_grad)
    grad_qkv = slot(
        [proj_flow] + back_flows[1] + back_flows[2], lambda: attend_back(mask, qkv, grad_attended)
    )
    qkv_grad = slot(
        [proj_flow] + back_flows[1],
        lambda: jnp.dot(convolved.T, grad_qkv, preferred_element_type=full).astype(low),
    )
    qkv_grad = qkv_grad.reshape(chips, 2 * part, -1)
    qkv_flow = sums(qkv_grad[..., :qkv_half], qkv_grad[..., qkv_half:])

    def rows_near(array, which):
        size = PLANE // 2 + STRIP
        near = lax.dynamic_slice_in_dim(
            array.reshape(4, PLANE, model), which * (PLANE - size), size, axis=1
        )
        return near.reshape(4 * size, model)

    def leave_attend():
        part_here = jnp.dot(grad_qkv, qkv_full.T, preferred_element_type=full).astype(low)
        return rows_near(part_here, core), swap_core(rows_near(part_here, 1 - core))

    grad_conv = slot([qkv_flow] + back_flows[2], leave_attend)

    def leave_block():
        input_grad, attn_tap_grad, mods_grad = conv_back(
            core, rows_near(canvas, core), *grad_conv, attn_taps, mods_a,
            grad_middle,
        )
        return attn_tap_grad[:9], input_grad, mods_grad[:2]

    attn_tap_grad, input_grad, attn_sums = slot(
        [qkv_flow, proj_flow] + back_flows[2], leave_block
    )
    def row_split(array, axis):
        pair = array.reshape((2, part) + array.shape[1:])
        kept, leaving = halves_of(pair, 0)
        arriving = swap_core(leaving)
        return jnp.stack(in_core_order(kept, arriving, core), axis=axis)

    slot.finish(sum(back_flows, []))
    grad_mods = jnp.concatenate([attn_sums, feed_sums[:4]], axis=0)
    tap_grads = [g[:9].reshape(9, chips, piece) for g in grads]
    ffn_tap_grad = jnp.concatenate(tap_grads, axis=2).transpose(1, 0, 2)
    attn_kept, attn_leaving = halves_of(attn_tap_grad.reshape(9, chips, 2, part), 2)

    def between_cores():
        both = (grad_mods + swap_core(grad_mods)).astype(low)
        return both, attn_kept + swap_core(attn_leaving)

    grad_mods, attn_tap_grad = slot([qkv_flow, proj_flow], between_cores)
    mods_flow = row_flow(grad_mods.reshape(-1), chip, chip_bits)
    tap_parts = jnp.concatenate(
        [ffn_tap_grad.reshape(chips, -1), attn_tap_grad.transpose(1, 0, 2).reshape(chips, -1)],
        axis=1,
    )
    tap_flow = scatter_flow([tap_parts], chip, chip_bits, sent=full)
    up_shares = slot.after(*[flows[0].result for flows in back_flows])
    down_shares = [flows[1].result for flows in back_flows]

    def split_up():
        up_all = jnp.stack(up_shares, axis=1).reshape(2 * part, CHUNKS, chips, piece)
        return row_split(up_all.transpose(0, 2, 1, 3), 2).reshape(part, -1)

    slot.finish([proj_flow])
    proj_share = proj_flow.result
    up_share = slot([qkv_flow, mods_flow, tap_flow], split_up)
    slot.finish([qkv_flow])
    qkv_share = qkv_flow.result

    def split_qkv():
        qkv_all = qkv_share.reshape(2 * part, pairs, 3, 128).transpose(0, 2, 1, 3)
        qkv_out = row_split(qkv_all, 2).reshape(part, -1)
        return qkv_out, lax.ppermute(proj_share, AXES, proj_back)

    qkv_out, proj_share = slot([mods_flow, tap_flow], split_qkv)
    slot.finish([mods_flow, tap_flow])
    down_share = jnp.concatenate(down_shares, axis=0)

    grad_mods_all = mods_flow.result
    mod_grad = jnp.dot(lifted.T, grad_mods_all, preferred_element_type=full)
    (cond_grad,) = lift_pull(jnp.dot(grad_mods_all, mod_weight.T, preferred_element_type=full))
    table_grad = jnp.dot(picks.astype(full).T, cond_grad, precision=highest)
    tap_share = tap_flow.result
    ffn_share = tap_share[: 9 * share].reshape(9, share)
    kernel_share = tap_share[9 * share :].reshape(9, part)

    return (
        layer_out,
        input_grad[None],
        mod_grad,
        table_grad,
        kernel_share,
        qkv_out,
        proj_share,
        up_share,
        ffn_share,
        down_share,
        feed_sums[1:2],
    )


def solution(mesh):
    return jax.shard_map(
        on_device,
        mesh=mesh,
        in_specs=(
            P(AXES, None, None),
            P(),
            P(),
            P(),
            P(AXES, None, None),
            P(AXES, None),
            P(None, AXES),
            P(None, AXES),
            P(AXES, None),
            P(AXES, None),
            P(AXES, None),
            P(None, AXES),
            P(AXES, None),
        ),
        out_specs=(
            P(AXES, None, None),
            P(AXES, None, None),
            P(AXES, None),
            P(None, AXES),
            P(None, AXES),
            P(AXES, None),
            P(AXES, None),
            P(AXES, None),
            P(None, AXES),
            P(AXES, None),
            P(AXES, None),
        ),
        check_vma=False,
    )
```

```python
import functools
import math

import jax
import jax.numpy as jnp
from jax import lax
from jax.experimental import pallas as pl
from jax.experimental.pallas import tpu as pltpu
from jax.sharding import PartitionSpec as P

HEAD = 64
SIDE = 32
HALF_SIDE = SIDE // 2
STRIP = HALF_SIDE
PLANE = HALF_SIDE * HALF_SIDE
PADDED = PLANE + 2 * STRIP
TILE = 256
CHUNKS = 3

highest = lax.Precision.HIGHEST
ln_epsilon = 1e-06
masked_score = -1000000000.0
low = jnp.bfloat16
full = jnp.float32
AXES = ("dp", "fsdp")


def device_count():
    return lax.axis_size("dp") * lax.axis_size("fsdp")


def swap(x, bit):
    return lax.ppermute(x, AXES, [(i, i ^ 1 << bit) for i in range(device_count())])


def swap_core(x):
    return swap(x, 0)


def gather_order(chip_bits, colour):
    order = list(range(chip_bits - 1, -1, -1))
    if colour and chip_bits > 1:
        order[-1], order[-2] = order[-2], order[-1]
    return order


class Flow:
    def __init__(self, steps):
        self.steps = steps
        self.wanted = next(steps)
        self.result = None

    def arrive(self, array):
        try:
            self.wanted = self.steps.send(array)
        except StopIteration as end:
            self.wanted, self.result = None, end.value


class Slots:
    def __init__(self, token):
        self.token = token

    def after(self, *arrays):
        arrays, self.token = lax.optimization_barrier((arrays, self.token))
        return arrays

    def finish(self, flows):
        while any(flow.wanted is not None for flow in flows):
            self(flows)

    def __call__(self, flows, work=lambda: ()):
        flows = [flow for flow in flows if flow.wanted is not None]
        wanted = [flow.wanted for flow in flows]
        leaving, self.token = lax.optimization_barrier(
            ([[array for array, _ in pairs] for pairs in wanted], self.token)
        )
        arriving = [
            [swap(array, bit + 1) for array, (_, bit) in zip(arrays, pairs)]
            for arrays, pairs in zip(leaving, wanted)
        ]
        arriving, result, self.token = lax.optimization_barrier((arriving, work(), self.token))
        for flow, arrays in zip(flows, arriving):
            flow.arrive(arrays)
        return result


def join(held, arriving):
    return [jnp.concatenate(pair, axis=0) for pair in zip(held, arriving)]


def near_steps(shards, chip_bits):
    held = [shard[None] for shard in shards]
    for bit in range(chip_bits - 1, 1, -1):
        arriving = yield [(array, bit) for array in held]
        held = join(held, arriving)
    return held


def one_colour_steps(shard, chip_bits):
    held = shard[None]
    for bit in range(chip_bits - 1, 0, -1):
        (arriving,) = yield [(held, bit)]
        held = jnp.concatenate([held, arriving], axis=0)
    (arriving,) = yield [(held, 0)]
    return held, arriving


def core_steps(array):
    (arriving,) = yield [(array, -1)]
    return arriving


def far_steps(held):
    arriving = yield [(held[0], 1), (held[1], 0)]
    held = join(held, arriving)
    arriving = yield [(held[0], 0), (held[1], 1)]
    return list(zip(held, arriving))


def assemble_body(steps, chip_ref, *refs):
    *piece_refs, out_ref = refs
    which = pl.program_id(0) // steps
    top = chip_ref[1]
    for index, piece_ref in enumerate(piece_refs):

        @pl.when(which == index)
        def _():
            for k in range(4):
                out_ref[jnp.bitwise_xor(top, (k & 1) << 1 | k >> 1), 0] = piece_ref[k]


def assemble(pieces, order, chip):
    chips = sum(piece.shape[0] for piece in pieces)
    rows, columns = pieces[0].shape[1:]
    if chips < 4 or len(pieces) * pieces[0].shape[0] != chips or pieces[0].shape[0] % 4:
        raise ValueError("unexpected mesh")
    rest = len(order) - 2
    steps = pieces[0].shape[0] // 4
    chip_words = jnp.stack([jnp.bitwise_and(chip, (1 << rest) - 1), chip >> rest]).astype(jnp.int32)

    def out_map(step, words):
        at = words[0]
        for position, bit in enumerate(order[2:]):
            at = jnp.bitwise_xor(at, jnp.bitwise_and(step >> position, 1) << bit)
        return (0, at, 0, 0)

    def piece_map(index):
        return lambda step, words: (jnp.clip(step - index * steps, 0, steps - 1), 0, 0)

    out = pl.pallas_call(
        functools.partial(assemble_body, steps),
        grid_spec=pltpu.PrefetchScalarGridSpec(
            num_scalar_prefetch=1,
            grid=(chips // 4,),
            in_specs=[
                pl.BlockSpec((4, rows, columns), piece_map(index)) for index in range(len(pieces))
            ],
            out_specs=pl.BlockSpec((4, 1, rows, columns), out_map),
        ),
        out_shape=jax.ShapeDtypeStruct((4, chips // 4, rows, columns), pieces[0].dtype),
        cost_estimate=pl.CostEstimate(
            flops=0, bytes_accessed=4 * chips * rows * columns, transcendentals=0
        ),
        name="assemble",
    )(chip_words, *pieces)
    return out.reshape(chips, rows, columns)


def at_bit(array, axis, bit):
    return lax.dynamic_index_in_dim(array, bit, axis, keepdims=False)


def halves_at(held, axis, mine, sent):
    leaving = sum(at_bit(h, axis, 1 - mine).astype(full) for h in held).astype(sent)
    staying = sum(at_bit(h, axis, mine).astype(full) for h in held).astype(sent)
    return leaving, staying


def scatter_steps(parts, chip, chip_bits, sent):
    orders = [gather_order(chip_bits, colour)[::-1] for colour in range(len(parts))]
    lefts = [list(range(chip_bits - 1, -1, -1)) for _ in parts]
    held = [[array.reshape((2,) * chip_bits + array.shape[1:])] for array in parts]
    for step in range(chip_bits):
        if step == 2 and len(held) == 2:
            held = [[jnp.concatenate(pair, axis=-1) for pair in zip(*held)]]
        leaving, staying = [], []
        for order, left, arrays in zip(orders, lefts, held):
            bit = order[step]
            axis = left.index(bit)
            left.remove(bit)
            going, kept = halves_at(arrays, axis, jnp.bitwise_and(chip >> bit, 1), sent)
            leaving.append((going, bit))
            staying.append(kept)
        arriving = yield leaving
        held = [list(pair) for pair in zip(staying, arriving)]
    ((kept, arrived),) = held
    return kept.astype(full) + arrived.astype(full)


def halving_steps(leaving, staying, order):
    (arriving,) = yield [(leaving, order[0])]
    for bit in order[1:]:
        half = staying.shape[0] // 2
        leaving, staying = [
            (staying[at].astype(full) + arriving[at].astype(full)).astype(low)
            for at in (slice(half, None), slice(half))
        ]
        (arriving,) = yield [(leaving, bit)]
    return (staying.astype(full) + arriving.astype(full))[0]


def owners(colour, chip, chip_bits):
    order = gather_order(chip_bits, colour)
    spots = jnp.arange(1 << chip_bits)
    bits = list(enumerate(order))
    owner = sum((jnp.bitwise_and(spots >> at, 1) << bit) for at, bit in bits)
    apart = jnp.bitwise_xor(spots, chip)
    place = sum((jnp.bitwise_and(apart >> bit, 1) << at) for at, bit in bits)
    return jnp.bitwise_xor(owner, chip), place


def scatter_flow(parts, chip, chip_bits, sent=low):
    return Flow(scatter_steps(parts, chip, chip_bits, sent))


def row_steps(row, chip, chip_bits, first_bit):
    held = row[None]
    for bit in range(chip_bits):
        (arriving,) = yield [(held, bit + first_bit - 1)]
        held = jnp.concatenate([held, arriving], axis=0)
    places = jnp.arange(1 << chip_bits)
    pick = jnp.bitwise_xor(places, chip)[:, None] == places[None, :]
    return jnp.dot(pick.astype(held.dtype), held, preferred_element_type=full).astype(held.dtype)


def row_flow(row, chip, chip_bits, first_bit=1):
    return Flow(row_steps(row, chip, chip_bits, first_bit))


def run(flow):
    while flow.wanted is not None:
        flow.arrive([swap(array, bit + 1) for array, bit in flow.wanted])
    return flow.result


def to_phases(block_in, row_count):
    width = block_in.shape[-1]
    split_grid = block_in.reshape(row_count // 2, 2, HALF_SIDE, 2, width)
    return split_grid.transpose(1, 3, 0, 2, 4).reshape(4, row_count // 2 * HALF_SIDE, width)


def from_phases(block_in, row_count):
    width = block_in.shape[-1]
    split_grid = block_in.reshape(2, 2, row_count // 2, HALF_SIDE, width)
    return split_grid.transpose(2, 0, 3, 1, 4).reshape(row_count * SIDE, width)


def in_core_order(mine, other, core):
    return jnp.where(core == 0, mine, other), jnp.where(core == 0, other, mine)


def join_halves(mine, other, core):
    return jnp.stack(in_core_order(mine, other, core), axis=1).reshape(-1, mine.shape[-1])


def half_of(joined, which):
    width = joined.shape[-1]
    return at_bit(joined.reshape(4, 2, -1, width), 1, which)


def layer_norm(values):
    average = jnp.mean(values, axis=-1, keepdims=True)
    centred = values - average
    variance = jnp.mean(centred * centred, axis=-1, keepdims=True)
    return centred * lax.rsqrt(variance + ln_epsilon)


def modulate(values, shift_by, scale_by):
    return layer_norm(values) * (1.0 + scale_by) + shift_by


def sinusoid(steps_in, width):
    halfway = width // 2
    frequency = jnp.exp(-math.log(10000.0) * jnp.arange(halfway, dtype=jnp.float32) / halfway)
    angles = steps_in.astype(jnp.float32)[..., None] * frequency
    return jnp.concatenate([jnp.cos(angles), jnp.sin(angles)], axis=-1)


def softmax_of(query, key, allowed):
    raw = lax.dot_general(query, key, (((1,), (1,)), ((), ())), preferred_element_type=full)
    scores = jnp.where(allowed, raw * HEAD ** (-0.5), masked_score)
    shifted = jnp.exp(scores - jnp.max(scores, axis=-1, keepdims=True))
    return shifted / jnp.sum(shifted, axis=-1, keepdims=True)


def head_lanes(shape, head):
    lanes = lax.broadcasted_iota(jnp.int32, shape, 1)
    return jnp.logical_and(lanes >= head * HEAD, lanes < (head + 1) * HEAD)


def attend_body(mask_ref, qkv_ref, out_ref):
    allowed = mask_ref[...] > 0.5

    @pl.loop(0, 4)
    def _(phase):
        rows = pl.ds(pl.multiple_of(phase * PLANE, PLANE), PLANE)
        query = qkv_ref[rows, :128]
        key = qkv_ref[rows, 128:256]
        value = qkv_ref[rows, 256:]
        total = None
        for head in range(2):
            here = head_lanes(key.shape, head)
            probs = softmax_of(query, jnp.where(here, key, jnp.zeros_like(key)), allowed)
            part = jnp.dot(
                probs.astype(low),
                jnp.where(here, value, jnp.zeros_like(value)),
                preferred_element_type=full,
            )
            total = part if total is None else total + part
        out_ref[rows, :] = total.astype(low)


def attend_back_body(mask_ref, qkv_ref, grad_ref, out_ref):
    allowed = mask_ref[...] > 0.5

    @pl.loop(0, 4)
    def _(phase):
        rows = pl.ds(pl.multiple_of(phase * PLANE, PLANE), PLANE)
        query = qkv_ref[rows, :128]
        key = qkv_ref[rows, 128:256]
        value = qkv_ref[rows, 256:]
        grad = grad_ref[rows, :]
        by_rows = (((0,), (0,)), ((), ()))
        totals = [None, None, None]
        for head in range(2):
            here = head_lanes(key.shape, head)
            blank = jnp.zeros_like(key)
            key_here = jnp.where(here, key, blank)
            query_here = jnp.where(here, query, blank)
            value_here = jnp.where(here, value, blank)
            grad_here = jnp.where(here, grad, blank)
            weights = softmax_of(query, key_here, allowed)
            grad_probs = lax.dot_general(
                grad, value_here, (((1,), (1,)), ((), ())), preferred_element_type=full
            )
            delta = jnp.sum(grad_probs * weights, axis=-1, keepdims=True)
            grad_scores = (weights * (grad_probs - delta)).astype(low)
            parts = (
                jnp.dot(grad_scores, key_here, preferred_element_type=full),
                lax.dot_general(grad_scores, query_here, by_rows, preferred_element_type=full),
                lax.dot_general(
                    weights.astype(low), grad_here, by_rows, preferred_element_type=full
                ),
            )
            totals = [p if t is None else t + p for t, p in zip(totals, parts)]
        out_ref[rows, :128] = (totals[0] * HEAD ** (-0.5)).astype(low)
        out_ref[rows, 128:256] = (totals[1] * HEAD ** (-0.5)).astype(low)
        out_ref[rows, 256:] = totals[2].astype(low)


def attend(mask, qkv):
    tokens, width = qkv.shape
    pairs = width // 384
    return pl.pallas_call(
        attend_body,
        grid=(pairs,),
        in_specs=[
            pl.BlockSpec((PLANE, PLANE), lambda j: (0, 0)),
            pl.BlockSpec((tokens, 384), lambda j: (0, j)),
        ],
        out_specs=pl.BlockSpec((tokens, 128), lambda j: (0, j)),
        out_shape=jax.ShapeDtypeStruct((tokens, pairs * 128), low),
        cost_estimate=pl.CostEstimate(
            flops=pairs * 2 * 4 * 4 * PLANE * PLANE * 256,
            bytes_accessed=8 * tokens * pairs * 128,
            transcendentals=pairs * 8 * PLANE * PLANE,
        ),
        name="attend",
    )(mask, qkv)


def attend_back(mask, qkv, grad):
    tokens, width = qkv.shape
    pairs = width // 384
    return pl.pallas_call(
        attend_back_body,
        grid=(pairs,),
        in_specs=[
            pl.BlockSpec((PLANE, PLANE), lambda j: (0, 0)),
            pl.BlockSpec((tokens, 384), lambda j: (0, j)),
            pl.BlockSpec((tokens, 128), lambda j: (0, j)),
        ],
        out_specs=pl.BlockSpec((tokens, 384), lambda j: (0, j)),
        out_shape=jax.ShapeDtypeStruct((tokens, width), low),
        cost_estimate=pl.CostEstimate(
            flops=pairs * 2 * 4 * 10 * PLANE * PLANE * 256,
            bytes_accessed=14 * tokens * pairs * 128,
            transcendentals=pairs * 8 * PLANE * PLANE,
        ),
        name="attend_back",
    )(mask, qkv, grad)


def strip_at(ref, row_phase, column_phase, row):
    start = pl.multiple_of((row + 1) * STRIP, STRIP)
    return ref[2 * row_phase + column_phase, pl.ds(start, STRIP), :]


def near_strips(ref, row):
    tokens = lax.broadcasted_iota(jnp.int32, (STRIP, ref.shape[-1]), 0)
    loaded = {}
    for row_phase, at in ((1, row - 1), (0, row), (1, row), (0, row + 1)):
        even = strip_at(ref, row_phase, 0, at)
        odd = strip_at(ref, row_phase, 1, at)
        before = jnp.where(tokens == 0, 0.0, pltpu.roll(odd, 1, 0))
        after = jnp.where(tokens == STRIP - 1, 0.0, pltpu.roll(even, STRIP - 1, 0))
        loaded[len(loaded)] = ((before, even, odd), (even, odd, after))
    return {0: (loaded[0], loaded[1], loaded[2]), 1: (loaded[1], loaded[2], loaded[3])}


def conv_strip(near, kernel, row_phase, column_phase):
    total = None
    for i in range(3):
        for j in range(3):
            term = near[row_phase][i][column_phase][j] * kernel[3 * i + j : 3 * i + j + 1, :]
            total = term if total is None else total + term
    return total


def feed_body(
    spread,
    words_ref,
    norm_ref,
    norm_t_ref,
    grad_ref,
    *refs,
):
    pieces = 2 if spread else 1
    up_refs, refs = refs[:pieces], refs[pieces:]
    down_refs, refs = refs[:pieces], refs[pieces:]
    kernel_ref, staying_ref, leaving_ref, *refs = refs
    up_grad_refs, refs = refs[:pieces], refs[pieces:]
    down_grad_refs, refs = refs[:pieces], refs[pieces:]
    kernel_grad_ref, branch_acc, back_acc, hidden, widened_grad, act_grad, act, hidden_grad = refs[
        :8
    ]
    step = pl.program_id(0)
    core = words_ref[0]
    by_columns = (((1,), (1,)), ((), ()))
    width = kernel_ref.shape[1]
    model = norm_t_ref.shape[0]
    up_ref, down_ref = up_refs[0], down_refs[0]
    if spread:
        up_ref, down_all = refs[8:]
        half, share, _ = up_refs[0].shape
        piece = down_refs[0].shape[1]
        chips = 2 * half
        down_ref = down_all.at[pl.ds(pl.multiple_of(step * width, width), width), :]

        for which in range(2):

            @pl.loop(0, half)
            def _(spot):
                start = pl.multiple_of(words_ref[1 + which * half + spot] * share, share)
                up_ref[pl.ds(start, share), :] = up_refs[which][spot]

            @pl.when(step == 0)
            def _():
                @pl.loop(0, half)
                def _(spot):
                    owner = words_ref[1 + chips + which * half + spot]
                    start = pl.multiple_of(owner * piece, piece)
                    down_all[pl.ds(start, piece), :] = down_refs[which][spot]

    @pl.when(step == 0)
    def _():
        blank = jnp.zeros((STRIP, width), full)
        for plane in range(4):
            for ref in (hidden, widened_grad):
                ref[plane, pl.ds(0, STRIP), :] = blank
                ref[plane, pl.ds(PLANE + STRIP, STRIP), :] = blank
        branch_acc[...] = jnp.zeros_like(branch_acc)
        back_acc[...] = jnp.zeros_like(back_acc)

    @pl.loop(0, 4)
    def _(plane):
        rows = pl.ds(pl.multiple_of(plane * PLANE, PLANE), PLANE)
        hidden[plane, pl.ds(STRIP, PLANE), :] = jnp.dot(
            norm_ref[rows, :], up_ref[...], preferred_element_type=full
        )
        act_grad[rows, :] = lax.dot_general(
            grad_ref[rows, :], down_ref[...], by_columns, preferred_element_type=full
        )

    kernel = kernel_ref[...]

    def forward_strip(row, sums):
        near = near_strips(hidden, row)
        sums = list(sums)
        for row_phase in range(2):
            for column_phase in range(2):
                plane = 2 * row_phase + column_phase
                wide = conv_strip(near, kernel, row_phase, column_phase)
                square = wide * wide
                bend = math.sqrt(2.0 / math.pi) * (wide + 0.044715 * wide * square)
                curve = jnp.tanh(bend)
                half = 0.5 * (1.0 + curve)
                slope = half + 0.5 * wide * (1.0 - curve * curve) * (
                    math.sqrt(2.0 / math.pi) * (1.0 + 3 * 0.044715 * square)
                )
                at = pl.ds(pl.multiple_of(plane * PLANE + row * STRIP, STRIP), STRIP)
                act[at, :] = (wide * half).astype(low)
                grad_here = slope * act_grad[at, :]
                widened_grad[plane, pl.ds(pl.multiple_of((row + 1) * STRIP, STRIP), STRIP), :] = (
                    grad_here
                )
                for i in range(3):
                    for j in range(3):
                        product = near[row_phase][i][column_phase][j] * grad_here
                        sums[3 * i + j] = sums[3 * i + j] + (product[:8] + product[8:])
        return tuple(sums)

    sums = lax.fori_loop(
        0, HALF_SIDE, forward_strip, tuple(jnp.zeros((8, width), full) for _ in range(9))
    )
    kernel_grad_ref[...] = jnp.concatenate(
        [jnp.sum(s, axis=0, keepdims=True) for s in sums] + [jnp.zeros((7, width), full)], axis=0
    )

    flipped = [kernel[8 - t : 9 - t, :] for t in range(9)]
    flipped = jnp.concatenate(flipped, axis=0)

    @pl.loop(0, HALF_SIDE)
    def _(row):
        near = near_strips(widened_grad, row)
        for row_phase in range(2):
            for column_phase in range(2):
                plane = 2 * row_phase + column_phase
                at = pl.ds(pl.multiple_of(plane * PLANE + row * STRIP, STRIP), STRIP)
                hidden_grad[at, :] = conv_strip(near, flipped, row_phase, column_phase).astype(low)

    @pl.loop(0, 4)
    def _(plane):
        rows = pl.ds(pl.multiple_of(plane * PLANE, PLANE), PLANE)
        branch_acc[rows, :] += jnp.dot(act[rows, :], down_ref[...], preferred_element_type=full)
        back_acc[rows, :] += lax.dot_general(
            hidden_grad[rows, :], up_ref[...], by_columns, preferred_element_type=full
        )

    if spread:
        for which in range(2):

            @pl.loop(0, half // 4)
            def _(group):
                lhs = []
                for k in range(4):
                    owner = words_ref[1 + which * half + 4 * group + k]
                    start = pl.multiple_of(owner * share, share)
                    lhs.append(norm_t_ref[pl.ds(start, share), :])
                result = jnp.dot(
                    jnp.concatenate(lhs, axis=0), hidden_grad[...], preferred_element_type=full
                ).astype(low)
                for k in range(4):
                    up_grad_refs[which][4 * group + k] = result[k * share : (k + 1) * share]

    else:

        @pl.loop(0, model // TILE)
        def _(tile):
            rows = pl.ds(pl.multiple_of(tile * TILE, TILE), TILE)
            up_grad_refs[0][rows, :] = jnp.dot(
                norm_t_ref[rows, :], hidden_grad[...], preferred_element_type=full
            ).astype(low)

    down_grad = lax.dot_general(
        act[...], grad_ref[...], (((0,), (0,)), ((), ())), preferred_element_type=full
    ).astype(low)
    if spread:
        for k in range(width // piece):
            place = words_ref[1 + 2 * chips + step * (width // piece) + k]
            for which in range(2):

                @pl.when(place // half == which)
                def _():
                    down_grad_refs[which][place - which * half] = down_grad[
                        k * piece : (k + 1) * piece
                    ]

    else:
        down_grad_refs[0][...] = down_grad

    @pl.when(step == pl.num_programs(0) - 1)
    def _():
        for ref, which in ((staying_ref, core), (leaving_ref, 1 - core)):
            for index, acc in enumerate((branch_acc, back_acc)):
                for plane in range(4):
                    start = plane * PLANE + pl.multiple_of(which * (PLANE // 2), PLANE // 2)
                    ref[index, plane] = acc[pl.ds(start, PLANE // 2), :].astype(low)


def feed_forward(norm, norm_t, grad, up, down, kernel, words):
    tokens, model = norm.shape
    channels = kernel.shape[1]
    width = TILE
    spread = len(up) == 2
    whole = lambda j, words: (0, 0)
    half = lambda j, words: (0, 0, 0, 0)
    across = lambda j, words: (0, j)
    once = pl.Buffered(1)
    piece_scratch = []
    if spread:
        deep = lambda j, words: (0, 0, 0)
        up_spec = pl.BlockSpec(up[0].shape[:2] + (width,), lambda j, words: (0, 0, j))
        down_spec = pl.BlockSpec(down[0].shape, deep, pipeline_mode=once)
        down_grad_spec = pl.BlockSpec(down[0].shape, deep)
        piece_scratch = [pltpu.VMEM((model, width), low), pltpu.VMEM((channels, model), low)]
    else:
        up_spec = pl.BlockSpec((model, width), across)
        down_spec = down_grad_spec = pl.BlockSpec((width, model), lambda j, words: (j, 0))
    halves = jax.ShapeDtypeStruct((2, 4, PLANE // 2, model), low)
    like = lambda arrays: [jax.ShapeDtypeStruct(array.shape, low) for array in arrays]
    out = pl.pallas_call(
        functools.partial(feed_body, spread),
        grid_spec=pltpu.PrefetchScalarGridSpec(
            num_scalar_prefetch=1,
            grid=(channels // width,),
            in_specs=[
                pl.BlockSpec((tokens, model), whole, pipeline_mode=once),
                pl.BlockSpec((model, tokens), whole, pipeline_mode=once),
                pl.BlockSpec((tokens, model), whole, pipeline_mode=once),
                *[up_spec] * len(up),
                *[down_spec] * len(down),
                pl.BlockSpec((16, width), across),
            ],
            out_specs=[
                pl.BlockSpec(halves.shape, half),
                pl.BlockSpec(halves.shape, half),
                *[up_spec] * len(up),
                *[down_grad_spec] * len(down),
                pl.BlockSpec((16, width), across),
            ],
            scratch_shapes=[
                pltpu.VMEM((tokens, model), full),
                pltpu.VMEM((tokens, model), full),
                pltpu.VMEM((4, PADDED, width), full),
                pltpu.VMEM((4, PADDED, width), full),
                pltpu.VMEM((tokens, width), full),
                pltpu.VMEM((tokens, width), low),
                pltpu.VMEM((tokens, width), low),
            ]
            + piece_scratch,
        ),
        out_shape=[halves, halves]
        + like(up)
        + like(down)
        + [jax.ShapeDtypeStruct((16, channels), full)],
        compiler_params=pltpu.CompilerParams(vmem_limit_bytes=63 * 1024 * 1024),
        cost_estimate=pl.CostEstimate(
            flops=12 * tokens * model * channels,
            bytes_accessed=8 * model * channels + 10 * tokens * model,
            transcendentals=tokens * channels,
        ),
        name="feed_forward",
    )(words, norm, norm_t, grad, *up, *down, kernel)
    staying, leaving, *grads, kernel_grad = out
    return staying, leaving, grads[: len(up)], grads[len(up) :], kernel_grad


def token_stats(x_ref, average, scale):
    @pl.loop(0, x_ref.shape[0] // STRIP)
    def _(strip):
        rows = pl.ds(pl.multiple_of(strip * STRIP, STRIP), STRIP)
        values = x_ref[rows, :].astype(full)
        mean = jnp.mean(values, axis=-1, keepdims=True)
        centred = values - mean
        variance = jnp.mean(centred * centred, axis=-1, keepdims=True)
        average[rows, :] = jnp.broadcast_to(mean, (STRIP, 128))
        scale[rows, :] = jnp.broadcast_to(lax.rsqrt(variance + ln_epsilon), (STRIP, 128))


def normed_strip(x_ref, average, scale, rows, columns):
    width = columns.size
    wide = lambda ref: jnp.concatenate([ref[rows, :]] * (width // 128), axis=1)
    return (x_ref[rows, columns].astype(full) - wide(average)) * wide(scale)


def frame_zeros(refs):
    for ref in refs:
        blank = jnp.zeros((STRIP, ref.shape[-1]), full)
        for plane in range(4):
            ref[plane, pl.ds(0, STRIP), :] = blank
            ref[plane, pl.ds(ref.shape[1] - STRIP, STRIP), :] = blank


def conv_in_body(x_ref, kernel_ref, mods_ref, out_ref, average, scale, normed):
    step = pl.program_id(0)
    width = out_ref.shape[1]
    columns = pl.ds(pl.multiple_of(step * width, width), width)

    @pl.when(step == 0)
    def _():
        token_stats(x_ref, average, scale)
        frame_zeros([normed])

    shift_by = mods_ref[0:1, :]
    scale_by = 1.0 + mods_ref[1:2, :]

    @pl.loop(0, HALF_SIDE)
    def _(row):
        for plane in range(4):
            rows = pl.ds(pl.multiple_of(plane * PLANE + row * STRIP, STRIP), STRIP)
            normed[plane, pl.ds(pl.multiple_of((row + 1) * STRIP, STRIP), STRIP), :] = (
                normed_strip(x_ref, average, scale, rows, columns) * scale_by + shift_by
            )

    kernel = kernel_ref[...]

    @pl.loop(0, HALF_SIDE)
    def _(row):
        near = near_strips(normed, row)
        for row_phase in range(2):
            for column_phase in range(2):
                plane = 2 * row_phase + column_phase
                at = pl.ds(pl.multiple_of(plane * PLANE + row * STRIP, STRIP), STRIP)
                out_ref[at, :] = conv_strip(near, kernel, row_phase, column_phase).astype(low)


def conv_in(canvas, kernel, mods):
    tokens, model = canvas.shape
    return pl.pallas_call(
        conv_in_body,
        grid=(model // TILE,),
        in_specs=[
            pl.BlockSpec((tokens, model), lambda j: (0, 0), pipeline_mode=pl.Buffered(1)),
            pl.BlockSpec((16, TILE), lambda j: (0, j)),
            pl.BlockSpec((8, TILE), lambda j: (0, j)),
        ],
        out_specs=pl.BlockSpec((tokens, TILE), lambda j: (0, j)),
        out_shape=jax.ShapeDtypeStruct((tokens, model), low),
        scratch_shapes=[
            pltpu.VMEM((tokens, 128), full),
            pltpu.VMEM((tokens, 128), full),
            pltpu.VMEM((4, PADDED, TILE), full),
        ],
        cost_estimate=pl.CostEstimate(
            flops=30 * tokens * model, bytes_accessed=4 * tokens * model, transcendentals=tokens
        ),
        name="conv_in",
    )(canvas, kernel, mods)


def conv_back_body(
    core_ref,
    x_ref,
    kept_ref,
    arriving_ref,
    kernel_ref,
    mods_ref,
    middle_ref,
    out_ref,
    kernel_grad_ref,
    mods_grad_ref,
    average,
    scale,
    normed,
    upstream,
    held,
    sum_plain,
    sum_normed,
    woven,
):
    step = pl.program_id(0)
    core = core_ref[0]
    width = kept_ref.shape[1]
    near_rows = x_ref.shape[0] // 4 // STRIP
    own_rows = near_rows - 1
    columns = pl.ds(pl.multiple_of(step * width, width), width)

    def near_at(plane, row):
        return pl.ds(pl.multiple_of((plane * near_rows + row) * STRIP, STRIP), STRIP)

    def own_at(plane, row):
        return pl.ds(pl.multiple_of((plane * own_rows + row) * STRIP, STRIP), STRIP)

    @pl.when(step == 0)
    def _():
        token_stats(x_ref, average, scale)
        frame_zeros([normed, upstream])
        sum_plain[...] = jnp.zeros_like(sum_plain)
        sum_normed[...] = jnp.zeros_like(sum_normed)

    shift_by = mods_ref[0:1, :]
    scale_by = 1.0 + mods_ref[1:2, :]

    @pl.loop(0, near_rows)
    def _(row):
        for plane in range(4):
            rows = near_at(plane, row)
            padded = pl.ds(pl.multiple_of((row + 1) * STRIP, STRIP), STRIP)
            normed[plane, padded, :] = (
                normed_strip(x_ref, average, scale, rows, columns) * scale_by + shift_by
            )
            upstream[plane, padded, :] = kept_ref[rows, :].astype(full) + arriving_ref[
                rows, :
            ].astype(full)

    kernel = kernel_ref[...]
    flipped = jnp.concatenate([kernel[8 - t : 9 - t, :] for t in range(9)], axis=0)

    def kernel_strip(row, sums):
        near = near_strips(normed, row + core)
        sums = list(sums)
        for row_phase in range(2):
            for column_phase in range(2):
                grad_here = strip_at(upstream, row_phase, column_phase, row + core)
                for i in range(3):
                    for j in range(3):
                        product = near[row_phase][i][column_phase][j] * grad_here
                        sums[3 * i + j] = sums[3 * i + j] + (product[:8] + product[8:])
        return tuple(sums)

    def fold(sums, rows):
        return jnp.concatenate(
            [jnp.sum(s, axis=0, keepdims=True) for s in sums]
            + [jnp.zeros((rows - len(sums), width), full)],
            axis=0,
        )

    blank = jnp.zeros((8, width), full)
    kernel_grad_ref[...] = fold(lax.fori_loop(0, own_rows, kernel_strip, (blank,) * 9), 16)

    def input_strip(row, sums):
        near = near_strips(upstream, row + core)
        shift_sum, scale_sum = sums
        for row_phase in range(2):
            for column_phase in range(2):
                plane = 2 * row_phase + column_phase
                grad = conv_strip(near, flipped, row_phase, column_phase)
                plain = normed_strip(x_ref, average, scale, near_at(plane, row + core), columns)
                shift_sum = shift_sum + (grad[:8] + grad[8:])
                product = grad * plain
                scale_sum = scale_sum + (product[:8] + product[8:])
                scaled = grad * scale_by
                rows = own_at(plane, row)
                held[step, rows, :] = scaled
                product = scaled * plain
                sum_plain[rows, :] += sum(scaled[:, k : k + 128] for k in range(0, width, 128))
                sum_normed[rows, :] += sum(product[:, k : k + 128] for k in range(0, width, 128))
        return shift_sum, scale_sum

    mods_grad_ref[...] = fold(lax.fori_loop(0, own_rows, input_strip, (blank,) * 2), 8)

    @pl.when(step == pl.num_programs(0) - 1)
    def _():
        model = x_ref.shape[1]

        @pl.loop(0, own_rows)
        def _(row):
            for plane in range(4):
                rows = own_at(plane, row)
                near = near_at(plane, row + core)
                mean_plain = jnp.sum(sum_plain[rows, :], axis=-1, keepdims=True) / model
                mean_normed = jnp.sum(sum_normed[rows, :], axis=-1, keepdims=True) / model
                for block in range(model // width):
                    at = pl.ds(block * width, width)
                    plain = normed_strip(x_ref, average, scale, near, at)
                    spread = jnp.concatenate([scale[near, :]] * (width // 128), axis=1)
                    result = middle_ref[rows, at] + spread * (
                        held[block, rows, :] - mean_plain - plain * mean_normed
                    )
                    for lane in range(0, width, 128):
                        woven[(block * width + lane) // 128, pl.ds(plane % 2, STRIP, stride=2), :] = (
                            result[:, lane : lane + 128]
                        )
                if plane % 2 == 1:
                    start = pl.multiple_of((2 * row + plane // 2) * SIDE, SIDE)
                    for lane in range(model // 128):
                        out_ref[pl.ds(start, SIDE), lane * 128 : lane * 128 + 128] = woven[lane]


def conv_back(core, x_near, kept, arriving, kernel, mods, grad_middle):
    near_tokens, model = x_near.shape
    own_tokens = grad_middle.shape[0]
    once = pl.Buffered(1)
    whole = lambda j, words: (0, 0)
    across = lambda j, words: (0, j)
    padded = near_tokens // 4 + 2 * STRIP
    return pl.pallas_call(
        conv_back_body,
        grid_spec=pltpu.PrefetchScalarGridSpec(
            num_scalar_prefetch=1,
            grid=(model // TILE,),
            in_specs=[
                pl.BlockSpec((near_tokens, model), whole, pipeline_mode=once),
                pl.BlockSpec((near_tokens, TILE), across),
                pl.BlockSpec((near_tokens, TILE), across),
                pl.BlockSpec((16, TILE), across),
                pl.BlockSpec((8, TILE), across),
                pl.BlockSpec((own_tokens, model), whole, pipeline_mode=once),
            ],
            out_specs=[
                pl.BlockSpec((own_tokens, model), whole),
                pl.BlockSpec((16, TILE), across),
                pl.BlockSpec((8, TILE), across),
            ],
            scratch_shapes=[
                pltpu.VMEM((near_tokens, 128), full),
                pltpu.VMEM((near_tokens, 128), full),
                pltpu.VMEM((4, padded, TILE), full),
                pltpu.VMEM((4, padded, TILE), full),
                pltpu.VMEM((model // TILE, own_tokens, TILE), full),
                pltpu.VMEM((own_tokens, 128), full),
                pltpu.VMEM((own_tokens, 128), full),
                pltpu.VMEM((model // 128, SIDE, 128), full),
            ],
        ),
        out_shape=[
            jax.ShapeDtypeStruct((own_tokens, model), full),
            jax.ShapeDtypeStruct((16, model), full),
            jax.ShapeDtypeStruct((8, model), full),
        ],
        cost_estimate=pl.CostEstimate(
            flops=70 * own_tokens * model,
            bytes_accessed=14 * own_tokens * model,
            transcendentals=near_tokens,
        ),
        name="conv_back",
    )(core[None].astype(jnp.int32), x_near, kept, arriving, kernel, mods, grad_middle)


def row_stats(values):
    mean = jnp.mean(values, axis=-1, keepdims=True)
    centred = values - mean
    scale = lax.rsqrt(jnp.mean(centred * centred, axis=-1, keepdims=True) + ln_epsilon)
    return centred * scale, scale


def enter_feed_body(x_ref, part_ref, other_ref, grad_ref, mods_ref, norm_ref, norm_t_ref, out_ref):
    @pl.loop(0, x_ref.shape[0] // STRIP)
    def _(strip):
        rows = pl.ds(pl.multiple_of(strip * STRIP, STRIP), STRIP)
        branch = part_ref[rows, :].astype(full) + other_ref[rows, :].astype(full)
        plain, _ = row_stats(x_ref[rows, :].astype(full) + mods_ref[0:1, :] * branch)
        normed = plain * (1.0 + mods_ref[2:3, :]) + mods_ref[1:2, :]
        norm_ref[rows, :] = normed.astype(low)
        out_ref[rows, :] = (grad_ref[rows, :].astype(full) * mods_ref[3:4, :]).astype(low)

    norm_t_ref[...] = norm_ref[...].T


def enter_feed(canvas, part, other, grad, mods):
    tokens, model = canvas.shape
    rows = PLANE // 2
    along = pl.BlockSpec((rows, model), lambda j: (j, 0))
    return pl.pallas_call(
        enter_feed_body,
        grid=(tokens // rows,),
        in_specs=[along] * 4 + [pl.BlockSpec((8, model), lambda j: (0, 0))],
        out_specs=[along, pl.BlockSpec((model, rows), lambda j: (0, j)), along],
        out_shape=[
            jax.ShapeDtypeStruct((tokens, model), low),
            jax.ShapeDtypeStruct((model, tokens), low),
            jax.ShapeDtypeStruct((tokens, model), low),
        ],
        cost_estimate=pl.CostEstimate(flops=1000, bytes_accessed=1000, transcendentals=0),
        name="enter_feed",
    )(canvas, part, other, grad, mods)


def leave_feed_body(words_ref, x_ref, part_ref, other_ref, grad_ref, mods_ref, *refs):
    *kept_refs, out_ref, middle_grad_ref, branch_grad_ref, sums_ref, totals = refs
    plane = pl.program_id(0)

    @pl.when(plane == 0)
    def _():
        totals[...] = jnp.zeros_like(totals)

    @pl.loop(0, x_ref.shape[0] // STRIP)
    def _(strip):
        rows = pl.ds(pl.multiple_of(strip * STRIP, STRIP), STRIP)
        gate_a, gate_f = mods_ref[0:1, :], mods_ref[3:4, :]
        branch_a = part_ref[rows, :].astype(full) + other_ref[rows, :].astype(full)
        middle = x_ref[rows, :].astype(full) + gate_a * branch_a
        plain, scale = row_stats(middle)
        branch_f = sum(ref[0, 0, rows, :].astype(full) for ref in kept_refs)
        back = sum(ref[1, 0, rows, :].astype(full) for ref in kept_refs)
        grad = grad_ref[rows, :].astype(full)
        out_ref[rows, :] = (middle + gate_f * branch_f).astype(low)
        scaled = back * (1.0 + mods_ref[2:3, :])
        mean_plain = jnp.mean(scaled, axis=-1, keepdims=True)
        mean_normed = jnp.mean(scaled * plain, axis=-1, keepdims=True)
        grad_middle = grad + scale * (scaled - mean_plain - plain * mean_normed)
        middle_grad_ref[rows, :] = grad_middle
        branch_grad_ref[rows, :] = (grad_middle * gate_a).astype(low)
        products = (grad_middle * branch_a, back, back * plain, grad * branch_f)
        for index, product in enumerate(products):
            totals[index] += product[:8] + product[8:]

    @pl.when(plane == pl.num_programs(0) - 1)
    def _():
        lines = [jnp.sum(totals[k], axis=0, keepdims=True) for k in range(4)]
        sums_ref[...] = jnp.concatenate(lines + [jnp.zeros_like(sums_ref[:4])], axis=0)


def leave_feed(words, canvas, part, other, grad, mods, kept):
    model = canvas.shape[1]
    rows = PLANE // 2
    own = pl.BlockSpec((rows, model), lambda j, words: (2 * j + words[0], 0))
    half = pl.BlockSpec((rows, model), lambda j, words: (j, 0))
    whole = pl.BlockSpec((8, model), lambda j, words: (0, 0))
    return pl.pallas_call(
        leave_feed_body,
        grid_spec=pltpu.PrefetchScalarGridSpec(
            num_scalar_prefetch=1,
            grid=(4,),
            in_specs=[own] * 4
            + [whole]
            + [pl.BlockSpec((2, 1, rows, model), lambda j, words: (0, j, 0, 0))] * len(kept),
            out_specs=[half, half, half, whole],
            scratch_shapes=[pltpu.VMEM((4, 8, model), full)],
        ),
        out_shape=[
            jax.ShapeDtypeStruct((4 * rows, model), low),
            jax.ShapeDtypeStruct((4 * rows, model), full),
            jax.ShapeDtypeStruct((4 * rows, model), low),
            jax.ShapeDtypeStruct((8, model), full),
        ],
        cost_estimate=pl.CostEstimate(flops=1000, bytes_accessed=1000, transcendentals=0),
        name="leave_feed",
    )(words, canvas, part, other, grad, mods, *kept)


def on_device(
    tokens,
    seg_ids,
    timesteps,
    labels,
    cotangent,
    mod_weight,
    class_table,
    attn_kernel,
    qkv_weight,
    proj_weight,
    up_weight,
    ffn_kernel,
    down_weight,
):
    devices = device_count()
    chips = devices // 2
    chip_bits = chips.bit_length() - 1
    rank = lax.axis_index("dp") * lax.axis_size("fsdp") + lax.axis_index("fsdp")
    core = rank % 2
    chip = rank // 2
    _, half_tokens, model = tokens.shape
    half_rows = half_tokens // SIDE
    class_count = class_table.shape[0]
    part = model // devices
    share = down_weight.shape[0]
    piece = share // CHUNKS
    pairs = model // HEAD // 4

    def halves_of(array, axis):
        return at_bit(array, axis, core), at_bit(array, axis, 1 - core)

    def row_pair(array, axis):
        kept, leaving = halves_of(array, axis)
        arriving = swap_core(leaving)
        return jnp.concatenate(in_core_order(kept, arriving, core), axis=0)

    qkv_split = qkv_weight.reshape(part, 3, 2, pairs, 128).transpose(0, 2, 3, 1, 4)
    qkv_rows = row_pair(qkv_split.reshape(part, 2, pairs * 384), 1)
    qkv_half = pairs * 384 // 2

    picks = labels[:, None] == jnp.arange(class_count)[None, :]
    angles_here = lax.dynamic_slice_in_dim(sinusoid(timesteps, model), rank * part, part, axis=1)
    cond = angles_here + jnp.dot(picks.astype(low), class_table, preferred_element_type=full)
    lift_value, lift_pull = jax.vjp(jax.nn.silu, cond)
    lifted = lift_value.astype(low)
    mods_part = jnp.dot(lifted, mod_weight, preferred_element_type=full)

    slot = Slots(jnp.zeros((8, 128), full))
    near = lambda *shards: Flow(near_steps(shards, chip_bits))
    sums = lambda *parts: scatter_flow(parts, chip, chip_bits)
    joined = lambda flow: [
        assemble(pieces, gather_order(chip_bits, colour), chip)
        for colour, pieces in enumerate(flow.result)
    ]
    mods_flow = scatter_flow([mods_part], chip, chip_bits, sent=full)
    qkv_near = near(qkv_rows)
    proj_there = [(r, r % chips * 2 + r // chips) for r in range(devices)]
    proj_back = [(b, a) for a, b in proj_there]

    def first_work():
        phases = [to_phases(array[0], half_rows) for array in (tokens, cotangent)]
        return *phases, lax.ppermute(proj_weight, AXES, proj_there)

    mine, upstream, proj_rows = slot([qkv_near, mods_flow], first_work)

    up_weight, ffn_kernel, attn_kernel = slot.after(up_weight, ffn_kernel, attn_kernel)
    up_split = up_weight.reshape(part, chips, 2, CHUNKS, piece).transpose(0, 2, 3, 1, 4)
    up_rows = row_pair(up_split.reshape(part, 2, CHUNKS, chips * piece), 1)
    proj_flow = Flow(one_colour_steps(proj_rows, chip_bits))
    canvas = slot(
        [qkv_near, mods_flow, proj_flow], lambda: join_halves(mine, swap_core(mine), core)
    )
    slot.finish([qkv_near])
    tap_count = 9 * (share + part)
    tap_words = jnp.concatenate([ffn_kernel.reshape(-1), attn_kernel.reshape(-1)])
    tap_words = jnp.pad(tap_words, (0, -tap_count % 128))
    taps = run(row_flow(tap_words, rank, chip_bits + 1, 0))
    ffn_taps = taps[:, : 9 * share].reshape(chips, 2, 9, share)
    ffn_taps = at_bit(ffn_taps, 1, core).reshape(chips, 9, CHUNKS, piece)
    ffn_taps = ffn_taps.transpose(2, 1, 0, 3).reshape(CHUNKS, 9, chips * piece).astype(full)
    ffn_taps = jnp.pad(ffn_taps, ((0, 0), (0, 7), (0, 0)))
    attn_taps = taps[:, 9 * share : tap_count].reshape(devices, 9, part)
    attn_taps = attn_taps.transpose(1, 0, 2).reshape(9, model).astype(full)
    attn_taps = jnp.pad(attn_taps, ((0, 7), (0, 0)))

    spot = jnp.arange(PLANE)
    quadrant = 2 * (spot // (PLANE // 2)) + spot % HALF_SIDE // (HALF_SIDE // 2)
    quadrants_here = at_bit(seg_ids, 0, chip)
    segment = jnp.sum(
        jnp.where(quadrant[:, None] == jnp.arange(4)[None, :], quadrants_here[None, :], 0), axis=1
    )
    mask = (segment[:, None] == segment[None, :]).astype(full)

    def far(arrays, where):
        return Flow(far_steps([array[at] for array, at in zip(arrays, where)]))

    wide = chips * piece
    later = range(CHUNKS - 1)
    feed_near = [
        near(up_rows[:, 0], down_weight[:piece]),
        near(up_rows[:, 1:].reshape(2 * part, -1), down_weight[piece:]),
    ]
    left, right = (Ellipsis, slice(qkv_half)), (Ellipsis, slice(qkv_half, None))
    qkv_flow = far(qkv_near.result * 2, (left, right))
    slot([qkv_flow, mods_flow, proj_flow, feed_near[0]])
    mods_half = run(mods_flow)
    mods = mods_half + swap_core(mods_half)
    shift_a, scale_a, gate_a, shift_f, scale_f, gate_f = jnp.split(mods, 6)

    mods_a = jnp.concatenate([shift_a[None], scale_a[None], jnp.zeros((6, model), full)], axis=0)

    convolved = slot(
        [qkv_flow, proj_flow, feed_near[0]], lambda: conv_in(canvas, attn_taps, mods_a)
    )
    slot.finish([qkv_flow, feed_near[0]])
    feed_flows = [far(feed_near[0].result, (Ellipsis, Ellipsis))]

    def project_in():
        weight = jnp.concatenate(
            [array.reshape(model, qkv_half) for array in joined(qkv_flow)], axis=1
        )
        return weight, jnp.dot(convolved, weight, preferred_element_type=full).astype(low)

    qkv_full, qkv = slot([proj_flow, feed_flows[0], feed_near[1]], project_in)
    (upstream,) = slot.after(upstream)
    grad_ph = join_halves(upstream, swap_core(upstream), core)
    slot.finish([proj_flow])

    def attend_and_assemble():
        weight = assemble(proj_flow.result, gather_order(chip_bits, 0), chip)
        return attend(mask, qkv), weight.reshape(-1, model)

    attended, proj_full = slot([feed_flows[0], feed_near[1]], attend_and_assemble)
    slot.finish([feed_near[1]])
    for t in later:
        columns, rows = slice(t * wide, t * wide + wide), slice(t * piece, t * piece + piece)
        feed_flows.append(far(feed_near[1].result, ((Ellipsis, columns), (slice(None), rows))))

    mods_f = jnp.concatenate(
        [gate_a[None], shift_f[None], scale_f[None], gate_f[None], jnp.zeros((4, model), full)]
    )

    def project_out():
        branch_part = jnp.dot(attended, proj_full, preferred_element_type=full).astype(low)
        other = swap_core(branch_part)
        return branch_part, other, *enter_feed(canvas, branch_part, other, grad_ph, mods_f)

    branch_part, branch_other, norm, norm_t, grad_branch_f = slot(feed_flows[:2], project_out)

    kept = []
    grads = [None] * CHUNKS

    spread = 2 * part % STRIP == 0 and piece % STRIP == 0 and chips >= 8
    up_owner, _ = owners(0, chip, chip_bits)
    down_owner, down_place = owners(1, chip, chip_bits)
    words = jnp.concatenate([core[None], up_owner, down_owner, down_place]).astype(jnp.int32)

    def feed(t):
        def work():
            if spread:
                up, down = feed_flows[t].result
            else:
                up, down = joined(feed_flows[t])
                up, down = [up.reshape(model, -1)], [down.reshape(-1, model)]
            return feed_forward(norm, norm_t, grad_branch_f, up, down, ffn_taps[t], words)

        return work

    back_flows = [[] for _ in range(CHUNKS)]

    def run_feed(flows, t):
        slot.finish(feed_flows[t : t + 1])
        staying, leaving, up_grad, down_grad, tap_grad = slot(flows, feed(t))
        kept.append((staying, Flow(core_steps(leaving))))
        grads[t] = tap_grad
        if spread:
            back_flows[t] = [
                Flow(halving_steps(*grad[::-1], gather_order(chip_bits, colour)[::-1]))
                for colour, grad in enumerate((up_grad, down_grad))
            ]
        else:
            back_flows[t] = [
                sums(up_grad[0].reshape(chips, 2 * part, -1)),
                sums(down_grad[0].reshape(chips, piece, model)),
            ]

    run_feed(feed_flows[1:], 0)
    run_feed(feed_flows[2:] + back_flows[0] + [kept[0][1]], 1)
    run_feed(back_flows[0] + back_flows[1] + [kept[1][1]], 2)

    def after_feed():
        parts = [array for staying, exchange in kept for array in (staying, run(exchange))]
        return leave_feed(words[:1], canvas, branch_part, branch_other, grad_ph, mods_f, parts)

    layer_out, grad_middle, grad_branch_mine, feed_sums = slot(
        back_flows[0] + back_flows[2], after_feed
    )
    grad_branch_mine = grad_branch_mine.reshape(4, -1, model)
    layer_out = from_phases(layer_out.reshape(4, -1, model), half_rows)[None]

    def enter_attend():
        grad_branch_a = join_halves(grad_branch_mine, swap_core(grad_branch_mine), core)
        grad_attended = jnp.dot(grad_branch_a, proj_full.T, preferred_element_type=full)
        proj_grad = jnp.dot(attended.T, grad_branch_a, preferred_element_type=full)
        return grad_attended.astype(low), proj_grad.astype(low)

    grad_attended, proj_grad = slot(back_flows[0] + back_flows[1], enter_attend)
    proj_grad = proj_grad.reshape(chips, -1, model)
    proj_flow = sums(proj_grad)
    grad_qkv = slot(
        [proj_flow] + back_flows[1] + back_flows[2], lambda: attend_back(mask, qkv, grad_attended)
    )
    qkv_grad = slot(
        [proj_flow] + back_flows[1],
        lambda: jnp.dot(convolved.T, grad_qkv, preferred_element_type=full).astype(low),
    )
    qkv_grad = qkv_grad.reshape(chips, 2 * part, -1)
    qkv_flow = sums(qkv_grad[..., :qkv_half], qkv_grad[..., qkv_half:])

    def rows_near(array, which):
        size = PLANE // 2 + STRIP
        near = lax.dynamic_slice_in_dim(
            array.reshape(4, PLANE, model), which * (PLANE - size), size, axis=1
        )
        return near.reshape(4 * size, model)

    def leave_attend():
        part_here = jnp.dot(grad_qkv, qkv_full.T, preferred_element_type=full).astype(low)
        return rows_near(part_here, core), swap_core(rows_near(part_here, 1 - core))

    grad_conv = slot([qkv_flow] + back_flows[2], leave_attend)

    def leave_block():
        input_grad, attn_tap_grad, mods_grad = conv_back(
            core, rows_near(canvas, core), *grad_conv, attn_taps, mods_a,
            grad_middle,
        )
        return attn_tap_grad[:9], input_grad, mods_grad[:2]

    attn_tap_grad, input_grad, attn_sums = slot(
        [qkv_flow, proj_flow] + back_flows[2], leave_block
    )
    def row_split(array, axis):
        pair = array.reshape((2, part) + array.shape[1:])
        kept, leaving = halves_of(pair, 0)
        arriving = swap_core(leaving)
        return jnp.stack(in_core_order(kept, arriving, core), axis=axis)

    slot.finish(sum(back_flows, []))
    grad_mods = jnp.concatenate([attn_sums, feed_sums[:4]], axis=0)
    tap_grads = [g[:9].reshape(9, chips, piece) for g in grads]
    ffn_tap_grad = jnp.concatenate(tap_grads, axis=2).transpose(1, 0, 2)
    attn_kept, attn_leaving = halves_of(attn_tap_grad.reshape(9, chips, 2, part), 2)

    def between_cores():
        both = (grad_mods + swap_core(grad_mods)).astype(low)
        return both, attn_kept + swap_core(attn_leaving)

    grad_mods, attn_tap_grad = slot([qkv_flow, proj_flow], between_cores)
    mods_flow = row_flow(grad_mods.reshape(-1), chip, chip_bits)
    tap_parts = jnp.concatenate(
        [ffn_tap_grad.reshape(chips, -1), attn_tap_grad.transpose(1, 0, 2).reshape(chips, -1)],
        axis=1,
    )
    tap_flow = scatter_flow([tap_parts], chip, chip_bits, sent=full)
    up_shares = slot.after(*[flows[0].result for flows in back_flows])
    down_shares = [flows[1].result for flows in back_flows]

    def split_up():
        up_all = jnp.stack(up_shares, axis=1).reshape(2 * part, CHUNKS, chips, piece)
        return row_split(up_all.transpose(0, 2, 1, 3), 2).reshape(part, -1)

    slot.finish([proj_flow])

    def last_work():
        proj_share = lax.ppermute(proj_flow.result, AXES, proj_back)
        return run(mods_flow), run(tap_flow), split_up(), proj_share

    grad_mods_all, tap_share, up_share, proj_share = slot([qkv_flow], last_work)
    slot.finish([qkv_flow])
    qkv_share = qkv_flow.result

    def split_qkv():
        qkv_all = qkv_share.reshape(2 * part, pairs, 3, 128).transpose(0, 2, 1, 3)
        return row_split(qkv_all, 2).reshape(part, -1)

    qkv_out = split_qkv()
    down_share = jnp.concatenate(down_shares, axis=0)

    mod_grad = jnp.dot(lifted.T, grad_mods_all, preferred_element_type=full)
    (cond_grad,) = lift_pull(jnp.dot(grad_mods_all, mod_weight.T, preferred_element_type=full))
    table_grad = jnp.dot(picks.astype(full).T, cond_grad, precision=highest)
    ffn_share = tap_share[: 9 * share].reshape(9, share)
    kernel_share = tap_share[9 * share :].reshape(9, part)

    return (
        layer_out,
        input_grad[None],
        mod_grad,
        table_grad,
        kernel_share,
        qkv_out,
        proj_share,
        up_share,
        ffn_share,
        down_share,
        feed_sums[1:2],
    )


def solution(mesh):
    return jax.shard_map(
        on_device,
        mesh=mesh,
        in_specs=(
            P(AXES, None, None),
            P(),
            P(),
            P(),
            P(AXES, None, None),
            P(AXES, None),
            P(None, AXES),
            P(None, AXES),
            P(AXES, None),
            P(AXES, None),
            P(AXES, None),
            P(None, AXES),
            P(AXES, None),
        ),
        out_specs=(
            P(AXES, None, None),
            P(AXES, None, None),
            P(AXES, None),
            P(None, AXES),
            P(None, AXES),
            P(AXES, None),
            P(AXES, None),
            P(AXES, None),
            P(None, AXES),
            P(AXES, None),
            P(AXES, None),
        ),
        check_vma=False,
    )
```
